32 devices in a mesh: dp: 16 (over z, y, core), tensor: 2 (over x).
Axes of the slice: x: 2, y: 2, z: 4, core: 2. Of those that a mesh axis runs over, the one named last changes fastest.
Arguments:
- tokens_in: bfloat16 [24576, 1152], P(('dp', 'tensor')), may hold values from -6 to 6
- condition: bfloat16 [96, 1152], P('dp'), may hold values from -6 to 6
- ada_weight: bfloat16 [1152, 6912], replicated, may hold values from -0.1875 to 0.1875
- ada_bias: bfloat16 [6912], replicated, may hold values from -1.75 to 1.75
- qkv_weight: bfloat16 [1152, 3, 1152], P(None, None, 'tensor'), may hold values from -0.1875 to 0.1875
- qv_bias: bfloat16 [2, 1152], P(None, 'tensor'), may hold values from -1.75 to 1.75
- out_weight: bfloat16 [1152, 1152], P('tensor'), may hold values from -2 to 2
- out_bias: bfloat16 [1152], replicated, may hold values from -1.75 to 1.75
- up_weight: bfloat16 [1152, 4608], P(None, 'tensor'), may hold values from -0.1875 to 0.1875
- up_bias: bfloat16 [4608], P('tensor'), may hold values from -1.75 to 1.75
- down_weight: bfloat16 [4608, 1152], P('tensor'), may hold values from -0.09375 to 0.09375
- down_bias: bfloat16 [1152], replicated, may hold values from -1.75 to 1.75
- proj_in: bfloat16 [1152, 2048], replicated, may hold values from -0.1875 to 0.1875
- proj_in_bias: bfloat16 [2048], replicated, may hold values from -1.75 to 1.75
- proj_mid: bfloat16 [2048, 2048], replicated, may hold values from -0.125 to 0.125
- proj_mid_bias: bfloat16 [2048], replicated, may hold values from -1.75 to 1.75
- proj_last: bfloat16 [2048, 768], replicated, may hold values from -0.125 to 0.125
- proj_last_bias: bfloat16 [768], replicated, may hold values from -1.75 to 1.75
- enc_features: bfloat16 [24576, 768], P('dp'), may hold values from -6 to 6
- image_ids: int32 [24576], P('dp'), may hold values from 0 to 5, as said below
- target_rows: int32 [24576], P(('dp', 'tensor')), may hold values from 0 to 24575, as said below
- out_grad: bfloat16 [24576, 1152], P(('dp', 'tensor')), may hold values from -12 to 12
Outputs:
- block_out: bfloat16 [24576, 1152], P(('dp', 'tensor'))
- grad_tokens: float32 [24576, 1152], P(('dp', 'tensor'))
- grad_condition: float32 [96, 1152], P('dp')
- grad_ada_weight: float32 [1152, 6912], P(None, ('dp', 'tensor'))
- grad_ada_bias: float32 [6912], P(('dp', 'tensor'))
- grad_qkv_weight: float32 [1152, 3, 1152], P('dp', None, 'tensor')
- grad_qv_bias: float32 [2, 1152], P(None, 'tensor')
- grad_out_weight: float32 [1152, 1152], P('tensor', 'dp')
- grad_out_bias: float32 [1152], replicated
- grad_up_weight: float32 [1152, 4608], P('dp', 'tensor')
- grad_up_bias: float32 [4608], P('tensor')
- grad_down_weight: float32 [4608, 1152], P('tensor', 'dp')
- grad_down_bias: float32 [1152], replicated
- grad_proj_in: float32 [1152, 2048], P(None, ('dp', 'tensor'))
- grad_proj_in_bias: float32 [2048], replicated
- grad_proj_mid: float32 [2048, 2048], P(None, ('dp', 'tensor'))
- grad_proj_mid_bias: float32 [2048], replicated
- grad_proj_last: float32 [2048, 768], P(None, ('dp', 'tensor'))
- grad_proj_last_bias: float32 [768], replicated
The draws below stay inside these ranges and needn't reach their ends.
Inputs may be any that keep to these rules, and one draw needn't show every extreme that they name: `image_ids`: within each block of 1536 tokens (one index of dp) the ids start at 0 and rise by one from image to image; each image holds 256 or 1024 tokens; a block holds k images of 1024 tokens and 6 - 4 * k of 256, and every k from 0 to 1 occurs in some block. `target_rows`: each token's row is the position, counted over all 24576 tokens, of a token of the same image.
All inputs are finite; a program needn't handle non-finite values.
Results may differ from the reference program's by a relative error of at most 0.025.
Values may be sent and summed in bfloat16 or wider, within the bound.
A program may use at most 576 MiB of HBM per device.

```python
import jax
import jax.numpy as jnp
from jax import lax

D = 1152
HEADS = 16
HEAD_DIM = 72
FF = 4608
PROJ = 2048
ENC = 768
SHORT = 256
UNITS = 6
TOK_DEV = 1536
TOKENS = 24576
IMAGES = 96
N_DP = 16


def image_layout(key):
    most_long = min(2, UNITS // 4)
    offset = jax.random.randint(jax.random.fold_in(key, 11), (), 0, most_long + 1)
    order_key = jax.random.fold_in(key, 12)

    def one_shard(shard):
        long_count = (shard + offset) % (most_long + 1)
        image_count = UNITS - 3 * long_count
        slot = jnp.arange(UNITS, dtype=jnp.int32)
        units = jnp.where(slot < long_count, 4, jnp.where(slot < image_count, 1, 0)).astype(jnp.int32)
        priority = jax.random.permutation(jax.random.fold_in(order_key, shard), UNITS).astype(jnp.int32)
        priority = jnp.where(slot < image_count, priority, UNITS + slot)
        order = jnp.argsort(priority, stable=True)
        lengths = units[order]
        ends = jnp.cumsum(lengths).astype(jnp.int32)
        starts = ends - lengths
        unit_image = jnp.sum((ends[None, :] <= slot[:, None]).astype(jnp.int32), axis=1).astype(jnp.int32)
        return (unit_image, starts[unit_image], lengths[unit_image])
    return jax.vmap(one_shard)(jnp.arange(N_DP, dtype=jnp.int32))


def draw_image_ids(key, part):
    unit_image, unit_start, unit_length = image_layout(key)
    return jnp.repeat(unit_image, SHORT, axis=1).reshape(-1).astype(jnp.int32)


def draw_target_rows(key, part):
    unit_image, unit_start, unit_length = image_layout(key)
    start_tokens = jnp.repeat(unit_start * SHORT, SHORT, axis=1).astype(jnp.int32)
    length_tokens = jnp.repeat(unit_length * SHORT, SHORT, axis=1).astype(jnp.int32)
    picked = jax.random.randint(jax.random.fold_in(key, 13), start_tokens.shape, 0, length_tokens).astype(jnp.int32)
    within = start_tokens + picked
    position = jnp.arange(TOK_DEV, dtype=jnp.int32)[None, :]
    within = jnp.where(position == 0, 0, within)
    within = jnp.where(position == TOK_DEV - 1, TOK_DEV - 1, within)
    base_rows = (jnp.arange(N_DP, dtype=jnp.int32) * TOK_DEV)[:, None]
    return (base_rows + within).reshape(-1).astype(jnp.int32)


def spiked(array, own_key, source, target, shards_of, factor):
    owner, partner = [(jnp.arange(array.shape[axis_at]) // (array.shape[axis_at] // shards_of)).reshape([-1 if axis == axis_at else 1 for axis in range(array.ndim)]) for axis_at in (source, target)]
    chosen = jax.random.permutation(own_key, shards_of)[partner]
    strong = (owner == chosen) | (owner == (partner + shards_of // 2) % shards_of)
    return jnp.where(strong, factor * array, array)


def shard_levels(own_key, shape, pieces, smallest, top_value):
    def one(dim, shards_of):
        heights = jax.random.uniform(jax.random.fold_in(jax.random.fold_in(own_key, 6), dim), (shards_of,), jnp.float32, smallest / len(pieces), top_value / len(pieces))
        return jnp.repeat(jnp.exp(heights), shape[dim] // shards_of).reshape((-1,) + (1,) * (len(shape) - dim - 1))

    level = one(*pieces[0])
    for cut in pieces[1:]:
        level = level * one(*cut)
    return level


def gaussian(stream_key, shape, spread, limit, cuts=(), kind=jnp.bfloat16):
    result = jax.random.normal(stream_key, shape, jnp.float32) * spread
    if len(cuts) > 0:
        result = shard_levels(stream_key, shape, cuts, -0.22, 0.18) * result
    return jnp.clip(result, min=-limit, max=limit).astype(kind)


def gaussian_with(rng, extent, spread, reach, cuts, heavy, kind=jnp.bfloat16):
    array = spread * jax.random.normal(rng, extent, jnp.float32)
    if cuts:
        array = array * shard_levels(rng, extent, cuts, -0.22, 0.18)
    return jnp.clip(spiked(array, jax.random.fold_in(rng, 3), *heavy), -reach, reach).astype(kind)


def setup_inputs(seed: int = 0) -> dict:
    key_list = jax.random.split(jax.random.key(seed), 23)
    tokens_in = gaussian(key_list[0], (TOKENS, D), 1.0, 6.0, ((0, 32),))
    condition = gaussian(key_list[1], (IMAGES, D), 1.0, 6.0, ((0, 16),))
    ada_weight = gaussian(key_list[2], (D, 6 * D), D ** -0.5, 0.1875)
    ada_bias = gaussian(key_list[3], (6 * D,), 0.3, 1.75)
    qkv_weight = gaussian(key_list[4], (D, 3, D), D ** -0.5, 0.1875, ((2, 2),))
    qv_bias = gaussian(key_list[5], (2, D), 0.3, 1.75, ((1, 2),))
    out_weight = gaussian(key_list[6], (D, D), (max(D // 128, 8)) ** -0.5, 2.0, ((0, 2),))
    out_bias = gaussian(key_list[7], (D,), 0.3, 1.75)
    up_weight = gaussian(key_list[8], (D, FF), D ** -0.5, 0.1875, ((1, 2),))
    up_bias = gaussian(key_list[9], (FF,), 0.3, 1.75, ((0, 2),))
    down_weight = gaussian(key_list[10], (FF, D), FF ** -0.5, 0.09375, ((0, 2),))
    down_bias = gaussian(key_list[11], (D,), 0.3, 1.75)
    proj_in = gaussian(key_list[12], (D, PROJ), D ** -0.5, 0.1875)
    proj_in_bias = gaussian(key_list[13], (PROJ,), 0.3, 1.75)
    proj_mid = gaussian(key_list[14], (PROJ, PROJ), PROJ ** -0.5, 0.125)
    proj_mid_bias = gaussian(key_list[15], (PROJ,), 0.3, 1.75)
    proj_last = gaussian(key_list[16], (PROJ, ENC), PROJ ** -0.5, 0.125)
    proj_last_bias = gaussian(key_list[17], (ENC,), 0.3, 1.75)
    enc_features = gaussian(key_list[18], (TOKENS, ENC), 1.0, 6.0, ((0, 16),))
    image_ids = draw_image_ids(jax.random.fold_in(key_list[22], 71), 0)
    target_rows = draw_target_rows(jax.random.fold_in(key_list[22], 71), 0)
    out_grad = gaussian_with(key_list[21], (TOKENS, D), 1.0, 12.0, ((0, 32),), (0, 1, 32, 2.75))
    return {"tokens_in": tokens_in, "condition": condition, "ada_weight": ada_weight, "ada_bias": ada_bias, "qkv_weight": qkv_weight, "qv_bias": qv_bias, "out_weight": out_weight, "out_bias": out_bias, "up_weight": up_weight, "up_bias": up_bias, "down_weight": down_weight, "down_bias": down_bias, "proj_in": proj_in, "proj_in_bias": proj_in_bias, "proj_mid": proj_mid, "proj_mid_bias": proj_mid_bias, "proj_last": proj_last, "proj_last_bias": proj_last_bias, "enc_features": enc_features, "image_ids": image_ids, "target_rows": target_rows, "out_grad": out_grad}


@jax.custom_vjp
def low(v):
    return lax.optimization_barrier(v.astype(jnp.bfloat16)).astype(jnp.float32)

@jax.custom_vjp
def low_back(v):
    return v

def low_keep(v):
    return (low(v), None)

def low_pass(kept, grad):
    return (grad,)

def back_keep(v):
    return (v, None)

def back_low(kept, grad):
    return (low(grad),)
low.defvjp(low_keep, low_pass)
low_back.defvjp(back_keep, back_low)
highest = lax.Precision.HIGHEST
eps_norm = 1e-06
repa_weight = 1000.0
neg_fill = -1e+30

def matmul(left_arg, right_arg):
    return jnp.dot(left_arg, right_arg, precision=highest, preferred_element_type=jnp.float32)

def layer_norm(values):
    center = values - lax.optimization_barrier(jnp.mean(values, axis=-1, keepdims=True))
    return center * lax.rsqrt(lax.optimization_barrier(jnp.mean(center * center, axis=-1, keepdims=True)) + eps_norm)

def gelu_tanh(values):
    return jax.nn.gelu(values, approximate=True)

def align_loss(projected, target_vals):
    inner = lax.optimization_barrier(jnp.sum(projected * target_vals, axis=1))
    norm_pred = lax.rsqrt(lax.optimization_barrier(jnp.sum(projected * projected, axis=1)) + eps_norm)
    norm_target = lax.rsqrt(lax.optimization_barrier(jnp.sum(target_vals * target_vals, axis=1)) + eps_norm)
    return -repa_weight * jnp.sum(inner * norm_pred * norm_target)

def attention(queries, key_rows, values, image_ids):
    scores = low_back(jnp.einsum('qhd,khd->hqk', queries, key_rows, precision=highest) * HEAD_DIM ** (-0.5))
    same_image = image_ids[:, None] == image_ids[None, :]
    scores = jnp.where(same_image[None], scores, neg_fill)
    exponent = jnp.exp(scores - lax.optimization_barrier(jnp.max(scores, axis=2, keepdims=True)))
    weights_soft = low(exponent / lax.optimization_barrier(jnp.sum(exponent, axis=2, keepdims=True)))
    return jnp.einsum('hqk,khd->qhd', weights_soft, values, precision=highest)

def shard_block(weights, features, shard_in):
    cond_float, ada_weight, ada_bias, qkv_weight, qv_bias, out_weight, out_bias, up_weight, up_bias, down_weight, down_bias, proj_in, proj_in_bias, proj_mid, proj_mid_bias, proj_last, proj_last_bias = weights
    tokens_in, image_ids, target_rows, shard_index = shard_in
    condition = lax.dynamic_slice_in_dim(cond_float, shard_index * UNITS, UNITS)
    modulation = low_back(matmul(low(jax.nn.silu(condition)), ada_weight)) + ada_bias
    per_token = modulation[image_ids]
    shift_one, scale_one, gate_one, shift_two, scale_two, gate_two = jnp.split(per_token, 6, axis=1)
    attn_in = low(layer_norm(tokens_in) * (1.0 + scale_one) + shift_one)
    qkv = low_back(jnp.einsum('td,dcf->tcf', attn_in, qkv_weight, precision=highest))
    queries = low(qkv[:, 0] + qv_bias[0]).reshape(TOK_DEV, HEADS, HEAD_DIM)
    key_rows = low(qkv[:, 1]).reshape(TOK_DEV, HEADS, HEAD_DIM)
    values = low(qkv[:, 2] + qv_bias[1]).reshape(TOK_DEV, HEADS, HEAD_DIM)
    attended = low(low_back(attention(queries, key_rows, values, image_ids))).reshape(TOK_DEV, D)
    attn_branch = low_back(matmul(attended, out_weight)) + out_bias
    mid = tokens_in + gate_one * attn_branch
    mlp_in = low(layer_norm(mid) * (1.0 + scale_two) + shift_two)
    pre_act = low_back(matmul(mlp_in, up_weight)) + up_bias
    hidden = low(gelu_tanh(pre_act))
    mlp_branch = low_back(matmul(hidden, down_weight)) + down_bias
    block_value = mid + gate_two * mlp_branch
    block_low = low(block_value)
    first = low(jax.nn.silu(low_back(matmul(block_low, proj_in)) + proj_in_bias))
    second = low(jax.nn.silu(low_back(matmul(first, proj_mid)) + proj_mid_bias))
    projected = low_back(matmul(second, proj_last)) + proj_last_bias
    target_vals = features[target_rows]
    return (block_value, align_loss(projected, target_vals))

def reference(tokens_in, condition, ada_weight, ada_bias, qkv_weight, qv_bias, out_weight, out_bias, up_weight, up_bias, down_weight, down_bias, proj_in, proj_in_bias, proj_mid, proj_mid_bias, proj_last, proj_last_bias, enc_features, image_ids, target_rows, out_grad):
    params = tuple((matrix.astype(jnp.float32) for matrix in (tokens_in, condition, ada_weight, ada_bias, qkv_weight, qv_bias, out_weight, out_bias, up_weight, up_bias, down_weight, down_bias, proj_in, proj_in_bias, proj_mid, proj_mid_bias, proj_last, proj_last_bias)))
    features = enc_features.astype(jnp.float32)
    shard_ids = jnp.arange(N_DP, dtype=jnp.int32)

    def whole(params):
        tokens_float = params[0]
        weights = params[1:]

        def one_shard(shard_in):
            return shard_block(weights, features, shard_in)
        shard_out, shard_loss = lax.map(jax.checkpoint(one_shard), (tokens_float.reshape(N_DP, TOK_DEV, D), image_ids.reshape(N_DP, TOK_DEV), target_rows.reshape(N_DP, TOK_DEV), shard_ids))
        return (shard_out.reshape(TOKENS, D), jnp.sum(shard_loss))
    outputs, pull = jax.vjp(whole, params)
    grads = pull((out_grad.astype(jnp.float32), jnp.ones((), jnp.float32)))[0]
    return (outputs[0].astype(jnp.bfloat16), grads[0], grads[1], grads[2], grads[3], grads[4], grads[5], grads[6], grads[7], grads[8], grads[9], grads[10], grads[11], grads[12], grads[13], grads[14], grads[15], grads[16], grads[17])
```

```python
import functools

import jax
import jax.numpy as jnp
from jax import lax
from jax.experimental import pallas as pl
from jax.experimental.pallas import tpu as pltpu
from jax.sharding import PartitionSpec as P

HEAD_DIM = 72
SHORT = 256


highest = lax.Precision.HIGHEST
eps_norm = 1e-06
repa_weight = 1000.0
neg_fill = -1e30


def dot_nt(left_arg, right_arg):
    return lax.dot_general(
        left_arg, right_arg, (((1,), (1,)), ((), ())), preferred_element_type=jnp.float32
    )


def dot_tn(left_arg, right_arg, precision=None):
    return lax.dot_general(
        left_arg,
        right_arg,
        (((0,), (0,)), ((), ())),
        precision=precision,
        preferred_element_type=jnp.float32,
    )


def layer_norm(values):
    center = values - jnp.mean(values, axis=-1, keepdims=True)
    inv_std = lax.rsqrt(jnp.mean(center * center, axis=-1, keepdims=True) + eps_norm)
    return (center * inv_std, inv_std)


def norm_back(normed, inv_std, grad_normed):
    return inv_std * (
        grad_normed
        - jnp.mean(grad_normed, axis=-1, keepdims=True)
        - normed * jnp.mean(grad_normed * normed, axis=-1, keepdims=True)
    )


def gelu_tanh(values):
    return jax.nn.gelu(values, approximate=True)


def align_loss(projected, target_vals):
    inner = jnp.sum(projected * target_vals, axis=1)
    norm_pred = lax.rsqrt(jnp.sum(projected * projected, axis=1) + eps_norm)
    norm_target = lax.rsqrt(jnp.sum(target_vals * target_vals, axis=1) + eps_norm)
    return -repa_weight * jnp.sum(inner * norm_pred * norm_target)


def block_rows(total_rows, unit_rows):
    count = total_rows // unit_rows
    best = 1
    for parts in range(1, count + 1):
        if count % parts == 0 and parts * unit_rows <= 1024:
            best = parts
    return best * unit_rows


def block_scores(queries, key_rows, image_ids, row_start, starts, block_len, score_scale):
    query_blk = queries[row_start : row_start + block_len]
    row_ids = image_ids[row_start : row_start + block_len]
    pieces = []
    for col_start in starts:

        def compute_block(col_start=col_start):
            products = (
                jnp.einsum(
                    "qhd,khd->hqk",
                    query_blk,
                    key_rows[col_start : col_start + block_len],
                    preferred_element_type=jnp.float32,
                )
                * score_scale
            )
            same_image = row_ids[:, None] == image_ids[col_start : col_start + block_len][None, :]
            return jnp.where(same_image[None], products, neg_fill)

        pieces.append(compute_block())
    return jnp.concatenate(pieces, axis=2)


def attention_forward(queries, key_rows, values, image_ids, block_len, score_scale):
    starts = list(range(0, queries.shape[0], block_len))
    outputs = []
    log_sums = []
    for row_start in starts:
        scores = block_scores(
            queries, key_rows, image_ids, row_start, starts, block_len, score_scale
        )
        row_max = jnp.max(scores, axis=2, keepdims=True)
        exponent = jnp.exp(scores - row_max)
        row_total = jnp.sum(exponent, axis=2, keepdims=True)
        prob_low = (exponent / row_total).astype(jnp.bfloat16)
        log_sums.append(row_max + jnp.log(row_total))
        summed = jnp.zeros((block_len, queries.shape[1], queries.shape[2]), jnp.float32)
        for position, col_start in enumerate(starts):

            def weigh_block(position=position, col_start=col_start, prob_low=prob_low):
                return jnp.einsum(
                    "hqk,khd->qhd",
                    prob_low[:, :, position * block_len : (position + 1) * block_len],
                    values[col_start : col_start + block_len],
                    preferred_element_type=jnp.float32,
                )

            summed = summed + weigh_block()
        outputs.append(summed.astype(jnp.bfloat16))
    return (jnp.concatenate(outputs, axis=0), jnp.concatenate(log_sums, axis=1))


def attention_backward(
    queries, key_rows, values, image_ids, log_sums, grad_heads, block_len, score_scale
):
    starts = list(range(0, queries.shape[0], block_len))
    grad_keys = jnp.zeros(key_rows.shape, jnp.float32)
    grad_values = jnp.zeros(values.shape, jnp.float32)
    grad_query_list = []
    for row_start in starts:
        query_blk = queries[row_start : row_start + block_len]
        grad_blk = grad_heads[row_start : row_start + block_len]
        scores = block_scores(
            queries, key_rows, image_ids, row_start, starts, block_len, score_scale
        )
        soft = jnp.exp(scores - log_sums[:, row_start : row_start + block_len])
        grad_pieces = []
        for col_start in starts:

            def pull_block(col_start=col_start):
                return jnp.einsum(
                    "qhd,khd->hqk",
                    grad_blk,
                    values[col_start : col_start + block_len],
                    preferred_element_type=jnp.float32,
                )

            grad_pieces.append(pull_block())
        grad_soft = jnp.concatenate(grad_pieces, axis=2)
        inner = jnp.sum(soft * grad_soft, axis=2, keepdims=True)
        grad_scores = (soft * (grad_soft - inner)).astype(jnp.bfloat16)
        soft_low = soft.astype(jnp.bfloat16)
        grad_query = jnp.zeros(query_blk.shape, jnp.float32)
        for position, col_start in enumerate(starts):

            def both_grads(position=position, col_start=col_start):
                piece = grad_scores[:, :, position * block_len : (position + 1) * block_len]
                soft_piece = soft_low[:, :, position * block_len : (position + 1) * block_len]
                return (
                    jnp.einsum(
                        "hqk,khd->qhd",
                        piece,
                        key_rows[col_start : col_start + block_len],
                        preferred_element_type=jnp.float32,
                    ),
                    jnp.einsum(
                        "hqk,qhd->khd", piece, query_blk, preferred_element_type=jnp.float32
                    ),
                    jnp.einsum(
                        "hqk,qhd->khd", soft_piece, grad_blk, preferred_element_type=jnp.float32
                    ),
                )

            part_query, part_key, part_value = both_grads()
            grad_query = grad_query + part_query
            grad_keys = grad_keys.at[col_start : col_start + block_len].add(part_key)
            grad_values = grad_values.at[col_start : col_start + block_len].add(part_value)
        grad_query_list.append(grad_query * score_scale)
    return (jnp.concatenate(grad_query_list, axis=0), grad_keys * score_scale, grad_values)


def column_set(matrix, data_count, tensor_count, tensor_rank):
    shaped = matrix.reshape(matrix.shape[0], data_count, tensor_count, -1)
    return lax.dynamic_index_in_dim(shaped, tensor_rank, axis=2, keepdims=False).reshape(
        matrix.shape[0], -1
    )


def shards(
    tokens_in,
    condition,
    ada_weight,
    ada_bias,
    qkv_weight,
    qv_bias,
    out_weight,
    out_bias,
    up_weight,
    up_bias,
    down_weight,
    down_bias,
    proj_in,
    proj_in_bias,
    proj_mid,
    proj_mid_bias,
    proj_last,
    proj_last_bias,
    enc_features,
    image_ids,
    target_rows,
    out_grad,
):
    tensor_count = lax.axis_size("tensor")
    data_count = lax.axis_size("dp")
    tensor_rank = lax.axis_index("tensor")
    data_rank = lax.axis_index("dp")
    local_rows, model_width = tokens_in.shape
    shard_rows = image_ids.shape[0]
    slot_count = condition.shape[0]
    local_cols = qkv_weight.shape[2]
    local_hidden = up_weight.shape[1]
    head_count = local_cols // HEAD_DIM
    score_scale = HEAD_DIM ** (-0.5)
    block_len = block_rows(shard_rows, SHORT)
    my_ids = lax.dynamic_slice_in_dim(image_ids, tensor_rank * local_rows, local_rows)
    one_hot = (my_ids[:, None] == jnp.arange(slot_count, dtype=jnp.int32)[None, :]).astype(
        jnp.float32
    )
    cond_float = condition.astype(jnp.float32)
    silu_cond, silu_back = jax.vjp(jax.nn.silu, cond_float)
    silu_low = silu_cond.astype(jnp.bfloat16)
    modulation = jnp.dot(
        silu_low, ada_weight, preferred_element_type=jnp.float32
    ) + ada_bias.astype(jnp.float32)
    per_token = jnp.dot(one_hot, modulation, precision=highest, preferred_element_type=jnp.float32)
    shift_one, scale_one, gate_one, shift_two, scale_two, gate_two = jnp.split(per_token, 6, axis=1)
    resid = tokens_in.astype(jnp.float32)
    normed_one, inv_one = layer_norm(resid)
    attn_in = (normed_one * (1.0 + scale_one) + shift_one).astype(jnp.bfloat16)
    attn_all = lax.all_gather(attn_in, "tensor", axis=0, tiled=True)
    qkv_flat_weight = qkv_weight.reshape(model_width, 3 * local_cols)
    qkv_flat = jnp.dot(attn_all, qkv_flat_weight, preferred_element_type=jnp.float32)
    bias_float = qv_bias.astype(jnp.float32)
    queries = (
        (qkv_flat[:, :local_cols] + bias_float[0])
        .astype(jnp.bfloat16)
        .reshape(shard_rows, head_count, HEAD_DIM)
    )
    key_rows = (
        qkv_flat[:, local_cols : 2 * local_cols]
        .astype(jnp.bfloat16)
        .reshape(shard_rows, head_count, HEAD_DIM)
    )
    values = (
        (qkv_flat[:, 2 * local_cols :] + bias_float[1])
        .astype(jnp.bfloat16)
        .reshape(shard_rows, head_count, HEAD_DIM)
    )
    attended, log_sums = attention_forward(
        queries, key_rows, values, image_ids, block_len, score_scale
    )
    attended = attended.reshape(shard_rows, local_cols)
    attn_branch = lax.psum_scatter(
        jnp.dot(attended, out_weight, preferred_element_type=jnp.float32).astype(jnp.bfloat16),
        "tensor",
        scatter_dimension=0,
        tiled=True,
    ).astype(jnp.float32) + out_bias.astype(jnp.float32)
    mid = resid + gate_one * attn_branch
    normed_two, inv_two = layer_norm(mid)
    mlp_in = (normed_two * (1.0 + scale_two) + shift_two).astype(jnp.bfloat16)
    mlp_all = lax.all_gather(mlp_in, "tensor", axis=0, tiled=True)
    pre_act = jnp.dot(mlp_all, up_weight, preferred_element_type=jnp.float32) + up_bias.astype(
        jnp.float32
    )
    act_value, act_back = jax.vjp(gelu_tanh, pre_act)
    hidden = act_value.astype(jnp.bfloat16)
    mlp_branch = lax.psum_scatter(
        jnp.dot(hidden, down_weight, preferred_element_type=jnp.float32).astype(jnp.bfloat16),
        "tensor",
        scatter_dimension=0,
        tiled=True,
    ).astype(jnp.float32) + down_bias.astype(jnp.float32)
    block_value = mid + gate_two * mlp_branch
    block_low = block_value.astype(jnp.bfloat16)
    first_pre = jnp.dot(
        block_low, proj_in, preferred_element_type=jnp.float32
    ) + proj_in_bias.astype(jnp.float32)
    first_value, first_back = jax.vjp(jax.nn.silu, first_pre)
    first_low = first_value.astype(jnp.bfloat16)
    second_pre = jnp.dot(
        first_low, proj_mid, preferred_element_type=jnp.float32
    ) + proj_mid_bias.astype(jnp.float32)
    second_value, second_back = jax.vjp(jax.nn.silu, second_pre)
    second_low = second_value.astype(jnp.bfloat16)
    projected = jnp.dot(
        second_low, proj_last, preferred_element_type=jnp.float32
    ) + proj_last_bias.astype(jnp.float32)
    target_vals = jnp.take(enc_features, target_rows - data_rank * shard_rows, axis=0).astype(
        jnp.float32
    )
    loss_value, loss_back = jax.vjp(lambda predicted: align_loss(predicted, target_vals), projected)
    grad_projected = loss_back(jnp.ones((), jnp.float32))[0]
    grad_last_low = grad_projected.astype(jnp.bfloat16)
    grad_second = second_back(dot_nt(grad_last_low, proj_last))[0]
    grad_second_low = grad_second.astype(jnp.bfloat16)
    grad_first = first_back(dot_nt(grad_second_low, proj_mid))[0]
    grad_first_low = grad_first.astype(jnp.bfloat16)
    grad_block = out_grad.astype(jnp.float32) + dot_nt(grad_first_low, proj_in)
    gate_two_grad = mlp_branch * grad_block
    grad_mlp_branch = gate_two * grad_block
    grad_mlp_all = lax.all_gather(
        grad_mlp_branch.astype(jnp.bfloat16), "tensor", axis=0, tiled=True
    )
    grad_down_local = dot_tn(hidden, grad_mlp_all)
    grad_pre = act_back(dot_nt(grad_mlp_all, down_weight))[0]
    grad_pre_low = grad_pre.astype(jnp.bfloat16)
    grad_up_local = dot_tn(mlp_all, grad_pre_low)
    up_bias_local = jnp.sum(grad_pre, axis=0)
    grad_mlp_in = lax.psum_scatter(
        dot_nt(grad_pre_low, up_weight).astype(jnp.bfloat16),
        "tensor",
        scatter_dimension=0,
        tiled=True,
    ).astype(jnp.float32)
    scale_two_grad = grad_mlp_in * normed_two
    grad_mid = grad_block + norm_back(normed_two, inv_two, grad_mlp_in * (1.0 + scale_two))
    gate_one_grad = attn_branch * grad_mid
    grad_attn_branch = gate_one * grad_mid
    grad_attn_all = lax.all_gather(
        grad_attn_branch.astype(jnp.bfloat16), "tensor", axis=0, tiled=True
    )
    grad_out_local = dot_tn(attended, grad_attn_all)
    grad_heads = (
        dot_nt(grad_attn_all, out_weight)
        .astype(jnp.bfloat16)
        .reshape(shard_rows, head_count, HEAD_DIM)
    )
    grad_queries, grad_keys, grad_values = attention_backward(
        queries, key_rows, values, image_ids, log_sums, grad_heads, block_len, score_scale
    )
    grad_queries = grad_queries.reshape(shard_rows, local_cols)
    grad_keys = grad_keys.reshape(shard_rows, local_cols)
    grad_values = grad_values.reshape(shard_rows, local_cols)
    qv_local = jnp.stack([jnp.sum(grad_queries, axis=0), jnp.sum(grad_values, axis=0)])
    grad_qkv_low = jnp.concatenate([grad_queries, grad_keys, grad_values], axis=1).astype(
        jnp.bfloat16
    )
    grad_qkv_local = dot_tn(attn_all, grad_qkv_low).reshape(model_width, 3, local_cols)
    grad_attn_in = lax.psum_scatter(
        dot_nt(grad_qkv_low, qkv_flat_weight).astype(jnp.bfloat16),
        "tensor",
        scatter_dimension=0,
        tiled=True,
    ).astype(jnp.float32)
    scale_one_grad = grad_attn_in * normed_one
    grad_tokens = grad_mid + norm_back(normed_one, inv_one, grad_attn_in * (1.0 + scale_one))
    token_mod_grad = jnp.concatenate(
        [grad_attn_in, scale_one_grad, gate_one_grad, grad_mlp_in, scale_two_grad, gate_two_grad],
        axis=1,
    )
    slot_grad_part = dot_tn(one_hot, token_mod_grad, precision=highest)
    slot_grad = lax.psum(slot_grad_part.astype(jnp.bfloat16), "tensor").astype(jnp.float32)
    slot_low = slot_grad.astype(jnp.bfloat16)
    grad_condition = silu_back(dot_nt(slot_low, ada_weight))[0]
    ada_cols = dot_tn(silu_low, column_set(slot_low, data_count, tensor_count, tensor_rank))
    ada_bias_cols = jnp.sum(
        column_set(slot_grad, data_count, tensor_count, tensor_rank), axis=0, keepdims=True
    )
    block_grads = (
        lax.psum_scatter(
            grad_qkv_local.astype(jnp.bfloat16), "dp", scatter_dimension=0, tiled=True
        ).astype(jnp.float32),
        lax.psum_scatter(
            grad_out_local.astype(jnp.bfloat16), "dp", scatter_dimension=1, tiled=True
        ).astype(jnp.float32),
        lax.psum_scatter(
            grad_up_local.astype(jnp.bfloat16), "dp", scatter_dimension=0, tiled=True
        ).astype(jnp.float32),
        lax.psum_scatter(
            grad_down_local.astype(jnp.bfloat16), "dp", scatter_dimension=1, tiled=True
        ).astype(jnp.float32),
        lax.psum_scatter(
            ada_cols.astype(jnp.bfloat16), "dp", scatter_dimension=1, tiled=True
        ).astype(jnp.float32),
        lax.psum_scatter(
            ada_bias_cols.astype(jnp.bfloat16), "dp", scatter_dimension=1, tiled=True
        ).astype(jnp.float32),
    )
    qv_full = lax.dynamic_update_slice_in_dim(
        jnp.zeros((2, model_width), jnp.float32), qv_local, tensor_rank * local_cols, axis=1
    )
    up_full = lax.dynamic_update_slice_in_dim(
        jnp.zeros((local_hidden * tensor_count,), jnp.float32),
        up_bias_local,
        tensor_rank * local_hidden,
        axis=0,
    )
    bias_sums = lax.psum(
        (
            qv_full,
            up_full,
            jnp.sum(grad_attn_branch, axis=0),
            jnp.sum(grad_mlp_branch, axis=0),
            jnp.sum(grad_first, axis=0),
            jnp.sum(grad_second, axis=0),
            jnp.sum(grad_projected, axis=0),
        ),
        ("dp", "tensor"),
    )
    qv_grad = lax.dynamic_slice_in_dim(bias_sums[0], tensor_rank * local_cols, local_cols, axis=1)
    up_bias_grad = lax.dynamic_slice_in_dim(
        bias_sums[1], tensor_rank * local_hidden, local_hidden, axis=0
    )
    proj_grads = (
        lax.psum_scatter(
            dot_tn(block_low, grad_first_low), ("dp", "tensor"), scatter_dimension=1, tiled=True
        ),
        lax.psum_scatter(
            dot_tn(first_low, grad_second_low), ("dp", "tensor"), scatter_dimension=1, tiled=True
        ),
        lax.psum_scatter(
            dot_tn(second_low, grad_last_low), ("dp", "tensor"), scatter_dimension=1, tiled=True
        ),
    )
    return (
        block_low,
        grad_tokens,
        grad_condition,
        block_grads[4],
        block_grads[5].reshape(-1),
        block_grads[0],
        qv_grad,
        block_grads[1],
        bias_sums[2],
        block_grads[2],
        up_bias_grad,
        block_grads[3],
        bias_sums[3],
        proj_grads[0],
        bias_sums[4],
        proj_grads[1],
        bias_sums[5],
        proj_grads[2],
        bias_sums[6],
    )


LANES = 128
MESH = pl.DeviceIdType.MESH
bf16 = jnp.bfloat16
f32 = jnp.float32


def pairs_of(move):
    found = []
    for index in range(32):
        x, core, y, z = index % 2, (index // 2) % 2, (index // 4) % 2, index // 8
        z2, y2, c2, x2 = move(z, y, core, x)
        if (z2, y2, c2, x2) != (z, y, core, x):
            found.append((index, ((z2 * 2 + y2) * 2 + c2) * 2 + x2))
    return found


def send(value, move):
    return lax.ppermute(value, ("dp", "tensor"), pairs_of(move))


def to_diag(z, y, c, x):
    return (z, y, x, c)


def to_cycle(z, y, c, x):
    return (z, y, c, c) if c != x else (z, y, 1 - c, x)


def to_core(z, y, c, x):
    return (z, y, 1 - c, x)


def to_x(z, y, c, x):
    return (z, y, c, 1 - x)


def to_y(z, y, c, x):
    return (z, 1 - y, c, x)


def to_z_near(z, y, c, x):
    return (z ^ 1, y, c, x)


def to_z_far(z, y, c, x):
    return (z ^ 2, y, c, x)


def pick(array, index, axis):
    return lax.dynamic_index_in_dim(array, index, axis=axis, keepdims=False)


def halve(array, axis, bit, move):
    got = send(pick(array, 1 - bit, axis), move)
    kept = pick(array, bit, axis)
    return (kept.astype(f32) + got.astype(f32)).astype(bf16)


def gather_kernel(own_ref, out_ref, local_sem, send_sem, recv_sem):
    dp = lax.axis_index("dp")
    x = lax.axis_index("tensor")
    core = dp % 2
    other = dp + 1 - 2 * core
    barrier = pltpu.get_barrier_semaphore()
    pl.semaphore_signal(barrier, inc=1, device_id=(other, x), device_id_type=MESH)
    pl.semaphore_wait(barrier, 1)
    away = pltpu.make_async_remote_copy(
        src_ref=own_ref,
        dst_ref=out_ref.at[core],
        send_sem=send_sem,
        recv_sem=recv_sem,
        device_id=(other, x),
        device_id_type=MESH,
    )
    away.start()
    here = pltpu.make_async_copy(own_ref, out_ref.at[core], local_sem)
    here.start()
    here.wait()
    away.wait()


def gather_cores(own):
    rows, width = own.shape
    return pl.pallas_call(
        gather_kernel,
        out_shape=jax.ShapeDtypeStruct((2, rows, width), own.dtype),
        in_specs=[pl.BlockSpec(memory_space=pltpu.VMEM)],
        out_specs=pl.BlockSpec(memory_space=pl.ANY),
        scratch_shapes=[pltpu.SemaphoreType.DMA] * 3,
        compiler_params=pltpu.CompilerParams(collective_id=0, has_side_effects=True, vmem_limit_bytes=16 << 20),
        cost_estimate=pl.CostEstimate(flops=0, bytes_accessed=12000000, transcendentals=0),
        name="gather_cores",
    )(own).reshape(2 * rows, width)


def attend_kernel(factor, starts, counts, q_ref, k_ref, v_ref, o_ref):
    def unit(index, carry):
        rows = pl.ds(pl.multiple_of(index * SHORT, SHORT), SHORT)

        def run(length):
            cols = pl.ds(pl.multiple_of(starts[index] * SHORT, SHORT), length)
            scores = dot_nt(k_ref[cols, :], q_ref[rows, :])
            top = jnp.max(scores, axis=0, keepdims=True)
            exponent = jnp.exp((scores - top) * factor)
            total = jnp.sum(exponent, axis=0, keepdims=True)
            prob_low = (exponent * (1.0 / total)).astype(bf16)
            summed = dot_tn(v_ref[cols, :], prob_low)
            o_ref[rows, :] = summed.T.astype(bf16)

        @pl.when(counts[index] == 1)
        def _():
            run(SHORT)

        @pl.when(counts[index] != 1)
        def _():
            run(4 * SHORT)

        return carry

    lax.fori_loop(0, q_ref.shape[0] // SHORT, unit, 0)


def attend(starts, counts, qkv, heads, factor):
    rows = qkv.shape[0]

    def spec(part):
        return pl.BlockSpec((rows, LANES), lambda h, *_: (0, part * heads + h))

    return pl.pallas_call(
        functools.partial(attend_kernel, factor),
        out_shape=jax.ShapeDtypeStruct((rows, heads * LANES), bf16),
        grid_spec=pltpu.PrefetchScalarGridSpec(
            num_scalar_prefetch=2,
            grid=(heads,),
            in_specs=[spec(0), spec(1), spec(2)],
            out_specs=spec(0),
        ),
        compiler_params=pltpu.CompilerParams(vmem_limit_bytes=48 << 20),
        cost_estimate=pl.CostEstimate(flops=20 * 10**9, bytes_accessed=13 * 10**6, transcendentals=10**7),
        name="attend",
    )(starts, counts, qkv, qkv, qkv)


def attend_back_kernel(
    factor, starts, counts, q_ref, k_ref, v_ref, g_ref, out_ref, bias_ref, key_acc, value_acc, query_low
):
    part = pl.program_id(1)
    rows_all = q_ref.shape[0]

    @pl.when(part == 0)
    def _():
        key_acc[...] = jnp.zeros_like(key_acc)
        value_acc[...] = jnp.zeros_like(value_acc)
        bias_ref[...] = jnp.zeros_like(bias_ref)

        def unit(index, carry):
            rows = pl.ds(pl.multiple_of(index * SHORT, SHORT), SHORT)

            def run(length):
                cols = pl.ds(pl.multiple_of(starts[index] * SHORT, SHORT), length)
                queries = q_ref[rows, :]
                grads = g_ref[rows, :]
                keys = k_ref[cols, :]
                scores = dot_nt(keys, queries)
                top = jnp.max(scores, axis=0, keepdims=True)
                exponent = jnp.exp((scores - top) * factor)
                total = jnp.sum(exponent, axis=0, keepdims=True)
                soft = exponent * (1.0 / total)
                grad_soft = dot_nt(v_ref[cols, :], grads)
                inner = jnp.sum(soft * grad_soft, axis=0, keepdims=True)
                grad_scores = (soft * (grad_soft - inner)).astype(bf16)
                value_acc[cols, :] += jnp.dot(soft.astype(bf16), grads, preferred_element_type=f32)
                key_acc[cols, :] += jnp.dot(grad_scores, queries, preferred_element_type=f32)
                grad_query = dot_tn(keys, grad_scores).T * factor
                query_low[rows, :] = grad_query.astype(bf16)
                bias_ref[0:1, :] += jnp.sum(grad_query, axis=0, keepdims=True)

            @pl.when(counts[index] == 1)
            def _():
                run(SHORT)

            @pl.when(counts[index] != 1)
            def _():
                run(4 * SHORT)

            return carry

        lax.fori_loop(0, rows_all // SHORT, unit, 0)
        bias_ref[1:2, :] = jnp.sum(value_acc[...], axis=0, keepdims=True)
        out_ref[...] = query_low[...]

    @pl.when(part == 1)
    def _():
        out_ref[...] = (key_acc[...] * factor).astype(bf16)

    @pl.when(part == 2)
    def _():
        out_ref[...] = value_acc[...].astype(bf16)


def attend_back(starts, counts, qkv, grad_heads, heads, factor):
    rows = qkv.shape[0]

    def spec(part):
        return pl.BlockSpec((rows, LANES), lambda h, p, *_: (0, part * heads + h))

    return pl.pallas_call(
        functools.partial(attend_back_kernel, factor),
        out_shape=(
            jax.ShapeDtypeStruct((rows, 3 * heads * LANES), bf16),
            jax.ShapeDtypeStruct((8, heads * LANES), f32),
        ),
        grid_spec=pltpu.PrefetchScalarGridSpec(
            num_scalar_prefetch=2,
            grid=(heads, 3),
            in_specs=[spec(0), spec(1), spec(2), spec(0)],
            out_specs=(
                pl.BlockSpec((rows, LANES), lambda h, p, *_: (0, p * heads + h)),
                pl.BlockSpec((8, LANES), lambda h, p, *_: (0, h)),
            ),
            scratch_shapes=[
                pltpu.VMEM((rows, LANES), f32),
                pltpu.VMEM((rows, LANES), f32),
                pltpu.VMEM((rows, LANES), bf16),
            ],
        ),
        compiler_params=pltpu.CompilerParams(vmem_limit_bytes=48 << 20),
        cost_estimate=pl.CostEstimate(flops=40 * 10**9, bytes_accessed=25 * 10**6, transcendentals=10**7),
        name="attend_back",
    )(starts, counts, qkv, qkv, qkv, grad_heads)


def after(value, earlier):
    return lax.optimization_barrier((value, earlier))[0]


def paired_shards(
    tokens_in,
    condition,
    ada_weight,
    ada_bias,
    qkv_weight,
    qv_bias,
    out_weight,
    out_bias,
    up_weight,
    up_bias,
    down_weight,
    down_bias,
    proj_in,
    proj_in_bias,
    proj_mid,
    proj_mid_bias,
    proj_last,
    proj_last_bias,
    enc_features,
    image_ids,
    target_rows,
    out_grad,
):
    dp = lax.axis_index("dp")
    x = lax.axis_index("tensor")
    core = dp % 2
    y = (dp // 2) % 2
    z = dp // 4
    z_near = z % 2
    z_far = z // 2
    place = dp * 2 + x
    home = core == x
    group = (dp // 2) * 2 + x
    local_rows, width = tokens_in.shape
    shard_rows = image_ids.shape[0]
    slots = condition.shape[0]
    units = local_rows // SHORT
    local_cols = qkv_weight.shape[2]
    local_hidden = up_weight.shape[1]
    heads = local_cols // HEAD_DIM
    padded = heads * LANES
    factor = HEAD_DIM ** (-0.5)

    def swap(value):
        return jnp.where(home, value, send(value, to_diag))

    tokens = swap(tokens_in)
    packed_ids = send(image_ids, to_core)
    ids = jnp.where(home, image_ids, packed_ids)
    cond_low = jnp.where(home, condition, send(condition, to_core))
    qkv_half = swap(after(qkv_weight.reshape(width, 3 * local_cols), tokens))
    out_half = swap(after(out_weight, qkv_half))
    up_half = swap(after(up_weight, out_half))
    down_half = swap(after(down_weight, up_half))
    features = jnp.where(home, enc_features, send(enc_features, to_core))
    rows_low = swap(after(target_rows, down_half))
    grad_out = swap(after(out_grad, down_half))
    bias_pack = jnp.concatenate([qv_bias.reshape(-1), up_bias])
    bias_half = swap(bias_pack).astype(f32)
    qv_half = bias_half[: 2 * local_cols].reshape(2, local_cols)
    up_bias_half = bias_half[2 * local_cols :]

    unit_ids = ids.reshape(-1, SHORT)[:, 0]
    same = unit_ids[:, None] == unit_ids[None, :]
    starts = jnp.argmax(same, axis=1).astype(jnp.int32)
    counts = jnp.sum(same.astype(jnp.int32), axis=1).astype(jnp.int32)
    my_units = lax.dynamic_slice_in_dim(unit_ids, core * units, units)
    one_hot = (my_units[:, None] == jnp.arange(slots, dtype=jnp.int32)[None, :]).astype(f32)

    silu_cond, silu_back = jax.vjp(jax.nn.silu, cond_low.astype(f32))
    silu_low = silu_cond.astype(bf16)
    silu_all = lax.dynamic_update_index_in_dim(jnp.zeros((16, slots, width), bf16), silu_low, group, axis=0)
    for move in (to_x, to_y, to_z_near, to_z_far):
        silu_all = silu_all + send(silu_all, move)
    modulation = jnp.dot(silu_low, ada_weight, preferred_element_type=f32) + ada_bias.astype(f32)
    per_unit = jnp.dot(one_hot, modulation, precision=highest, preferred_element_type=f32)
    shift_one, scale_one, gate_one, shift_two, scale_two, gate_two = [
        piece[:, None, :] for piece in jnp.split(per_unit, 6, axis=1)
    ]

    def by_unit(array):
        return array.reshape(units, SHORT, -1)

    def flat(array):
        return array.reshape(local_rows, -1)

    def reduce_cores(left, matrix, product):
        mine = lax.dynamic_slice_in_dim(left, core * local_rows, local_rows)
        theirs = lax.dynamic_slice_in_dim(left, (1 - core) * local_rows, local_rows)
        got = send(product(theirs, matrix).astype(bf16), to_core)
        return product(mine, matrix).astype(bf16).astype(f32) + got.astype(f32)

    def dot_nn(left, right):
        return jnp.dot(left, right, preferred_element_type=f32)

    resid = by_unit(tokens.astype(f32))
    normed_one, inv_one = layer_norm(resid)
    attn_in = flat((normed_one * (1.0 + scale_one) + shift_one).astype(bf16))
    attn_all = gather_cores(attn_in)

    def pad_heads(array):
        lead = array.shape[:-1]
        shaped = array.reshape(lead + (-1, HEAD_DIM))
        widths = [(0, 0)] * (len(lead) + 1) + [(0, LANES - HEAD_DIM)]
        return jnp.pad(shaped, widths).reshape(lead + (-1,))

    qkv_pad = pad_heads(qkv_half)
    out_pad = jnp.pad(
        out_half.reshape(heads, HEAD_DIM, width), ((0, 0), (0, LANES - HEAD_DIM), (0, 0))
    ).reshape(padded, width)
    qkv_bias = pad_heads(jnp.concatenate([qv_half[0], jnp.zeros_like(qv_half[0]), qv_half[1]]))
    qkv = (dot_nn(attn_all, qkv_pad) + qkv_bias).astype(bf16)
    attended = attend(starts, counts, qkv, heads, factor)
    attn_branch = by_unit(reduce_cores(attended, out_pad, dot_nn) + out_bias.astype(f32))
    mid = resid + gate_one * attn_branch

    normed_two, inv_two = layer_norm(mid)
    mlp_in = flat((normed_two * (1.0 + scale_two) + shift_two).astype(bf16))
    mlp_all = gather_cores(mlp_in)
    pre_act = dot_nn(mlp_all, up_half) + up_bias_half
    act_value, act_back = jax.vjp(gelu_tanh, pre_act)
    hidden = act_value.astype(bf16)
    mlp_branch = by_unit(reduce_cores(hidden, down_half, dot_nn) + down_bias.astype(f32))
    block_value = mid + gate_two * mlp_branch
    block_low = flat(block_value.astype(bf16))

    first_pre = dot_nn(block_low, proj_in) + proj_in_bias.astype(f32)
    first_value, first_back = jax.vjp(jax.nn.silu, first_pre)
    first_low = first_value.astype(bf16)
    second_pre = dot_nn(first_low, proj_mid) + proj_mid_bias.astype(f32)
    second_value, second_back = jax.vjp(jax.nn.silu, second_pre)
    second_low = second_value.astype(bf16)
    projected = dot_nn(second_low, proj_last) + proj_last_bias.astype(f32)
    target_vals = jnp.take(features, rows_low - group * shard_rows, axis=0).astype(f32)
    loss_back = jax.vjp(lambda predicted: align_loss(predicted, target_vals), projected)[1]
    grad_projected = loss_back(jnp.ones((), f32))[0]
    grad_last_low = grad_projected.astype(bf16)
    grad_second = second_back(dot_nt(grad_last_low, proj_last))[0]
    grad_second_low = grad_second.astype(bf16)
    grad_first = first_back(dot_nt(grad_second_low, proj_mid))[0]
    grad_first_low = grad_first.astype(bf16)
    grad_block = by_unit(grad_out.astype(f32) + dot_nt(grad_first_low, proj_in))

    grad_mlp_branch = gate_two * grad_block
    grad_mlp_all = gather_cores(flat(grad_mlp_branch.astype(bf16)))
    grad_pre = act_back(dot_nt(grad_mlp_all, down_half))[0]
    grad_pre_low = grad_pre.astype(bf16)
    grad_mlp_in = by_unit(reduce_cores(grad_pre_low, up_half, dot_nt))
    grad_mid = grad_block + norm_back(normed_two, inv_two, grad_mlp_in * (1.0 + scale_two))

    grad_attn_branch = gate_one * grad_mid
    grad_attn_all = gather_cores(flat(grad_attn_branch.astype(bf16)))
    grad_heads = dot_nt(grad_attn_all, out_pad).astype(bf16)
    grad_qkv, qkv_bias_sums = attend_back(starts, counts, qkv, grad_heads, heads, factor)
    grad_attn_in = by_unit(reduce_cores(grad_qkv, qkv_pad, dot_nt))
    grad_tokens = grad_mid + norm_back(normed_one, inv_one, grad_attn_in * (1.0 + scale_one))

    def spread(array, rows):
        return array.reshape(2, 2, 2, 2, rows, array.shape[-1])

    def over_zy(array):
        array = halve(array, 2, y, to_y)
        array = halve(array, 1, z_near, to_z_near)
        return halve(array, 0, z_far, to_z_far)

    def over_pair(array, axis):
        turned = send(pick(array, 1 - x, axis), to_cycle)
        straight = swap(pick(array, x, axis))
        return (turned.astype(f32) + straight.astype(f32)).astype(bf16)

    proj_rows = proj_in.shape[1] // 32
    grads_in = dot_tn(grad_first_low, block_low).astype(bf16)
    grads_mid = dot_tn(grad_second_low, first_low).astype(bf16)
    grads_last = dot_tn(grad_last_low, second_low).astype(bf16)

    def over_all(array):
        rows = array.shape[0] // 32
        array = array.reshape(2, 2, 2, 2, 2, rows, array.shape[1])
        array = halve(array, 3, core, to_core)
        array = halve(array, 2, y, to_y)
        array = halve(array, 2, x, to_x)
        array = halve(array, 1, z_near, to_z_near)
        return halve(array, 0, z_far, to_z_far)

    near_in = over_all(grads_in)
    near_mid = over_all(grads_mid)
    last = over_all(grads_last)

    grads_down = dot_tn(grad_mlp_all, hidden).astype(bf16)
    grads_up = dot_tn(mlp_all, grad_pre_low).astype(bf16)
    row_count = width // 16
    up_sum = over_zy(over_pair(spread(grads_up, row_count), 3))
    down_sum = over_zy(over_pair(spread(grads_down, row_count), 3))

    grads_out = dot_tn(grad_attn_all, attended).astype(bf16)
    grads_qkv = dot_tn(attn_all, grad_qkv).astype(bf16)

    def trim(array):
        return array.reshape(array.shape[:-1] + (-1, LANES))[..., :HEAD_DIM].reshape(array.shape[:-1] + (-1,))

    qkv_sum = over_pair(over_zy(spread(trim(grads_qkv), row_count)), 0)
    out_sum = over_pair(over_zy(spread(trim(grads_out), row_count)), 0)

    def unit_sum(array):
        return jnp.sum(array, axis=1)

    mod_units = jnp.concatenate(
        [
            unit_sum(grad_attn_in),
            unit_sum(grad_attn_in * normed_one),
            unit_sum(attn_branch * grad_mid),
            unit_sum(grad_mlp_in),
            unit_sum(grad_mlp_in * normed_two),
            unit_sum(mlp_branch * grad_block),
        ],
        axis=1,
    )
    slot_part = dot_tn(one_hot, mod_units, precision=highest)
    slot_grad = slot_part + send(slot_part, to_core)
    slot_low = slot_grad.astype(bf16)
    grad_condition = swap(silu_back(dot_nt(slot_low, ada_weight))[0])
    mod_cols = slot_low.shape[1] // 32
    slot_cols = slot_low.reshape(slots, 2, 2, 2, 2, 2, mod_cols)
    slot_cols = pick(slot_cols, core, 4)
    slot_mine = lax.dynamic_update_index_in_dim(
        jnp.zeros((16,) + slot_cols.shape, bf16), slot_cols, group, axis=0
    )
    for axis, bit, move in ((5, x, to_x), (4, y, to_y), (3, z_near, to_z_near), (2, z_far, to_z_far)):
        slot_mine = pick(slot_mine, bit, axis) + send(pick(slot_mine, 1 - bit, axis), move)
    slot_mine = slot_mine.reshape(16 * slots, mod_cols)
    grad_ada = dot_tn(silu_all.reshape(16 * slots, width), slot_mine)
    ada_bias_grad = jnp.sum(slot_mine.astype(f32), axis=0)

    qv_sums = trim(qkv_bias_sums[:2])
    qv_full = lax.dynamic_update_slice_in_dim(jnp.zeros((2, width), f32), qv_sums, core * local_cols, axis=1)
    up_full = lax.dynamic_update_slice_in_dim(
        jnp.zeros((2 * local_hidden,), f32), jnp.sum(grad_pre, axis=0), core * local_hidden, axis=0
    )
    pieces = [
        qv_full.reshape(-1),
        up_full,
        jnp.sum(flat(grad_attn_branch), axis=0),
        jnp.sum(flat(grad_mlp_branch), axis=0),
        jnp.sum(grad_first, axis=0),
        jnp.sum(grad_second, axis=0),
        jnp.sum(grad_projected, axis=0),
    ]
    sums = jnp.concatenate(pieces)
    for move in (to_core, to_x, to_y, to_z_near, to_z_far):
        sums = sums + send(sums, move)
    found = []
    offset = 0
    for piece in pieces:
        found.append(sums[offset : offset + piece.shape[0]])
        offset += piece.shape[0]
    qv_grad = lax.dynamic_slice_in_dim(found[0].reshape(2, width), x * local_cols, local_cols, axis=1)
    up_bias_grad = lax.dynamic_slice_in_dim(found[1], x * local_hidden, local_hidden, axis=0)

    block_out = swap(block_low)
    tokens_out = swap(flat(grad_tokens).astype(bf16))
    return (
        block_out,
        tokens_out.astype(f32),
        grad_condition,
        grad_ada,
        ada_bias_grad,
        qkv_sum.astype(f32).reshape(row_count, 3, local_cols),
        qv_grad,
        out_sum.astype(f32).T,
        found[2],
        up_sum.astype(f32),
        up_bias_grad,
        down_sum.astype(f32).T,
        found[3],
        near_in.astype(f32).T,
        found[4],
        near_mid.astype(f32).T,
        found[5],
        last.astype(f32).T,
        found[6],
    )


def solution(mesh):
    in_specs = (
        P(("dp", "tensor"), None),
        P("dp", None),
        P(),
        P(),
        P(None, None, "tensor"),
        P(None, "tensor"),
        P("tensor", None),
        P(),
        P(None, "tensor"),
        P("tensor"),
        P("tensor", None),
        P(),
        P(),
        P(),
        P(),
        P(),
        P(),
        P(),
        P("dp", None),
        P("dp"),
        P(("dp", "tensor")),
        P(("dp", "tensor"), None),
    )
    out_specs = (
        P(("dp", "tensor"), None),
        P(("dp", "tensor"), None),
        P("dp", None),
        P(None, ("dp", "tensor")),
        P(("dp", "tensor")),
        P("dp", None, "tensor"),
        P(None, "tensor"),
        P("tensor", "dp"),
        P(),
        P("dp", "tensor"),
        P("tensor"),
        P("tensor", "dp"),
        P(),
        P(None, ("dp", "tensor")),
        P(),
        P(None, ("dp", "tensor")),
        P(),
        P(None, ("dp", "tensor")),
        P(),
    )
    paired = mesh.shape["tensor"] == 2 and mesh.shape["dp"] == 16
    body = paired_shards if paired else shards
    return jax.shard_map(body, mesh=mesh, in_specs=in_specs, out_specs=out_specs, check_vma=False)
```

```python
import functools

import jax
import jax.numpy as jnp
from jax import lax
from jax.experimental import pallas as pl
from jax.experimental.pallas import tpu as pltpu
from jax.sharding import PartitionSpec as P

HEAD_DIM = 72
SHORT = 256


highest = lax.Precision.HIGHEST
eps_norm = 1e-06
repa_weight = 1000.0
neg_fill = -1e30


def dot_nt(left_arg, right_arg):
    return lax.dot_general(
        left_arg, right_arg, (((1,), (1,)), ((), ())), preferred_element_type=jnp.float32
    )


def dot_tn(left_arg, right_arg, precision=None):
    return lax.dot_general(
        left_arg,
        right_arg,
        (((0,), (0,)), ((), ())),
        precision=precision,
        preferred_element_type=jnp.float32,
    )


def layer_norm(values):
    center = values - jnp.mean(values, axis=-1, keepdims=True)
    inv_std = lax.rsqrt(jnp.mean(center * center, axis=-1, keepdims=True) + eps_norm)
    return (center * inv_std, inv_std)


def norm_back(normed, inv_std, grad_normed):
    return inv_std * (
        grad_normed
        - jnp.mean(grad_normed, axis=-1, keepdims=True)
        - normed * jnp.mean(grad_normed * normed, axis=-1, keepdims=True)
    )


def gelu_tanh(values):
    return jax.nn.gelu(values, approximate=True)


def align_loss(projected, target_vals):
    inner = jnp.sum(projected * target_vals, axis=1)
    norm_pred = lax.rsqrt(jnp.sum(projected * projected, axis=1) + eps_norm)
    norm_target = lax.rsqrt(jnp.sum(target_vals * target_vals, axis=1) + eps_norm)
    return -repa_weight * jnp.sum(inner * norm_pred * norm_target)


def block_rows(total_rows, unit_rows):
    count = total_rows // unit_rows
    best = 1
    for parts in range(1, count + 1):
        if count % parts == 0 and parts * unit_rows <= 1024:
            best = parts
    return best * unit_rows


def block_scores(queries, key_rows, image_ids, row_start, starts, block_len, score_scale):
    query_blk = queries[row_start : row_start + block_len]
    row_ids = image_ids[row_start : row_start + block_len]
    pieces = []
    for col_start in starts:

        def compute_block(col_start=col_start):
            products = (
                jnp.einsum(
                    "qhd,khd->hqk",
                    query_blk,
                    key_rows[col_start : col_start + block_len],
                    preferred_element_type=jnp.float32,
                )
                * score_scale
            )
            same_image = row_ids[:, None] == image_ids[col_start : col_start + block_len][None, :]
            return jnp.where(same_image[None], products, neg_fill)

        pieces.append(compute_block())
    return jnp.concatenate(pieces, axis=2)


def attention_forward(queries, key_rows, values, image_ids, block_len, score_scale):
    starts = list(range(0, queries.shape[0], block_len))
    outputs = []
    log_sums = []
    for row_start in starts:
        scores = block_scores(
            queries, key_rows, image_ids, row_start, starts, block_len, score_scale
        )
        row_max = jnp.max(scores, axis=2, keepdims=True)
        exponent = jnp.exp(scores - row_max)
        row_total = jnp.sum(exponent, axis=2, keepdims=True)
        prob_low = (exponent / row_total).astype(jnp.bfloat16)
        log_sums.append(row_max + jnp.log(row_total))
        summed = jnp.zeros((block_len, queries.shape[1], queries.shape[2]), jnp.float32)
        for position, col_start in enumerate(starts):

            def weigh_block(position=position, col_start=col_start, prob_low=prob_low):
                return jnp.einsum(
                    "hqk,khd->qhd",
                    prob_low[:, :, position * block_len : (position + 1) * block_len],
                    values[col_start : col_start + block_len],
                    preferred_element_type=jnp.float32,
                )

            summed = summed + weigh_block()
        outputs.append(summed.astype(jnp.bfloat16))
    return (jnp.concatenate(outputs, axis=0), jnp.concatenate(log_sums, axis=1))


def attention_backward(
    queries, key_rows, values, image_ids, log_sums, grad_heads, block_len, score_scale
):
    starts = list(range(0, queries.shape[0], block_len))
    grad_keys = jnp.zeros(key_rows.shape, jnp.float32)
    grad_values = jnp.zeros(values.shape, jnp.float32)
    grad_query_list = []
    for row_start in starts:
        query_blk = queries[row_start : row_start + block_len]
        grad_blk = grad_heads[row_start : row_start + block_len]
        scores = block_scores(
            queries, key_rows, image_ids, row_start, starts, block_len, score_scale
        )
        soft = jnp.exp(scores - log_sums[:, row_start : row_start + block_len])
        grad_pieces = []
        for col_start in starts:

            def pull_block(col_start=col_start):
                return jnp.einsum(
                    "qhd,khd->hqk",
                    grad_blk,
                    values[col_start : col_start + block_len],
                    preferred_element_type=jnp.float32,
                )

            grad_pieces.append(pull_block())
        grad_soft = jnp.concatenate(grad_pieces, axis=2)
        inner = jnp.sum(soft * grad_soft, axis=2, keepdims=True)
        grad_scores = (soft * (grad_soft - inner)).astype(jnp.bfloat16)
        soft_low = soft.astype(jnp.bfloat16)
        grad_query = jnp.zeros(query_blk.shape, jnp.float32)
        for position, col_start in enumerate(starts):

            def both_grads(position=position, col_start=col_start):
                piece = grad_scores[:, :, position * block_len : (position + 1) * block_len]
                soft_piece = soft_low[:, :, position * block_len : (position + 1) * block_len]
                return (
                    jnp.einsum(
                        "hqk,khd->qhd",
                        piece,
                        key_rows[col_start : col_start + block_len],
                        preferred_element_type=jnp.float32,
                    ),
                    jnp.einsum(
                        "hqk,qhd->khd", piece, query_blk, preferred_element_type=jnp.float32
                    ),
                    jnp.einsum(
                        "hqk,qhd->khd", soft_piece, grad_blk, preferred_element_type=jnp.float32
                    ),
                )

            part_query, part_key, part_value = both_grads()
            grad_query = grad_query + part_query
            grad_keys = grad_keys.at[col_start : col_start + block_len].add(part_key)
            grad_values = grad_values.at[col_start : col_start + block_len].add(part_value)
        grad_query_list.append(grad_query * score_scale)
    return (jnp.concatenate(grad_query_list, axis=0), grad_keys * score_scale, grad_values)


def column_set(matrix, data_count, tensor_count, tensor_rank):
    shaped = matrix.reshape(matrix.shape[0], data_count, tensor_count, -1)
    return lax.dynamic_index_in_dim(shaped, tensor_rank, axis=2, keepdims=False).reshape(
        matrix.shape[0], -1
    )


def shards(
    tokens_in,
    condition,
    ada_weight,
    ada_bias,
    qkv_weight,
    qv_bias,
    out_weight,
    out_bias,
    up_weight,
    up_bias,
    down_weight,
    down_bias,
    proj_in,
    proj_in_bias,
    proj_mid,
    proj_mid_bias,
    proj_last,
    proj_last_bias,
    enc_features,
    image_ids,
    target_rows,
    out_grad,
):
    tensor_count = lax.axis_size("tensor")
    data_count = lax.axis_size("dp")
    tensor_rank = lax.axis_index("tensor")
    data_rank = lax.axis_index("dp")
    local_rows, model_width = tokens_in.shape
    shard_rows = image_ids.shape[0]
    slot_count = condition.shape[0]
    local_cols = qkv_weight.shape[2]
    local_hidden = up_weight.shape[1]
    head_count = local_cols // HEAD_DIM
    score_scale = HEAD_DIM ** (-0.5)
    block_len = block_rows(shard_rows, SHORT)
    my_ids = lax.dynamic_slice_in_dim(image_ids, tensor_rank * local_rows, local_rows)
    one_hot = (my_ids[:, None] == jnp.arange(slot_count, dtype=jnp.int32)[None, :]).astype(
        jnp.float32
    )
    cond_float = condition.astype(jnp.float32)
    silu_cond, silu_back = jax.vjp(jax.nn.silu, cond_float)
    silu_low = silu_cond.astype(jnp.bfloat16)
    modulation = jnp.dot(
        silu_low, ada_weight, preferred_element_type=jnp.float32
    ) + ada_bias.astype(jnp.float32)
    per_token = jnp.dot(one_hot, modulation, precision=highest, preferred_element_type=jnp.float32)
    shift_one, scale_one, gate_one, shift_two, scale_two, gate_two = jnp.split(per_token, 6, axis=1)
    resid = tokens_in.astype(jnp.float32)
    normed_one, inv_one = layer_norm(resid)
    attn_in = (normed_one * (1.0 + scale_one) + shift_one).astype(jnp.bfloat16)
    attn_all = lax.all_gather(attn_in, "tensor", axis=0, tiled=True)
    qkv_flat_weight = qkv_weight.reshape(model_width, 3 * local_cols)
    qkv_flat = jnp.dot(attn_all, qkv_flat_weight, preferred_element_type=jnp.float32)
    bias_float = qv_bias.astype(jnp.float32)
    queries = (
        (qkv_flat[:, :local_cols] + bias_float[0])
        .astype(jnp.bfloat16)
        .reshape(shard_rows, head_count, HEAD_DIM)
    )
    key_rows = (
        qkv_flat[:, local_cols : 2 * local_cols]
        .astype(jnp.bfloat16)
        .reshape(shard_rows, head_count, HEAD_DIM)
    )
    values = (
        (qkv_flat[:, 2 * local_cols :] + bias_float[1])
        .astype(jnp.bfloat16)
        .reshape(shard_rows, head_count, HEAD_DIM)
    )
    attended, log_sums = attention_forward(
        queries, key_rows, values, image_ids, block_len, score_scale
    )
    attended = attended.reshape(shard_rows, local_cols)
    attn_branch = lax.psum_scatter(
        jnp.dot(attended, out_weight, preferred_element_type=jnp.float32).astype(jnp.bfloat16),
        "tensor",
        scatter_dimension=0,
        tiled=True,
    ).astype(jnp.float32) + out_bias.astype(jnp.float32)
    mid = resid + gate_one * attn_branch
    normed_two, inv_two = layer_norm(mid)
    mlp_in = (normed_two * (1.0 + scale_two) + shift_two).astype(jnp.bfloat16)
    mlp_all = lax.all_gather(mlp_in, "tensor", axis=0, tiled=True)
    pre_act = jnp.dot(mlp_all, up_weight, preferred_element_type=jnp.float32) + up_bias.astype(
        jnp.float32
    )
    act_value, act_back = jax.vjp(gelu_tanh, pre_act)
    hidden = act_value.astype(jnp.bfloat16)
    mlp_branch = lax.psum_scatter(
        jnp.dot(hidden, down_weight, preferred_element_type=jnp.float32).astype(jnp.bfloat16),
        "tensor",
        scatter_dimension=0,
        tiled=True,
    ).astype(jnp.float32) + down_bias.astype(jnp.float32)
    block_value = mid + gate_two * mlp_branch
    block_low = block_value.astype(jnp.bfloat16)
    first_pre = jnp.dot(
        block_low, proj_in, preferred_element_type=jnp.float32
    ) + proj_in_bias.astype(jnp.float32)
    first_value, first_back = jax.vjp(jax.nn.silu, first_pre)
    first_low = first_value.astype(jnp.bfloat16)
    second_pre = jnp.dot(
        first_low, proj_mid, preferred_element_type=jnp.float32
    ) + proj_mid_bias.astype(jnp.float32)
    second_value, second_back = jax.vjp(jax.nn.silu, second_pre)
    second_low = second_value.astype(jnp.bfloat16)
    projected = jnp.dot(
        second_low, proj_last, preferred_element_type=jnp.float32
    ) + proj_last_bias.astype(jnp.float32)
    target_vals = jnp.take(enc_features, target_rows - data_rank * shard_rows, axis=0).astype(
        jnp.float32
    )
    loss_value, loss_back = jax.vjp(lambda predicted: align_loss(predicted, target_vals), projected)
    grad_projected = loss_back(jnp.ones((), jnp.float32))[0]
    grad_last_low = grad_projected.astype(jnp.bfloat16)
    grad_second = second_back(dot_nt(grad_last_low, proj_last))[0]
    grad_second_low = grad_second.astype(jnp.bfloat16)
    grad_first = first_back(dot_nt(grad_second_low, proj_mid))[0]
    grad_first_low = grad_first.astype(jnp.bfloat16)
    grad_block = out_grad.astype(jnp.float32) + dot_nt(grad_first_low, proj_in)
    gate_two_grad = mlp_branch * grad_block
    grad_mlp_branch = gate_two * grad_block
    grad_mlp_all = lax.all_gather(
        grad_mlp_branch.astype(jnp.bfloat16), "tensor", axis=0, tiled=True
    )
    grad_down_local = dot_tn(hidden, grad_mlp_all)
    grad_pre = act_back(dot_nt(grad_mlp_all, down_weight))[0]
    grad_pre_low = grad_pre.astype(jnp.bfloat16)
    grad_up_local = dot_tn(mlp_all, grad_pre_low)
    up_bias_local = jnp.sum(grad_pre, axis=0)
    grad_mlp_in = lax.psum_scatter(
        dot_nt(grad_pre_low, up_weight).astype(jnp.bfloat16),
        "tensor",
        scatter_dimension=0,
        tiled=True,
    ).astype(jnp.float32)
    scale_two_grad = grad_mlp_in * normed_two
    grad_mid = grad_block + norm_back(normed_two, inv_two, grad_mlp_in * (1.0 + scale_two))
    gate_one_grad = attn_branch * grad_mid
    grad_attn_branch = gate_one * grad_mid
    grad_attn_all = lax.all_gather(
        grad_attn_branch.astype(jnp.bfloat16), "tensor", axis=0, tiled=True
    )
    grad_out_local = dot_tn(attended, grad_attn_all)
    grad_heads = (
        dot_nt(grad_attn_all, out_weight)
        .astype(jnp.bfloat16)
        .reshape(shard_rows, head_count, HEAD_DIM)
    )
    grad_queries, grad_keys, grad_values = attention_backward(
        queries, key_rows, values, image_ids, log_sums, grad_heads, block_len, score_scale
    )
    grad_queries = grad_queries.reshape(shard_rows, local_cols)
    grad_keys = grad_keys.reshape(shard_rows, local_cols)
    grad_values = grad_values.reshape(shard_rows, local_cols)
    qv_local = jnp.stack([jnp.sum(grad_queries, axis=0), jnp.sum(grad_values, axis=0)])
    grad_qkv_low = jnp.concatenate([grad_queries, grad_keys, grad_values], axis=1).astype(
        jnp.bfloat16
    )
    grad_qkv_local = dot_tn(attn_all, grad_qkv_low).reshape(model_width, 3, local_cols)
    grad_attn_in = lax.psum_scatter(
        dot_nt(grad_qkv_low, qkv_flat_weight).astype(jnp.bfloat16),
        "tensor",
        scatter_dimension=0,
        tiled=True,
    ).astype(jnp.float32)
    scale_one_grad = grad_attn_in * normed_one
    grad_tokens = grad_mid + norm_back(normed_one, inv_one, grad_attn_in * (1.0 + scale_one))
    token_mod_grad = jnp.concatenate(
        [grad_attn_in, scale_one_grad, gate_one_grad, grad_mlp_in, scale_two_grad, gate_two_grad],
        axis=1,
    )
    slot_grad_part = dot_tn(one_hot, token_mod_grad, precision=highest)
    slot_grad = lax.psum(slot_grad_part.astype(jnp.bfloat16), "tensor").astype(jnp.float32)
    slot_low = slot_grad.astype(jnp.bfloat16)
    grad_condition = silu_back(dot_nt(slot_low, ada_weight))[0]
    ada_cols = dot_tn(silu_low, column_set(slot_low, data_count, tensor_count, tensor_rank))
    ada_bias_cols = jnp.sum(
        column_set(slot_grad, data_count, tensor_count, tensor_rank), axis=0, keepdims=True
    )
    block_grads = (
        lax.psum_scatter(
            grad_qkv_local.astype(jnp.bfloat16), "dp", scatter_dimension=0, tiled=True
        ).astype(jnp.float32),
        lax.psum_scatter(
            grad_out_local.astype(jnp.bfloat16), "dp", scatter_dimension=1, tiled=True
        ).astype(jnp.float32),
        lax.psum_scatter(
            grad_up_local.astype(jnp.bfloat16), "dp", scatter_dimension=0, tiled=True
        ).astype(jnp.float32),
        lax.psum_scatter(
            grad_down_local.astype(jnp.bfloat16), "dp", scatter_dimension=1, tiled=True
        ).astype(jnp.float32),
        lax.psum_scatter(
            ada_cols.astype(jnp.bfloat16), "dp", scatter_dimension=1, tiled=True
        ).astype(jnp.float32),
        lax.psum_scatter(
            ada_bias_cols.astype(jnp.bfloat16), "dp", scatter_dimension=1, tiled=True
        ).astype(jnp.float32),
    )
    qv_full = lax.dynamic_update_slice_in_dim(
        jnp.zeros((2, model_width), jnp.float32), qv_local, tensor_rank * local_cols, axis=1
    )
    up_full = lax.dynamic_update_slice_in_dim(
        jnp.zeros((local_hidden * tensor_count,), jnp.float32),
        up_bias_local,
        tensor_rank * local_hidden,
        axis=0,
    )
    bias_sums = lax.psum(
        (
            qv_full,
            up_full,
            jnp.sum(grad_attn_branch, axis=0),
            jnp.sum(grad_mlp_branch, axis=0),
            jnp.sum(grad_first, axis=0),
            jnp.sum(grad_second, axis=0),
            jnp.sum(grad_projected, axis=0),
        ),
        ("dp", "tensor"),
    )
    qv_grad = lax.dynamic_slice_in_dim(bias_sums[0], tensor_rank * local_cols, local_cols, axis=1)
    up_bias_grad = lax.dynamic_slice_in_dim(
        bias_sums[1], tensor_rank * local_hidden, local_hidden, axis=0
    )
    proj_grads = (
        lax.psum_scatter(
            dot_tn(block_low, grad_first_low), ("dp", "tensor"), scatter_dimension=1, tiled=True
        ),
        lax.psum_scatter(
            dot_tn(first_low, grad_second_low), ("dp", "tensor"), scatter_dimension=1, tiled=True
        ),
        lax.psum_scatter(
            dot_tn(second_low, grad_last_low), ("dp", "tensor"), scatter_dimension=1, tiled=True
        ),
    )
    return (
        block_low,
        grad_tokens,
        grad_condition,
        block_grads[4],
        block_grads[5].reshape(-1),
        block_grads[0],
        qv_grad,
        block_grads[1],
        bias_sums[2],
        block_grads[2],
        up_bias_grad,
        block_grads[3],
        bias_sums[3],
        proj_grads[0],
        bias_sums[4],
        proj_grads[1],
        bias_sums[5],
        proj_grads[2],
        bias_sums[6],
    )


LANES = 128
MESH = pl.DeviceIdType.MESH
TILE = 256
LOG2_E = 1.4426950408889634
bf16 = jnp.bfloat16
f32 = jnp.float32


def pairs_of(move):
    found = []
    for index in range(32):
        x, core, y, z = index % 2, (index // 2) % 2, (index // 4) % 2, index // 8
        z2, y2, c2, x2 = move(z, y, core, x)
        if (z2, y2, c2, x2) != (z, y, core, x):
            found.append((index, ((z2 * 2 + y2) * 2 + c2) * 2 + x2))
    return found


def send(value, move):
    return lax.ppermute(value, ("dp", "tensor"), pairs_of(move))


def to_diag(z, y, c, x):
    return (z, y, x, c)


def to_cycle(z, y, c, x):
    return (z, y, c, c) if c != x else (z, y, 1 - c, x)


def to_core(z, y, c, x):
    return (z, y, 1 - c, x)


def to_x(z, y, c, x):
    return (z, y, c, 1 - x)


def to_y(z, y, c, x):
    return (z, 1 - y, c, x)


def to_z_near(z, y, c, x):
    return (z ^ 1, y, c, x)


def to_z_far(z, y, c, x):
    return (z ^ 2, y, c, x)


def pick(array, index, axis):
    return lax.dynamic_index_in_dim(array, index, axis=axis, keepdims=False)


def gather_kernel(own_ref, out_ref, local_sem, send_sem, recv_sem):
    dp = lax.axis_index("dp")
    x = lax.axis_index("tensor")
    core = dp % 2
    other = dp + 1 - 2 * core
    barrier = pltpu.get_barrier_semaphore()
    pl.semaphore_signal(barrier, inc=1, device_id=(other, x), device_id_type=MESH)
    pl.semaphore_wait(barrier, 1)
    away = pltpu.make_async_remote_copy(
        src_ref=own_ref,
        dst_ref=out_ref.at[core],
        send_sem=send_sem,
        recv_sem=recv_sem,
        device_id=(other, x),
        device_id_type=MESH,
    )
    away.start()
    here = pltpu.make_async_copy(own_ref, out_ref.at[core], local_sem)
    here.start()
    here.wait()
    away.wait()


def gather_cores(own):
    rows, width = own.shape
    return pl.pallas_call(
        gather_kernel,
        out_shape=jax.ShapeDtypeStruct((2, rows, width), own.dtype),
        in_specs=[pl.BlockSpec(memory_space=pltpu.VMEM)],
        out_specs=pl.BlockSpec(memory_space=pl.ANY),
        scratch_shapes=[pltpu.SemaphoreType.DMA] * 3,
        compiler_params=pltpu.CompilerParams(collective_id=0, has_side_effects=True, vmem_limit_bytes=16 << 20),
        cost_estimate=pl.CostEstimate(flops=0, bytes_accessed=12000000, transcendentals=0),
        name="gather_cores",
    )(own).reshape(2 * rows, width)


def split_heads(flat_ref, heads_ref, parts, heads):
    heads_ref[...] = jnp.zeros_like(heads_ref)
    for part in range(parts):
        for head in range(heads):
            begin = (part * heads + head) * HEAD_DIM
            heads_ref[part * heads + head, :, 0:HEAD_DIM] = flat_ref[:, begin : begin + HEAD_DIM]


def join_heads(heads_ref, flat_ref, count):
    rows, columns = flat_ref.shape
    for block in range(rows // LANES):
        span = slice(block * LANES, (block + 1) * LANES)
        pieces = [heads_ref[head, span, 0:HEAD_DIM] for head in range(count)]
        if columns > count * HEAD_DIM:
            pieces.append(jnp.zeros((LANES, columns - count * HEAD_DIM), flat_ref.dtype))
        flat_ref[span, :] = jnp.concatenate(pieces, axis=1)


def per_image(count, run):
    @pl.when(count == 1)
    def _():
        run(SHORT)

    @pl.when(count != 1)
    def _():
        run(4 * SHORT)


def attend_kernel(heads, together, factor, starts, counts, qkv_ref, o_ref, log_ref, part_ref, o_heads):
    split_heads(qkv_ref, part_ref, 3, heads)
    unit_count = o_ref.shape[0] // SHORT

    def some_heads(step, carry):
        def unit(index, carry):
            rows = pl.ds(pl.multiple_of(index * SHORT, SHORT), SHORT)

            def run(length):
                cols = pl.ds(pl.multiple_of(starts[index] * SHORT, SHORT), length)
                for ahead in range(together):
                    head = step * together + ahead
                    scores = dot_nt(part_ref[heads + head, cols, :], part_ref[head, rows, :])
                    top = jnp.max(scores, axis=0, keepdims=True)
                    exponent = jnp.exp2((scores - top) * factor)
                    total = jnp.sum(exponent, axis=0, keepdims=True)
                    summed = dot_tn(part_ref[2 * heads + head, cols, :], exponent.astype(bf16))
                    o_heads[head, rows, :] = (summed * (1.0 / total)).T.astype(bf16)
                    log_ref[head * unit_count + index] = top * factor + jnp.log2(total)

            per_image(counts[index], run)
            return carry

        return lax.fori_loop(0, unit_count, unit, carry)

    lax.fori_loop(0, heads // together, some_heads, 0)
    join_heads(o_heads, o_ref, heads)


def whole_spec(space=pltpu.VMEM):
    return pl.BlockSpec(memory_space=space)


def attend(starts, counts, qkv, heads, out_cols):
    rows = qkv.shape[0]
    factor = HEAD_DIM ** (-0.5) * LOG2_E
    return pl.pallas_call(
        functools.partial(attend_kernel, heads, 2, factor),
        out_shape=(
            jax.ShapeDtypeStruct((rows, out_cols), bf16),
            jax.ShapeDtypeStruct((heads * (rows // SHORT), 1, SHORT), f32),
        ),
        in_specs=[whole_spec(pltpu.SMEM), whole_spec(pltpu.SMEM), whole_spec()],
        out_specs=(whole_spec(), whole_spec()),
        scratch_shapes=[
            pltpu.VMEM((3 * heads, rows, LANES), bf16),
            pltpu.VMEM((heads, rows, LANES), bf16),
        ],
        compiler_params=pltpu.CompilerParams(vmem_limit_bytes=40 << 20),
        cost_estimate=pl.CostEstimate(flops=20 * 10**9, bytes_accessed=13 * 10**6, transcendentals=10**7),
        name="attend",
    )(starts, counts, qkv)


def attend_back_kernel(
    heads,
    together,
    factor,
    starts,
    counts,
    qkv_ref,
    log_ref,
    grad_ref,
    out_ref,
    bias_ref,
    part_ref,
    grad_heads,
    key_acc,
    value_acc,
    sums,
):
    split_heads(qkv_ref, part_ref, 3, heads)
    split_heads(grad_ref, grad_heads, 1, heads)
    unit_count = out_ref.shape[0] // SHORT

    def some_heads(step, carry):
        key_acc[...] = jnp.zeros_like(key_acc)
        value_acc[...] = jnp.zeros_like(value_acc)
        for ahead in range(together):
            sums[step * together + ahead] = jnp.zeros((8, LANES), f32)

        def unit(index, carry):
            rows = pl.ds(pl.multiple_of(index * SHORT, SHORT), SHORT)

            def run(length):
                cols = pl.ds(pl.multiple_of(starts[index] * SHORT, SHORT), length)
                for ahead in range(together):
                    head = step * together + ahead
                    queries = part_ref[head, rows, :]
                    grads = grad_heads[head, rows, :]
                    keys = part_ref[heads + head, cols, :]
                    scores = dot_nt(keys, queries)
                    soft = jnp.exp2(scores * (factor * LOG2_E) - log_ref[head * unit_count + index])
                    grad_soft = dot_nt(part_ref[2 * heads + head, cols, :], grads)
                    product = soft * grad_soft
                    inner = jnp.sum(product, axis=0, keepdims=True)
                    grad_scores = (product - soft * inner).astype(bf16)
                    value_acc[ahead, cols, :] += jnp.dot(soft.astype(bf16), grads, preferred_element_type=f32)
                    key_acc[ahead, cols, :] += jnp.dot(grad_scores, queries, preferred_element_type=f32)
                    grad_query = dot_tn(keys, grad_scores).T * factor
                    sums[head, 0:1, :] += jnp.sum(grad_query, axis=0, keepdims=True)
                    part_ref[head, rows, :] = grad_query.astype(bf16)

            per_image(counts[index], run)
            return carry

        lax.fori_loop(0, unit_count, unit, 0)
        for ahead in range(together):
            head = step * together + ahead
            sums[head, 1:2, :] = jnp.sum(value_acc[ahead], axis=0, keepdims=True)
            part_ref[heads + head] = (key_acc[ahead] * factor).astype(bf16)
            part_ref[2 * heads + head] = value_acc[ahead].astype(bf16)
        return carry

    lax.fori_loop(0, heads // together, some_heads, 0)
    join_heads(part_ref, out_ref, 3 * heads)
    bias_ref[...] = jnp.concatenate([sums[head, :, 0:HEAD_DIM] for head in range(heads)], axis=1)


def attend_back(starts, counts, qkv, log_sums, grad_heads, heads):
    rows, columns = qkv.shape
    factor = HEAD_DIM ** (-0.5)
    together = 2
    return pl.pallas_call(
        functools.partial(attend_back_kernel, heads, together, factor),
        out_shape=(
            jax.ShapeDtypeStruct((rows, columns), bf16),
            jax.ShapeDtypeStruct((8, heads * HEAD_DIM), f32),
        ),
        in_specs=[whole_spec(pltpu.SMEM), whole_spec(pltpu.SMEM)] + [whole_spec()] * 3,
        out_specs=(whole_spec(), whole_spec()),
        scratch_shapes=[
            pltpu.VMEM((3 * heads, rows, LANES), bf16),
            pltpu.VMEM((heads, rows, LANES), bf16),
            pltpu.VMEM((together, rows, LANES), f32),
            pltpu.VMEM((together, rows, LANES), f32),
            pltpu.VMEM((heads, 8, LANES), f32),
        ],
        compiler_params=pltpu.CompilerParams(vmem_limit_bytes=48 << 20),
        cost_estimate=pl.CostEstimate(flops=40 * 10**9, bytes_accessed=25 * 10**6, transcendentals=10**7),
        name="attend_back",
    )(starts, counts, qkv, log_sums, grad_heads)


def reduce_kernel(
    grid_rows,
    first_jobs,
    second_jobs,
    proj_jobs,
    one_left,
    one_right,
    two_left,
    two_right,
    three_left,
    three_right,
    four_left,
    four_right,
    mid_left,
    mid_right,
    in_left,
    in_right,
    last_left,
    last_right,
    bias_ref,
    slot_ref,
    first_out,
    second_out,
    proj_out,
    bias_out,
    slot_out,
    stage,
    first_left,
    second_left,
    first_right,
    second_right,
    proj_stage,
    proj_left,
    proj_right,
    p0,
    p0_got,
    p1,
    p1_got,
    p2,
    p2_got,
    p3,
    p3_got,
    f0,
    f0_turn,
    f0_swap,
    f1,
    f1_got,
    f2,
    f2_got,
    s0,
    s0_got,
    s1,
    s1_got,
    s2,
    s2_turn,
    s2_swap,
    bias_got,
    slot_x,
    slot_y,
    slot_y_got,
    slot_z,
    slot_z_got,
    load_sem,
    first_load,
    second_load,
    proj_load,
    p0_sems,
    p1_sems,
    p2_sems,
    p3_sems,
    f0_sems,
    f1_sems,
    f2_sems,
    s0_sems,
    s1_sems,
    s2_sems,
    bias_sems,
    slot_sems,
    slot_z_sems,
    first_free,
    second_free,
):
    dp = lax.axis_index("dp")
    x = lax.axis_index("tensor")
    core = dp % 2
    y = (dp // 2) % 2
    z = dp // 4
    home = core == x
    away = core != x

    def device(z_at, y_at, core_at, x_at):
        return ((z_at * 2 + y_at) * 2 + core_at, x_at)

    turn_to = device(z, y, core + (1 - 2 * core) * (1 - jnp.abs(core - x)), x + (core - x))
    turn_from = device(z, y, x + 0 * core, x + (1 - 2 * x) * (1 - jnp.abs(core - x)))
    swap_peer = device(z, y, x, core)
    y_peer = device(z, 1 - y, core, x)

    def z_peer(ahead):
        return device(lax.rem(z + ahead, 4), y, core, x)

    barrier = pltpu.get_barrier_semaphore()
    near = [device(z, y, 1 - core, x), device(z, y, core, 1 - x), device(z, y, 1 - core, 1 - x), y_peer]
    for peer in near + [z_peer(1), z_peer(2), z_peer(3)]:
        pl.semaphore_signal(barrier, inc=1, device_id=peer, device_id_type=MESH)
    pl.semaphore_wait(barrier, 7)

    def remote(source, target, sems, index, peer):
        return pltpu.make_async_remote_copy(
            src_ref=source,
            dst_ref=target,
            send_sem=sems.at[(0,) + index],
            recv_sem=sems.at[(1,) + index],
            device_id=peer,
            device_id_type=MESH,
        )

    def added(*terms):
        total = terms[0].astype(f32)
        for term in terms[1:]:
            total = total + term.astype(f32)
        return total

    def load_left(source, through, target):
        height = source.shape[1]
        through = through if height == through.shape[1] else through.at[:, 0:height]
        copy = pltpu.make_async_copy(source, through, load_sem)
        copy.start()
        copy.wait()

        def block(index, carry):
            rows = pl.ds(pl.multiple_of(index * LANES, LANES), LANES)
            target[0:height, rows] = through[rows, :].T
            return carry

        lax.fori_loop(0, source.shape[0] // LANES, block, 0)

    def right_copy(source, tile, target, sems, slot):
        columns = pl.ds(pl.multiple_of(tile * TILE, TILE), TILE)
        return pltpu.make_async_copy(source.at[:, columns], target.at[slot], sems.at[slot])

    first_split = one_right.shape[1] // TILE
    second_split = three_right.shape[1] // TILE

    def first_right_do(job, slot, action):
        @pl.when(job < first_split)
        def _():
            action(right_copy(one_right, job, first_right, first_load, slot))

        @pl.when(job >= first_split)
        def _():
            action(right_copy(two_right, job - first_split, first_right, first_load, slot))

    def second_right_do(job, slot, action):
        @pl.when(job < second_split)
        def _():
            action(right_copy(three_right, job, second_right, second_load, slot))

        @pl.when(job >= second_split)
        def _():
            action(right_copy(four_right, job - second_split, second_right, second_load, slot))

    def begin(copy):
        copy.start()

    def finish(copy):
        copy.wait()

    def multiply(left, right, slot, keep):
        def block(at_z, carry):
            height = 4 * grid_rows
            span = pl.ds(pl.multiple_of(at_z * height, 32), height)
            product = jnp.dot(left[span, :], right[slot], preferred_element_type=f32)
            for at_y in range(2):
                for at_core in range(2):
                    low = (at_y * 2 + at_core) * grid_rows
                    keep(at_z, at_y, at_core, product[low : low + grid_rows, :].astype(bf16))
            return carry

        lax.fori_loop(0, 4, block, 0)

    def f0_copies(slot):
        turn = remote(f0.at[slot, 1 - x], f0_turn.at[slot], f0_sems, (0, slot), turn_to)
        swap = remote(f0.at[slot, x], f0_swap.at[slot], f0_sems, (1, slot), swap_peer)
        return turn, swap

    def f1_copy(slot):
        return remote(f1.at[slot, 1 - y], f1_got.at[slot], f1_sems, (slot,), y_peer)

    def f2_copy(slot, ahead):
        return remote(
            f2.at[slot, lax.rem(z + ahead, 4)], f2_got.at[slot, ahead - 1], f2_sems, (slot, ahead - 1), z_peer(ahead)
        )

    def s0_copy(slot):
        return remote(s0.at[slot, 1 - y], s0_got.at[slot], s0_sems, (slot,), y_peer)

    def s1_copy(slot, ahead):
        return remote(
            s1.at[slot, lax.rem(z + ahead, 4)], s1_got.at[slot, ahead - 1], s1_sems, (slot, ahead - 1), z_peer(ahead)
        )

    def s2_copies(slot):
        turn = remote(s2.at[slot, 1 - x], s2_turn.at[slot], s2_sems, (0, slot), turn_to)
        swap = remote(s2.at[slot, x], s2_swap.at[slot], s2_sems, (1, slot), swap_peer)
        return turn, swap

    def inside(job, count):
        return jnp.logical_and(job >= 0, job < count)

    first_right_do(0, 0, begin)
    second_right_do(0, 0, begin)

    def first_tick(tick):
        @pl.when(tick < first_jobs)
        def _():
            slot = lax.rem(tick, 2)
            first_right_do(tick, slot, finish)

            @pl.when(tick + 1 < first_jobs)
            def _():
                first_right_do(tick + 1, 1 - slot, begin)

            @pl.when(tick == 0)
            def _():
                load_left(one_left, stage, first_left)

            @pl.when(tick == first_split)
            def _():
                load_left(two_left, stage, first_left)

            def keep(at_z, at_y, at_core, value):
                f0[slot, at_core, at_y, at_z] = value

            multiply(first_left, first_right, slot, keep)

        last = tick - 3

        @pl.when(inside(last, first_jobs))
        def _():
            slot = lax.rem(last, 2)
            for ahead in (1, 2, 3):
                f2_copy(slot, ahead).wait()
            first_out[last] = added(f2[slot, z], f2_got[slot, 0], f2_got[slot, 1], f2_got[slot, 2])

        third = tick - 2

        @pl.when(inside(third, first_jobs))
        def _():
            slot = lax.rem(third, 2)
            f1_copy(slot).wait()
            f2[slot] = added(f1[slot, y], f1_got[slot]).astype(bf16)
            for ahead in (1, 2, 3):
                f2_copy(slot, ahead).start()

        second = tick - 1

        @pl.when(inside(second, first_jobs))
        def _():
            slot = lax.rem(second, 2)
            turn, swap = f0_copies(slot)
            turn.wait()

            @pl.when(home)
            def _():
                f1[slot] = added(f0_turn[slot], f0[slot, x]).astype(bf16)

            @pl.when(away)
            def _():
                swap.wait()
                f1[slot] = added(f0_turn[slot], f0_swap[slot]).astype(bf16)

            @pl.when(second + 2 < first_jobs)
            def _():
                pl.semaphore_signal(first_free, inc=1, device_id=turn_from, device_id_type=MESH)

            f1_copy(slot).start()

        @pl.when(tick < first_jobs)
        def _():
            slot = lax.rem(tick, 2)
            turn, swap = f0_copies(slot)

            @pl.when(tick >= 2)
            def _():
                pl.semaphore_wait(first_free, 1)

            turn.start()

            @pl.when(away)
            def _():
                swap.start()

    def second_tick(tick):
        @pl.when(tick < second_jobs)
        def _():
            slot = lax.rem(tick, 2)
            second_right_do(tick, slot, finish)

            @pl.when(tick + 1 < second_jobs)
            def _():
                second_right_do(tick + 1, 1 - slot, begin)

            @pl.when(tick == 0)
            def _():
                load_left(three_left, stage, second_left)

            @pl.when(tick == second_split)
            def _():
                load_left(four_left, stage, second_left)

            def keep(at_z, at_y, at_core, value):
                s0[slot, at_y, at_z, at_core] = value

            multiply(second_left, second_right, slot, keep)

        last = tick - 3

        @pl.when(inside(last, second_jobs))
        def _():
            slot = lax.rem(last, 2)
            turn, swap = s2_copies(slot)
            turn.wait()

            @pl.when(home)
            def _():
                second_out[last] = added(s2_turn[slot], s2[slot, x])

            @pl.when(away)
            def _():
                swap.wait()
                second_out[last] = added(s2_turn[slot], s2_swap[slot])

            @pl.when(last + 2 < second_jobs)
            def _():
                pl.semaphore_signal(second_free, inc=1, device_id=turn_from, device_id_type=MESH)

        third = tick - 2

        @pl.when(inside(third, second_jobs))
        def _():
            slot = lax.rem(third, 2)
            for ahead in (1, 2, 3):
                s1_copy(slot, ahead).wait()
            s2[slot] = added(s1[slot, z], s1_got[slot, 0], s1_got[slot, 1], s1_got[slot, 2]).astype(bf16)
            turn, swap = s2_copies(slot)

            @pl.when(third >= 2)
            def _():
                pl.semaphore_wait(second_free, 1)

            turn.start()

            @pl.when(away)
            def _():
                swap.start()

        second = tick - 1

        @pl.when(inside(second, second_jobs))
        def _():
            slot = lax.rem(second, 2)
            s0_copy(slot).wait()
            s1[slot] = added(s0[slot, y], s0_got[slot]).astype(bf16)
            for ahead in (1, 2, 3):
                s1_copy(slot, ahead).start()

        @pl.when(tick < second_jobs)
        def _():
            s0_copy(lax.rem(tick, 2)).start()

    mid_jobs = mid_right.shape[1] // TILE
    in_jobs = -(-in_right.shape[1] // TILE)
    in_left_over = in_right.shape[1] % TILE
    proj_rows = mid_left.shape[1] // 32
    last_rows = last_left.shape[1] // 32

    def proj_right_do(job, slot, action):
        def copy(source, tile, columns):
            start = pl.multiple_of(tile * columns, LANES)
            return pltpu.make_async_copy(
                source.at[:, pl.ds(start, columns)], proj_right.at[slot, :, pl.ds(0, columns)], proj_load.at[slot]
            )

        @pl.when(job < mid_jobs)
        def _():
            action(copy(mid_right, job, TILE))

        full = in_jobs - (1 if in_left_over else 0)

        @pl.when(inside(job - mid_jobs, full))
        def _():
            action(copy(in_right, job - mid_jobs, TILE))

        if in_left_over:

            @pl.when(job == mid_jobs + full)
            def _():
                rest = pltpu.make_async_copy(
                    in_right.at[:, pl.ds(full * TILE, in_left_over)],
                    proj_right.at[slot, :, pl.ds(0, in_left_over)],
                    proj_load.at[slot],
                )
                action(rest)

        @pl.when(job >= mid_jobs + in_jobs)
        def _():
            action(copy(last_right, job - mid_jobs - in_jobs, 2 * TILE))

    def p0_copy(slot):
        return remote(p0.at[slot, 1 - core], p0_got.at[slot], p0_sems, (slot,), device(z, y, 1 - core, x))

    def p1_copy(slot):
        return remote(p1.at[slot, 1 - x], p1_got.at[slot], p1_sems, (slot,), device(z, y, core, 1 - x))

    def p2_copy(slot):
        return remote(p2.at[slot, 1 - y], p2_got.at[slot], p2_sems, (slot,), y_peer)

    def p3_copy(slot, ahead):
        return remote(
            p3.at[slot, lax.rem(z + ahead, 4)], p3_got.at[slot, ahead - 1], p3_sems, (slot, ahead - 1), z_peer(ahead)
        )

    pltpu.make_async_copy(mid_right.at[:, pl.ds(0, TILE)], proj_right.at[0, :, pl.ds(0, TILE)], proj_load.at[0]).start()

    def proj_tick(tick):
        @pl.when(tick < proj_jobs)
        def _():
            slot = lax.rem(tick, 2)
            proj_right_do(tick, slot, finish)

            @pl.when(tick + 1 < proj_jobs)
            def _():
                proj_right_do(tick + 1, 1 - slot, begin)

            for at, source in ((0, mid_left), (mid_jobs, in_left), (mid_jobs + in_jobs, last_left)):

                @pl.when(tick == at)
                def _(source=source):
                    load_left(source, proj_stage, proj_left)

            shares = [(at_y, at_core, at_x) for at_y in range(2) for at_core in range(2) for at_x in range(2)]

            @pl.when(tick < mid_jobs + in_jobs)
            def _():
                def block(at_z, carry):
                    span = pl.ds(pl.multiple_of(at_z * 8 * proj_rows, 32), 8 * proj_rows)
                    right = proj_right[slot, :, 0:TILE]
                    product = jnp.dot(proj_left[span, :], right, preferred_element_type=f32).astype(bf16)
                    for low, (at_y, at_core, at_x) in enumerate(shares):
                        p0[slot, at_core, at_x, at_y, at_z] = product[low * proj_rows : (low + 1) * proj_rows, :]
                    return carry

                lax.fori_loop(0, 4, block, 0)

            @pl.when(tick >= mid_jobs + in_jobs)
            def _():
                def block(at_z, carry):
                    span = pl.ds(pl.multiple_of(at_z * 8 * last_rows, 32), 8 * last_rows)
                    for half in range(2):
                        right = proj_right[slot, :, half * TILE : (half + 1) * TILE]
                        product = jnp.dot(proj_left[span, :], right, preferred_element_type=f32)
                        begin_row = half * proj_rows // 2
                        for low, (at_y, at_core, at_x) in enumerate(shares):
                            p0[slot, at_core, at_x, at_y, at_z, begin_row : begin_row + last_rows, :] = product[
                                low * last_rows : (low + 1) * last_rows, :
                            ].astype(bf16)
                    return carry

                lax.fori_loop(0, 4, block, 0)

        fifth = tick - 4

        @pl.when(inside(fifth, proj_jobs))
        def _():
            slot = lax.rem(fifth, 2)
            for ahead in (1, 2, 3):
                p3_copy(slot, ahead).wait()
            proj_out[fifth] = added(p3[slot, z], p3_got[slot, 0], p3_got[slot, 1], p3_got[slot, 2])

        fourth = tick - 3

        @pl.when(inside(fourth, proj_jobs))
        def _():
            slot = lax.rem(fourth, 2)
            p2_copy(slot).wait()
            p3[slot] = added(p2[slot, y], p2_got[slot]).astype(bf16)
            for ahead in (1, 2, 3):
                p3_copy(slot, ahead).start()

        third = tick - 2

        @pl.when(inside(third, proj_jobs))
        def _():
            slot = lax.rem(third, 2)
            p1_copy(slot).wait()
            p2[slot] = added(p1[slot, x], p1_got[slot]).astype(bf16)
            p2_copy(slot).start()

        second = tick - 1

        @pl.when(inside(second, proj_jobs))
        def _():
            slot = lax.rem(second, 2)
            p0_copy(slot).wait()
            p1[slot] = added(p0[slot, core], p0_got[slot]).astype(bf16)
            p1_copy(slot).start()

        @pl.when(tick < proj_jobs)
        def _():
            p0_copy(lax.rem(tick, 2)).start()

    bias_peers = [
        device(z, y, 1 - core, x),
        device(z, y, core, 1 - x),
        y_peer,
        device(z + 1 - 2 * lax.rem(z, 2), y, core, x),
        device(lax.rem(z + 2, 4), y, core, x),
    ]

    def bias_copy(step):
        return remote(bias_out, bias_got.at[step], bias_sems, (step,), bias_peers[step])

    def slot_x_copy():
        return remote(slot_ref.at[1 - x], slot_x, slot_sems, (0,), device(z, y, core, 1 - x))

    def slot_y_copy():
        return remote(slot_y.at[1 - y], slot_y_got, slot_sems, (1,), y_peer)

    def slot_z_copy(ahead):
        return remote(
            slot_z.at[lax.rem(z + ahead, 4)], slot_z_got.at[ahead - 1], slot_z_sems, (ahead - 1,), z_peer(ahead)
        )

    def small_tick(tick):
        @pl.when(tick == 0)
        def _():
            bias_out[...] = bias_ref[...]
            slot_x_copy().start()

        for step in range(5):

            @pl.when(tick == step + 1)
            def _(step=step):
                bias_copy(step).wait()
                bias_out[...] = bias_out[...] + bias_got[step]

        for step in range(5):

            @pl.when(tick == step)
            def _(step=step):
                bias_copy(step).start()

        @pl.when(tick == 1)
        def _():
            slot_x_copy().wait()
            for at_y in range(2):
                slot_y[at_y, x] = slot_ref[x, at_y]
                slot_y[at_y, 1 - x] = slot_x[at_y]
            slot_y_copy().start()

        @pl.when(tick == 2)
        def _():
            slot_y_copy().wait()
            for at_z in range(4):
                slot_z[at_z, y] = slot_y[y, :, at_z]
                slot_z[at_z, 1 - y] = slot_y_got[:, at_z]
            for ahead in (1, 2, 3):
                slot_z_copy(ahead).start()

        @pl.when(tick == 3)
        def _():
            slot_out[z] = slot_z[z]
            for ahead in (1, 2, 3):
                slot_z_copy(ahead).wait()
                slot_out[lax.rem(z + 4 - ahead, 4)] = slot_z_got[ahead - 1]

    def tick_body(tick, carry):
        small_tick(tick)
        second_tick(tick)
        proj_tick(tick)

        @pl.when(lax.rem(tick, 4) != 3)
        def _():
            first_tick(tick // 4 * 3 + lax.rem(tick, 4))

        return carry

    ticks = max(second_jobs + 3, proj_jobs + 4, -(-4 * (first_jobs + 3) // 3))
    lax.fori_loop(0, ticks, tick_body, 0)


def reduce_grads(one, two, three, four, mid, first, last, bias, slots):
    tokens, width = one[0].shape
    grid_rows = width // 16
    first_jobs = (one[1].shape[1] + two[1].shape[1]) // TILE
    second_jobs = (three[1].shape[1] + four[1].shape[1]) // TILE
    proj_jobs = mid[1].shape[1] // TILE + -(-first[1].shape[1] // TILE) + last[1].shape[1] // (2 * TILE)
    proj_tokens, proj_hidden = mid[0].shape
    proj_tile = (proj_hidden // 32, TILE)
    tile = (grid_rows, TILE)
    dma = pltpu.SemaphoreType.DMA
    slot_tail = slots.shape[-2:]

    def low(*lead):
        return pltpu.VMEM(lead + tile, bf16)

    scratch = [
        pltpu.VMEM((tokens, width), bf16),
        pltpu.VMEM((width, tokens), bf16),
        pltpu.VMEM((width, tokens), bf16),
        pltpu.VMEM((2, tokens, TILE), bf16),
        pltpu.VMEM((2, tokens, TILE), bf16),
        pltpu.VMEM((proj_tokens, proj_hidden), bf16),
        pltpu.VMEM((proj_hidden, proj_tokens), bf16),
        pltpu.VMEM((2, proj_tokens, 2 * TILE), bf16),
        pltpu.VMEM((2, 2, 2, 2, 4) + proj_tile, bf16),
        pltpu.VMEM((2, 2, 2, 4) + proj_tile, bf16),
        pltpu.VMEM((2, 2, 2, 4) + proj_tile, bf16),
        pltpu.VMEM((2, 2, 4) + proj_tile, bf16),
        pltpu.VMEM((2, 2, 4) + proj_tile, bf16),
        pltpu.VMEM((2, 4) + proj_tile, bf16),
        pltpu.VMEM((2, 4) + proj_tile, bf16),
        pltpu.VMEM((2, 3) + proj_tile, bf16),
        low(2, 2, 2, 4),
        low(2, 2, 4),
        low(2, 2, 4),
        low(2, 2, 4),
        low(2, 4),
        low(2, 4),
        low(2, 3),
        low(2, 2, 4, 2),
        low(2, 4, 2),
        low(2, 4, 2),
        low(2, 3, 2),
        low(2, 2),
        low(2),
        low(2),
        pltpu.VMEM((5,) + bias.shape, f32),
        pltpu.VMEM((2, 4) + slot_tail, f32),
        pltpu.VMEM((2, 2, 4) + slot_tail, f32),
        pltpu.VMEM((2, 4) + slot_tail, f32),
        pltpu.VMEM((4, 2, 2) + slot_tail, f32),
        pltpu.VMEM((3, 2, 2) + slot_tail, f32),
        dma,
        dma((2,)),
        dma((2,)),
        dma((2,)),
        dma((2, 2)),
        dma((2, 2)),
        dma((2, 2)),
        dma((2, 2, 3)),
        dma((2, 2, 2)),
        dma((2, 2)),
        dma((2, 2, 3)),
        dma((2, 2)),
        dma((2, 2, 3)),
        dma((2, 2, 2)),
        dma((2, 5)),
        dma((2, 2)),
        dma((2, 3)),
        pltpu.SemaphoreType.REGULAR,
        pltpu.SemaphoreType.REGULAR,
    ]
    return pl.pallas_call(
        functools.partial(reduce_kernel, grid_rows, first_jobs, second_jobs, proj_jobs),
        out_shape=(
            jax.ShapeDtypeStruct((first_jobs,) + tile, f32),
            jax.ShapeDtypeStruct((second_jobs,) + tile, f32),
            jax.ShapeDtypeStruct((proj_jobs,) + proj_tile, f32),
            jax.ShapeDtypeStruct(bias.shape, f32),
            jax.ShapeDtypeStruct((4, 2, 2) + slot_tail, f32),
        ),
        in_specs=[whole_spec(pl.ANY)] * 14 + [whole_spec()] * 2,
        out_specs=(whole_spec(),) * 5,
        scratch_shapes=scratch,
        compiler_params=pltpu.CompilerParams(
            collective_id=1, has_side_effects=True, vmem_limit_bytes=52 << 20
        ),
        cost_estimate=pl.CostEstimate(flops=10**11, bytes_accessed=10**8, transcendentals=0),
        name="reduce_grads",
    )(*one, *two, *three, *four, *mid, *first, *last, bias, slots)


def after(value, earlier):
    return lax.optimization_barrier((value, earlier))[0]


def paired_shards(
    tokens_in,
    condition,
    ada_weight,
    ada_bias,
    qkv_weight,
    qv_bias,
    out_weight,
    out_bias,
    up_weight,
    up_bias,
    down_weight,
    down_bias,
    proj_in,
    proj_in_bias,
    proj_mid,
    proj_mid_bias,
    proj_last,
    proj_last_bias,
    enc_features,
    image_ids,
    target_rows,
    out_grad,
):
    dp = lax.axis_index("dp")
    x = lax.axis_index("tensor")
    core = dp % 2
    y = (dp // 2) % 2
    z = dp // 4
    z_near = z % 2
    z_far = z // 2
    place = dp * 2 + x
    home = core == x
    group = (dp // 2) * 2 + x
    local_rows, width = tokens_in.shape
    shard_rows = image_ids.shape[0]
    slots = condition.shape[0]
    units = local_rows // SHORT
    local_cols = qkv_weight.shape[2]
    local_hidden = up_weight.shape[1]
    heads = local_cols // HEAD_DIM
    qkv_cols = -(-3 * local_cols // TILE) * TILE
    out_cols = -(-local_cols // TILE) * TILE

    def swap(value):
        return jnp.where(home, value, send(value, to_diag))

    tokens = swap(tokens_in)
    packed_ids = send(image_ids, to_core)
    ids = jnp.where(home, image_ids, packed_ids)
    cond_low = jnp.where(home, condition, send(condition, to_core))
    qkv_half = swap(after(qkv_weight.reshape(width, 3 * local_cols), tokens))
    out_half = swap(after(out_weight, qkv_half))
    up_half = swap(after(up_weight, out_half))
    down_half = swap(after(down_weight, up_half))
    features = jnp.where(home, enc_features, send(enc_features, to_core))
    rows_low = swap(after(target_rows, down_half))
    grad_out = swap(after(out_grad, down_half))
    bias_pack = jnp.concatenate([qv_bias.reshape(-1), up_bias])
    bias_half = swap(bias_pack).astype(f32)
    qv_half = bias_half[: 2 * local_cols].reshape(2, local_cols)
    up_bias_half = bias_half[2 * local_cols :]

    unit_ids = ids.reshape(-1, SHORT)[:, 0]
    same = unit_ids[:, None] == unit_ids[None, :]
    starts = jnp.argmax(same, axis=1).astype(jnp.int32)
    counts = jnp.sum(same.astype(jnp.int32), axis=1).astype(jnp.int32)
    my_units = lax.dynamic_slice_in_dim(unit_ids, core * units, units)
    one_hot = (my_units[:, None] == jnp.arange(slots, dtype=jnp.int32)[None, :]).astype(f32)

    silu_cond, silu_back = jax.vjp(jax.nn.silu, cond_low.astype(f32))
    silu_low = silu_cond.astype(bf16)
    modulation = jnp.dot(silu_low, ada_weight, preferred_element_type=f32) + ada_bias.astype(f32)
    per_unit = jnp.dot(one_hot, modulation, precision=highest, preferred_element_type=f32)
    shift_one, scale_one, gate_one, shift_two, scale_two, gate_two = [
        piece[:, None, :] for piece in jnp.split(per_unit, 6, axis=1)
    ]

    def by_unit(array):
        return array.reshape(units, SHORT, -1)

    def flat(array):
        return array.reshape(local_rows, -1)

    def reduce_cores(left, matrix, product):
        mine = lax.dynamic_slice_in_dim(left, core * local_rows, local_rows)
        theirs = lax.dynamic_slice_in_dim(left, (1 - core) * local_rows, local_rows)
        got = send(product(theirs, matrix).astype(bf16), to_core)
        return product(mine, matrix).astype(bf16).astype(f32) + got.astype(f32)

    def dot_nn(left, right):
        return jnp.dot(left, right, preferred_element_type=f32)

    resid = by_unit(tokens.astype(f32))
    normed_one, inv_one = layer_norm(resid)
    attn_in = flat((normed_one * (1.0 + scale_one) + shift_one).astype(bf16))
    attn_all = gather_cores(attn_in)

    qkv_pad = jnp.pad(qkv_half, ((0, 0), (0, qkv_cols - 3 * local_cols)))
    out_pad = jnp.pad(out_half, ((0, out_cols - local_cols), (0, 0)))
    qkv_bias = jnp.concatenate(
        [qv_half[0], jnp.zeros_like(qv_half[0]), qv_half[1], jnp.zeros((qkv_cols - 3 * local_cols,), f32)]
    )
    qkv = (dot_nn(attn_all, qkv_pad) + qkv_bias).astype(bf16)
    attended, log_sums = attend(starts, counts, qkv, heads, out_cols)
    attn_branch = by_unit(reduce_cores(attended, out_pad, dot_nn) + out_bias.astype(f32))
    mid = resid + gate_one * attn_branch

    normed_two, inv_two = layer_norm(mid)
    mlp_in = flat((normed_two * (1.0 + scale_two) + shift_two).astype(bf16))
    mlp_all = gather_cores(mlp_in)
    pre_act = dot_nn(mlp_all, up_half) + up_bias_half
    act_value, act_back = jax.vjp(gelu_tanh, pre_act)
    hidden = act_value.astype(bf16)
    mlp_branch = by_unit(reduce_cores(hidden, down_half, dot_nn) + down_bias.astype(f32))
    block_value = mid + gate_two * mlp_branch
    block_low = flat(block_value.astype(bf16))

    first_pre = dot_nn(block_low, proj_in) + proj_in_bias.astype(f32)
    first_value, first_back = jax.vjp(jax.nn.silu, first_pre)
    first_low = first_value.astype(bf16)
    second_pre = dot_nn(first_low, proj_mid) + proj_mid_bias.astype(f32)
    second_value, second_back = jax.vjp(jax.nn.silu, second_pre)
    second_low = second_value.astype(bf16)
    projected = dot_nn(second_low, proj_last) + proj_last_bias.astype(f32)
    target_vals = jnp.take(features, rows_low - group * shard_rows, axis=0).astype(f32)
    loss_back = jax.vjp(lambda predicted: align_loss(predicted, target_vals), projected)[1]
    grad_projected = loss_back(jnp.ones((), f32))[0]
    grad_last_low = grad_projected.astype(bf16)
    grad_second = second_back(dot_nt(grad_last_low, proj_last))[0]
    grad_second_low = grad_second.astype(bf16)
    grad_first = first_back(dot_nt(grad_second_low, proj_mid))[0]
    grad_first_low = grad_first.astype(bf16)
    grad_block = by_unit(grad_out.astype(f32) + dot_nt(grad_first_low, proj_in))

    silu_all = lax.dynamic_update_index_in_dim(
        jnp.zeros((16, slots, width), bf16), after(silu_low, first_low), group, axis=0
    )
    for move in (to_x, to_y, to_z_near, to_z_far):
        silu_all = silu_all + send(silu_all, move)

    grad_mlp_branch = gate_two * grad_block
    grad_mlp_all = gather_cores(flat(grad_mlp_branch.astype(bf16)))
    grad_pre = act_back(dot_nt(grad_mlp_all, down_half))[0]
    grad_pre_low = grad_pre.astype(bf16)
    grad_mlp_in = by_unit(reduce_cores(grad_pre_low, up_half, dot_nt))
    grad_mid = grad_block + norm_back(normed_two, inv_two, grad_mlp_in * (1.0 + scale_two))

    grad_attn_branch = gate_one * grad_mid
    grad_attn_all = gather_cores(flat(grad_attn_branch.astype(bf16)))
    grad_heads = dot_nt(grad_attn_all, out_pad).astype(bf16)
    grad_qkv, qkv_bias_sums = attend_back(starts, counts, qkv, log_sums, grad_heads, heads)
    grad_attn_in = by_unit(reduce_cores(grad_qkv, qkv_pad, dot_nt))
    grad_tokens = grad_mid + norm_back(normed_one, inv_one, grad_attn_in * (1.0 + scale_one))

    def unit_sum(array):
        return jnp.sum(array, axis=1)

    mod_units = jnp.concatenate(
        [
            unit_sum(grad_attn_in),
            unit_sum(grad_attn_in * normed_one),
            unit_sum(attn_branch * grad_mid),
            unit_sum(grad_mlp_in),
            unit_sum(grad_mlp_in * normed_two),
            unit_sum(mlp_branch * grad_block),
        ],
        axis=1,
    )
    slot_part = dot_tn(one_hot, mod_units, precision=highest)
    slot_grad = slot_part + send(slot_part, to_core)
    slot_low = slot_grad.astype(bf16)
    grad_condition = swap(silu_back(dot_nt(slot_low, ada_weight))[0])
    mod_cols = slot_low.shape[1] // 32
    slot_cols = pick(slot_grad.reshape(slots, 4, 2, 2, 2, mod_cols), core, 3).transpose(3, 2, 1, 0, 4)
    slot_cols = jnp.pad(slot_cols, ((0, 0),) * 3 + ((0, 8 - slots), (0, -mod_cols % LANES)))

    qv_sums = qkv_bias_sums[:2]
    qv_full = lax.dynamic_update_slice_in_dim(jnp.zeros((2, width), f32), qv_sums, core * local_cols, axis=1)
    up_full = lax.dynamic_update_slice_in_dim(
        jnp.zeros((2 * local_hidden,), f32), jnp.sum(grad_pre, axis=0), core * local_hidden, axis=0
    )
    pieces = [
        qv_full.reshape(-1),
        up_full,
        jnp.sum(flat(grad_attn_branch), axis=0),
        jnp.sum(flat(grad_mlp_branch), axis=0),
        jnp.sum(grad_first, axis=0),
        jnp.sum(grad_second, axis=0),
        jnp.sum(grad_projected, axis=0),
    ]
    packed = jnp.concatenate(pieces)
    packed = jnp.pad(packed, (0, -packed.shape[0] % (8 * LANES))).reshape(-1, LANES)
    first_sum, second_sum, proj_sum, sums, slot_sum = reduce_grads(
        (grad_mlp_all, hidden),
        (grad_attn_all, attended),
        (mlp_all, grad_pre_low),
        (attn_all, grad_qkv),
        (grad_second_low, first_low),
        (grad_first_low, block_low),
        (grad_last_low, second_low),
        packed,
        slot_cols,
    )
    sums = sums.reshape(-1)
    slot_mine = slot_sum.reshape(16, 8, -1)[:, :slots, :mod_cols].astype(bf16).reshape(16 * slots, mod_cols)
    grad_ada = dot_tn(silu_all.reshape(16 * slots, width), slot_mine)
    ada_bias_grad = jnp.sum(slot_mine.astype(f32), axis=0)
    row_count = width // 16

    def columns(tiles):
        return tiles.transpose(1, 0, 2).reshape(tiles.shape[1], -1)

    def rows(tiles):
        return tiles.transpose(0, 2, 1).reshape(-1, tiles.shape[1])

    down_tiles = local_hidden // TILE
    sum_down = rows(first_sum[:down_tiles])
    sum_out = rows(first_sum[down_tiles:])[:local_cols]
    sum_up = columns(second_sum[:down_tiles])
    sum_qkv = columns(second_sum[down_tiles:])[:, : 3 * local_cols].reshape(row_count, 3, local_cols)
    mid_tiles = proj_mid.shape[0] // TILE
    in_tiles = -(-width // TILE)
    sum_mid = rows(proj_sum[:mid_tiles])
    sum_in = rows(proj_sum[mid_tiles : mid_tiles + in_tiles])[:width]
    last_share = proj_last.shape[1] // 32
    last_tiles = proj_sum[mid_tiles + in_tiles :]
    last_tiles = last_tiles.reshape(last_tiles.shape[0] * 2, -1, TILE)[:, :last_share]
    sum_last = rows(last_tiles)
    found = []
    offset = 0
    for piece in pieces:
        found.append(sums[offset : offset + piece.shape[0]])
        offset += piece.shape[0]
    qv_grad = lax.dynamic_slice_in_dim(found[0].reshape(2, width), x * local_cols, local_cols, axis=1)
    up_bias_grad = lax.dynamic_slice_in_dim(found[1], x * local_hidden, local_hidden, axis=0)

    block_out = swap(block_low)
    tokens_out = swap(flat(grad_tokens).astype(bf16))
    return (
        block_out,
        tokens_out.astype(f32),
        grad_condition,
        grad_ada,
        ada_bias_grad,
        sum_qkv,
        qv_grad,
        sum_out,
        found[2],
        sum_up,
        up_bias_grad,
        sum_down,
        found[3],
        sum_in,
        found[4],
        sum_mid,
        found[5],
        sum_last,
        found[6],
    )


def solution(mesh):
    in_specs = (
        P(("dp", "tensor"), None),
        P("dp", None),
        P(),
        P(),
        P(None, None, "tensor"),
        P(None, "tensor"),
        P("tensor", None),
        P(),
        P(None, "tensor"),
        P("tensor"),
        P("tensor", None),
        P(),
        P(),
        P(),
        P(),
        P(),
        P(),
        P(),
        P("dp", None),
        P("dp"),
        P(("dp", "tensor")),
        P(("dp", "tensor"), None),
    )
    out_specs = (
        P(("dp", "tensor"), None),
        P(("dp", "tensor"), None),
        P("dp", None),
        P(None, ("dp", "tensor")),
        P(("dp", "tensor")),
        P("dp", None, "tensor"),
        P(None, "tensor"),
        P("tensor", "dp"),
        P(),
        P("dp", "tensor"),
        P("tensor"),
        P("tensor", "dp"),
        P(),
        P(None, ("dp", "tensor")),
        P(),
        P(None, ("dp", "tensor")),
        P(),
        P(None, ("dp", "tensor")),
        P(),
    )
    paired = mesh.shape["tensor"] == 2 and mesh.shape["dp"] == 16
    body = paired_shards if paired else shards
    return jax.shard_map(body, mesh=mesh, in_specs=in_specs, out_specs=out_specs, check_vma=False)
```

```python
import functools

import jax
import jax.numpy as jnp
from jax import lax
from jax.experimental import pallas as pl
from jax.experimental.pallas import tpu as pltpu
from jax.sharding import PartitionSpec as P

HEAD_DIM = 72
SHORT = 256


highest = lax.Precision.HIGHEST
eps_norm = 1e-06
repa_weight = 1000.0
neg_fill = -1e30


def dot_nt(left_arg, right_arg):
    return lax.dot_general(
        left_arg, right_arg, (((1,), (1,)), ((), ())), preferred_element_type=jnp.float32
    )


def dot_tn(left_arg, right_arg, precision=None):
    return lax.dot_general(
        left_arg,
        right_arg,
        (((0,), (0,)), ((), ())),
        precision=precision,
        preferred_element_type=jnp.float32,
    )


def layer_norm(values):
    center = values - jnp.mean(values, axis=-1, keepdims=True)
    inv_std = lax.rsqrt(jnp.mean(center * center, axis=-1, keepdims=True) + eps_norm)
    return (center * inv_std, inv_std)


def norm_back(normed, inv_std, grad_normed):
    return inv_std * (
        grad_normed
        - jnp.mean(grad_normed, axis=-1, keepdims=True)
        - normed * jnp.mean(grad_normed * normed, axis=-1, keepdims=True)
    )


def gelu_tanh(values):
    return jax.nn.gelu(values, approximate=True)


def align_loss(projected, target_vals):
    inner = jnp.sum(projected * target_vals, axis=1)
    norm_pred = lax.rsqrt(jnp.sum(projected * projected, axis=1) + eps_norm)
    norm_target = lax.rsqrt(jnp.sum(target_vals * target_vals, axis=1) + eps_norm)
    return -repa_weight * jnp.sum(inner * norm_pred * norm_target)


def block_rows(total_rows, unit_rows):
    count = total_rows // unit_rows
    best = 1
    for parts in range(1, count + 1):
        if count % parts == 0 and parts * unit_rows <= 1024:
            best = parts
    return best * unit_rows


def block_scores(queries, key_rows, image_ids, row_start, starts, block_len, score_scale):
    query_blk = queries[row_start : row_start + block_len]
    row_ids = image_ids[row_start : row_start + block_len]
    pieces = []
    for col_start in starts:

        def compute_block(col_start=col_start):
            products = (
                jnp.einsum(
                    "qhd,khd->hqk",
                    query_blk,
                    key_rows[col_start : col_start + block_len],
                    preferred_element_type=jnp.float32,
                )
                * score_scale
            )
            same_image = row_ids[:, None] == image_ids[col_start : col_start + block_len][None, :]
            return jnp.where(same_image[None], products, neg_fill)

        pieces.append(compute_block())
    return jnp.concatenate(pieces, axis=2)


def attention_forward(queries, key_rows, values, image_ids, block_len, score_scale):
    starts = list(range(0, queries.shape[0], block_len))
    outputs = []
    log_sums = []
    for row_start in starts:
        scores = block_scores(
            queries, key_rows, image_ids, row_start, starts, block_len, score_scale
        )
        row_max = jnp.max(scores, axis=2, keepdims=True)
        exponent = jnp.exp(scores - row_max)
        row_total = jnp.sum(exponent, axis=2, keepdims=True)
        prob_low = (exponent / row_total).astype(jnp.bfloat16)
        log_sums.append(row_max + jnp.log(row_total))
        summed = jnp.zeros((block_len, queries.shape[1], queries.shape[2]), jnp.float32)
        for position, col_start in enumerate(starts):

            def weigh_block(position=position, col_start=col_start, prob_low=prob_low):
                return jnp.einsum(
                    "hqk,khd->qhd",
                    prob_low[:, :, position * block_len : (position + 1) * block_len],
                    values[col_start : col_start + block_len],
                    preferred_element_type=jnp.float32,
                )

            summed = summed + weigh_block()
        outputs.append(summed.astype(jnp.bfloat16))
    return (jnp.concatenate(outputs, axis=0), jnp.concatenate(log_sums, axis=1))


def attention_backward(
    queries, key_rows, values, image_ids, log_sums, grad_heads, block_len, score_scale
):
    starts = list(range(0, queries.shape[0], block_len))
    grad_keys = jnp.zeros(key_rows.shape, jnp.float32)
    grad_values = jnp.zeros(values.shape, jnp.float32)
    grad_query_list = []
    for row_start in starts:
        query_blk = queries[row_start : row_start + block_len]
        grad_blk = grad_heads[row_start : row_start + block_len]
        scores = block_scores(
            queries, key_rows, image_ids, row_start, starts, block_len, score_scale
        )
        soft = jnp.exp(scores - log_sums[:, row_start : row_start + block_len])
        grad_pieces = []
        for col_start in starts:

            def pull_block(col_start=col_start):
                return jnp.einsum(
                    "qhd,khd->hqk",
                    grad_blk,
                    values[col_start : col_start + block_len],
                    preferred_element_type=jnp.float32,
                )

            grad_pieces.append(pull_block())
        grad_soft = jnp.concatenate(grad_pieces, axis=2)
        inner = jnp.sum(soft * grad_soft, axis=2, keepdims=True)
        grad_scores = (soft * (grad_soft - inner)).astype(jnp.bfloat16)
        soft_low = soft.astype(jnp.bfloat16)
        grad_query = jnp.zeros(query_blk.shape, jnp.float32)
        for position, col_start in enumerate(starts):

            def both_grads(position=position, col_start=col_start):
                piece = grad_scores[:, :, position * block_len : (position + 1) * block_len]
                soft_piece = soft_low[:, :, position * block_len : (position + 1) * block_len]
                return (
                    jnp.einsum(
                        "hqk,khd->qhd",
                        piece,
                        key_rows[col_start : col_start + block_len],
                        preferred_element_type=jnp.float32,
                    ),
                    jnp.einsum(
                        "hqk,qhd->khd", piece, query_blk, preferred_element_type=jnp.float32
                    ),
                    jnp.einsum(
                        "hqk,qhd->khd", soft_piece, grad_blk, preferred_element_type=jnp.float32
                    ),
                )

            part_query, part_key, part_value = both_grads()
            grad_query = grad_query + part_query
            grad_keys = grad_keys.at[col_start : col_start + block_len].add(part_key)
            grad_values = grad_values.at[col_start : col_start + block_len].add(part_value)
        grad_query_list.append(grad_query * score_scale)
    return (jnp.concatenate(grad_query_list, axis=0), grad_keys * score_scale, grad_values)


def column_set(matrix, data_count, tensor_count, tensor_rank):
    shaped = matrix.reshape(matrix.shape[0], data_count, tensor_count, -1)
    return lax.dynamic_index_in_dim(shaped, tensor_rank, axis=2, keepdims=False).reshape(
        matrix.shape[0], -1
    )


def shards(
    tokens_in,
    condition,
    ada_weight,
    ada_bias,
    qkv_weight,
    qv_bias,
    out_weight,
    out_bias,
    up_weight,
    up_bias,
    down_weight,
    down_bias,
    proj_in,
    proj_in_bias,
    proj_mid,
    proj_mid_bias,
    proj_last,
    proj_last_bias,
    enc_features,
    image_ids,
    target_rows,
    out_grad,
):
    tensor_count = lax.axis_size("tensor")
    data_count = lax.axis_size("dp")
    tensor_rank = lax.axis_index("tensor")
    data_rank = lax.axis_index("dp")
    local_rows, model_width = tokens_in.shape
    shard_rows = image_ids.shape[0]
    slot_count = condition.shape[0]
    local_cols = qkv_weight.shape[2]
    local_hidden = up_weight.shape[1]
    head_count = local_cols // HEAD_DIM
    score_scale = HEAD_DIM ** (-0.5)
    block_len = block_rows(shard_rows, SHORT)
    my_ids = lax.dynamic_slice_in_dim(image_ids, tensor_rank * local_rows, local_rows)
    one_hot = (my_ids[:, None] == jnp.arange(slot_count, dtype=jnp.int32)[None, :]).astype(
        jnp.float32
    )
    cond_float = condition.astype(jnp.float32)
    silu_cond, silu_back = jax.vjp(jax.nn.silu, cond_float)
    silu_low = silu_cond.astype(jnp.bfloat16)
    modulation = jnp.dot(
        silu_low, ada_weight, preferred_element_type=jnp.float32
    ) + ada_bias.astype(jnp.float32)
    per_token = jnp.dot(one_hot, modulation, precision=highest, preferred_element_type=jnp.float32)
    shift_one, scale_one, gate_one, shift_two, scale_two, gate_two = jnp.split(per_token, 6, axis=1)
    resid = tokens_in.astype(jnp.float32)
    normed_one, inv_one = layer_norm(resid)
    attn_in = (normed_one * (1.0 + scale_one) + shift_one).astype(jnp.bfloat16)
    attn_all = lax.all_gather(attn_in, "tensor", axis=0, tiled=True)
    qkv_flat_weight = qkv_weight.reshape(model_width, 3 * local_cols)
    qkv_flat = jnp.dot(attn_all, qkv_flat_weight, preferred_element_type=jnp.float32)
    bias_float = qv_bias.astype(jnp.float32)
    queries = (
        (qkv_flat[:, :local_cols] + bias_float[0])
        .astype(jnp.bfloat16)
        .reshape(shard_rows, head_count, HEAD_DIM)
    )
    key_rows = (
        qkv_flat[:, local_cols : 2 * local_cols]
        .astype(jnp.bfloat16)
        .reshape(shard_rows, head_count, HEAD_DIM)
    )
    values = (
        (qkv_flat[:, 2 * local_cols :] + bias_float[1])
        .astype(jnp.bfloat16)
        .reshape(shard_rows, head_count, HEAD_DIM)
    )
    attended, log_sums = attention_forward(
        queries, key_rows, values, image_ids, block_len, score_scale
    )
    attended = attended.reshape(shard_rows, local_cols)
    attn_branch = lax.psum_scatter(
        jnp.dot(attended, out_weight, preferred_element_type=jnp.float32).astype(jnp.bfloat16),
        "tensor",
        scatter_dimension=0,
        tiled=True,
    ).astype(jnp.float32) + out_bias.astype(jnp.float32)
    mid = resid + gate_one * attn_branch
    normed_two, inv_two = layer_norm(mid)
    mlp_in = (normed_two * (1.0 + scale_two) + shift_two).astype(jnp.bfloat16)
    mlp_all = lax.all_gather(mlp_in, "tensor", axis=0, tiled=True)
    pre_act = jnp.dot(mlp_all, up_weight, preferred_element_type=jnp.float32) + up_bias.astype(
        jnp.float32
    )
    act_value, act_back = jax.vjp(gelu_tanh, pre_act)
    hidden = act_value.astype(jnp.bfloat16)
    mlp_branch = lax.psum_scatter(
        jnp.dot(hidden, down_weight, preferred_element_type=jnp.float32).astype(jnp.bfloat16),
        "tensor",
        scatter_dimension=0,
        tiled=True,
    ).astype(jnp.float32) + down_bias.astype(jnp.float32)
    block_value = mid + gate_two * mlp_branch
    block_low = block_value.astype(jnp.bfloat16)
    first_pre = jnp.dot(
        block_low, proj_in, preferred_element_type=jnp.float32
    ) + proj_in_bias.astype(jnp.float32)
    first_value, first_back = jax.vjp(jax.nn.silu, first_pre)
    first_low = first_value.astype(jnp.bfloat16)
    second_pre = jnp.dot(
        first_low, proj_mid, preferred_element_type=jnp.float32
    ) + proj_mid_bias.astype(jnp.float32)
    second_value, second_back = jax.vjp(jax.nn.silu, second_pre)
    second_low = second_value.astype(jnp.bfloat16)
    projected = jnp.dot(
        second_low, proj_last, preferred_element_type=jnp.float32
    ) + proj_last_bias.astype(jnp.float32)
    target_vals = jnp.take(enc_features, target_rows - data_rank * shard_rows, axis=0).astype(
        jnp.float32
    )
    loss_value, loss_back = jax.vjp(lambda predicted: align_loss(predicted, target_vals), projected)
    grad_projected = loss_back(jnp.ones((), jnp.float32))[0]
    grad_last_low = grad_projected.astype(jnp.bfloat16)
    grad_second = second_back(dot_nt(grad_last_low, proj_last))[0]
    grad_second_low = grad_second.astype(jnp.bfloat16)
    grad_first = first_back(dot_nt(grad_second_low, proj_mid))[0]
    grad_first_low = grad_first.astype(jnp.bfloat16)
    grad_block = out_grad.astype(jnp.float32) + dot_nt(grad_first_low, proj_in)
    gate_two_grad = mlp_branch * grad_block
    grad_mlp_branch = gate_two * grad_block
    grad_mlp_all = lax.all_gather(
        grad_mlp_branch.astype(jnp.bfloat16), "tensor", axis=0, tiled=True
    )
    grad_down_local = dot_tn(hidden, grad_mlp_all)
    grad_pre = act_back(dot_nt(grad_mlp_all, down_weight))[0]
    grad_pre_low = grad_pre.astype(jnp.bfloat16)
    grad_up_local = dot_tn(mlp_all, grad_pre_low)
    up_bias_local = jnp.sum(grad_pre, axis=0)
    grad_mlp_in = lax.psum_scatter(
        dot_nt(grad_pre_low, up_weight).astype(jnp.bfloat16),
        "tensor",
        scatter_dimension=0,
        tiled=True,
    ).astype(jnp.float32)
    scale_two_grad = grad_mlp_in * normed_two
    grad_mid = grad_block + norm_back(normed_two, inv_two, grad_mlp_in * (1.0 + scale_two))
    gate_one_grad = attn_branch * grad_mid
    grad_attn_branch = gate_one * grad_mid
    grad_attn_all = lax.all_gather(
        grad_attn_branch.astype(jnp.bfloat16), "tensor", axis=0, tiled=True
    )
    grad_out_local = dot_tn(attended, grad_attn_all)
    grad_heads = (
        dot_nt(grad_attn_all, out_weight)
        .astype(jnp.bfloat16)
        .reshape(shard_rows, head_count, HEAD_DIM)
    )
    grad_queries, grad_keys, grad_values = attention_backward(
        queries, key_rows, values, image_ids, log_sums, grad_heads, block_len, score_scale
    )
    grad_queries = grad_queries.reshape(shard_rows, local_cols)
    grad_keys = grad_keys.reshape(shard_rows, local_cols)
    grad_values = grad_values.reshape(shard_rows, local_cols)
    qv_local = jnp.stack([jnp.sum(grad_queries, axis=0), jnp.sum(grad_values, axis=0)])
    grad_qkv_low = jnp.concatenate([grad_queries, grad_keys, grad_values], axis=1).astype(
        jnp.bfloat16
    )
    grad_qkv_local = dot_tn(attn_all, grad_qkv_low).reshape(model_width, 3, local_cols)
    grad_attn_in = lax.psum_scatter(
        dot_nt(grad_qkv_low, qkv_flat_weight).astype(jnp.bfloat16),
        "tensor",
        scatter_dimension=0,
        tiled=True,
    ).astype(jnp.float32)
    scale_one_grad = grad_attn_in * normed_one
    grad_tokens = grad_mid + norm_back(normed_one, inv_one, grad_attn_in * (1.0 + scale_one))
    token_mod_grad = jnp.concatenate(
        [grad_attn_in, scale_one_grad, gate_one_grad, grad_mlp_in, scale_two_grad, gate_two_grad],
        axis=1,
    )
    slot_grad_part = dot_tn(one_hot, token_mod_grad, precision=highest)
    slot_grad = lax.psum(slot_grad_part.astype(jnp.bfloat16), "tensor").astype(jnp.float32)
    slot_low = slot_grad.astype(jnp.bfloat16)
    grad_condition = silu_back(dot_nt(slot_low, ada_weight))[0]
    ada_cols = dot_tn(silu_low, column_set(slot_low, data_count, tensor_count, tensor_rank))
    ada_bias_cols = jnp.sum(
        column_set(slot_grad, data_count, tensor_count, tensor_rank), axis=0, keepdims=True
    )
    block_grads = (
        lax.psum_scatter(
            grad_qkv_local.astype(jnp.bfloat16), "dp", scatter_dimension=0, tiled=True
        ).astype(jnp.float32),
        lax.psum_scatter(
            grad_out_local.astype(jnp.bfloat16), "dp", scatter_dimension=1, tiled=True
        ).astype(jnp.float32),
        lax.psum_scatter(
            grad_up_local.astype(jnp.bfloat16), "dp", scatter_dimension=0, tiled=True
        ).astype(jnp.float32),
        lax.psum_scatter(
            grad_down_local.astype(jnp.bfloat16), "dp", scatter_dimension=1, tiled=True
        ).astype(jnp.float32),
        lax.psum_scatter(
            ada_cols.astype(jnp.bfloat16), "dp", scatter_dimension=1, tiled=True
        ).astype(jnp.float32),
        lax.psum_scatter(
            ada_bias_cols.astype(jnp.bfloat16), "dp", scatter_dimension=1, tiled=True
        ).astype(jnp.float32),
    )
    qv_full = lax.dynamic_update_slice_in_dim(
        jnp.zeros((2, model_width), jnp.float32), qv_local, tensor_rank * local_cols, axis=1
    )
    up_full = lax.dynamic_update_slice_in_dim(
        jnp.zeros((local_hidden * tensor_count,), jnp.float32),
        up_bias_local,
        tensor_rank * local_hidden,
        axis=0,
    )
    bias_sums = lax.psum(
        (
            qv_full,
            up_full,
            jnp.sum(grad_attn_branch, axis=0),
            jnp.sum(grad_mlp_branch, axis=0),
            jnp.sum(grad_first, axis=0),
            jnp.sum(grad_second, axis=0),
            jnp.sum(grad_projected, axis=0),
        ),
        ("dp", "tensor"),
    )
    qv_grad = lax.dynamic_slice_in_dim(bias_sums[0], tensor_rank * local_cols, local_cols, axis=1)
    up_bias_grad = lax.dynamic_slice_in_dim(
        bias_sums[1], tensor_rank * local_hidden, local_hidden, axis=0
    )
    proj_grads = (
        lax.psum_scatter(
            dot_tn(block_low, grad_first_low), ("dp", "tensor"), scatter_dimension=1, tiled=True
        ),
        lax.psum_scatter(
            dot_tn(first_low, grad_second_low), ("dp", "tensor"), scatter_dimension=1, tiled=True
        ),
        lax.psum_scatter(
            dot_tn(second_low, grad_last_low), ("dp", "tensor"), scatter_dimension=1, tiled=True
        ),
    )
    return (
        block_low,
        grad_tokens,
        grad_condition,
        block_grads[4],
        block_grads[5].reshape(-1),
        block_grads[0],
        qv_grad,
        block_grads[1],
        bias_sums[2],
        block_grads[2],
        up_bias_grad,
        block_grads[3],
        bias_sums[3],
        proj_grads[0],
        bias_sums[4],
        proj_grads[1],
        bias_sums[5],
        proj_grads[2],
        bias_sums[6],
    )


LANES = 128
MESH = pl.DeviceIdType.MESH
TILE = 256
LOG2_E = 1.4426950408889634
bf16 = jnp.bfloat16
f32 = jnp.float32


def pairs_of(move):
    found = []
    for index in range(32):
        x, core, y, z = index % 2, (index // 2) % 2, (index // 4) % 2, index // 8
        z2, y2, c2, x2 = move(z, y, core, x)
        if (z2, y2, c2, x2) != (z, y, core, x):
            found.append((index, ((z2 * 2 + y2) * 2 + c2) * 2 + x2))
    return found


def send(value, move):
    return lax.ppermute(value, ("dp", "tensor"), pairs_of(move))


def to_diag(z, y, c, x):
    return (z, y, x, c)


def to_cycle(z, y, c, x):
    return (z, y, c, c) if c != x else (z, y, 1 - c, x)


def to_core(z, y, c, x):
    return (z, y, 1 - c, x)


def to_x(z, y, c, x):
    return (z, y, c, 1 - x)


def to_y(z, y, c, x):
    return (z, 1 - y, c, x)


def to_swapped_y(z, y, c, x):
    return (z, 1 - y, c, x) if c != x else (z, y, c, x)


def to_z_near(z, y, c, x):
    return (z ^ 1, y, c, x)


def to_z_far(z, y, c, x):
    return (z ^ 2, y, c, x)


def pick(array, index, axis):
    return lax.dynamic_index_in_dim(array, index, axis=axis, keepdims=False)


def gather_kernel(own_ref, out_ref, local_sem, send_sem, recv_sem):
    dp = lax.axis_index("dp")
    x = lax.axis_index("tensor")
    core = dp % 2
    other = dp + 1 - 2 * core
    barrier = pltpu.get_barrier_semaphore()
    pl.semaphore_signal(barrier, inc=1, device_id=(other, x), device_id_type=MESH)
    pl.semaphore_wait(barrier, 1)
    away = pltpu.make_async_remote_copy(
        src_ref=own_ref,
        dst_ref=out_ref.at[core],
        send_sem=send_sem,
        recv_sem=recv_sem,
        device_id=(other, x),
        device_id_type=MESH,
    )
    away.start()
    here = pltpu.make_async_copy(own_ref, out_ref.at[core], local_sem)
    here.start()
    here.wait()
    away.wait()


def gather_cores(own):
    rows, width = own.shape
    return pl.pallas_call(
        gather_kernel,
        out_shape=jax.ShapeDtypeStruct((2, rows, width), own.dtype),
        in_specs=[pl.BlockSpec(memory_space=pltpu.VMEM)],
        out_specs=pl.BlockSpec(memory_space=pl.ANY),
        scratch_shapes=[pltpu.SemaphoreType.DMA] * 3,
        compiler_params=pltpu.CompilerParams(collective_id=0, has_side_effects=True, vmem_limit_bytes=16 << 20),
        cost_estimate=pl.CostEstimate(flops=0, bytes_accessed=12000000, transcendentals=0),
        name="gather_cores",
    )(own).reshape(2 * rows, width)


def split_heads(flat_ref, heads_ref, parts, heads):
    heads_ref[...] = jnp.zeros_like(heads_ref)
    for part in range(parts):
        for head in range(heads):
            begin = (part * heads + head) * HEAD_DIM
            heads_ref[part * heads + head, :, 0:HEAD_DIM] = flat_ref[:, begin : begin + HEAD_DIM]


def join_heads(heads_ref, flat_ref, count):
    rows, columns = flat_ref.shape
    for block in range(rows // LANES):
        span = slice(block * LANES, (block + 1) * LANES)
        pieces = [heads_ref[head, span, 0:HEAD_DIM] for head in range(count)]
        if columns > count * HEAD_DIM:
            pieces.append(jnp.zeros((LANES, columns - count * HEAD_DIM), flat_ref.dtype))
        flat_ref[span, :] = jnp.concatenate(pieces, axis=1)


def per_image(count, run):
    @pl.when(count == 1)
    def _():
        run(SHORT)

    @pl.when(count != 1)
    def _():
        run(4 * SHORT)


def attend_kernel(heads, together, factor, starts, counts, qkv_ref, o_ref, log_ref, part_ref, o_heads):
    split_heads(qkv_ref, part_ref, 3, heads)
    unit_count = o_ref.shape[0] // SHORT

    def some_heads(step, carry):
        def unit(index, carry):
            rows = pl.ds(pl.multiple_of(index * SHORT, SHORT), SHORT)

            def run(length):
                cols = pl.ds(pl.multiple_of(starts[index] * SHORT, SHORT), length)
                for ahead in range(together):
                    head = step * together + ahead
                    scores = dot_nt(part_ref[heads + head, cols, :], part_ref[head, rows, :])
                    top = jnp.max(scores, axis=0, keepdims=True)
                    exponent = jnp.exp2((scores - top) * factor)
                    total = jnp.sum(exponent, axis=0, keepdims=True)
                    summed = dot_tn(part_ref[2 * heads + head, cols, :], exponent.astype(bf16))
                    o_heads[head, rows, :] = (summed * (1.0 / total)).T.astype(bf16)
                    log_ref[head * unit_count + index] = top * factor + jnp.log2(total)

            per_image(counts[index], run)
            return carry

        return lax.fori_loop(0, unit_count, unit, carry)

    lax.fori_loop(0, heads // together, some_heads, 0)
    join_heads(o_heads, o_ref, heads)


def whole_spec(space=pltpu.VMEM):
    return pl.BlockSpec(memory_space=space)


def attend(starts, counts, qkv, heads, out_cols):
    rows = qkv.shape[0]
    factor = HEAD_DIM ** (-0.5) * LOG2_E
    return pl.pallas_call(
        functools.partial(attend_kernel, heads, 2, factor),
        out_shape=(
            jax.ShapeDtypeStruct((rows, out_cols), bf16),
            jax.ShapeDtypeStruct((heads * (rows // SHORT), 1, SHORT), f32),
        ),
        in_specs=[whole_spec(pltpu.SMEM), whole_spec(pltpu.SMEM), whole_spec()],
        out_specs=(whole_spec(), whole_spec()),
        scratch_shapes=[
            pltpu.VMEM((3 * heads, rows, LANES), bf16),
            pltpu.VMEM((heads, rows, LANES), bf16),
        ],
        compiler_params=pltpu.CompilerParams(vmem_limit_bytes=40 << 20),
        cost_estimate=pl.CostEstimate(flops=20 * 10**9, bytes_accessed=13 * 10**6, transcendentals=10**7),
        name="attend",
    )(starts, counts, qkv)


def attend_back_kernel(
    heads,
    together,
    factor,
    starts,
    counts,
    qkv_ref,
    log_ref,
    grad_ref,
    out_ref,
    bias_ref,
    part_ref,
    grad_heads,
    key_acc,
    value_acc,
    sums,
):
    split_heads(qkv_ref, part_ref, 3, heads)
    split_heads(grad_ref, grad_heads, 1, heads)
    unit_count = out_ref.shape[0] // SHORT

    def some_heads(step, carry):
        key_acc[...] = jnp.zeros_like(key_acc)
        value_acc[...] = jnp.zeros_like(value_acc)
        for ahead in range(together):
            sums[step * together + ahead] = jnp.zeros((8, LANES), f32)

        def unit(index, carry):
            rows = pl.ds(pl.multiple_of(index * SHORT, SHORT), SHORT)

            def run(length):
                cols = pl.ds(pl.multiple_of(starts[index] * SHORT, SHORT), length)
                for ahead in range(together):
                    head = step * together + ahead
                    queries = part_ref[head, rows, :]
                    grads = grad_heads[head, rows, :]
                    keys = part_ref[heads + head, cols, :]
                    scores = dot_nt(keys, queries)
                    soft = jnp.exp2(scores * (factor * LOG2_E) - log_ref[head * unit_count + index])
                    grad_soft = dot_nt(part_ref[2 * heads + head, cols, :], grads)
                    product = soft * grad_soft
                    inner = jnp.sum(product, axis=0, keepdims=True)
                    grad_scores = (product - soft * inner).astype(bf16)
                    value_acc[ahead, cols, :] += jnp.dot(soft.astype(bf16), grads, preferred_element_type=f32)
                    key_acc[ahead, cols, :] += jnp.dot(grad_scores, queries, preferred_element_type=f32)
                    grad_query = dot_tn(keys, grad_scores).T * factor
                    sums[head, 0:1, :] += jnp.sum(grad_query, axis=0, keepdims=True)
                    part_ref[head, rows, :] = grad_query.astype(bf16)

            per_image(counts[index], run)
            return carry

        lax.fori_loop(0, unit_count, unit, 0)
        for ahead in range(together):
            head = step * together + ahead
            sums[head, 1:2, :] = jnp.sum(value_acc[ahead], axis=0, keepdims=True)
            part_ref[heads + head] = (key_acc[ahead] * factor).astype(bf16)
            part_ref[2 * heads + head] = value_acc[ahead].astype(bf16)
        return carry

    lax.fori_loop(0, heads // together, some_heads, 0)
    join_heads(part_ref, out_ref, 3 * heads)
    bias_ref[...] = jnp.concatenate([sums[head, :, 0:HEAD_DIM] for head in range(heads)], axis=1)


def attend_back(starts, counts, qkv, log_sums, grad_heads, heads):
    rows, columns = qkv.shape
    factor = HEAD_DIM ** (-0.5)
    together = 2
    return pl.pallas_call(
        functools.partial(attend_back_kernel, heads, together, factor),
        out_shape=(
            jax.ShapeDtypeStruct((rows, columns), bf16),
            jax.ShapeDtypeStruct((8, heads * HEAD_DIM), f32),
        ),
        in_specs=[whole_spec(pltpu.SMEM), whole_spec(pltpu.SMEM)] + [whole_spec()] * 3,
        out_specs=(whole_spec(), whole_spec()),
        scratch_shapes=[
            pltpu.VMEM((3 * heads, rows, LANES), bf16),
            pltpu.VMEM((heads, rows, LANES), bf16),
            pltpu.VMEM((together, rows, LANES), f32),
            pltpu.VMEM((together, rows, LANES), f32),
            pltpu.VMEM((heads, 8, LANES), f32),
        ],
        compiler_params=pltpu.CompilerParams(vmem_limit_bytes=48 << 20),
        cost_estimate=pl.CostEstimate(flops=40 * 10**9, bytes_accessed=25 * 10**6, transcendentals=10**7),
        name="attend_back",
    )(starts, counts, qkv, log_sums, grad_heads)


def reduce_kernel(
    grid_rows,
    first_jobs,
    second_jobs,
    proj_jobs,
    one_left,
    one_right,
    two_left,
    two_right,
    three_left,
    three_right,
    four_left,
    four_right,
    mid_left,
    mid_right,
    in_left,
    in_right,
    last_left,
    last_right,
    bias_ref,
    slot_ref,
    silu_ref,
    slot_low_ref,
    ada_ref,
    first_out,
    second_out,
    proj_out,
    bias_out,
    slot_out,
    silu_out,
    cond_out,
    stage,
    first_left,
    second_left,
    first_right,
    second_right,
    proj_stage,
    proj_left,
    proj_right,
    p0,
    p0_got,
    p1,
    p1_got,
    p2,
    p2_got,
    p3,
    p3_got,
    f0,
    f0_turn,
    f0_swap,
    f1,
    f1_got,
    f2,
    f2_got,
    s0,
    s0_got,
    s1,
    s1_got,
    s2,
    s2_turn,
    s2_swap,
    bias_got,
    slot_x,
    slot_y,
    slot_y_got,
    slot_z,
    slot_z_got,
    silu_x,
    silu_y,
    silu_y_got,
    silu_z,
    silu_z_got,
    ada_tile,
    cond_acc,
    load_sem,
    first_load,
    second_load,
    proj_load,
    p0_sems,
    p1_sems,
    p2_sems,
    p3_sems,
    f0_sems,
    f1_sems,
    f2_sems,
    s0_sems,
    s1_sems,
    s2_sems,
    bias_sems,
    slot_sems,
    slot_z_sems,
    silu_sems,
    silu_z_sems,
    ada_sems,
    cond_sems,
    first_free,
    second_free,
):
    dp = lax.axis_index("dp")
    x = lax.axis_index("tensor")
    core = dp % 2
    y = (dp // 2) % 2
    z = dp // 4
    home = core == x
    away = core != x

    def device(z_at, y_at, core_at, x_at):
        return ((z_at * 2 + y_at) * 2 + core_at, x_at)

    turn_to = device(z, y, core + (1 - 2 * core) * (1 - jnp.abs(core - x)), x + (core - x))
    turn_from = device(z, y, x + 0 * core, x + (1 - 2 * x) * (1 - jnp.abs(core - x)))
    swap_peer = device(z, y, x, core)
    y_peer = device(z, 1 - y, core, x)

    def z_peer(ahead):
        return device(lax.rem(z + ahead, 4), y, core, x)

    barrier = pltpu.get_barrier_semaphore()
    near = [device(z, y, 1 - core, x), device(z, y, core, 1 - x), device(z, y, 1 - core, 1 - x), y_peer]
    for peer in near + [z_peer(1), z_peer(2), z_peer(3)]:
        pl.semaphore_signal(barrier, inc=1, device_id=peer, device_id_type=MESH)
    pl.semaphore_wait(barrier, 7)

    def remote(source, target, sems, index, peer):
        return pltpu.make_async_remote_copy(
            src_ref=source,
            dst_ref=target,
            send_sem=sems.at[(0,) + index],
            recv_sem=sems.at[(1,) + index],
            device_id=peer,
            device_id_type=MESH,
        )

    def added(*terms):
        total = terms[0].astype(f32)
        for term in terms[1:]:
            total = total + term.astype(f32)
        return total

    def load_left(source, through, target):
        height = source.shape[1]
        through = through if height == through.shape[1] else through.at[:, 0:height]
        copy = pltpu.make_async_copy(source, through, load_sem)
        copy.start()
        copy.wait()

        def block(index, carry):
            rows = pl.ds(pl.multiple_of(index * LANES, LANES), LANES)
            target[0:height, rows] = through[rows, :].T
            return carry

        lax.fori_loop(0, source.shape[0] // LANES, block, 0)

    def right_copy(source, tile, target, sems, slot):
        columns = pl.ds(pl.multiple_of(tile * TILE, TILE), TILE)
        return pltpu.make_async_copy(source.at[:, columns], target.at[slot], sems.at[slot])

    first_split = one_right.shape[1] // TILE
    second_split = three_right.shape[1] // TILE

    def first_right_do(job, slot, action):
        @pl.when(job < first_split)
        def _():
            action(right_copy(one_right, job, first_right, first_load, slot))

        @pl.when(job >= first_split)
        def _():
            action(right_copy(two_right, job - first_split, first_right, first_load, slot))

    def second_right_do(job, slot, action):
        @pl.when(job < second_split)
        def _():
            action(right_copy(three_right, job, second_right, second_load, slot))

        @pl.when(job >= second_split)
        def _():
            action(right_copy(four_right, job - second_split, second_right, second_load, slot))

    def begin(copy):
        copy.start()

    def finish(copy):
        copy.wait()

    def multiply(left, right, slot, keep):
        def block(at_z, carry):
            height = 4 * grid_rows
            span = pl.ds(pl.multiple_of(at_z * height, 32), height)
            product = jnp.dot(left[span, :], right[slot], preferred_element_type=f32)
            for at_y in range(2):
                for at_core in range(2):
                    low = (at_y * 2 + at_core) * grid_rows
                    keep(at_z, at_y, at_core, product[low : low + grid_rows, :].astype(bf16))
            return carry

        lax.fori_loop(0, 4, block, 0)

    def f0_copies(slot):
        turn = remote(f0.at[slot, 1 - x], f0_turn.at[slot], f0_sems, (0, slot), turn_to)
        swap = remote(f0.at[slot, x], f0_swap.at[slot], f0_sems, (1, slot), swap_peer)
        return turn, swap

    def f1_copy(slot):
        return remote(f1.at[slot, 1 - y], f1_got.at[slot], f1_sems, (slot,), y_peer)

    def f2_copy(slot, ahead):
        return remote(
            f2.at[slot, lax.rem(z + ahead, 4)], f2_got.at[slot, ahead - 1], f2_sems, (slot, ahead - 1), z_peer(ahead)
        )

    def s0_copy(slot):
        return remote(s0.at[slot, 1 - y], s0_got.at[slot], s0_sems, (slot,), y_peer)

    def s1_copy(slot, ahead):
        return remote(
            s1.at[slot, lax.rem(z + ahead, 4)], s1_got.at[slot, ahead - 1], s1_sems, (slot, ahead - 1), z_peer(ahead)
        )

    def s2_copies(slot):
        turn = remote(s2.at[slot, 1 - x], s2_turn.at[slot], s2_sems, (0, slot), turn_to)
        swap = remote(s2.at[slot, x], s2_swap.at[slot], s2_sems, (1, slot), swap_peer)
        return turn, swap

    def inside(job, count):
        return jnp.logical_and(job >= 0, job < count)

    first_right_do(0, 0, begin)
    second_right_do(0, 0, begin)

    def first_tick(tick):
        @pl.when(tick < first_jobs)
        def _():
            slot = lax.rem(tick, 2)
            first_right_do(tick, slot, finish)

            @pl.when(tick + 1 < first_jobs)
            def _():
                first_right_do(tick + 1, 1 - slot, begin)

            @pl.when(tick == 0)
            def _():
                load_left(one_left, stage, first_left)

            @pl.when(tick == first_split)
            def _():
                load_left(two_left, stage, first_left)

            def keep(at_z, at_y, at_core, value):
                f0[slot, at_core, at_y, at_z] = value

            multiply(first_left, first_right, slot, keep)

        last = tick - 3

        @pl.when(inside(last, first_jobs))
        def _():
            slot = lax.rem(last, 2)
            for ahead in (1, 2, 3):
                f2_copy(slot, ahead).wait()
            first_out[last] = added(f2[slot, z], f2_got[slot, 0], f2_got[slot, 1], f2_got[slot, 2])

        third = tick - 2

        @pl.when(inside(third, first_jobs))
        def _():
            slot = lax.rem(third, 2)
            f1_copy(slot).wait()
            f2[slot] = added(f1[slot, y], f1_got[slot]).astype(bf16)
            for ahead in (1, 2, 3):
                f2_copy(slot, ahead).start()

        second = tick - 1

        @pl.when(inside(second, first_jobs))
        def _():
            slot = lax.rem(second, 2)
            turn, swap = f0_copies(slot)
            turn.wait()

            @pl.when(home)
            def _():
                f1[slot] = added(f0_turn[slot], f0[slot, x]).astype(bf16)

            @pl.when(away)
            def _():
                swap.wait()
                f1[slot] = added(f0_turn[slot], f0_swap[slot]).astype(bf16)

            @pl.when(second + 2 < first_jobs)
            def _():
                pl.semaphore_signal(first_free, inc=1, device_id=turn_from, device_id_type=MESH)

            f1_copy(slot).start()

        @pl.when(tick < first_jobs)
        def _():
            slot = lax.rem(tick, 2)
            turn, swap = f0_copies(slot)

            @pl.when(tick >= 2)
            def _():
                pl.semaphore_wait(first_free, 1)

            turn.start()

            @pl.when(away)
            def _():
                swap.start()

    def second_tick(tick):
        @pl.when(tick < second_jobs)
        def _():
            slot = lax.rem(tick, 2)
            second_right_do(tick, slot, finish)

            @pl.when(tick + 1 < second_jobs)
            def _():
                second_right_do(tick + 1, 1 - slot, begin)

            @pl.when(tick == 0)
            def _():
                load_left(three_left, stage, second_left)

            @pl.when(tick == second_split)
            def _():
                load_left(four_left, stage, second_left)

            def keep(at_z, at_y, at_core, value):
                s0[slot, at_y, at_z, at_core] = value

            multiply(second_left, second_right, slot, keep)

        last = tick - 3

        @pl.when(inside(last, second_jobs))
        def _():
            slot = lax.rem(last, 2)
            turn, swap = s2_copies(slot)
            turn.wait()

            @pl.when(home)
            def _():
                second_out[last] = added(s2_turn[slot], s2[slot, x])

            @pl.when(away)
            def _():
                swap.wait()
                second_out[last] = added(s2_turn[slot], s2_swap[slot])

            @pl.when(last + 2 < second_jobs)
            def _():
                pl.semaphore_signal(second_free, inc=1, device_id=turn_from, device_id_type=MESH)

        third = tick - 2

        @pl.when(inside(third, second_jobs))
        def _():
            slot = lax.rem(third, 2)
            for ahead in (1, 2, 3):
                s1_copy(slot, ahead).wait()
            s2[slot] = added(s1[slot, z], s1_got[slot, 0], s1_got[slot, 1], s1_got[slot, 2]).astype(bf16)
            turn, swap = s2_copies(slot)

            @pl.when(third >= 2)
            def _():
                pl.semaphore_wait(second_free, 1)

            turn.start()

            @pl.when(away)
            def _():
                swap.start()

        second = tick - 1

        @pl.when(inside(second, second_jobs))
        def _():
            slot = lax.rem(second, 2)
            s0_copy(slot).wait()
            s1[slot] = added(s0[slot, y], s0_got[slot]).astype(bf16)
            for ahead in (1, 2, 3):
                s1_copy(slot, ahead).start()

        @pl.when(tick < second_jobs)
        def _():
            s0_copy(lax.rem(tick, 2)).start()

    mid_jobs = mid_right.shape[1] // TILE
    in_jobs = -(-in_right.shape[1] // TILE)
    in_left_over = in_right.shape[1] % TILE
    proj_rows = mid_left.shape[1] // 32
    last_rows = last_left.shape[1] // 32

    def proj_right_do(job, slot, action):
        def copy(source, tile, columns):
            start = pl.multiple_of(tile * columns, LANES)
            return pltpu.make_async_copy(
                source.at[:, pl.ds(start, columns)], proj_right.at[slot, :, pl.ds(0, columns)], proj_load.at[slot]
            )

        @pl.when(job < mid_jobs)
        def _():
            action(copy(mid_right, job, TILE))

        full = in_jobs - (1 if in_left_over else 0)

        @pl.when(inside(job - mid_jobs, full))
        def _():
            action(copy(in_right, job - mid_jobs, TILE))

        if in_left_over:

            @pl.when(job == mid_jobs + full)
            def _():
                rest = pltpu.make_async_copy(
                    in_right.at[:, pl.ds(full * TILE, in_left_over)],
                    proj_right.at[slot, :, pl.ds(0, in_left_over)],
                    proj_load.at[slot],
                )
                action(rest)

        @pl.when(job >= mid_jobs + in_jobs)
        def _():
            action(copy(last_right, job - mid_jobs - in_jobs, 2 * TILE))

    def p0_copy(slot):
        return remote(p0.at[slot, 1 - core], p0_got.at[slot], p0_sems, (slot,), device(z, y, 1 - core, x))

    def p1_copy(slot):
        return remote(p1.at[slot, 1 - x], p1_got.at[slot], p1_sems, (slot,), device(z, y, core, 1 - x))

    def p2_copy(slot):
        return remote(p2.at[slot, 1 - y], p2_got.at[slot], p2_sems, (slot,), y_peer)

    def p3_copy(slot, ahead):
        return remote(
            p3.at[slot, lax.rem(z + ahead, 4)], p3_got.at[slot, ahead - 1], p3_sems, (slot, ahead - 1), z_peer(ahead)
        )

    pltpu.make_async_copy(mid_right.at[:, pl.ds(0, TILE)], proj_right.at[0, :, pl.ds(0, TILE)], proj_load.at[0]).start()

    def proj_tick(tick):
        @pl.when(tick < proj_jobs)
        def _():
            slot = lax.rem(tick, 2)
            proj_right_do(tick, slot, finish)

            @pl.when(tick + 1 < proj_jobs)
            def _():
                proj_right_do(tick + 1, 1 - slot, begin)

            for at, source in ((0, mid_left), (mid_jobs, in_left), (mid_jobs + in_jobs, last_left)):

                @pl.when(tick == at)
                def _(source=source):
                    load_left(source, proj_stage, proj_left)

            shares = [(at_y, at_core, at_x) for at_y in range(2) for at_core in range(2) for at_x in range(2)]

            @pl.when(tick < mid_jobs + in_jobs)
            def _():
                def block(at_z, carry):
                    span = pl.ds(pl.multiple_of(at_z * 8 * proj_rows, 32), 8 * proj_rows)
                    right = proj_right[slot, :, 0:TILE]
                    product = jnp.dot(proj_left[span, :], right, preferred_element_type=f32).astype(bf16)
                    for low, (at_y, at_core, at_x) in enumerate(shares):
                        p0[slot, at_core, at_x, at_y, at_z] = product[low * proj_rows : (low + 1) * proj_rows, :]
                    return carry

                lax.fori_loop(0, 4, block, 0)

            @pl.when(tick >= mid_jobs + in_jobs)
            def _():
                def block(at_z, carry):
                    span = pl.ds(pl.multiple_of(at_z * 8 * last_rows, 32), 8 * last_rows)
                    for half in range(2):
                        right = proj_right[slot, :, half * TILE : (half + 1) * TILE]
                        product = jnp.dot(proj_left[span, :], right, preferred_element_type=f32)
                        begin_row = half * proj_rows // 2
                        for low, (at_y, at_core, at_x) in enumerate(shares):
                            p0[slot, at_core, at_x, at_y, at_z, begin_row : begin_row + last_rows, :] = product[
                                low * last_rows : (low + 1) * last_rows, :
                            ].astype(bf16)
                    return carry

                lax.fori_loop(0, 4, block, 0)

        fifth = tick - 4

        @pl.when(inside(fifth, proj_jobs))
        def _():
            slot = lax.rem(fifth, 2)
            for ahead in (1, 2, 3):
                p3_copy(slot, ahead).wait()
            proj_out[fifth] = added(p3[slot, z], p3_got[slot, 0], p3_got[slot, 1], p3_got[slot, 2])

        fourth = tick - 3

        @pl.when(inside(fourth, proj_jobs))
        def _():
            slot = lax.rem(fourth, 2)
            p2_copy(slot).wait()
            p3[slot] = added(p2[slot, y], p2_got[slot]).astype(bf16)
            for ahead in (1, 2, 3):
                p3_copy(slot, ahead).start()

        third = tick - 2

        @pl.when(inside(third, proj_jobs))
        def _():
            slot = lax.rem(third, 2)
            p1_copy(slot).wait()
            p2[slot] = added(p1[slot, x], p1_got[slot]).astype(bf16)
            p2_copy(slot).start()

        second = tick - 1

        @pl.when(inside(second, proj_jobs))
        def _():
            slot = lax.rem(second, 2)
            p0_copy(slot).wait()
            p1[slot] = added(p0[slot, core], p0_got[slot]).astype(bf16)
            p1_copy(slot).start()

        @pl.when(tick < proj_jobs)
        def _():
            p0_copy(lax.rem(tick, 2)).start()

    bias_peers = [
        device(z, y, 1 - core, x),
        device(z, y, core, 1 - x),
        y_peer,
        device(z + 1 - 2 * lax.rem(z, 2), y, core, x),
        device(lax.rem(z + 2, 4), y, core, x),
    ]

    def bias_copy(step):
        return remote(bias_out, bias_got.at[step], bias_sems, (step,), bias_peers[step])

    def slot_x_copy():
        return remote(slot_ref.at[1 - x], slot_x, slot_sems, (0,), device(z, y, core, 1 - x))

    def slot_y_copy():
        return remote(slot_y.at[1 - y], slot_y_got, slot_sems, (1,), y_peer)

    def slot_z_copy(ahead):
        return remote(
            slot_z.at[lax.rem(z + ahead, 4)], slot_z_got.at[ahead - 1], slot_z_sems, (ahead - 1,), z_peer(ahead)
        )

    def silu_x_copy():
        return remote(silu_ref, silu_x, silu_sems, (0,), device(z, y, core, 1 - x))

    def silu_y_copy():
        return remote(silu_y, silu_y_got, silu_sems, (1,), y_peer)

    def silu_z_copy(ahead):
        return remote(silu_z, silu_z_got.at[ahead - 1], silu_z_sems, (ahead - 1,), z_peer(ahead))

    def small_tick(tick):
        @pl.when(tick == 0)
        def _():
            bias_out[...] = bias_ref[...]
            slot_x_copy().start()
            silu_x_copy().start()

        for step in range(5):

            @pl.when(tick == step + 1)
            def _(step=step):
                bias_copy(step).wait()
                bias_out[...] = bias_out[...] + bias_got[step]

        for step in range(5):

            @pl.when(tick == step)
            def _(step=step):
                bias_copy(step).start()

        @pl.when(tick == 1)
        def _():
            slot_x_copy().wait()
            for at_y in range(2):
                slot_y[at_y, x] = slot_ref[x, at_y]
                slot_y[at_y, 1 - x] = slot_x[at_y]
            slot_y_copy().start()
            silu_x_copy().wait()
            silu_y[x] = silu_ref[...]
            silu_y[1 - x] = silu_x[...]
            silu_y_copy().start()

        @pl.when(tick == 2)
        def _():
            slot_y_copy().wait()
            for at_z in range(4):
                slot_z[at_z, y] = slot_y[y, :, at_z]
                slot_z[at_z, 1 - y] = slot_y_got[:, at_z]
            silu_y_copy().wait()
            silu_z[y] = silu_y[...]
            silu_z[1 - y] = silu_y_got[...]
            for ahead in (1, 2, 3):
                slot_z_copy(ahead).start()
                silu_z_copy(ahead).start()

        @pl.when(tick == 3)
        def _():
            slot_out[z] = slot_z[z]
            silu_out[z] = silu_z[...]
            for ahead in (1, 2, 3):
                slot_z_copy(ahead).wait()
                slot_out[lax.rem(z + 4 - ahead, 4)] = slot_z_got[ahead - 1]
                silu_z_copy(ahead).wait()
                silu_out[lax.rem(z + 4 - ahead, 4)] = silu_z_got[ahead - 1]

    ada_cols = ada_tile.shape[2]
    ada_tiles = ada_ref.shape[1] // ada_cols
    cond_copy = remote(cond_acc, cond_out, cond_sems, (), swap_peer)

    def ada_copy(tile, slot):
        columns = pl.ds(pl.multiple_of(tile * ada_cols, LANES), ada_cols)
        return pltpu.make_async_copy(ada_ref.at[:, columns], ada_tile.at[slot], ada_sems.at[slot])

    def cond_tick(tick):
        tile = tick - 4

        @pl.when(tile == -1)
        def _():
            cond_acc[...] = jnp.zeros_like(cond_acc)

        @pl.when(inside(tile + 1, ada_tiles))
        def _():
            ada_copy(tile + 1, lax.rem(tile + 1, 2)).start()

        @pl.when(inside(tile, ada_tiles))
        def _():
            slot = lax.rem(tile, 2)
            ada_copy(tile, slot).wait()
            columns = pl.ds(pl.multiple_of(tile * ada_cols, LANES), ada_cols)
            cond_acc[...] += dot_nt(slot_low_ref[:, columns], ada_tile[slot])

        @pl.when(tile == ada_tiles)
        def _():
            @pl.when(home)
            def _():
                cond_out[...] = cond_acc[...]

            @pl.when(away)
            def _():
                cond_copy.start()

        @pl.when(jnp.logical_and(tile == ada_tiles + 1, away))
        def _():
            cond_copy.wait()

    def tick_body(tick, carry):
        small_tick(tick)
        cond_tick(tick)
        second_tick(tick)
        proj_tick(tick)

        @pl.when(lax.rem(tick, 4) != 3)
        def _():
            first_tick(tick // 4 * 3 + lax.rem(tick, 4))

        return carry

    ticks = max(second_jobs + 3, proj_jobs + 4, ada_tiles + 6, -(-4 * (first_jobs + 3) // 3))
    lax.fori_loop(0, ticks, tick_body, 0)


def reduce_grads(one, two, three, four, mid, first, last, bias, slots, silu, slot_low, ada_weight):
    tokens, width = one[0].shape
    grid_rows = width // 16
    first_jobs = (one[1].shape[1] + two[1].shape[1]) // TILE
    second_jobs = (three[1].shape[1] + four[1].shape[1]) // TILE
    proj_jobs = mid[1].shape[1] // TILE + -(-first[1].shape[1] // TILE) + last[1].shape[1] // (2 * TILE)
    proj_tokens, proj_hidden = mid[0].shape
    proj_tile = (proj_hidden // 32, TILE)
    tile = (grid_rows, TILE)
    dma = pltpu.SemaphoreType.DMA
    slot_tail = slots.shape[-2:]

    def low(*lead):
        return pltpu.VMEM(lead + tile, bf16)

    scratch = [
        pltpu.VMEM((tokens, width), bf16),
        pltpu.VMEM((width, tokens), bf16),
        pltpu.VMEM((width, tokens), bf16),
        pltpu.VMEM((2, tokens, TILE), bf16),
        pltpu.VMEM((2, tokens, TILE), bf16),
        pltpu.VMEM((proj_tokens, proj_hidden), bf16),
        pltpu.VMEM((proj_hidden, proj_tokens), bf16),
        pltpu.VMEM((2, proj_tokens, 2 * TILE), bf16),
        pltpu.VMEM((2, 2, 2, 2, 4) + proj_tile, bf16),
        pltpu.VMEM((2, 2, 2, 4) + proj_tile, bf16),
        pltpu.VMEM((2, 2, 2, 4) + proj_tile, bf16),
        pltpu.VMEM((2, 2, 4) + proj_tile, bf16),
        pltpu.VMEM((2, 2, 4) + proj_tile, bf16),
        pltpu.VMEM((2, 4) + proj_tile, bf16),
        pltpu.VMEM((2, 4) + proj_tile, bf16),
        pltpu.VMEM((2, 3) + proj_tile, bf16),
        low(2, 2, 2, 4),
        low(2, 2, 4),
        low(2, 2, 4),
        low(2, 2, 4),
        low(2, 4),
        low(2, 4),
        low(2, 3),
        low(2, 2, 4, 2),
        low(2, 4, 2),
        low(2, 4, 2),
        low(2, 3, 2),
        low(2, 2),
        low(2),
        low(2),
        pltpu.VMEM((5,) + bias.shape, f32),
        pltpu.VMEM((2, 4) + slot_tail, f32),
        pltpu.VMEM((2, 2, 4) + slot_tail, f32),
        pltpu.VMEM((2, 4) + slot_tail, f32),
        pltpu.VMEM((4, 2, 2) + slot_tail, f32),
        pltpu.VMEM((3, 2, 2) + slot_tail, f32),
        pltpu.VMEM(silu.shape, bf16),
        pltpu.VMEM((2,) + silu.shape, bf16),
        pltpu.VMEM((2,) + silu.shape, bf16),
        pltpu.VMEM((2, 2) + silu.shape, bf16),
        pltpu.VMEM((3, 2, 2) + silu.shape, bf16),
        pltpu.VMEM((2, ada_weight.shape[0], ada_weight.shape[1] // 9), bf16),
        pltpu.VMEM((8, ada_weight.shape[0]), f32),
        dma,
        dma((2,)),
        dma((2,)),
        dma((2,)),
        dma((2, 2)),
        dma((2, 2)),
        dma((2, 2)),
        dma((2, 2, 3)),
        dma((2, 2, 2)),
        dma((2, 2)),
        dma((2, 2, 3)),
        dma((2, 2)),
        dma((2, 2, 3)),
        dma((2, 2, 2)),
        dma((2, 5)),
        dma((2, 2)),
        dma((2, 3)),
        dma((2, 2)),
        dma((2, 3)),
        dma((2,)),
        dma((2,)),
        pltpu.SemaphoreType.REGULAR,
        pltpu.SemaphoreType.REGULAR,
    ]
    return pl.pallas_call(
        functools.partial(reduce_kernel, grid_rows, first_jobs, second_jobs, proj_jobs),
        out_shape=(
            jax.ShapeDtypeStruct((first_jobs,) + tile, f32),
            jax.ShapeDtypeStruct((second_jobs,) + tile, f32),
            jax.ShapeDtypeStruct((proj_jobs,) + proj_tile, f32),
            jax.ShapeDtypeStruct(bias.shape, f32),
            jax.ShapeDtypeStruct((4, 2, 2) + slot_tail, f32),
            jax.ShapeDtypeStruct((4, 2, 2) + silu.shape, bf16),
            jax.ShapeDtypeStruct((8, ada_weight.shape[0]), f32),
        ),
        in_specs=[whole_spec(pl.ANY)] * 14 + [whole_spec()] * 4 + [whole_spec(pl.ANY)],
        out_specs=(whole_spec(),) * 7,
        scratch_shapes=scratch,
        compiler_params=pltpu.CompilerParams(
            collective_id=1, has_side_effects=True, vmem_limit_bytes=52 << 20
        ),
        cost_estimate=pl.CostEstimate(flops=10**11, bytes_accessed=10**8, transcendentals=0),
        name="reduce_grads",
    )(*one, *two, *three, *four, *mid, *first, *last, bias, slots, silu, slot_low, ada_weight)


def fetch_kernel(
    tokens_ref,
    qkv_ref,
    cond_ref,
    ada_ref,
    ada_bias_ref,
    tokens_out,
    qkv_out,
    cond_out,
    mod_out,
    ada_tile,
    token_hold,
    qkv_hold,
    token_sems,
    cond_sems,
    x_sems,
    y_sems,
    z_sems,
    local_sems,
    ada_sems,
):
    dp = lax.axis_index("dp")
    x = lax.axis_index("tensor")
    core = dp % 2
    y = (dp // 2) % 2
    z = dp // 4
    z_near = lax.rem(z, 2)
    home = core == x
    away = core != x
    pieces = x_sems.shape[1]
    quarter = qkv_ref.shape[0] // 4
    height = quarter // pieces

    def device(z_at, y_at, core_at, x_at):
        return ((z_at * 2 + y_at) * 2 + core_at, x_at)

    core_peer = device(z, y, 1 - core, x)
    swap_peer = device(z, y, x, core)
    y_peer = device(z, 1 - y, core, x)
    z_peer = device(z + 1 - 2 * z_near, y, core, x)
    barrier = pltpu.get_barrier_semaphore()
    peers = [core_peer, device(z, y, core, 1 - x), device(z, y, 1 - core, 1 - x), y_peer, z_peer]
    for peer in peers:
        pl.semaphore_signal(barrier, inc=1, device_id=peer, device_id_type=MESH)
    pl.semaphore_wait(barrier, len(peers))

    def remote(source, target, sems, index, peer):
        return pltpu.make_async_remote_copy(
            src_ref=source,
            dst_ref=target,
            send_sem=sems.at[(0,) + index],
            recv_sem=sems.at[(1,) + index],
            device_id=peer,
            device_id_type=MESH,
        )

    def span(y_at, piece):
        return pl.ds(pl.multiple_of((y_at * 2 + z_near) * quarter + piece * height, 32), height)

    def x_copy(piece):
        return remote(qkv_ref.at[span(y, piece), :], qkv_out.at[span(y, piece), :], x_sems, (piece,), swap_peer)

    def y_copy(piece):
        return remote(qkv_out.at[span(y, piece), :], qkv_out.at[span(y, piece), :], y_sems, (piece,), y_peer)

    def z_copy(piece, other):
        y_at = 1 - y if other else y
        rows = span(y_at, piece)
        return remote(qkv_out.at[rows, :], qkv_out.at[rows, :], z_sems, (int(other), piece), z_peer)

    token_copy = remote(tokens_ref, tokens_out, token_sems, (), swap_peer)
    cond_copy = remote(cond_ref, cond_out, cond_sems, (), core_peer)
    local_in = [
        pltpu.make_async_copy(tokens_ref, token_hold, local_sems.at[0]),
        pltpu.make_async_copy(qkv_ref, qkv_hold, local_sems.at[1]),
    ]
    local_out = [
        pltpu.make_async_copy(token_hold, tokens_out, local_sems.at[2]),
        pltpu.make_async_copy(qkv_hold, qkv_out, local_sems.at[3]),
    ]

    @pl.when(away)
    def _():
        for piece in range(pieces):
            x_copy(piece).start()
        token_copy.start()

    @pl.when(home)
    def _():
        cond_copy.start()
        for copy in local_in:
            copy.start()
        cond_out[...] = cond_ref[...]

    tile_cols = ada_tile.shape[2]
    tiles = ada_ref.shape[1] // tile_cols

    def ada_copy(tile, slot):
        columns = pl.ds(pl.multiple_of(tile * tile_cols, LANES), tile_cols)
        return pltpu.make_async_copy(ada_ref.at[:, columns], ada_tile.at[slot], ada_sems.at[slot])

    ada_copy(0, 0).start()

    @pl.when(away)
    def _():
        cond_copy.wait_recv()

    cond = cond_out[...].astype(f32)
    low = (cond / (1.0 + jnp.exp(-cond))).astype(bf16)

    def modulate(tile, carry):
        slot = lax.rem(tile, 2)
        ada_copy(tile, slot).wait()

        @pl.when(tile + 1 < tiles)
        def _():
            ada_copy(tile + 1, 1 - slot).start()

        columns = pl.ds(pl.multiple_of(tile * tile_cols, LANES), tile_cols)
        product = jnp.dot(low, ada_tile[slot], preferred_element_type=f32)
        mod_out[:, columns] = product + ada_bias_ref[:, columns].astype(f32)
        return carry

    lax.fori_loop(0, tiles, modulate, 0)

    @pl.when(away)
    def _():
        for piece in range(pieces):
            x_copy(piece).wait_recv()
            y_copy(piece).start()
            z_copy(piece, False).start()
        for piece in range(pieces):
            y_copy(piece).wait_recv()
            z_copy(piece, True).start()
        token_copy.wait()
        for piece in range(pieces):
            x_copy(piece).wait_send()
            y_copy(piece).wait_send()
            z_copy(piece, False).wait()
            z_copy(piece, True).wait()

    @pl.when(home)
    def _():
        cond_copy.wait_send()
        for copy, onward in zip(local_in, local_out):
            copy.wait()
            onward.start()
        for copy in local_out:
            copy.wait()


def fetch(tokens, qkv, condition, ada_weight, ada_bias):
    pieces = 3
    dma = pltpu.SemaphoreType.DMA
    return pl.pallas_call(
        fetch_kernel,
        out_shape=(
            jax.ShapeDtypeStruct(tokens.shape, bf16),
            jax.ShapeDtypeStruct(qkv.shape, bf16),
            jax.ShapeDtypeStruct(condition.shape, bf16),
            jax.ShapeDtypeStruct((condition.shape[0], ada_weight.shape[1]), f32),
        ),
        in_specs=[whole_spec(pl.ANY), whole_spec(pl.ANY), whole_spec(), whole_spec(pl.ANY), whole_spec()],
        out_specs=(whole_spec(pl.ANY), whole_spec(pl.ANY), whole_spec(), whole_spec()),
        scratch_shapes=[
            pltpu.VMEM((2, ada_weight.shape[0], ada_weight.shape[1] // 9), bf16),
            pltpu.VMEM(tokens.shape, bf16),
            pltpu.VMEM(qkv.shape, bf16),
            dma((2,)),
            dma((2,)),
            dma((2, pieces)),
            dma((2, pieces)),
            dma((2, 2, pieces)),
            dma((4,)),
            dma((2,)),
        ],
        compiler_params=pltpu.CompilerParams(
            collective_id=2, has_side_effects=True, vmem_limit_bytes=56 << 20
        ),
        cost_estimate=pl.CostEstimate(flops=10**10, bytes_accessed=3 * 10**7, transcendentals=0),
        name="fetch",
    )(tokens, qkv, condition, ada_weight, ada_bias.reshape(1, -1))


def after(value, earlier):
    return lax.optimization_barrier((value, earlier))[0]


def paired_shards(
    tokens_in,
    condition,
    ada_weight,
    ada_bias,
    qkv_weight,
    qv_bias,
    out_weight,
    out_bias,
    up_weight,
    up_bias,
    down_weight,
    down_bias,
    proj_in,
    proj_in_bias,
    proj_mid,
    proj_mid_bias,
    proj_last,
    proj_last_bias,
    enc_features,
    image_ids,
    target_rows,
    out_grad,
):
    dp = lax.axis_index("dp")
    x = lax.axis_index("tensor")
    core = dp % 2
    y = (dp // 2) % 2
    z = dp // 4
    z_near = z % 2
    z_far = z // 2
    place = dp * 2 + x
    home = core == x
    group = (dp // 2) * 2 + x
    local_rows, width = tokens_in.shape
    shard_rows = image_ids.shape[0]
    slots = condition.shape[0]
    units = local_rows // SHORT
    local_cols = qkv_weight.shape[2]
    local_hidden = up_weight.shape[1]
    heads = local_cols // HEAD_DIM
    qkv_cols = -(-3 * local_cols // TILE) * TILE
    out_cols = -(-local_cols // TILE) * TILE

    def swap(value):
        return jnp.where(home, value, send(value, to_diag))

    tokens, qkv_half, cond_low, modulation = fetch(
        tokens_in, qkv_weight.reshape(width, 3 * local_cols), condition, ada_weight, ada_bias
    )
    packed_ids = send(image_ids, to_core)
    ids = jnp.where(home, image_ids, packed_ids)

    def over_x(weight, earlier):
        own = lax.dynamic_slice_in_dim(weight, y * (weight.shape[0] // 2), weight.shape[0] // 2)
        return send(after(own, earlier), to_diag)

    def over_y(weight, first):
        second = send(first, to_swapped_y)
        first, second, whole = lax.optimization_barrier((first, second, weight))
        halves = whole.reshape((2,) + first.shape)
        mine = jnp.arange(2).reshape(2, 1, 1) == y
        return jnp.where(home, halves, jnp.where(mine, first[None], second[None])).reshape(weight.shape)

    out_first = over_x(out_weight, tokens)
    up_first = over_x(up_weight, tokens)
    down_first = over_x(down_weight, up_first)
    out_half = over_y(out_weight, out_first)
    up_half = over_y(up_weight, up_first)
    features = jnp.where(home, enc_features, send(enc_features, to_core))
    rows_low = swap(after(target_rows, up_first))
    grad_out = swap(after(out_grad, down_first))
    bias_pack = jnp.concatenate([qv_bias.reshape(-1), up_bias])
    bias_half = swap(bias_pack).astype(f32)
    qv_half = bias_half[: 2 * local_cols].reshape(2, local_cols)
    up_bias_half = bias_half[2 * local_cols :]

    unit_ids = ids.reshape(-1, SHORT)[:, 0]
    same = unit_ids[:, None] == unit_ids[None, :]
    starts = jnp.argmax(same, axis=1).astype(jnp.int32)
    counts = jnp.sum(same.astype(jnp.int32), axis=1).astype(jnp.int32)
    my_units = lax.dynamic_slice_in_dim(unit_ids, core * units, units)
    one_hot = (my_units[:, None] == jnp.arange(slots, dtype=jnp.int32)[None, :]).astype(f32)

    silu_low = jax.nn.silu(cond_low.astype(f32)).astype(bf16)
    per_unit = jnp.dot(one_hot, modulation, precision=highest, preferred_element_type=f32)
    shift_one, scale_one, gate_one, shift_two, scale_two, gate_two = [
        piece[:, None, :] for piece in jnp.split(per_unit, 6, axis=1)
    ]

    def by_unit(array):
        return array.reshape(units, SHORT, -1)

    def flat(array):
        return array.reshape(local_rows, -1)

    def reduce_cores(left, matrix, product):
        mine = lax.dynamic_slice_in_dim(left, core * local_rows, local_rows)
        theirs = lax.dynamic_slice_in_dim(left, (1 - core) * local_rows, local_rows)
        got = send(product(theirs, matrix).astype(bf16), to_core)
        return product(mine, matrix).astype(bf16).astype(f32) + got.astype(f32)

    def dot_nn(left, right):
        return jnp.dot(left, right, preferred_element_type=f32)

    resid = by_unit(tokens.astype(f32))
    normed_one, inv_one = layer_norm(resid)
    attn_in = flat((normed_one * (1.0 + scale_one) + shift_one).astype(bf16))
    attn_all = gather_cores(attn_in)

    qkv_pad = jnp.pad(qkv_half, ((0, 0), (0, qkv_cols - 3 * local_cols)))
    out_pad = jnp.pad(out_half, ((0, out_cols - local_cols), (0, 0)))
    qkv_bias = jnp.concatenate(
        [qv_half[0], jnp.zeros_like(qv_half[0]), qv_half[1], jnp.zeros((qkv_cols - 3 * local_cols,), f32)]
    )
    qkv = (dot_nn(attn_all, qkv_pad) + qkv_bias).astype(bf16)
    qkv = after(qkv, (out_first, up_first))
    attended, log_sums = attend(starts, counts, qkv, heads, out_cols)
    attended, down_first = lax.optimization_barrier((attended, down_first))
    down_half = over_y(down_weight, down_first)
    attn_branch = by_unit(reduce_cores(attended, out_pad, dot_nn) + out_bias.astype(f32))
    mid = resid + gate_one * attn_branch

    normed_two, inv_two = layer_norm(mid)
    mlp_in = flat((normed_two * (1.0 + scale_two) + shift_two).astype(bf16))
    mlp_all = gather_cores(mlp_in)
    pre_act = dot_nn(mlp_all, up_half) + up_bias_half
    act_value, act_back = jax.vjp(gelu_tanh, pre_act)
    hidden = act_value.astype(bf16)
    mlp_branch = by_unit(reduce_cores(hidden, down_half, dot_nn) + down_bias.astype(f32))
    block_value = mid + gate_two * mlp_branch
    block_low = flat(block_value.astype(bf16))

    first_pre = dot_nn(block_low, proj_in) + proj_in_bias.astype(f32)
    first_value, first_back = jax.vjp(jax.nn.silu, first_pre)
    first_low = first_value.astype(bf16)
    second_pre = dot_nn(first_low, proj_mid) + proj_mid_bias.astype(f32)
    second_value, second_back = jax.vjp(jax.nn.silu, second_pre)
    second_low = second_value.astype(bf16)
    projected = dot_nn(second_low, proj_last) + proj_last_bias.astype(f32)
    target_vals = jnp.take(features, rows_low - group * shard_rows, axis=0).astype(f32)
    loss_back = jax.vjp(lambda predicted: align_loss(predicted, target_vals), projected)[1]
    grad_projected = loss_back(jnp.ones((), f32))[0]
    grad_last_low = grad_projected.astype(bf16)
    grad_second = second_back(dot_nt(grad_last_low, proj_last))[0]
    grad_second_low = grad_second.astype(bf16)
    grad_first = first_back(dot_nt(grad_second_low, proj_mid))[0]
    grad_first_low = grad_first.astype(bf16)
    grad_block = by_unit(grad_out.astype(f32) + dot_nt(grad_first_low, proj_in))

    grad_mlp_branch = gate_two * grad_block
    grad_mlp_all = gather_cores(flat(grad_mlp_branch.astype(bf16)))
    grad_pre = act_back(dot_nt(grad_mlp_all, down_half))[0]
    grad_pre_low = grad_pre.astype(bf16)
    grad_mlp_in = by_unit(reduce_cores(grad_pre_low, up_half, dot_nt))
    grad_mid = grad_block + norm_back(normed_two, inv_two, grad_mlp_in * (1.0 + scale_two))

    grad_attn_branch = gate_one * grad_mid
    grad_attn_all = gather_cores(flat(grad_attn_branch.astype(bf16)))
    grad_heads = dot_nt(grad_attn_all, out_pad).astype(bf16)
    grad_qkv, qkv_bias_sums = attend_back(starts, counts, qkv, log_sums, grad_heads, heads)
    grad_attn_in = by_unit(reduce_cores(grad_qkv, qkv_pad, dot_nt))
    grad_tokens = grad_mid + norm_back(normed_one, inv_one, grad_attn_in * (1.0 + scale_one))

    def unit_sum(array):
        return jnp.sum(array, axis=1)

    mod_units = jnp.concatenate(
        [
            unit_sum(grad_attn_in),
            unit_sum(grad_attn_in * normed_one),
            unit_sum(attn_branch * grad_mid),
            unit_sum(grad_mlp_in),
            unit_sum(grad_mlp_in * normed_two),
            unit_sum(mlp_branch * grad_block),
        ],
        axis=1,
    )
    slot_part = dot_tn(one_hot, mod_units, precision=highest)
    slot_grad = slot_part + send(slot_part, to_core)
    slot_low = slot_grad.astype(bf16)
    mod_cols = slot_low.shape[1] // 32
    slot_cols = pick(slot_grad.reshape(slots, 4, 2, 2, 2, mod_cols), core, 3).transpose(3, 2, 1, 0, 4)
    slot_cols = jnp.pad(slot_cols, ((0, 0),) * 3 + ((0, 8 - slots), (0, -mod_cols % LANES)))

    qv_sums = qkv_bias_sums[:2]
    qv_full = lax.dynamic_update_slice_in_dim(jnp.zeros((2, width), f32), qv_sums, core * local_cols, axis=1)
    up_full = lax.dynamic_update_slice_in_dim(
        jnp.zeros((2 * local_hidden,), f32), jnp.sum(grad_pre, axis=0), core * local_hidden, axis=0
    )
    pieces = [
        qv_full.reshape(-1),
        up_full,
        jnp.sum(flat(grad_attn_branch), axis=0),
        jnp.sum(flat(grad_mlp_branch), axis=0),
        jnp.sum(grad_first, axis=0),
        jnp.sum(grad_second, axis=0),
        jnp.sum(grad_projected, axis=0),
    ]
    packed = jnp.concatenate(pieces)
    packed = jnp.pad(packed, (0, -packed.shape[0] % (8 * LANES))).reshape(-1, LANES)
    first_sum, second_sum, proj_sum, sums, slot_sum, silu_sum, cond_sum = reduce_grads(
        (grad_mlp_all, hidden),
        (grad_attn_all, attended),
        (mlp_all, grad_pre_low),
        (attn_all, grad_qkv),
        (grad_second_low, first_low),
        (grad_first_low, block_low),
        (grad_last_low, second_low),
        packed,
        slot_cols,
        jnp.pad(silu_low, ((0, 8 - slots), (0, 0))),
        jnp.pad(slot_low, ((0, 8 - slots), (0, 0))),
        ada_weight,
    )
    grad_condition = jax.vjp(jax.nn.silu, condition.astype(f32))[1](cond_sum[:slots])[0]
    sums = sums.reshape(-1)
    slot_mine = slot_sum.reshape(16, 8, -1)[:, :slots, :mod_cols].astype(bf16).reshape(16 * slots, mod_cols)
    grad_ada = dot_tn(silu_sum.reshape(16, 8, width)[:, :slots].reshape(16 * slots, width), slot_mine)
    ada_bias_grad = jnp.sum(slot_mine.astype(f32), axis=0)
    row_count = width // 16

    def columns(tiles):
        return tiles.transpose(1, 0, 2).reshape(tiles.shape[1], -1)

    def rows(tiles):
        return tiles.transpose(0, 2, 1).reshape(-1, tiles.shape[1])

    down_tiles = local_hidden // TILE
    sum_down = rows(first_sum[:down_tiles])
    sum_out = rows(first_sum[down_tiles:])[:local_cols]
    sum_up = columns(second_sum[:down_tiles])
    sum_qkv = columns(second_sum[down_tiles:])[:, : 3 * local_cols].reshape(row_count, 3, local_cols)
    mid_tiles = proj_mid.shape[0] // TILE
    in_tiles = -(-width // TILE)
    sum_mid = rows(proj_sum[:mid_tiles])
    sum_in = rows(proj_sum[mid_tiles : mid_tiles + in_tiles])[:width]
    last_share = proj_last.shape[1] // 32
    last_tiles = proj_sum[mid_tiles + in_tiles :]
    last_tiles = last_tiles.reshape(last_tiles.shape[0] * 2, -1, TILE)[:, :last_share]
    sum_last = rows(last_tiles)
    found = []
    offset = 0
    for piece in pieces:
        found.append(sums[offset : offset + piece.shape[0]])
        offset += piece.shape[0]
    qv_grad = lax.dynamic_slice_in_dim(found[0].reshape(2, width), x * local_cols, local_cols, axis=1)
    up_bias_grad = lax.dynamic_slice_in_dim(found[1], x * local_hidden, local_hidden, axis=0)

    block_out = swap(block_low)
    tokens_out = swap(flat(grad_tokens).astype(bf16))
    return (
        block_out,
        tokens_out.astype(f32),
        grad_condition,
        grad_ada,
        ada_bias_grad,
        sum_qkv,
        qv_grad,
        sum_out,
        found[2],
        sum_up,
        up_bias_grad,
        sum_down,
        found[3],
        sum_in,
        found[4],
        sum_mid,
        found[5],
        sum_last,
        found[6],
    )


def solution(mesh):
    in_specs = (
        P(("dp", "tensor"), None),
        P("dp", None),
        P(),
        P(),
        P(None, None, "tensor"),
        P(None, "tensor"),
        P("tensor", None),
        P(),
        P(None, "tensor"),
        P("tensor"),
        P("tensor", None),
        P(),
        P(),
        P(),
        P(),
        P(),
        P(),
        P(),
        P("dp", None),
        P("dp"),
        P(("dp", "tensor")),
        P(("dp", "tensor"), None),
    )
    out_specs = (
        P(("dp", "tensor"), None),
        P(("dp", "tensor"), None),
        P("dp", None),
        P(None, ("dp", "tensor")),
        P(("dp", "tensor")),
        P("dp", None, "tensor"),
        P(None, "tensor"),
        P("tensor", "dp"),
        P(),
        P("dp", "tensor"),
        P("tensor"),
        P("tensor", "dp"),
        P(),
        P(None, ("dp", "tensor")),
        P(),
        P(None, ("dp", "tensor")),
        P(),
        P(None, ("dp", "tensor")),
        P(),
    )
    paired = mesh.shape["tensor"] == 2 and mesh.shape["dp"] == 16
    body = paired_shards if paired else shards
    return jax.shard_map(body, mesh=mesh, in_specs=in_specs, out_specs=out_specs, check_vma=False)
```

```python
import functools

import jax
import jax.numpy as jnp
from jax import lax
from jax.experimental import pallas as pl
from jax.experimental.pallas import tpu as pltpu
from jax.sharding import PartitionSpec as P

HEAD_DIM = 72
SHORT = 256


highest = lax.Precision.HIGHEST
eps_norm = 1e-06
repa_weight = 1000.0
neg_fill = -1e30


def dot_nt(left_arg, right_arg):
    return lax.dot_general(
        left_arg, right_arg, (((1,), (1,)), ((), ())), preferred_element_type=jnp.float32
    )


def dot_tn(left_arg, right_arg, precision=None):
    return lax.dot_general(
        left_arg,
        right_arg,
        (((0,), (0,)), ((), ())),
        precision=precision,
        preferred_element_type=jnp.float32,
    )


def layer_norm(values):
    center = values - jnp.mean(values, axis=-1, keepdims=True)
    inv_std = lax.rsqrt(jnp.mean(center * center, axis=-1, keepdims=True) + eps_norm)
    return (center * inv_std, inv_std)


def norm_back(normed, inv_std, grad_normed):
    return inv_std * (
        grad_normed
        - jnp.mean(grad_normed, axis=-1, keepdims=True)
        - normed * jnp.mean(grad_normed * normed, axis=-1, keepdims=True)
    )


def gelu_tanh(values):
    return jax.nn.gelu(values, approximate=True)


def align_loss(projected, target_vals):
    inner = jnp.sum(projected * target_vals, axis=1)
    norm_pred = lax.rsqrt(jnp.sum(projected * projected, axis=1) + eps_norm)
    norm_target = lax.rsqrt(jnp.sum(target_vals * target_vals, axis=1) + eps_norm)
    return -repa_weight * jnp.sum(inner * norm_pred * norm_target)


def block_rows(total_rows, unit_rows):
    count = total_rows // unit_rows
    best = 1
    for parts in range(1, count + 1):
        if count % parts == 0 and parts * unit_rows <= 1024:
            best = parts
    return best * unit_rows


def block_scores(queries, key_rows, image_ids, row_start, starts, block_len, score_scale):
    query_blk = queries[row_start : row_start + block_len]
    row_ids = image_ids[row_start : row_start + block_len]
    pieces = []
    for col_start in starts:

        def compute_block(col_start=col_start):
            products = (
                jnp.einsum(
                    "qhd,khd->hqk",
                    query_blk,
                    key_rows[col_start : col_start + block_len],
                    preferred_element_type=jnp.float32,
                )
                * score_scale
            )
            same_image = row_ids[:, None] == image_ids[col_start : col_start + block_len][None, :]
            return jnp.where(same_image[None], products, neg_fill)

        pieces.append(compute_block())
    return jnp.concatenate(pieces, axis=2)


def attention_forward(queries, key_rows, values, image_ids, block_len, score_scale):
    starts = list(range(0, queries.shape[0], block_len))
    outputs = []
    log_sums = []
    for row_start in starts:
        scores = block_scores(
            queries, key_rows, image_ids, row_start, starts, block_len, score_scale
        )
        row_max = jnp.max(scores, axis=2, keepdims=True)
        exponent = jnp.exp(scores - row_max)
        row_total = jnp.sum(exponent, axis=2, keepdims=True)
        prob_low = (exponent / row_total).astype(jnp.bfloat16)
        log_sums.append(row_max + jnp.log(row_total))
        summed = jnp.zeros((block_len, queries.shape[1], queries.shape[2]), jnp.float32)
        for position, col_start in enumerate(starts):

            def weigh_block(position=position, col_start=col_start, prob_low=prob_low):
                return jnp.einsum(
                    "hqk,khd->qhd",
                    prob_low[:, :, position * block_len : (position + 1) * block_len],
                    values[col_start : col_start + block_len],
                    preferred_element_type=jnp.float32,
                )

            summed = summed + weigh_block()
        outputs.append(summed.astype(jnp.bfloat16))
    return (jnp.concatenate(outputs, axis=0), jnp.concatenate(log_sums, axis=1))


def attention_backward(
    queries, key_rows, values, image_ids, log_sums, grad_heads, block_len, score_scale
):
    starts = list(range(0, queries.shape[0], block_len))
    grad_keys = jnp.zeros(key_rows.shape, jnp.float32)
    grad_values = jnp.zeros(values.shape, jnp.float32)
    grad_query_list = []
    for row_start in starts:
        query_blk = queries[row_start : row_start + block_len]
        grad_blk = grad_heads[row_start : row_start + block_len]
        scores = block_scores(
            queries, key_rows, image_ids, row_start, starts, block_len, score_scale
        )
        soft = jnp.exp(scores - log_sums[:, row_start : row_start + block_len])
        grad_pieces = []
        for col_start in starts:

            def pull_block(col_start=col_start):
                return jnp.einsum(
                    "qhd,khd->hqk",
                    grad_blk,
                    values[col_start : col_start + block_len],
                    preferred_element_type=jnp.float32,
                )

            grad_pieces.append(pull_block())
        grad_soft = jnp.concatenate(grad_pieces, axis=2)
        inner = jnp.sum(soft * grad_soft, axis=2, keepdims=True)
        grad_scores = (soft * (grad_soft - inner)).astype(jnp.bfloat16)
        soft_low = soft.astype(jnp.bfloat16)
        grad_query = jnp.zeros(query_blk.shape, jnp.float32)
        for position, col_start in enumerate(starts):

            def both_grads(position=position, col_start=col_start):
                piece = grad_scores[:, :, position * block_len : (position + 1) * block_len]
                soft_piece = soft_low[:, :, position * block_len : (position + 1) * block_len]
                return (
                    jnp.einsum(
                        "hqk,khd->qhd",
                        piece,
                        key_rows[col_start : col_start + block_len],
                        preferred_element_type=jnp.float32,
                    ),
                    jnp.einsum(
                        "hqk,qhd->khd", piece, query_blk, preferred_element_type=jnp.float32
                    ),
                    jnp.einsum(
                        "hqk,qhd->khd", soft_piece, grad_blk, preferred_element_type=jnp.float32
                    ),
                )

            part_query, part_key, part_value = both_grads()
            grad_query = grad_query + part_query
            grad_keys = grad_keys.at[col_start : col_start + block_len].add(part_key)
            grad_values = grad_values.at[col_start : col_start + block_len].add(part_value)
        grad_query_list.append(grad_query * score_scale)
    return (jnp.concatenate(grad_query_list, axis=0), grad_keys * score_scale, grad_values)


def column_set(matrix, data_count, tensor_count, tensor_rank):
    shaped = matrix.reshape(matrix.shape[0], data_count, tensor_count, -1)
    return lax.dynamic_index_in_dim(shaped, tensor_rank, axis=2, keepdims=False).reshape(
        matrix.shape[0], -1
    )


def shards(
    tokens_in,
    condition,
    ada_weight,
    ada_bias,
    qkv_weight,
    qv_bias,
    out_weight,
    out_bias,
    up_weight,
    up_bias,
    down_weight,
    down_bias,
    proj_in,
    proj_in_bias,
    proj_mid,
    proj_mid_bias,
    proj_last,
    proj_last_bias,
    enc_features,
    image_ids,
    target_rows,
    out_grad,
):
    tensor_count = lax.axis_size("tensor")
    data_count = lax.axis_size("dp")
    tensor_rank = lax.axis_index("tensor")
    data_rank = lax.axis_index("dp")
    local_rows, model_width = tokens_in.shape
    shard_rows = image_ids.shape[0]
    slot_count = condition.shape[0]
    local_cols = qkv_weight.shape[2]
    local_hidden = up_weight.shape[1]
    head_count = local_cols // HEAD_DIM
    score_scale = HEAD_DIM ** (-0.5)
    block_len = block_rows(shard_rows, SHORT)
    my_ids = lax.dynamic_slice_in_dim(image_ids, tensor_rank * local_rows, local_rows)
    one_hot = (my_ids[:, None] == jnp.arange(slot_count, dtype=jnp.int32)[None, :]).astype(
        jnp.float32
    )
    cond_float = condition.astype(jnp.float32)
    silu_cond, silu_back = jax.vjp(jax.nn.silu, cond_float)
    silu_low = silu_cond.astype(jnp.bfloat16)
    modulation = jnp.dot(
        silu_low, ada_weight, preferred_element_type=jnp.float32
    ) + ada_bias.astype(jnp.float32)
    per_token = jnp.dot(one_hot, modulation, precision=highest, preferred_element_type=jnp.float32)
    shift_one, scale_one, gate_one, shift_two, scale_two, gate_two = jnp.split(per_token, 6, axis=1)
    resid = tokens_in.astype(jnp.float32)
    normed_one, inv_one = layer_norm(resid)
    attn_in = (normed_one * (1.0 + scale_one) + shift_one).astype(jnp.bfloat16)
    attn_all = lax.all_gather(attn_in, "tensor", axis=0, tiled=True)
    qkv_flat_weight = qkv_weight.reshape(model_width, 3 * local_cols)
    qkv_flat = jnp.dot(attn_all, qkv_flat_weight, preferred_element_type=jnp.float32)
    bias_float = qv_bias.astype(jnp.float32)
    queries = (
        (qkv_flat[:, :local_cols] + bias_float[0])
        .astype(jnp.bfloat16)
        .reshape(shard_rows, head_count, HEAD_DIM)
    )
    key_rows = (
        qkv_flat[:, local_cols : 2 * local_cols]
        .astype(jnp.bfloat16)
        .reshape(shard_rows, head_count, HEAD_DIM)
    )
    values = (
        (qkv_flat[:, 2 * local_cols :] + bias_float[1])
        .astype(jnp.bfloat16)
        .reshape(shard_rows, head_count, HEAD_DIM)
    )
    attended, log_sums = attention_forward(
        queries, key_rows, values, image_ids, block_len, score_scale
    )
    attended = attended.reshape(shard_rows, local_cols)
    attn_branch = lax.psum_scatter(
        jnp.dot(attended, out_weight, preferred_element_type=jnp.float32).astype(jnp.bfloat16),
        "tensor",
        scatter_dimension=0,
        tiled=True,
    ).astype(jnp.float32) + out_bias.astype(jnp.float32)
    mid = resid + gate_one * attn_branch
    normed_two, inv_two = layer_norm(mid)
    mlp_in = (normed_two * (1.0 + scale_two) + shift_two).astype(jnp.bfloat16)
    mlp_all = lax.all_gather(mlp_in, "tensor", axis=0, tiled=True)
    pre_act = jnp.dot(mlp_all, up_weight, preferred_element_type=jnp.float32) + up_bias.astype(
        jnp.float32
    )
    act_value, act_back = jax.vjp(gelu_tanh, pre_act)
    hidden = act_value.astype(jnp.bfloat16)
    mlp_branch = lax.psum_scatter(
        jnp.dot(hidden, down_weight, preferred_element_type=jnp.float32).astype(jnp.bfloat16),
        "tensor",
        scatter_dimension=0,
        tiled=True,
    ).astype(jnp.float32) + down_bias.astype(jnp.float32)
    block_value = mid + gate_two * mlp_branch
    block_low = block_value.astype(jnp.bfloat16)
    first_pre = jnp.dot(
        block_low, proj_in, preferred_element_type=jnp.float32
    ) + proj_in_bias.astype(jnp.float32)
    first_value, first_back = jax.vjp(jax.nn.silu, first_pre)
    first_low = first_value.astype(jnp.bfloat16)
    second_pre = jnp.dot(
        first_low, proj_mid, preferred_element_type=jnp.float32
    ) + proj_mid_bias.astype(jnp.float32)
    second_value, second_back = jax.vjp(jax.nn.silu, second_pre)
    second_low = second_value.astype(jnp.bfloat16)
    projected = jnp.dot(
        second_low, proj_last, preferred_element_type=jnp.float32
    ) + proj_last_bias.astype(jnp.float32)
    target_vals = jnp.take(enc_features, target_rows - data_rank * shard_rows, axis=0).astype(
        jnp.float32
    )
    loss_value, loss_back = jax.vjp(lambda predicted: align_loss(predicted, target_vals), projected)
    grad_projected = loss_back(jnp.ones((), jnp.float32))[0]
    grad_last_low = grad_projected.astype(jnp.bfloat16)
    grad_second = second_back(dot_nt(grad_last_low, proj_last))[0]
    grad_second_low = grad_second.astype(jnp.bfloat16)
    grad_first = first_back(dot_nt(grad_second_low, proj_mid))[0]
    grad_first_low = grad_first.astype(jnp.bfloat16)
    grad_block = out_grad.astype(jnp.float32) + dot_nt(grad_first_low, proj_in)
    gate_two_grad = mlp_branch * grad_block
    grad_mlp_branch = gate_two * grad_block
    grad_mlp_all = lax.all_gather(
        grad_mlp_branch.astype(jnp.bfloat16), "tensor", axis=0, tiled=True
    )
    grad_down_local = dot_tn(hidden, grad_mlp_all)
    grad_pre = act_back(dot_nt(grad_mlp_all, down_weight))[0]
    grad_pre_low = grad_pre.astype(jnp.bfloat16)
    grad_up_local = dot_tn(mlp_all, grad_pre_low)
    up_bias_local = jnp.sum(grad_pre, axis=0)
    grad_mlp_in = lax.psum_scatter(
        dot_nt(grad_pre_low, up_weight).astype(jnp.bfloat16),
        "tensor",
        scatter_dimension=0,
        tiled=True,
    ).astype(jnp.float32)
    scale_two_grad = grad_mlp_in * normed_two
    grad_mid = grad_block + norm_back(normed_two, inv_two, grad_mlp_in * (1.0 + scale_two))
    gate_one_grad = attn_branch * grad_mid
    grad_attn_branch = gate_one * grad_mid
    grad_attn_all = lax.all_gather(
        grad_attn_branch.astype(jnp.bfloat16), "tensor", axis=0, tiled=True
    )
    grad_out_local = dot_tn(attended, grad_attn_all)
    grad_heads = (
        dot_nt(grad_attn_all, out_weight)
        .astype(jnp.bfloat16)
        .reshape(shard_rows, head_count, HEAD_DIM)
    )
    grad_queries, grad_keys, grad_values = attention_backward(
        queries, key_rows, values, image_ids, log_sums, grad_heads, block_len, score_scale
    )
    grad_queries = grad_queries.reshape(shard_rows, local_cols)
    grad_keys = grad_keys.reshape(shard_rows, local_cols)
    grad_values = grad_values.reshape(shard_rows, local_cols)
    qv_local = jnp.stack([jnp.sum(grad_queries, axis=0), jnp.sum(grad_values, axis=0)])
    grad_qkv_low = jnp.concatenate([grad_queries, grad_keys, grad_values], axis=1).astype(
        jnp.bfloat16
    )
    grad_qkv_local = dot_tn(attn_all, grad_qkv_low).reshape(model_width, 3, local_cols)
    grad_attn_in = lax.psum_scatter(
        dot_nt(grad_qkv_low, qkv_flat_weight).astype(jnp.bfloat16),
        "tensor",
        scatter_dimension=0,
        tiled=True,
    ).astype(jnp.float32)
    scale_one_grad = grad_attn_in * normed_one
    grad_tokens = grad_mid + norm_back(normed_one, inv_one, grad_attn_in * (1.0 + scale_one))
    token_mod_grad = jnp.concatenate(
        [grad_attn_in, scale_one_grad, gate_one_grad, grad_mlp_in, scale_two_grad, gate_two_grad],
        axis=1,
    )
    slot_grad_part = dot_tn(one_hot, token_mod_grad, precision=highest)
    slot_grad = lax.psum(slot_grad_part.astype(jnp.bfloat16), "tensor").astype(jnp.float32)
    slot_low = slot_grad.astype(jnp.bfloat16)
    grad_condition = silu_back(dot_nt(slot_low, ada_weight))[0]
    ada_cols = dot_tn(silu_low, column_set(slot_low, data_count, tensor_count, tensor_rank))
    ada_bias_cols = jnp.sum(
        column_set(slot_grad, data_count, tensor_count, tensor_rank), axis=0, keepdims=True
    )
    block_grads = (
        lax.psum_scatter(
            grad_qkv_local.astype(jnp.bfloat16), "dp", scatter_dimension=0, tiled=True
        ).astype(jnp.float32),
        lax.psum_scatter(
            grad_out_local.astype(jnp.bfloat16), "dp", scatter_dimension=1, tiled=True
        ).astype(jnp.float32),
        lax.psum_scatter(
            grad_up_local.astype(jnp.bfloat16), "dp", scatter_dimension=0, tiled=True
        ).astype(jnp.float32),
        lax.psum_scatter(
            grad_down_local.astype(jnp.bfloat16), "dp", scatter_dimension=1, tiled=True
        ).astype(jnp.float32),
        lax.psum_scatter(
            ada_cols.astype(jnp.bfloat16), "dp", scatter_dimension=1, tiled=True
        ).astype(jnp.float32),
        lax.psum_scatter(
            ada_bias_cols.astype(jnp.bfloat16), "dp", scatter_dimension=1, tiled=True
        ).astype(jnp.float32),
    )
    qv_full = lax.dynamic_update_slice_in_dim(
        jnp.zeros((2, model_width), jnp.float32), qv_local, tensor_rank * local_cols, axis=1
    )
    up_full = lax.dynamic_update_slice_in_dim(
        jnp.zeros((local_hidden * tensor_count,), jnp.float32),
        up_bias_local,
        tensor_rank * local_hidden,
        axis=0,
    )
    bias_sums = lax.psum(
        (
            qv_full,
            up_full,
            jnp.sum(grad_attn_branch, axis=0),
            jnp.sum(grad_mlp_branch, axis=0),
            jnp.sum(grad_first, axis=0),
            jnp.sum(grad_second, axis=0),
            jnp.sum(grad_projected, axis=0),
        ),
        ("dp", "tensor"),
    )
    qv_grad = lax.dynamic_slice_in_dim(bias_sums[0], tensor_rank * local_cols, local_cols, axis=1)
    up_bias_grad = lax.dynamic_slice_in_dim(
        bias_sums[1], tensor_rank * local_hidden, local_hidden, axis=0
    )
    proj_grads = (
        lax.psum_scatter(
            dot_tn(block_low, grad_first_low), ("dp", "tensor"), scatter_dimension=1, tiled=True
        ),
        lax.psum_scatter(
            dot_tn(first_low, grad_second_low), ("dp", "tensor"), scatter_dimension=1, tiled=True
        ),
        lax.psum_scatter(
            dot_tn(second_low, grad_last_low), ("dp", "tensor"), scatter_dimension=1, tiled=True
        ),
    )
    return (
        block_low,
        grad_tokens,
        grad_condition,
        block_grads[4],
        block_grads[5].reshape(-1),
        block_grads[0],
        qv_grad,
        block_grads[1],
        bias_sums[2],
        block_grads[2],
        up_bias_grad,
        block_grads[3],
        bias_sums[3],
        proj_grads[0],
        bias_sums[4],
        proj_grads[1],
        bias_sums[5],
        proj_grads[2],
        bias_sums[6],
    )


LANES = 128
MESH = pl.DeviceIdType.MESH
TILE = 256
GAP = 2
SLOTS = 2 * GAP
LOG2_E = 1.4426950408889634
GELU_SCALE = 0.7978845608028654
GELU_CUBE = 0.044715
bf16 = jnp.bfloat16
f32 = jnp.float32


def pairs_of(move):
    found = []
    for index in range(32):
        x, core, y, z = index % 2, (index // 2) % 2, (index // 4) % 2, index // 8
        z2, y2, c2, x2 = move(z, y, core, x)
        if (z2, y2, c2, x2) != (z, y, core, x):
            found.append((index, ((z2 * 2 + y2) * 2 + c2) * 2 + x2))
    return found


def send(value, move):
    return lax.ppermute(value, ("dp", "tensor"), pairs_of(move))


def to_diag(z, y, c, x):
    return (z, y, x, c)


def to_cycle(z, y, c, x):
    return (z, y, c, c) if c != x else (z, y, 1 - c, x)


def to_core(z, y, c, x):
    return (z, y, 1 - c, x)


def to_x(z, y, c, x):
    return (z, y, c, 1 - x)


def to_y(z, y, c, x):
    return (z, 1 - y, c, x)


def to_swapped_y(z, y, c, x):
    return (z, 1 - y, c, x) if c != x else (z, y, c, x)


def to_z_near(z, y, c, x):
    return (z ^ 1, y, c, x)


def to_z_far(z, y, c, x):
    return (z ^ 2, y, c, x)


def pick(array, index, axis):
    return lax.dynamic_index_in_dim(array, index, axis=axis, keepdims=False)


def gather_kernel(own_ref, out_ref, local_sem, send_sem, recv_sem):
    dp = lax.axis_index("dp")
    x = lax.axis_index("tensor")
    core = dp % 2
    other = dp + 1 - 2 * core
    barrier = pltpu.get_barrier_semaphore()
    pl.semaphore_signal(barrier, inc=1, device_id=(other, x), device_id_type=MESH)
    pl.semaphore_wait(barrier, 1)
    away = pltpu.make_async_remote_copy(
        src_ref=own_ref,
        dst_ref=out_ref.at[core],
        send_sem=send_sem,
        recv_sem=recv_sem,
        device_id=(other, x),
        device_id_type=MESH,
    )
    away.start()
    here = pltpu.make_async_copy(own_ref, out_ref.at[core], local_sem)
    here.start()
    here.wait()
    away.wait()


def gather_cores(own):
    rows, width = own.shape
    return pl.pallas_call(
        gather_kernel,
        out_shape=jax.ShapeDtypeStruct((2, rows, width), own.dtype),
        in_specs=[pl.BlockSpec(memory_space=pltpu.VMEM)],
        out_specs=pl.BlockSpec(memory_space=pl.ANY),
        scratch_shapes=[pltpu.SemaphoreType.DMA] * 3,
        compiler_params=pltpu.CompilerParams(collective_id=0, has_side_effects=True, vmem_limit_bytes=16 << 20),
        cost_estimate=pl.CostEstimate(flops=0, bytes_accessed=12000000, transcendentals=0),
        name="gather_cores",
    )(own).reshape(2 * rows, width)


def split_heads(flat_ref, heads_ref, parts, heads):
    heads_ref[...] = jnp.zeros_like(heads_ref)
    for part in range(parts):
        for head in range(heads):
            begin = (part * heads + head) * HEAD_DIM
            heads_ref[part * heads + head, :, 0:HEAD_DIM] = flat_ref[:, begin : begin + HEAD_DIM]


def join_heads(heads_ref, flat_ref, count):
    rows, columns = flat_ref.shape
    for block in range(rows // LANES):
        span = slice(block * LANES, (block + 1) * LANES)
        pieces = [heads_ref[head, span, 0:HEAD_DIM] for head in range(count)]
        if columns > count * HEAD_DIM:
            pieces.append(jnp.zeros((LANES, columns - count * HEAD_DIM), flat_ref.dtype))
        flat_ref[span, :] = jnp.concatenate(pieces, axis=1)


def per_image(count, run):
    @pl.when(count == 1)
    def _():
        run(SHORT)

    @pl.when(count != 1)
    def _():
        run(4 * SHORT)


def attend_kernel(heads, together, factor, starts, counts, qkv_ref, o_ref, log_ref, part_ref, o_heads):
    split_heads(qkv_ref, part_ref, 3, heads)
    unit_count = o_ref.shape[0] // SHORT

    def some_heads(step, carry):
        def unit(index, carry):
            rows = pl.ds(pl.multiple_of(index * SHORT, SHORT), SHORT)

            def run(length):
                cols = pl.ds(pl.multiple_of(starts[index] * SHORT, SHORT), length)
                for ahead in range(together):
                    head = step * together + ahead
                    scores = dot_nt(part_ref[heads + head, cols, :], part_ref[head, rows, :])
                    top = jnp.max(scores, axis=0, keepdims=True)
                    exponent = jnp.exp2((scores - top) * factor)
                    total = jnp.sum(exponent, axis=0, keepdims=True)
                    summed = dot_tn(part_ref[2 * heads + head, cols, :], exponent.astype(bf16))
                    o_heads[head, rows, :] = (summed * (1.0 / total)).T.astype(bf16)
                    log_ref[head * unit_count + index] = top * factor + jnp.log2(total)

            per_image(counts[index], run)
            return carry

        return lax.fori_loop(0, unit_count, unit, carry)

    lax.fori_loop(0, heads // together, some_heads, 0)
    join_heads(o_heads, o_ref, heads)


def whole_spec(space=pltpu.VMEM):
    return pl.BlockSpec(memory_space=space)


def attend(starts, counts, qkv, heads, out_cols):
    rows = qkv.shape[0]
    factor = HEAD_DIM ** (-0.5) * LOG2_E
    return pl.pallas_call(
        functools.partial(attend_kernel, heads, 4, factor),
        out_shape=(
            jax.ShapeDtypeStruct((rows, out_cols), bf16),
            jax.ShapeDtypeStruct((heads * (rows // SHORT), 1, SHORT), f32),
        ),
        in_specs=[whole_spec(pltpu.SMEM), whole_spec(pltpu.SMEM), whole_spec()],
        out_specs=(whole_spec(), whole_spec()),
        scratch_shapes=[
            pltpu.VMEM((3 * heads, rows, LANES), bf16),
            pltpu.VMEM((heads, rows, LANES), bf16),
        ],
        compiler_params=pltpu.CompilerParams(vmem_limit_bytes=40 << 20),
        cost_estimate=pl.CostEstimate(flops=20 * 10**9, bytes_accessed=13 * 10**6, transcendentals=10**7),
        name="attend",
    )(starts, counts, qkv)


def attend_back_kernel(
    heads,
    together,
    factor,
    starts,
    counts,
    qkv_ref,
    log_ref,
    grad_ref,
    out_ref,
    bias_ref,
    part_ref,
    grad_heads,
    key_acc,
    value_acc,
    sums,
):
    split_heads(qkv_ref, part_ref, 3, heads)
    split_heads(grad_ref, grad_heads, 1, heads)
    unit_count = out_ref.shape[0] // SHORT

    def some_heads(step, carry):
        key_acc[...] = jnp.zeros_like(key_acc)
        value_acc[...] = jnp.zeros_like(value_acc)
        for ahead in range(together):
            sums[step * together + ahead] = jnp.zeros((8, LANES), f32)

        def unit(index, carry):
            rows = pl.ds(pl.multiple_of(index * SHORT, SHORT), SHORT)

            def run(length):
                cols = pl.ds(pl.multiple_of(starts[index] * SHORT, SHORT), length)
                for ahead in range(together):
                    head = step * together + ahead
                    queries = part_ref[head, rows, :]
                    grads = grad_heads[head, rows, :]
                    keys = part_ref[heads + head, cols, :]
                    scores = dot_nt(keys, queries)
                    soft = jnp.exp2(scores * (factor * LOG2_E) - log_ref[head * unit_count + index])
                    grad_soft = dot_nt(part_ref[2 * heads + head, cols, :], grads)
                    product = soft * grad_soft
                    inner = jnp.sum(product, axis=0, keepdims=True)
                    grad_scores = (product - soft * inner).astype(bf16)
                    value_acc[ahead, cols, :] += jnp.dot(soft.astype(bf16), grads, preferred_element_type=f32)
                    key_acc[ahead, cols, :] += jnp.dot(grad_scores, queries, preferred_element_type=f32)
                    grad_query = dot_tn(keys, grad_scores).T * factor
                    sums[head, 0:1, :] += jnp.sum(grad_query, axis=0, keepdims=True)
                    part_ref[head, rows, :] = grad_query.astype(bf16)

            per_image(counts[index], run)
            return carry

        lax.fori_loop(0, unit_count, unit, 0)
        for ahead in range(together):
            head = step * together + ahead
            sums[head, 1:2, :] = jnp.sum(value_acc[ahead], axis=0, keepdims=True)
            part_ref[heads + head] = (key_acc[ahead] * factor).astype(bf16)
            part_ref[2 * heads + head] = value_acc[ahead].astype(bf16)
        return carry

    lax.fori_loop(0, heads // together, some_heads, 0)
    join_heads(part_ref, out_ref, 3 * heads)
    bias_ref[...] = jnp.concatenate([sums[head, :, 0:HEAD_DIM] for head in range(heads)], axis=1)


def attend_back(starts, counts, qkv, log_sums, grad_heads, heads):
    rows, columns = qkv.shape
    factor = HEAD_DIM ** (-0.5)
    together = 4
    return pl.pallas_call(
        functools.partial(attend_back_kernel, heads, together, factor),
        out_shape=(
            jax.ShapeDtypeStruct((rows, columns), bf16),
            jax.ShapeDtypeStruct((8, heads * HEAD_DIM), f32),
        ),
        in_specs=[whole_spec(pltpu.SMEM), whole_spec(pltpu.SMEM)] + [whole_spec()] * 3,
        out_specs=(whole_spec(), whole_spec()),
        scratch_shapes=[
            pltpu.VMEM((3 * heads, rows, LANES), bf16),
            pltpu.VMEM((heads, rows, LANES), bf16),
            pltpu.VMEM((together, rows, LANES), f32),
            pltpu.VMEM((together, rows, LANES), f32),
            pltpu.VMEM((heads, 8, LANES), f32),
        ],
        compiler_params=pltpu.CompilerParams(vmem_limit_bytes=48 << 20),
        cost_estimate=pl.CostEstimate(flops=40 * 10**9, bytes_accessed=25 * 10**6, transcendentals=10**7),
        name="attend_back",
    )(starts, counts, qkv, log_sums, grad_heads)


def reduce_kernel(
    grid_rows,
    first_jobs,
    second_jobs,
    one_left,
    one_right,
    two_left,
    two_right,
    three_left,
    three_right,
    four_left,
    four_right,
    bias_ref,
    slot_ref,
    silu_ref,
    slot_low_ref,
    ada_ref,
    first_out,
    second_out,
    bias_out,
    slot_out,
    silu_out,
    cond_out,
    stage,
    first_left,
    second_left,
    first_right,
    second_right,
    f0,
    f0_turn,
    f0_swap,
    f1,
    f1_got,
    f2,
    f2_got,
    s0,
    s0_got,
    s1,
    s1_got,
    s2,
    s2_turn,
    s2_swap,
    bias_got,
    slot_x,
    slot_y,
    slot_y_got,
    slot_z,
    slot_z_got,
    silu_x,
    silu_y,
    silu_y_got,
    silu_z,
    silu_z_got,
    ada_tile,
    cond_acc,
    load_sem,
    first_load,
    second_load,
    f0_sems,
    f1_sems,
    f2_sems,
    s0_sems,
    s1_sems,
    s2_sems,
    bias_sems,
    slot_sems,
    slot_z_sems,
    silu_sems,
    silu_z_sems,
    ada_sems,
    cond_sems,
    first_free,
    second_free,
):
    dp = lax.axis_index("dp")
    x = lax.axis_index("tensor")
    core = dp % 2
    y = (dp // 2) % 2
    z = dp // 4
    home = core == x
    away = core != x

    def device(z_at, y_at, core_at, x_at):
        return ((z_at * 2 + y_at) * 2 + core_at, x_at)

    turn_to = device(z, y, core + (1 - 2 * core) * (1 - jnp.abs(core - x)), x + (core - x))
    turn_from = device(z, y, x + 0 * core, x + (1 - 2 * x) * (1 - jnp.abs(core - x)))
    swap_peer = device(z, y, x, core)
    y_peer = device(z, 1 - y, core, x)

    def z_peer(ahead):
        return device(lax.rem(z + ahead, 4), y, core, x)

    barrier = pltpu.get_barrier_semaphore()
    near = [device(z, y, 1 - core, x), device(z, y, core, 1 - x), device(z, y, 1 - core, 1 - x), y_peer]
    for peer in near + [z_peer(1), z_peer(2), z_peer(3)]:
        pl.semaphore_signal(barrier, inc=1, device_id=peer, device_id_type=MESH)
    pl.semaphore_wait(barrier, 7)

    def remote(source, target, sems, index, peer):
        return pltpu.make_async_remote_copy(
            src_ref=source,
            dst_ref=target,
            send_sem=sems.at[(0,) + index],
            recv_sem=sems.at[(1,) + index],
            device_id=peer,
            device_id_type=MESH,
        )

    def added(*terms):
        total = terms[0].astype(f32)
        for term in terms[1:]:
            total = total + term.astype(f32)
        return total

    def load_left(source, through, target):
        height = source.shape[1]
        through = through if height == through.shape[1] else through.at[:, 0:height]
        copy = pltpu.make_async_copy(source, through, load_sem)
        copy.start()
        copy.wait()

        def block(index, carry):
            rows = pl.ds(pl.multiple_of(index * LANES, LANES), LANES)
            target[0:height, rows] = through[rows, :].T
            return carry

        lax.fori_loop(0, source.shape[0] // LANES, block, 0)

    def right_copy(source, tile, target, sems, slot):
        columns = pl.ds(pl.multiple_of(tile * TILE, TILE), TILE)
        return pltpu.make_async_copy(source.at[:, columns], target.at[slot], sems.at[slot])

    first_split = one_right.shape[1] // TILE
    second_split = three_right.shape[1] // TILE

    def first_right_do(job, slot, action):
        @pl.when(job < first_split)
        def _():
            action(right_copy(one_right, job, first_right, first_load, slot))

        @pl.when(job >= first_split)
        def _():
            action(right_copy(two_right, job - first_split, first_right, first_load, slot))

    def second_right_do(job, slot, action):
        @pl.when(job < second_split)
        def _():
            action(right_copy(three_right, job, second_right, second_load, slot))

        @pl.when(job >= second_split)
        def _():
            action(right_copy(four_right, job - second_split, second_right, second_load, slot))

    def begin(copy):
        copy.start()

    def finish(copy):
        copy.wait()

    def multiply(left, right, slot, keep):
        def block(at_z, carry):
            height = 4 * grid_rows
            span = pl.ds(pl.multiple_of(at_z * height, 32), height)
            product = jnp.dot(left[span, :], right[slot], preferred_element_type=f32)
            for at_y in range(2):
                for at_core in range(2):
                    low = (at_y * 2 + at_core) * grid_rows
                    part = product[low : low + grid_rows, :]
                    stacked = jnp.concatenate([part[:, :LANES], part[:, LANES:]], axis=0)
                    keep(at_z, at_y, at_core, stacked.astype(bf16))
            return carry

        lax.fori_loop(0, 4, block, 0)

    def f0_copies(slot):
        turn = remote(f0.at[slot, 1 - x], f0_turn.at[slot], f0_sems, (0, slot), turn_to)
        swap = remote(f0.at[slot, x], f0_swap.at[slot], f0_sems, (1, slot), swap_peer)
        return turn, swap

    def f1_copy(slot):
        return remote(f1.at[slot, 1 - y], f1_got.at[slot], f1_sems, (slot,), y_peer)

    def f2_copy(slot, ahead):
        return remote(
            f2.at[slot, lax.rem(z + ahead, 4)], f2_got.at[slot, ahead - 1], f2_sems, (slot, ahead - 1), z_peer(ahead)
        )

    def s0_copy(slot):
        return remote(s0.at[slot, 1 - y], s0_got.at[slot], s0_sems, (slot,), y_peer)

    def s1_copy(slot, ahead):
        return remote(
            s1.at[slot, lax.rem(z + ahead, 4)], s1_got.at[slot, ahead - 1], s1_sems, (slot, ahead - 1), z_peer(ahead)
        )

    def s2_copies(slot):
        turn = remote(s2.at[slot, 1 - x], s2_turn.at[slot], s2_sems, (0, slot), turn_to)
        swap = remote(s2.at[slot, x], s2_swap.at[slot], s2_sems, (1, slot), swap_peer)
        return turn, swap

    def inside(job, count):
        return jnp.logical_and(job >= 0, job < count)

    first_right_do(0, 0, begin)
    second_right_do(0, 0, begin)

    def first_tick(tick):
        @pl.when(tick < first_jobs)
        def _():
            slot = lax.rem(tick, 2)
            first_right_do(tick, slot, finish)

            @pl.when(tick + 1 < first_jobs)
            def _():
                first_right_do(tick + 1, 1 - slot, begin)

            @pl.when(tick == 0)
            def _():
                load_left(one_left, stage, first_left)

            @pl.when(tick == first_split)
            def _():
                load_left(two_left, stage, first_left)

            def keep(at_z, at_y, at_core, value):
                f0[lax.rem(tick, SLOTS), at_core, at_y, at_z] = value

            multiply(first_left, first_right, slot, keep)

        last = tick - 3 * GAP

        @pl.when(inside(last, first_jobs))
        def _():
            slot = lax.rem(last, SLOTS)
            for ahead in (1, 2, 3):
                f2_copy(slot, ahead).wait()
            first_out[last] = added(f2[slot, z], f2_got[slot, 0], f2_got[slot, 1], f2_got[slot, 2])

        third = tick - 2 * GAP

        @pl.when(inside(third, first_jobs))
        def _():
            slot = lax.rem(third, SLOTS)
            f1_copy(slot).wait()
            f2[slot] = added(f1[slot, y], f1_got[slot]).astype(bf16)
            for ahead in (1, 2, 3):
                f2_copy(slot, ahead).start()

        second = tick - GAP

        @pl.when(inside(second, first_jobs))
        def _():
            slot = lax.rem(second, SLOTS)
            turn, swap = f0_copies(slot)
            turn.wait()

            @pl.when(home)
            def _():
                f1[slot] = added(f0_turn[slot], f0[slot, x]).astype(bf16)

            @pl.when(away)
            def _():
                swap.wait()
                f1[slot] = added(f0_turn[slot], f0_swap[slot]).astype(bf16)

            @pl.when(second + SLOTS < first_jobs)
            def _():
                pl.semaphore_signal(first_free, inc=1, device_id=turn_from, device_id_type=MESH)

            f1_copy(slot).start()

        @pl.when(tick < first_jobs)
        def _():
            slot = lax.rem(tick, SLOTS)
            turn, swap = f0_copies(slot)

            @pl.when(tick >= SLOTS)
            def _():
                pl.semaphore_wait(first_free, 1)

            turn.start()

            @pl.when(away)
            def _():
                swap.start()

    def second_tick(tick):
        @pl.when(tick < second_jobs)
        def _():
            slot = lax.rem(tick, 2)
            second_right_do(tick, slot, finish)

            @pl.when(tick + 1 < second_jobs)
            def _():
                second_right_do(tick + 1, 1 - slot, begin)

            @pl.when(tick == 0)
            def _():
                load_left(three_left, stage, second_left)

            @pl.when(tick == second_split)
            def _():
                load_left(four_left, stage, second_left)

            def keep(at_z, at_y, at_core, value):
                s0[lax.rem(tick, SLOTS), at_y, at_z, at_core] = value

            multiply(second_left, second_right, slot, keep)

        last = tick - 3 * GAP

        @pl.when(inside(last, second_jobs))
        def _():
            slot = lax.rem(last, SLOTS)
            turn, swap = s2_copies(slot)
            turn.wait()

            @pl.when(home)
            def _():
                second_out[last] = added(s2_turn[slot], s2[slot, x])

            @pl.when(away)
            def _():
                swap.wait()
                second_out[last] = added(s2_turn[slot], s2_swap[slot])

            @pl.when(last + SLOTS < second_jobs)
            def _():
                pl.semaphore_signal(second_free, inc=1, device_id=turn_from, device_id_type=MESH)

        third = tick - 2 * GAP

        @pl.when(inside(third, second_jobs))
        def _():
            slot = lax.rem(third, SLOTS)
            for ahead in (1, 2, 3):
                s1_copy(slot, ahead).wait()
            s2[slot] = added(s1[slot, z], s1_got[slot, 0], s1_got[slot, 1], s1_got[slot, 2]).astype(bf16)
            turn, swap = s2_copies(slot)

            @pl.when(third >= SLOTS)
            def _():
                pl.semaphore_wait(second_free, 1)

            turn.start()

            @pl.when(away)
            def _():
                swap.start()

        second = tick - GAP

        @pl.when(inside(second, second_jobs))
        def _():
            slot = lax.rem(second, SLOTS)
            s0_copy(slot).wait()
            s1[slot] = added(s0[slot, y], s0_got[slot]).astype(bf16)
            for ahead in (1, 2, 3):
                s1_copy(slot, ahead).start()

        @pl.when(tick < second_jobs)
        def _():
            s0_copy(lax.rem(tick, SLOTS)).start()

    bias_peers = [
        device(z, y, 1 - core, x),
        device(z, y, core, 1 - x),
        y_peer,
        device(z + 1 - 2 * lax.rem(z, 2), y, core, x),
        device(lax.rem(z + 2, 4), y, core, x),
    ]

    def bias_copy(step):
        return remote(bias_out, bias_got.at[step], bias_sems, (step,), bias_peers[step])

    def slot_x_copy():
        return remote(slot_ref.at[1 - x], slot_x, slot_sems, (0,), device(z, y, core, 1 - x))

    def slot_y_copy():
        return remote(slot_y.at[1 - y], slot_y_got, slot_sems, (1,), y_peer)

    def slot_z_copy(ahead):
        return remote(
            slot_z.at[lax.rem(z + ahead, 4)], slot_z_got.at[ahead - 1], slot_z_sems, (ahead - 1,), z_peer(ahead)
        )

    def silu_x_copy():
        return remote(silu_ref, silu_x, silu_sems, (0,), device(z, y, core, 1 - x))

    def silu_y_copy():
        return remote(silu_y, silu_y_got, silu_sems, (1,), y_peer)

    def silu_z_copy(ahead):
        return remote(silu_z, silu_z_got.at[ahead - 1], silu_z_sems, (ahead - 1,), z_peer(ahead))

    def small_tick(tick):
        @pl.when(tick == 0)
        def _():
            bias_out[...] = bias_ref[...]
            slot_x_copy().start()
            silu_x_copy().start()

        for step in range(5):

            @pl.when(tick == step + 1)
            def _(step=step):
                bias_copy(step).wait()
                bias_out[...] = bias_out[...] + bias_got[step]

        for step in range(5):

            @pl.when(tick == step)
            def _(step=step):
                bias_copy(step).start()

        @pl.when(tick == 1)
        def _():
            slot_x_copy().wait()
            for at_y in range(2):
                slot_y[at_y, x] = slot_ref[x, at_y]
                slot_y[at_y, 1 - x] = slot_x[at_y]
            slot_y_copy().start()
            silu_x_copy().wait()
            silu_y[x] = silu_ref[...]
            silu_y[1 - x] = silu_x[...]
            silu_y_copy().start()

        @pl.when(tick == 2)
        def _():
            slot_y_copy().wait()
            for at_z in range(4):
                slot_z[at_z, y] = slot_y[y, :, at_z]
                slot_z[at_z, 1 - y] = slot_y_got[:, at_z]
            silu_y_copy().wait()
            silu_z[y] = silu_y[...]
            silu_z[1 - y] = silu_y_got[...]
            for ahead in (1, 2, 3):
                slot_z_copy(ahead).start()
                silu_z_copy(ahead).start()

        @pl.when(tick == 3)
        def _():
            slot_out[z] = slot_z[z]
            silu_out[z] = silu_z[...]
            for ahead in (1, 2, 3):
                slot_z_copy(ahead).wait()
                slot_out[lax.rem(z + 4 - ahead, 4)] = slot_z_got[ahead - 1]
                silu_z_copy(ahead).wait()
                silu_out[lax.rem(z + 4 - ahead, 4)] = silu_z_got[ahead - 1]

    ada_cols = ada_tile.shape[2]
    ada_tiles = ada_ref.shape[1] // ada_cols
    cond_copy = remote(cond_acc, cond_out, cond_sems, (), swap_peer)

    def ada_copy(tile, slot):
        columns = pl.ds(pl.multiple_of(tile * ada_cols, LANES), ada_cols)
        return pltpu.make_async_copy(ada_ref.at[:, columns], ada_tile.at[slot], ada_sems.at[slot])

    def cond_tick(tick):
        tile = tick - 4

        @pl.when(tile == -1)
        def _():
            cond_acc[...] = jnp.zeros_like(cond_acc)

        @pl.when(inside(tile + 1, ada_tiles))
        def _():
            ada_copy(tile + 1, lax.rem(tile + 1, 2)).start()

        @pl.when(inside(tile, ada_tiles))
        def _():
            slot = lax.rem(tile, 2)
            ada_copy(tile, slot).wait()
            columns = pl.ds(pl.multiple_of(tile * ada_cols, LANES), ada_cols)
            cond_acc[...] += dot_nt(slot_low_ref[:, columns], ada_tile[slot])

        @pl.when(tile == ada_tiles)
        def _():
            @pl.when(home)
            def _():
                cond_out[...] = cond_acc[...]

            @pl.when(away)
            def _():
                cond_copy.start()

        @pl.when(jnp.logical_and(tile == ada_tiles + 1, away))
        def _():
            cond_copy.wait()

    def tick_body(tick, carry):
        small_tick(tick)
        cond_tick(tick)
        first_tick(tick)

        @pl.when(lax.rem(tick, 3) != 2)
        def _():
            second_tick(tick // 3 * 2 + lax.rem(tick, 3))

        return carry

    ticks = max(first_jobs + 3 * GAP, ada_tiles + 6, -(-3 * (second_jobs + 3 * GAP) // 2))
    lax.fori_loop(0, ticks, tick_body, 0)


def reduce_grads(one, two, three, four, bias, slots, silu, slot_low, ada_weight):
    tokens, width = one[0].shape
    grid_rows = width // 16
    first_jobs = (one[1].shape[1] + two[1].shape[1]) // TILE
    second_jobs = (three[1].shape[1] + four[1].shape[1]) // TILE
    tile = (grid_rows * TILE // LANES, LANES)
    dma = pltpu.SemaphoreType.DMA
    slot_tail = slots.shape[-2:]

    def low(*lead):
        return pltpu.VMEM(lead + tile, bf16)

    scratch = [
        pltpu.VMEM((tokens, width), bf16),
        pltpu.VMEM((width, tokens), bf16),
        pltpu.VMEM((width, tokens), bf16),
        pltpu.VMEM((2, tokens, TILE), bf16),
        pltpu.VMEM((2, tokens, TILE), bf16),
        low(SLOTS, 2, 2, 4),
        low(SLOTS, 2, 4),
        low(SLOTS, 2, 4),
        low(SLOTS, 2, 4),
        low(SLOTS, 4),
        low(SLOTS, 4),
        low(SLOTS, 3),
        low(SLOTS, 2, 4, 2),
        low(SLOTS, 4, 2),
        low(SLOTS, 4, 2),
        low(SLOTS, 3, 2),
        low(SLOTS, 2),
        low(SLOTS),
        low(SLOTS),
        pltpu.VMEM((5,) + bias.shape, f32),
        pltpu.VMEM((2, 4) + slot_tail, f32),
        pltpu.VMEM((2, 2, 4) + slot_tail, f32),
        pltpu.VMEM((2, 4) + slot_tail, f32),
        pltpu.VMEM((4, 2, 2) + slot_tail, f32),
        pltpu.VMEM((3, 2, 2) + slot_tail, f32),
        pltpu.VMEM(silu.shape, bf16),
        pltpu.VMEM((2,) + silu.shape, bf16),
        pltpu.VMEM((2,) + silu.shape, bf16),
        pltpu.VMEM((2, 2) + silu.shape, bf16),
        pltpu.VMEM((3, 2, 2) + silu.shape, bf16),
        pltpu.VMEM((2, ada_weight.shape[0], ada_weight.shape[1] // 9), bf16),
        pltpu.VMEM((8, ada_weight.shape[0]), f32),
        dma,
        dma((2,)),
        dma((2,)),
        dma((2, 2, SLOTS)),
        dma((2, SLOTS)),
        dma((2, SLOTS, 3)),
        dma((2, SLOTS)),
        dma((2, SLOTS, 3)),
        dma((2, 2, SLOTS)),
        dma((2, 5)),
        dma((2, 2)),
        dma((2, 3)),
        dma((2, 2)),
        dma((2, 3)),
        dma((2,)),
        dma((2,)),
        pltpu.SemaphoreType.REGULAR,
        pltpu.SemaphoreType.REGULAR,
    ]
    return pl.pallas_call(
        functools.partial(reduce_kernel, grid_rows, first_jobs, second_jobs),
        out_shape=(
            jax.ShapeDtypeStruct((first_jobs,) + tile, f32),
            jax.ShapeDtypeStruct((second_jobs,) + tile, f32),
            jax.ShapeDtypeStruct(bias.shape, f32),
            jax.ShapeDtypeStruct((4, 2, 2) + slot_tail, f32),
            jax.ShapeDtypeStruct((4, 2, 2) + silu.shape, bf16),
            jax.ShapeDtypeStruct((8, ada_weight.shape[0]), f32),
        ),
        in_specs=[whole_spec(pl.ANY)] * 8 + [whole_spec()] * 4 + [whole_spec(pl.ANY)],
        out_specs=(whole_spec(),) * 6,
        scratch_shapes=scratch,
        compiler_params=pltpu.CompilerParams(
            collective_id=1, has_side_effects=True, vmem_limit_bytes=52 << 20
        ),
        cost_estimate=pl.CostEstimate(flops=10**11, bytes_accessed=10**8, transcendentals=0),
        name="reduce_grads",
    )(*one, *two, *three, *four, bias, slots, silu, slot_low, ada_weight)


def mlp_back_kernel(
    proj_jobs,
    own_ref,
    pre_ref,
    down_ref,
    up_ref,
    mid_left,
    mid_right,
    in_left,
    in_right,
    last_left,
    last_right,
    all_out,
    low_out,
    in_out,
    bias_out,
    proj_out,
    pre_tile,
    low_tile,
    part_send,
    part_got,
    proj_stage,
    proj_left,
    proj_right,
    p0,
    p0_got,
    p1,
    p1_got,
    p2,
    p2_got,
    p3,
    p3_got,
    pre_sems,
    low_sems,
    own_sems,
    part_sems,
    load_sem,
    proj_load,
    p0_sems,
    p1_sems,
    p2_sems,
    p3_sems,
):
    dp = lax.axis_index("dp")
    x = lax.axis_index("tensor")
    core = dp % 2
    y = (dp // 2) % 2
    z = dp // 4

    def device(z_at, y_at, core_at, x_at):
        return ((z_at * 2 + y_at) * 2 + core_at, x_at)

    y_peer = device(z, 1 - y, core, x)

    def z_peer(ahead):
        return device(lax.rem(z + ahead, 4), y, core, x)

    barrier = pltpu.get_barrier_semaphore()
    near = [device(z, y, 1 - core, x), device(z, y, core, 1 - x), device(z, y, 1 - core, 1 - x), y_peer]
    for peer in near + [z_peer(1), z_peer(2), z_peer(3)]:
        pl.semaphore_signal(barrier, inc=1, device_id=peer, device_id_type=MESH)
    pl.semaphore_wait(barrier, 7)

    def remote(source, target, sems, index, peer):
        return pltpu.make_async_remote_copy(
            src_ref=source,
            dst_ref=target,
            send_sem=sems.at[(0,) + index],
            recv_sem=sems.at[(1,) + index],
            device_id=peer,
            device_id_type=MESH,
        )

    def added(*terms):
        total = terms[0].astype(f32)
        for term in terms[1:]:
            total = total + term.astype(f32)
        return total

    def load_left(source, through, target):
        height = source.shape[1]
        through = through if height == through.shape[1] else through.at[:, 0:height]
        copy = pltpu.make_async_copy(source, through, load_sem)
        copy.start()
        copy.wait()

        def block(index, carry):
            rows = pl.ds(pl.multiple_of(index * LANES, LANES), LANES)
            target[0:height, rows] = through[rows, :].T
            return carry

        lax.fori_loop(0, source.shape[0] // LANES, block, 0)

    def begin(copy):
        copy.start()

    def finish(copy):
        copy.wait()

    def inside(job, count):
        return jnp.logical_and(job >= 0, job < count)

    core_peer = device(z, y, 1 - core, x)
    own_rows = own_ref.shape[0]
    tile_rows = pre_tile.shape[1]
    hidden = pre_ref.shape[1]
    half_tiles = own_rows // tile_rows

    def own_span(side):
        return pl.ds(pl.multiple_of(side * own_rows, 256), own_rows)

    own_copy = remote(own_ref, all_out.at[own_span(core), :], own_sems, (), core_peer)
    own_copy.start()
    all_out[own_span(core), :] = own_ref[...]
    bias_out[...] = jnp.zeros_like(bias_out)

    def tile_span(tile):
        side = jnp.where(tile < half_tiles, 1 - core, core)
        begin_row = side * own_rows + lax.rem(tile, half_tiles) * tile_rows
        return pl.ds(pl.multiple_of(begin_row, 256), tile_rows)

    def part_span(tile):
        return pl.ds(pl.multiple_of(lax.rem(tile, half_tiles) * tile_rows, 256), tile_rows)

    def pre_copy(tile, slot):
        return pltpu.make_async_copy(pre_ref.at[tile_span(tile), :], pre_tile.at[slot], pre_sems.at[slot])

    def low_copy(tile, slot):
        return pltpu.make_async_copy(low_tile.at[slot], low_out.at[tile_span(tile), :], low_sems.at[slot])

    def part_copy(tile):
        rows = part_span(tile)
        return remote(part_send.at[rows, :], part_got.at[rows, :], part_sems, (tile,), core_peer)

    pre_copy(0, 0).start()
    chunk = 768

    def mlp_tile(tile):
        slot = lax.rem(tile, 2)
        pre_copy(tile, slot).wait()

        @pl.when(tile + 1 < 2 * half_tiles)
        def _():
            pre_copy(tile + 1, 1 - slot).start()

        @pl.when(tile == 0)
        def _():
            own_copy.wait()

        @pl.when(tile >= 2)
        def _():
            low_copy(tile - 2, slot).wait()

        grads = all_out[tile_span(tile), :]
        for at in range(0, hidden, chunk):
            span = slice(at, at + chunk)
            value = pre_tile[slot, :, span]
            square = value * value
            curve = jnp.tanh(GELU_SCALE * (value + GELU_CUBE * (square * value)))
            slope = 0.5 * (1.0 + curve) + (0.5 * GELU_SCALE) * value * (1.0 - curve * curve) * (
                1.0 + (3.0 * GELU_CUBE) * square
            )
            grad = slope * dot_nt(grads, down_ref[span, :])
            bias_out[0:1, span] += jnp.sum(grad, axis=0, keepdims=True)
            low_tile[slot, :, span] = grad.astype(bf16)
        low_copy(tile, slot).start()
        part = dot_nt(low_tile[slot], up_ref[...])

        @pl.when(tile < half_tiles)
        def _():
            part_send[part_span(tile), :] = part.astype(bf16)
            part_copy(tile).start()

        @pl.when(tile >= half_tiles)
        def _():
            in_out[part_span(tile), :] = part

    mid_jobs = mid_right.shape[1] // TILE
    in_jobs = -(-in_right.shape[1] // TILE)
    in_left_over = in_right.shape[1] % TILE
    proj_rows = mid_left.shape[1] // 32
    last_rows = last_left.shape[1] // 32

    def proj_right_do(job, slot, action):
        def copy(source, tile, columns):
            start = pl.multiple_of(tile * columns, LANES)
            return pltpu.make_async_copy(
                source.at[:, pl.ds(start, columns)], proj_right.at[slot, :, pl.ds(0, columns)], proj_load.at[slot]
            )

        @pl.when(job < mid_jobs)
        def _():
            action(copy(mid_right, job, TILE))

        full = in_jobs - (1 if in_left_over else 0)

        @pl.when(inside(job - mid_jobs, full))
        def _():
            action(copy(in_right, job - mid_jobs, TILE))

        if in_left_over:

            @pl.when(job == mid_jobs + full)
            def _():
                rest = pltpu.make_async_copy(
                    in_right.at[:, pl.ds(full * TILE, in_left_over)],
                    proj_right.at[slot, :, pl.ds(0, in_left_over)],
                    proj_load.at[slot],
                )
                action(rest)

        @pl.when(job >= mid_jobs + in_jobs)
        def _():
            action(copy(last_right, job - mid_jobs - in_jobs, 2 * TILE))

    def p0_copy(slot):
        return remote(p0.at[slot, 1 - core], p0_got.at[slot], p0_sems, (slot,), device(z, y, 1 - core, x))

    def route(job):
        odd = lax.rem(job, 2)
        first = x + odd * (y - x)
        second = y + odd * (x - y)
        over_x = device(z, y, core, 1 - x)
        over_y = device(z, 1 - y, core, x)
        toward = tuple(a + odd * (b - a) for a, b in zip(over_x, over_y))
        onward = tuple(b + odd * (a - b) for a, b in zip(over_x, over_y))
        return odd, first, second, toward, onward

    def p1_copy(job):
        odd, first, second, toward, onward = route(job)
        slot = lax.rem(job, SLOTS)
        return remote(p1.at[slot, 1 - first], p1_got.at[slot], p1_sems, (slot,), toward)

    def p2_copy(job):
        odd, first, second, toward, onward = route(job)
        slot = lax.rem(job, SLOTS)
        return remote(p2.at[slot, 1 - second], p2_got.at[slot], p2_sems, (slot,), onward)

    def p3_copy(slot, ahead):
        return remote(
            p3.at[slot, lax.rem(z + ahead, 4)], p3_got.at[slot, ahead - 1], p3_sems, (slot, ahead - 1), z_peer(ahead)
        )

    pltpu.make_async_copy(mid_right.at[:, pl.ds(0, TILE)], proj_right.at[0, :, pl.ds(0, TILE)], proj_load.at[0]).start()

    def proj_tick(tick):
        @pl.when(tick < proj_jobs)
        def _():
            slot = lax.rem(tick, 2)
            odd = slot
            proj_right_do(tick, slot, finish)

            @pl.when(tick + 1 < proj_jobs)
            def _():
                proj_right_do(tick + 1, 1 - slot, begin)

            for at, source in ((0, mid_left), (mid_jobs, in_left), (mid_jobs + in_jobs, last_left)):

                @pl.when(tick == at)
                def _(source=source):
                    load_left(source, proj_stage, proj_left)

            shares = [(at_y, at_core, at_x) for at_y in range(2) for at_core in range(2) for at_x in range(2)]

            @pl.when(tick < mid_jobs + in_jobs)
            def _():
                def block(at_z, carry):
                    span = pl.ds(pl.multiple_of(at_z * 8 * proj_rows, 32), 8 * proj_rows)
                    right = proj_right[slot, :, 0:TILE]
                    product = jnp.dot(proj_left[span, :], right, preferred_element_type=f32).astype(bf16)
                    for low, (at_y, at_core, at_x) in enumerate(shares):
                        p0[lax.rem(tick, SLOTS), at_core, at_x + odd * (at_y - at_x), at_y + odd * (at_x - at_y), at_z] = product[low * proj_rows : (low + 1) * proj_rows, :]
                    return carry

                lax.fori_loop(0, 4, block, 0)

            @pl.when(tick >= mid_jobs + in_jobs)
            def _():
                def block(at_z, carry):
                    span = pl.ds(pl.multiple_of(at_z * 8 * last_rows, 32), 8 * last_rows)
                    for half in range(2):
                        right = proj_right[slot, :, half * TILE : (half + 1) * TILE]
                        product = jnp.dot(proj_left[span, :], right, preferred_element_type=f32)
                        begin_row = half * proj_rows // 2
                        for low, (at_y, at_core, at_x) in enumerate(shares):
                            p0[lax.rem(tick, SLOTS), at_core, at_x + odd * (at_y - at_x), at_y + odd * (at_x - at_y), at_z, begin_row : begin_row + last_rows, :] = product[
                                low * last_rows : (low + 1) * last_rows, :
                            ].astype(bf16)
                    return carry

                lax.fori_loop(0, 4, block, 0)

        fifth = tick - 4 * GAP

        @pl.when(inside(fifth, proj_jobs))
        def _():
            slot = lax.rem(fifth, SLOTS)
            for ahead in (1, 2, 3):
                p3_copy(slot, ahead).wait()
            proj_out[fifth] = added(p3[slot, z], p3_got[slot, 0], p3_got[slot, 1], p3_got[slot, 2])

        fourth = tick - 3 * GAP

        @pl.when(inside(fourth, proj_jobs))
        def _():
            slot = lax.rem(fourth, SLOTS)
            odd, first, second, toward, onward = route(fourth)
            p2_copy(fourth).wait()
            p3[slot] = added(p2[slot, second], p2_got[slot]).astype(bf16)
            for ahead in (1, 2, 3):
                p3_copy(slot, ahead).start()

        third = tick - 2 * GAP

        @pl.when(inside(third, proj_jobs))
        def _():
            slot = lax.rem(third, SLOTS)
            odd, first, second, toward, onward = route(third)
            p1_copy(third).wait()
            p2[slot] = added(p1[slot, first], p1_got[slot]).astype(bf16)
            p2_copy(third).start()

        second_job = tick - GAP

        @pl.when(inside(second_job, proj_jobs))
        def _():
            slot = lax.rem(second_job, SLOTS)
            p0_copy(slot).wait()
            p1[slot] = added(p0[slot, core], p0_got[slot]).astype(bf16)
            p1_copy(second_job).start()

        @pl.when(tick < proj_jobs)
        def _():
            p0_copy(lax.rem(tick, SLOTS)).start()

    def tick_body(tick, carry):
        proj_tick(tick)

        @pl.when(jnp.logical_and(lax.rem(tick, 4) == 3, tick // 4 < 2 * half_tiles))
        def _():
            mlp_tile(tick // 4)

        return carry

    lax.fori_loop(0, max(proj_jobs + 4 * GAP, 8 * half_tiles), tick_body, 0)
    for tile in range(2 * half_tiles - 2, 2 * half_tiles):
        low_copy(tile, tile % 2).wait()
    for tile in range(half_tiles):
        part_copy(tile).wait()
    in_out[...] = in_out[...] + part_got[...].astype(f32)


def mlp_back(own, pre_act, down_weight, up_weight, mid, first, last):
    rows, width = own.shape
    hidden = pre_act.shape[1]
    proj_jobs = mid[1].shape[1] // TILE + -(-first[1].shape[1] // TILE) + last[1].shape[1] // (2 * TILE)
    proj_tokens, proj_hidden = mid[0].shape
    tile = (proj_hidden // 32, TILE)
    dma = pltpu.SemaphoreType.DMA

    def low(*lead):
        return pltpu.VMEM(lead + tile, bf16)

    return pl.pallas_call(
        functools.partial(mlp_back_kernel, proj_jobs),
        out_shape=(
            jax.ShapeDtypeStruct((2 * rows, width), bf16),
            jax.ShapeDtypeStruct((2 * rows, hidden), bf16),
            jax.ShapeDtypeStruct((rows, width), f32),
            jax.ShapeDtypeStruct((8, hidden), f32),
            jax.ShapeDtypeStruct((proj_jobs,) + tile, f32),
        ),
        in_specs=[whole_spec(), whole_spec(pl.ANY), whole_spec(), whole_spec()] + [whole_spec(pl.ANY)] * 6,
        out_specs=(whole_spec(), whole_spec(pl.ANY), whole_spec(), whole_spec(), whole_spec()),
        scratch_shapes=[
            pltpu.VMEM((2, SHORT, hidden), f32),
            pltpu.VMEM((2, SHORT, hidden), bf16),
            pltpu.VMEM((rows, width), bf16),
            pltpu.VMEM((rows, width), bf16),
            pltpu.VMEM((proj_tokens, proj_hidden), bf16),
            pltpu.VMEM((proj_hidden, proj_tokens), bf16),
            pltpu.VMEM((2, proj_tokens, 2 * TILE), bf16),
            low(SLOTS, 2, 2, 2, 4),
            low(SLOTS, 2, 2, 4),
            low(SLOTS, 2, 2, 4),
            low(SLOTS, 2, 4),
            low(SLOTS, 2, 4),
            low(SLOTS, 4),
            low(SLOTS, 4),
            low(SLOTS, 3),
            dma((2,)),
            dma((2,)),
            dma((2,)),
            dma((2, rows // SHORT)),
            dma,
            dma((2,)),
            dma((2, SLOTS)),
            dma((2, SLOTS)),
            dma((2, SLOTS)),
            dma((2, SLOTS, 3)),
        ],
        compiler_params=pltpu.CompilerParams(
            collective_id=3, has_side_effects=True, vmem_limit_bytes=58 << 20
        ),
        cost_estimate=pl.CostEstimate(flops=3 * 10**10, bytes_accessed=5 * 10**7, transcendentals=0),
        name="mlp_back",
    )(own, pre_act, down_weight, up_weight, *mid, *first, *last)


def fetch_kernel(
    tokens_ref,
    qkv_ref,
    out_ref,
    cond_ref,
    bias_ref,
    ids_ref,
    ada_ref,
    ada_bias_ref,
    tokens_out,
    qkv_out,
    out_out,
    cond_out,
    bias_out,
    ids_out,
    mod_out,
    ada_tile,
    token_hold,
    qkv_hold,
    out_hold,
    token_sems,
    cond_sems,
    x_sems,
    y_sems,
    z_sems,
    local_sems,
    ada_sems,
):
    dp = lax.axis_index("dp")
    x = lax.axis_index("tensor")
    core = dp % 2
    y = (dp // 2) % 2
    z = dp // 4
    z_near = lax.rem(z, 2)
    home = core == x
    away = core != x
    pieces = x_sems.shape[1]
    quarter = qkv_ref.shape[0] // 4
    height = quarter // (pieces - 1)
    out_quarter = out_ref.shape[0] // 4

    def device(z_at, y_at, core_at, x_at):
        return ((z_at * 2 + y_at) * 2 + core_at, x_at)

    core_peer = device(z, y, 1 - core, x)
    swap_peer = device(z, y, x, core)
    y_peer = device(z, 1 - y, core, x)
    z_peer = device(z + 1 - 2 * z_near, y, core, x)
    barrier = pltpu.get_barrier_semaphore()
    peers = [core_peer, device(z, y, core, 1 - x), device(z, y, 1 - core, 1 - x), y_peer, z_peer]
    for peer in peers:
        pl.semaphore_signal(barrier, inc=1, device_id=peer, device_id_type=MESH)
    pl.semaphore_wait(barrier, len(peers))

    def remote(source, target, sems, index, peer):
        return pltpu.make_async_remote_copy(
            src_ref=source,
            dst_ref=target,
            send_sem=sems.at[(0,) + index],
            recv_sem=sems.at[(1,) + index],
            device_id=peer,
            device_id_type=MESH,
        )

    def part(whole, other, y_at, piece):
        at = y_at * 2 + z_near
        if piece == pieces - 1:
            return other.at[pl.ds(pl.multiple_of(at * out_quarter, 16), out_quarter), :]
        return whole.at[pl.ds(pl.multiple_of(at * quarter + piece * height, 32), height), :]

    def x_copy(piece):
        source = part(qkv_ref, out_ref, y, piece)
        return remote(source, part(qkv_out, out_out, y, piece), x_sems, (piece,), swap_peer)

    def y_copy(piece):
        here = part(qkv_out, out_out, y, piece)
        return remote(here, here, y_sems, (piece,), y_peer)

    def z_copy(piece, other):
        here = part(qkv_out, out_out, 1 - y if other else y, piece)
        return remote(here, here, z_sems, (int(other), piece), z_peer)

    token_copy = remote(tokens_ref, tokens_out, token_sems, (), swap_peer)
    cond_copy = remote(cond_ref, cond_out, cond_sems, (0,), core_peer)
    ids_copy = remote(ids_ref, ids_out, cond_sems, (1,), core_peer)
    bias_copy = remote(bias_ref, bias_out, cond_sems, (2,), swap_peer)
    local_in = [
        pltpu.make_async_copy(tokens_ref, token_hold, local_sems.at[0]),
        pltpu.make_async_copy(qkv_ref, qkv_hold, local_sems.at[1]),
        pltpu.make_async_copy(out_ref, out_hold, local_sems.at[2]),
    ]
    local_out = [
        pltpu.make_async_copy(token_hold, tokens_out, local_sems.at[3]),
        pltpu.make_async_copy(qkv_hold, qkv_out, local_sems.at[4]),
        pltpu.make_async_copy(out_hold, out_out, local_sems.at[5]),
    ]

    @pl.when(away)
    def _():
        for piece in range(pieces):
            x_copy(piece).start()
        bias_copy.start()

    @pl.when(home)
    def _():
        cond_copy.start()
        ids_copy.start()
        for copy in local_in:
            copy.start()
        cond_out[...] = cond_ref[...]
        ids_out[...] = ids_ref[...]
        bias_out[...] = bias_ref[...]

    tile_cols = ada_tile.shape[2]
    tiles = ada_ref.shape[1] // tile_cols

    def ada_copy(tile, slot):
        columns = pl.ds(tile * tile_cols, tile_cols)
        return pltpu.make_async_copy(ada_ref.at[:, columns], ada_tile.at[slot], ada_sems.at[slot])

    ada_copy(0, 0).start()

    @pl.when(away)
    def _():
        cond_copy.wait_recv()

    cond = cond_out[...].astype(f32)
    low = (cond / (1.0 + jnp.exp(-cond))).astype(bf16)

    def modulate(tile):
        slot = tile % 2
        ada_copy(tile, slot).wait()

        if tile + 1 < tiles:
            ada_copy(tile + 1, 1 - slot).start()

        columns = slice(tile * tile_cols, (tile + 1) * tile_cols)
        product = jnp.dot(low, ada_tile[slot], preferred_element_type=f32)
        mod_out[:, columns] = product + ada_bias_ref[:, columns].astype(f32)

    for tile in range(tiles):
        modulate(tile)
        if tile % 2 == 1 and tile // 2 < pieces:

            @pl.when(away)
            def _(piece=tile // 2):
                x_copy(piece).wait_recv()
                y_copy(piece).start()
                z_copy(piece, False).start()
                if piece == 0:
                    token_copy.start()

    @pl.when(away)
    def _():
        for piece in range(pieces):
            y_copy(piece).wait_recv()
            z_copy(piece, True).start()
        token_copy.wait()
        ids_copy.wait_recv()
        bias_copy.wait()
        for piece in range(pieces):
            x_copy(piece).wait_send()
            y_copy(piece).wait_send()
            z_copy(piece, False).wait()
            z_copy(piece, True).wait()

    @pl.when(home)
    def _():
        cond_copy.wait_send()
        ids_copy.wait_send()
        for copy, onward in zip(local_in, local_out):
            copy.wait()
            onward.start()
        for copy in local_out:
            copy.wait()


def fetch(tokens, qkv, out, condition, bias, ids, ada_weight, ada_bias):
    pieces = 4
    dma = pltpu.SemaphoreType.DMA
    return pl.pallas_call(
        fetch_kernel,
        out_shape=(
            jax.ShapeDtypeStruct(tokens.shape, bf16),
            jax.ShapeDtypeStruct(qkv.shape, bf16),
            jax.ShapeDtypeStruct(out.shape, bf16),
            jax.ShapeDtypeStruct(condition.shape, bf16),
            jax.ShapeDtypeStruct(bias.shape, bf16),
            jax.ShapeDtypeStruct(ids.shape, jnp.int32),
            jax.ShapeDtypeStruct((condition.shape[0], ada_weight.shape[1]), f32),
        ),
        in_specs=[whole_spec(pl.ANY)] * 3 + [whole_spec()] * 3 + [whole_spec(pl.ANY), whole_spec()],
        out_specs=(whole_spec(pl.ANY),) * 3 + (whole_spec(),) * 4,
        scratch_shapes=[
            pltpu.VMEM((2, ada_weight.shape[0], ada_weight.shape[1] // 9), bf16),
            pltpu.VMEM(tokens.shape, bf16),
            pltpu.VMEM(qkv.shape, bf16),
            pltpu.VMEM(out.shape, bf16),
            dma((2,)),
            dma((2, 3)),
            dma((2, pieces)),
            dma((2, pieces)),
            dma((2, 2, pieces)),
            dma((6,)),
            dma((2,)),
        ],
        compiler_params=pltpu.CompilerParams(
            collective_id=2, has_side_effects=True, vmem_limit_bytes=56 << 20
        ),
        cost_estimate=pl.CostEstimate(flops=10**10, bytes_accessed=3 * 10**7, transcendentals=0),
        name="fetch",
    )(tokens, qkv, out, condition, bias, ids, ada_weight, ada_bias.reshape(1, -1))


def after(value, earlier):
    return lax.optimization_barrier((value, earlier))[0]


def paired_shards(
    tokens_in,
    condition,
    ada_weight,
    ada_bias,
    qkv_weight,
    qv_bias,
    out_weight,
    out_bias,
    up_weight,
    up_bias,
    down_weight,
    down_bias,
    proj_in,
    proj_in_bias,
    proj_mid,
    proj_mid_bias,
    proj_last,
    proj_last_bias,
    enc_features,
    image_ids,
    target_rows,
    out_grad,
):
    dp = lax.axis_index("dp")
    x = lax.axis_index("tensor")
    core = dp % 2
    y = (dp // 2) % 2
    z = dp // 4
    z_near = z % 2
    z_far = z // 2
    place = dp * 2 + x
    home = core == x
    group = (dp // 2) * 2 + x
    local_rows, width = tokens_in.shape
    shard_rows = image_ids.shape[0]
    slots = condition.shape[0]
    units = local_rows // SHORT
    local_cols = qkv_weight.shape[2]
    local_hidden = up_weight.shape[1]
    heads = local_cols // HEAD_DIM
    qkv_cols = -(-3 * local_cols // TILE) * TILE
    out_cols = -(-local_cols // TILE) * TILE

    def swap(value):
        return jnp.where(home, value, send(value, to_diag))

    bias_pack = jnp.concatenate([qv_bias.reshape(-1), up_bias]).reshape(-1, LANES)
    tokens, qkv_half, out_half, cond_low, bias_half, ids, modulation = fetch(
        tokens_in,
        qkv_weight.reshape(width, 3 * local_cols),
        out_weight,
        condition,
        bias_pack,
        image_ids.reshape(-1, LANES),
        ada_weight,
        ada_bias,
    )
    bias_half = bias_half.reshape(-1).astype(f32)
    unit_ids = ids[:: SHORT // LANES, 0]

    def over_x(weight, earlier):
        own = lax.dynamic_slice_in_dim(weight, y * (weight.shape[0] // 2), weight.shape[0] // 2)
        return send(after(own, earlier), to_diag)

    def over_y(weight, first):
        second = send(first, to_swapped_y)
        first, second, whole = lax.optimization_barrier((first, second, weight))
        halves = whole.reshape((2,) + first.shape)
        mine = jnp.arange(2).reshape(2, 1, 1) == y
        return jnp.where(home, halves, jnp.where(mine, first[None], second[None])).reshape(weight.shape)

    up_first = over_x(up_weight, tokens)
    features = jnp.where(home, enc_features, send(enc_features, to_core))
    qv_half = bias_half[: 2 * local_cols].reshape(2, local_cols)
    up_bias_half = bias_half[2 * local_cols :]

    same = unit_ids[:, None] == unit_ids[None, :]
    starts = jnp.argmax(same, axis=1).astype(jnp.int32)
    counts = jnp.sum(same.astype(jnp.int32), axis=1).astype(jnp.int32)
    my_units = lax.dynamic_slice_in_dim(unit_ids, core * units, units)
    one_hot = (my_units[:, None] == jnp.arange(slots, dtype=jnp.int32)[None, :]).astype(f32)

    silu_low = jax.nn.silu(cond_low.astype(f32)).astype(bf16)
    per_unit = jnp.dot(one_hot, modulation, precision=highest, preferred_element_type=f32)
    shift_one, scale_one, gate_one, shift_two, scale_two, gate_two = [
        piece[:, None, :] for piece in jnp.split(per_unit, 6, axis=1)
    ]

    def by_unit(array):
        return array.reshape(units, SHORT, -1)

    def flat(array):
        return array.reshape(local_rows, -1)

    def reduce_cores(left, matrix, product):
        mine = lax.dynamic_slice_in_dim(left, core * local_rows, local_rows)
        theirs = lax.dynamic_slice_in_dim(left, (1 - core) * local_rows, local_rows)
        got = send(product(theirs, matrix).astype(bf16), to_core)
        return product(mine, matrix).astype(bf16).astype(f32) + got.astype(f32)

    def dot_nn(left, right):
        return jnp.dot(left, right, preferred_element_type=f32)

    resid = by_unit(tokens.astype(f32))
    normed_one, inv_one = layer_norm(resid)
    attn_in = flat((normed_one * (1.0 + scale_one) + shift_one).astype(bf16))
    attn_all = gather_cores(attn_in)

    qkv_pad = jnp.pad(qkv_half, ((0, 0), (0, qkv_cols - 3 * local_cols)))
    out_pad = jnp.pad(out_half, ((0, out_cols - local_cols), (0, 0)))
    qkv_bias = jnp.concatenate(
        [qv_half[0], jnp.zeros_like(qv_half[0]), qv_half[1], jnp.zeros((qkv_cols - 3 * local_cols,), f32)]
    )
    qkv = (dot_nn(attn_all, qkv_pad) + qkv_bias).astype(bf16)
    qkv, up_first = lax.optimization_barrier((qkv, up_first))
    up_half = over_y(up_weight, up_first)
    down_first = over_x(down_weight, up_first)
    attended, log_sums = attend(starts, counts, qkv, heads, out_cols)
    attended, down_first = lax.optimization_barrier((attended, down_first))
    down_half = over_y(down_weight, down_first)
    rows_low = swap(after(target_rows, down_first))
    grad_out = swap(after(out_grad, down_first))
    attn_branch = by_unit(reduce_cores(attended, out_pad, dot_nn) + out_bias.astype(f32))
    mid = resid + gate_one * attn_branch

    normed_two, inv_two = layer_norm(mid)
    mlp_in = flat((normed_two * (1.0 + scale_two) + shift_two).astype(bf16))
    mlp_all = gather_cores(mlp_in)
    pre_act = dot_nn(mlp_all, up_half) + up_bias_half
    hidden = gelu_tanh(pre_act).astype(bf16)
    mlp_branch = by_unit(reduce_cores(hidden, down_half, dot_nn) + down_bias.astype(f32))
    block_value = mid + gate_two * mlp_branch
    block_low = flat(block_value.astype(bf16))

    first_pre = dot_nn(block_low, proj_in) + proj_in_bias.astype(f32)
    first_value, first_back = jax.vjp(jax.nn.silu, first_pre)
    first_low = first_value.astype(bf16)
    second_pre = dot_nn(first_low, proj_mid) + proj_mid_bias.astype(f32)
    second_value, second_back = jax.vjp(jax.nn.silu, second_pre)
    second_low = second_value.astype(bf16)
    projected = dot_nn(second_low, proj_last) + proj_last_bias.astype(f32)
    target_vals = jnp.take(features, rows_low - group * shard_rows, axis=0).astype(f32)
    loss_back = jax.vjp(lambda predicted: align_loss(predicted, target_vals), projected)[1]
    grad_projected = loss_back(jnp.ones((), f32))[0]
    grad_last_low = grad_projected.astype(bf16)
    grad_second = second_back(dot_nt(grad_last_low, proj_last))[0]
    grad_second_low = grad_second.astype(bf16)
    grad_first = first_back(dot_nt(grad_second_low, proj_mid))[0]
    grad_first_low = grad_first.astype(bf16)
    grad_block = by_unit(grad_out.astype(f32) + dot_nt(grad_first_low, proj_in))

    grad_mlp_branch = gate_two * grad_block
    grad_mlp_all, grad_pre_low, grad_mlp_in, up_bias_sums, proj_sum = mlp_back(
        flat(grad_mlp_branch.astype(bf16)),
        pre_act,
        down_half,
        up_half,
        (grad_second_low, first_low),
        (grad_first_low, block_low),
        (grad_last_low, second_low),
    )
    grad_mlp_in = by_unit(grad_mlp_in)
    grad_mid = grad_block + norm_back(normed_two, inv_two, grad_mlp_in * (1.0 + scale_two))

    grad_attn_branch = gate_one * grad_mid
    grad_attn_all = gather_cores(flat(grad_attn_branch.astype(bf16)))
    grad_heads = dot_nt(grad_attn_all, out_pad).astype(bf16)
    grad_qkv, qkv_bias_sums = attend_back(starts, counts, qkv, log_sums, grad_heads, heads)
    grad_attn_in = by_unit(reduce_cores(grad_qkv, qkv_pad, dot_nt))
    grad_tokens = grad_mid + norm_back(normed_one, inv_one, grad_attn_in * (1.0 + scale_one))

    def unit_sum(array):
        return jnp.sum(array, axis=1)

    mod_units = jnp.concatenate(
        [
            unit_sum(grad_attn_in),
            unit_sum(grad_attn_in * normed_one),
            unit_sum(attn_branch * grad_mid),
            unit_sum(grad_mlp_in),
            unit_sum(grad_mlp_in * normed_two),
            unit_sum(mlp_branch * grad_block),
        ],
        axis=1,
    )
    slot_part = dot_tn(one_hot, mod_units, precision=highest)
    slot_grad = slot_part + send(slot_part, to_core)
    slot_low = slot_grad.astype(bf16)
    mod_cols = slot_low.shape[1] // 32
    slot_cols = pick(slot_grad.reshape(slots, 4, 2, 2, 2, mod_cols), core, 3).transpose(3, 2, 1, 0, 4)
    slot_cols = jnp.pad(slot_cols, ((0, 0),) * 3 + ((0, 8 - slots), (0, -mod_cols % LANES)))

    qv_sums = qkv_bias_sums[:2]
    qv_full = lax.dynamic_update_slice_in_dim(jnp.zeros((2, width), f32), qv_sums, core * local_cols, axis=1)
    up_full = lax.dynamic_update_slice_in_dim(
        jnp.zeros((2 * local_hidden,), f32), up_bias_sums[0], core * local_hidden, axis=0
    )
    pieces = [
        qv_full.reshape(-1),
        up_full,
        jnp.sum(flat(grad_attn_branch), axis=0),
        jnp.sum(flat(grad_mlp_branch), axis=0),
        jnp.sum(grad_first, axis=0),
        jnp.sum(grad_second, axis=0),
        jnp.sum(grad_projected, axis=0),
    ]
    packed = jnp.concatenate(pieces)
    packed = jnp.pad(packed, (0, -packed.shape[0] % (8 * LANES))).reshape(-1, LANES)
    first_sum, second_sum, sums, slot_sum, silu_sum, cond_sum = reduce_grads(
        (grad_mlp_all, hidden),
        (mlp_all, grad_pre_low),
        (attn_all, grad_qkv),
        (grad_attn_all, attended),
        packed,
        slot_cols,
        jnp.pad(silu_low, ((0, 8 - slots), (0, 0))),
        jnp.pad(slot_low, ((0, 8 - slots), (0, 0))),
        ada_weight,
    )
    grad_condition = jax.vjp(jax.nn.silu, condition.astype(f32))[1](cond_sum[:slots])[0]
    sums = sums.reshape(-1)
    slot_mine = slot_sum.reshape(16, 8, -1)[:, :slots, :mod_cols].astype(bf16).reshape(16 * slots, mod_cols)
    grad_ada = dot_tn(silu_sum.reshape(16, 8, width)[:, :slots].reshape(16 * slots, width), slot_mine)
    ada_bias_grad = jnp.sum(slot_mine.astype(f32), axis=0)
    row_count = width // 16

    def columns(tiles):
        return tiles.reshape(-1, row_count, LANES).transpose(1, 0, 2).reshape(row_count, -1)

    def rows(tiles, height):
        return tiles.reshape(-1, height, tiles.shape[-1]).transpose(0, 2, 1).reshape(-1, height)

    down_tiles = local_hidden // TILE
    sum_down = rows(first_sum[:down_tiles], row_count)
    sum_up = columns(first_sum[down_tiles:])
    qkv_tiles = qkv_cols // TILE
    sum_qkv = columns(second_sum[:qkv_tiles])[:, : 3 * local_cols].reshape(row_count, 3, local_cols)
    sum_out = rows(second_sum[qkv_tiles:], row_count)[:local_cols]
    mid_tiles = proj_mid.shape[0] // TILE
    in_tiles = -(-width // TILE)
    sum_mid = rows(proj_sum[:mid_tiles], proj_sum.shape[1])
    sum_in = rows(proj_sum[mid_tiles : mid_tiles + in_tiles], proj_sum.shape[1])[:width]
    last_share = proj_last.shape[1] // 32
    last_tiles = proj_sum[mid_tiles + in_tiles :]
    last_tiles = last_tiles.reshape(last_tiles.shape[0] * 2, -1, TILE)[:, :last_share]
    sum_last = rows(last_tiles, last_share)
    found = []
    offset = 0
    for piece in pieces:
        found.append(sums[offset : offset + piece.shape[0]])
        offset += piece.shape[0]
    qv_grad = lax.dynamic_slice_in_dim(found[0].reshape(2, width), x * local_cols, local_cols, axis=1)
    up_bias_grad = lax.dynamic_slice_in_dim(found[1], x * local_hidden, local_hidden, axis=0)

    block_out = swap(block_low)
    tokens_out = swap(flat(grad_tokens).astype(bf16))
    return (
        block_out,
        tokens_out.astype(f32),
        grad_condition,
        grad_ada,
        ada_bias_grad,
        sum_qkv,
        qv_grad,
        sum_out,
        found[2],
        sum_up,
        up_bias_grad,
        sum_down,
        found[3],
        sum_in,
        found[4],
        sum_mid,
        found[5],
        sum_last,
        found[6],
    )


def solution(mesh):
    in_specs = (
        P(("dp", "tensor"), None),
        P("dp", None),
        P(),
        P(),
        P(None, None, "tensor"),
        P(None, "tensor"),
        P("tensor", None),
        P(),
        P(None, "tensor"),
        P("tensor"),
        P("tensor", None),
        P(),
        P(),
        P(),
        P(),
        P(),
        P(),
        P(),
        P("dp", None),
        P("dp"),
        P(("dp", "tensor")),
        P(("dp", "tensor"), None),
    )
    out_specs = (
        P(("dp", "tensor"), None),
        P(("dp", "tensor"), None),
        P("dp", None),
        P(None, ("dp", "tensor")),
        P(("dp", "tensor")),
        P("dp", None, "tensor"),
        P(None, "tensor"),
        P("tensor", "dp"),
        P(),
        P("dp", "tensor"),
        P("tensor"),
        P("tensor", "dp"),
        P(),
        P(None, ("dp", "tensor")),
        P(),
        P(None, ("dp", "tensor")),
        P(),
        P(None, ("dp", "tensor")),
        P(),
    )
    paired = mesh.shape["tensor"] == 2 and mesh.shape["dp"] == 16
    body = paired_shards if paired else shards
    return jax.shard_map(body, mesh=mesh, in_specs=in_specs, out_specs=out_specs, check_vma=False)
```

```python
import functools

import jax
import jax.numpy as jnp
from jax import lax
from jax.experimental import pallas as pl
from jax.experimental.pallas import tpu as pltpu
from jax.sharding import PartitionSpec as P

HEAD_DIM = 72
SHORT = 256


highest = lax.Precision.HIGHEST
eps_norm = 1e-06
repa_weight = 1000.0
neg_fill = -1e30


def dot_nt(left_arg, right_arg):
    return lax.dot_general(
        left_arg, right_arg, (((1,), (1,)), ((), ())), preferred_element_type=jnp.float32
    )


def dot_tn(left_arg, right_arg, precision=None):
    return lax.dot_general(
        left_arg,
        right_arg,
        (((0,), (0,)), ((), ())),
        precision=precision,
        preferred_element_type=jnp.float32,
    )


def layer_norm(values):
    center = values - jnp.mean(values, axis=-1, keepdims=True)
    inv_std = lax.rsqrt(jnp.mean(center * center, axis=-1, keepdims=True) + eps_norm)
    return (center * inv_std, inv_std)


def norm_back(normed, inv_std, grad_normed):
    return inv_std * (
        grad_normed
        - jnp.mean(grad_normed, axis=-1, keepdims=True)
        - normed * jnp.mean(grad_normed * normed, axis=-1, keepdims=True)
    )


def gelu_tanh(values):
    return jax.nn.gelu(values, approximate=True)


def align_loss(projected, target_vals):
    inner = jnp.sum(projected * target_vals, axis=1)
    norm_pred = lax.rsqrt(jnp.sum(projected * projected, axis=1) + eps_norm)
    norm_target = lax.rsqrt(jnp.sum(target_vals * target_vals, axis=1) + eps_norm)
    return -repa_weight * jnp.sum(inner * norm_pred * norm_target)


def block_rows(total_rows, unit_rows):
    count = total_rows // unit_rows
    best = 1
    for parts in range(1, count + 1):
        if count % parts == 0 and parts * unit_rows <= 1024:
            best = parts
    return best * unit_rows


def block_scores(queries, key_rows, image_ids, row_start, starts, block_len, score_scale):
    query_blk = queries[row_start : row_start + block_len]
    row_ids = image_ids[row_start : row_start + block_len]
    pieces = []
    for col_start in starts:

        def compute_block(col_start=col_start):
            products = (
                jnp.einsum(
                    "qhd,khd->hqk",
                    query_blk,
                    key_rows[col_start : col_start + block_len],
                    preferred_element_type=jnp.float32,
                )
                * score_scale
            )
            same_image = row_ids[:, None] == image_ids[col_start : col_start + block_len][None, :]
            return jnp.where(same_image[None], products, neg_fill)

        pieces.append(compute_block())
    return jnp.concatenate(pieces, axis=2)


def attention_forward(queries, key_rows, values, image_ids, block_len, score_scale):
    starts = list(range(0, queries.shape[0], block_len))
    outputs = []
    log_sums = []
    for row_start in starts:
        scores = block_scores(
            queries, key_rows, image_ids, row_start, starts, block_len, score_scale
        )
        row_max = jnp.max(scores, axis=2, keepdims=True)
        exponent = jnp.exp(scores - row_max)
        row_total = jnp.sum(exponent, axis=2, keepdims=True)
        prob_low = (exponent / row_total).astype(jnp.bfloat16)
        log_sums.append(row_max + jnp.log(row_total))
        summed = jnp.zeros((block_len, queries.shape[1], queries.shape[2]), jnp.float32)
        for position, col_start in enumerate(starts):

            def weigh_block(position=position, col_start=col_start, prob_low=prob_low):
                return jnp.einsum(
                    "hqk,khd->qhd",
                    prob_low[:, :, position * block_len : (position + 1) * block_len],
                    values[col_start : col_start + block_len],
                    preferred_element_type=jnp.float32,
                )

            summed = summed + weigh_block()
        outputs.append(summed.astype(jnp.bfloat16))
    return (jnp.concatenate(outputs, axis=0), jnp.concatenate(log_sums, axis=1))


def attention_backward(
    queries, key_rows, values, image_ids, log_sums, grad_heads, block_len, score_scale
):
    starts = list(range(0, queries.shape[0], block_len))
    grad_keys = jnp.zeros(key_rows.shape, jnp.float32)
    grad_values = jnp.zeros(values.shape, jnp.float32)
    grad_query_list = []
    for row_start in starts:
        query_blk = queries[row_start : row_start + block_len]
        grad_blk = grad_heads[row_start : row_start + block_len]
        scores = block_scores(
            queries, key_rows, image_ids, row_start, starts, block_len, score_scale
        )
        soft = jnp.exp(scores - log_sums[:, row_start : row_start + block_len])
        grad_pieces = []
        for col_start in starts:

            def pull_block(col_start=col_start):
                return jnp.einsum(
                    "qhd,khd->hqk",
                    grad_blk,
                    values[col_start : col_start + block_len],
                    preferred_element_type=jnp.float32,
                )

            grad_pieces.append(pull_block())
        grad_soft = jnp.concatenate(grad_pieces, axis=2)
        inner = jnp.sum(soft * grad_soft, axis=2, keepdims=True)
        grad_scores = (soft * (grad_soft - inner)).astype(jnp.bfloat16)
        soft_low = soft.astype(jnp.bfloat16)
        grad_query = jnp.zeros(query_blk.shape, jnp.float32)
        for position, col_start in enumerate(starts):

            def both_grads(position=position, col_start=col_start):
                piece = grad_scores[:, :, position * block_len : (position + 1) * block_len]
                soft_piece = soft_low[:, :, position * block_len : (position + 1) * block_len]
                return (
                    jnp.einsum(
                        "hqk,khd->qhd",
                        piece,
                        key_rows[col_start : col_start + block_len],
                        preferred_element_type=jnp.float32,
                    ),
                    jnp.einsum(
                        "hqk,qhd->khd", piece, query_blk, preferred_element_type=jnp.float32
                    ),
                    jnp.einsum(
                        "hqk,qhd->khd", soft_piece, grad_blk, preferred_element_type=jnp.float32
                    ),
                )

            part_query, part_key, part_value = both_grads()
            grad_query = grad_query + part_query
            grad_keys = grad_keys.at[col_start : col_start + block_len].add(part_key)
            grad_values = grad_values.at[col_start : col_start + block_len].add(part_value)
        grad_query_list.append(grad_query * score_scale)
    return (jnp.concatenate(grad_query_list, axis=0), grad_keys * score_scale, grad_values)


def column_set(matrix, data_count, tensor_count, tensor_rank):
    shaped = matrix.reshape(matrix.shape[0], data_count, tensor_count, -1)
    return lax.dynamic_index_in_dim(shaped, tensor_rank, axis=2, keepdims=False).reshape(
        matrix.shape[0], -1
    )


def shards(
    tokens_in,
    condition,
    ada_weight,
    ada_bias,
    qkv_weight,
    qv_bias,
    out_weight,
    out_bias,
    up_weight,
    up_bias,
    down_weight,
    down_bias,
    proj_in,
    proj_in_bias,
    proj_mid,
    proj_mid_bias,
    proj_last,
    proj_last_bias,
    enc_features,
    image_ids,
    target_rows,
    out_grad,
):
    tensor_count = lax.axis_size("tensor")
    data_count = lax.axis_size("dp")
    tensor_rank = lax.axis_index("tensor")
    data_rank = lax.axis_index("dp")
    local_rows, model_width = tokens_in.shape
    shard_rows = image_ids.shape[0]
    slot_count = condition.shape[0]
    local_cols = qkv_weight.shape[2]
    local_hidden = up_weight.shape[1]
    head_count = local_cols // HEAD_DIM
    score_scale = HEAD_DIM ** (-0.5)
    block_len = block_rows(shard_rows, SHORT)
    my_ids = lax.dynamic_slice_in_dim(image_ids, tensor_rank * local_rows, local_rows)
    one_hot = (my_ids[:, None] == jnp.arange(slot_count, dtype=jnp.int32)[None, :]).astype(
        jnp.float32
    )
    cond_float = condition.astype(jnp.float32)
    silu_cond, silu_back = jax.vjp(jax.nn.silu, cond_float)
    silu_low = silu_cond.astype(jnp.bfloat16)
    modulation = jnp.dot(
        silu_low, ada_weight, preferred_element_type=jnp.float32
    ) + ada_bias.astype(jnp.float32)
    per_token = jnp.dot(one_hot, modulation, precision=highest, preferred_element_type=jnp.float32)
    shift_one, scale_one, gate_one, shift_two, scale_two, gate_two = jnp.split(per_token, 6, axis=1)
    resid = tokens_in.astype(jnp.float32)
    normed_one, inv_one = layer_norm(resid)
    attn_in = (normed_one * (1.0 + scale_one) + shift_one).astype(jnp.bfloat16)
    attn_all = lax.all_gather(attn_in, "tensor", axis=0, tiled=True)
    qkv_flat_weight = qkv_weight.reshape(model_width, 3 * local_cols)
    qkv_flat = jnp.dot(attn_all, qkv_flat_weight, preferred_element_type=jnp.float32)
    bias_float = qv_bias.astype(jnp.float32)
    queries = (
        (qkv_flat[:, :local_cols] + bias_float[0])
        .astype(jnp.bfloat16)
        .reshape(shard_rows, head_count, HEAD_DIM)
    )
    key_rows = (
        qkv_flat[:, local_cols : 2 * local_cols]
        .astype(jnp.bfloat16)
        .reshape(shard_rows, head_count, HEAD_DIM)
    )
    values = (
        (qkv_flat[:, 2 * local_cols :] + bias_float[1])
        .astype(jnp.bfloat16)
        .reshape(shard_rows, head_count, HEAD_DIM)
    )
    attended, log_sums = attention_forward(
        queries, key_rows, values, image_ids, block_len, score_scale
    )
    attended = attended.reshape(shard_rows, local_cols)
    attn_branch = lax.psum_scatter(
        jnp.dot(attended, out_weight, preferred_element_type=jnp.float32).astype(jnp.bfloat16),
        "tensor",
        scatter_dimension=0,
        tiled=True,
    ).astype(jnp.float32) + out_bias.astype(jnp.float32)
    mid = resid + gate_one * attn_branch
    normed_two, inv_two = layer_norm(mid)
    mlp_in = (normed_two * (1.0 + scale_two) + shift_two).astype(jnp.bfloat16)
    mlp_all = lax.all_gather(mlp_in, "tensor", axis=0, tiled=True)
    pre_act = jnp.dot(mlp_all, up_weight, preferred_element_type=jnp.float32) + up_bias.astype(
        jnp.float32
    )
    act_value, act_back = jax.vjp(gelu_tanh, pre_act)
    hidden = act_value.astype(jnp.bfloat16)
    mlp_branch = lax.psum_scatter(
        jnp.dot(hidden, down_weight, preferred_element_type=jnp.float32).astype(jnp.bfloat16),
        "tensor",
        scatter_dimension=0,
        tiled=True,
    ).astype(jnp.float32) + down_bias.astype(jnp.float32)
    block_value = mid + gate_two * mlp_branch
    block_low = block_value.astype(jnp.bfloat16)
    first_pre = jnp.dot(
        block_low, proj_in, preferred_element_type=jnp.float32
    ) + proj_in_bias.astype(jnp.float32)
    first_value, first_back = jax.vjp(jax.nn.silu, first_pre)
    first_low = first_value.astype(jnp.bfloat16)
    second_pre = jnp.dot(
        first_low, proj_mid, preferred_element_type=jnp.float32
    ) + proj_mid_bias.astype(jnp.float32)
    second_value, second_back = jax.vjp(jax.nn.silu, second_pre)
    second_low = second_value.astype(jnp.bfloat16)
    projected = jnp.dot(
        second_low, proj_last, preferred_element_type=jnp.float32
    ) + proj_last_bias.astype(jnp.float32)
    target_vals = jnp.take(enc_features, target_rows - data_rank * shard_rows, axis=0).astype(
        jnp.float32
    )
    loss_value, loss_back = jax.vjp(lambda predicted: align_loss(predicted, target_vals), projected)
    grad_projected = loss_back(jnp.ones((), jnp.float32))[0]
    grad_last_low = grad_projected.astype(jnp.bfloat16)
    grad_second = second_back(dot_nt(grad_last_low, proj_last))[0]
    grad_second_low = grad_second.astype(jnp.bfloat16)
    grad_first = first_back(dot_nt(grad_second_low, proj_mid))[0]
    grad_first_low = grad_first.astype(jnp.bfloat16)
    grad_block = out_grad.astype(jnp.float32) + dot_nt(grad_first_low, proj_in)
    gate_two_grad = mlp_branch * grad_block
    grad_mlp_branch = gate_two * grad_block
    grad_mlp_all = lax.all_gather(
        grad_mlp_branch.astype(jnp.bfloat16), "tensor", axis=0, tiled=True
    )
    grad_down_local = dot_tn(hidden, grad_mlp_all)
    grad_pre = act_back(dot_nt(grad_mlp_all, down_weight))[0]
    grad_pre_low = grad_pre.astype(jnp.bfloat16)
    grad_up_local = dot_tn(mlp_all, grad_pre_low)
    up_bias_local = jnp.sum(grad_pre, axis=0)
    grad_mlp_in = lax.psum_scatter(
        dot_nt(grad_pre_low, up_weight).astype(jnp.bfloat16),
        "tensor",
        scatter_dimension=0,
        tiled=True,
    ).astype(jnp.float32)
    scale_two_grad = grad_mlp_in * normed_two
    grad_mid = grad_block + norm_back(normed_two, inv_two, grad_mlp_in * (1.0 + scale_two))
    gate_one_grad = attn_branch * grad_mid
    grad_attn_branch = gate_one * grad_mid
    grad_attn_all = lax.all_gather(
        grad_attn_branch.astype(jnp.bfloat16), "tensor", axis=0, tiled=True
    )
    grad_out_local = dot_tn(attended, grad_attn_all)
    grad_heads = (
        dot_nt(grad_attn_all, out_weight)
        .astype(jnp.bfloat16)
        .reshape(shard_rows, head_count, HEAD_DIM)
    )
    grad_queries, grad_keys, grad_values = attention_backward(
        queries, key_rows, values, image_ids, log_sums, grad_heads, block_len, score_scale
    )
    grad_queries = grad_queries.reshape(shard_rows, local_cols)
    grad_keys = grad_keys.reshape(shard_rows, local_cols)
    grad_values = grad_values.reshape(shard_rows, local_cols)
    qv_local = jnp.stack([jnp.sum(grad_queries, axis=0), jnp.sum(grad_values, axis=0)])
    grad_qkv_low = jnp.concatenate([grad_queries, grad_keys, grad_values], axis=1).astype(
        jnp.bfloat16
    )
    grad_qkv_local = dot_tn(attn_all, grad_qkv_low).reshape(model_width, 3, local_cols)
    grad_attn_in = lax.psum_scatter(
        dot_nt(grad_qkv_low, qkv_flat_weight).astype(jnp.bfloat16),
        "tensor",
        scatter_dimension=0,
        tiled=True,
    ).astype(jnp.float32)
    scale_one_grad = grad_attn_in * normed_one
    grad_tokens = grad_mid + norm_back(normed_one, inv_one, grad_attn_in * (1.0 + scale_one))
    token_mod_grad = jnp.concatenate(
        [grad_attn_in, scale_one_grad, gate_one_grad, grad_mlp_in, scale_two_grad, gate_two_grad],
        axis=1,
    )
    slot_grad_part = dot_tn(one_hot, token_mod_grad, precision=highest)
    slot_grad = lax.psum(slot_grad_part.astype(jnp.bfloat16), "tensor").astype(jnp.float32)
    slot_low = slot_grad.astype(jnp.bfloat16)
    grad_condition = silu_back(dot_nt(slot_low, ada_weight))[0]
    ada_cols = dot_tn(silu_low, column_set(slot_low, data_count, tensor_count, tensor_rank))
    ada_bias_cols = jnp.sum(
        column_set(slot_grad, data_count, tensor_count, tensor_rank), axis=0, keepdims=True
    )
    block_grads = (
        lax.psum_scatter(
            grad_qkv_local.astype(jnp.bfloat16), "dp", scatter_dimension=0, tiled=True
        ).astype(jnp.float32),
        lax.psum_scatter(
            grad_out_local.astype(jnp.bfloat16), "dp", scatter_dimension=1, tiled=True
        ).astype(jnp.float32),
        lax.psum_scatter(
            grad_up_local.astype(jnp.bfloat16), "dp", scatter_dimension=0, tiled=True
        ).astype(jnp.float32),
        lax.psum_scatter(
            grad_down_local.astype(jnp.bfloat16), "dp", scatter_dimension=1, tiled=True
        ).astype(jnp.float32),
        lax.psum_scatter(
            ada_cols.astype(jnp.bfloat16), "dp", scatter_dimension=1, tiled=True
        ).astype(jnp.float32),
        lax.psum_scatter(
            ada_bias_cols.astype(jnp.bfloat16), "dp", scatter_dimension=1, tiled=True
        ).astype(jnp.float32),
    )
    qv_full = lax.dynamic_update_slice_in_dim(
        jnp.zeros((2, model_width), jnp.float32), qv_local, tensor_rank * local_cols, axis=1
    )
    up_full = lax.dynamic_update_slice_in_dim(
        jnp.zeros((local_hidden * tensor_count,), jnp.float32),
        up_bias_local,
        tensor_rank * local_hidden,
        axis=0,
    )
    bias_sums = lax.psum(
        (
            qv_full,
            up_full,
            jnp.sum(grad_attn_branch, axis=0),
            jnp.sum(grad_mlp_branch, axis=0),
            jnp.sum(grad_first, axis=0),
            jnp.sum(grad_second, axis=0),
            jnp.sum(grad_projected, axis=0),
        ),
        ("dp", "tensor"),
    )
    qv_grad = lax.dynamic_slice_in_dim(bias_sums[0], tensor_rank * local_cols, local_cols, axis=1)
    up_bias_grad = lax.dynamic_slice_in_dim(
        bias_sums[1], tensor_rank * local_hidden, local_hidden, axis=0
    )
    proj_grads = (
        lax.psum_scatter(
            dot_tn(block_low, grad_first_low), ("dp", "tensor"), scatter_dimension=1, tiled=True
        ),
        lax.psum_scatter(
            dot_tn(first_low, grad_second_low), ("dp", "tensor"), scatter_dimension=1, tiled=True
        ),
        lax.psum_scatter(
            dot_tn(second_low, grad_last_low), ("dp", "tensor"), scatter_dimension=1, tiled=True
        ),
    )
    return (
        block_low,
        grad_tokens,
        grad_condition,
        block_grads[4],
        block_grads[5].reshape(-1),
        block_grads[0],
        qv_grad,
        block_grads[1],
        bias_sums[2],
        block_grads[2],
        up_bias_grad,
        block_grads[3],
        bias_sums[3],
        proj_grads[0],
        bias_sums[4],
        proj_grads[1],
        bias_sums[5],
        proj_grads[2],
        bias_sums[6],
    )


LANES = 128
MESH = pl.DeviceIdType.MESH
TILE = 256
GAP = 2
SLOTS = 2 * GAP
LOG2_E = 1.4426950408889634
GELU_SCALE = 0.7978845608028654
GELU_CUBE = 0.044715
bf16 = jnp.bfloat16
f32 = jnp.float32


def pairs_of(move):
    found = []
    for index in range(32):
        x, core, y, z = index % 2, (index // 2) % 2, (index // 4) % 2, index // 8
        z2, y2, c2, x2 = move(z, y, core, x)
        if (z2, y2, c2, x2) != (z, y, core, x):
            found.append((index, ((z2 * 2 + y2) * 2 + c2) * 2 + x2))
    return found


def send(value, move):
    return lax.ppermute(value, ("dp", "tensor"), pairs_of(move))


def to_diag(z, y, c, x):
    return (z, y, x, c)


def to_cycle(z, y, c, x):
    return (z, y, c, c) if c != x else (z, y, 1 - c, x)


def to_core(z, y, c, x):
    return (z, y, 1 - c, x)


def to_x(z, y, c, x):
    return (z, y, c, 1 - x)


def to_y(z, y, c, x):
    return (z, 1 - y, c, x)


def to_swapped_y(z, y, c, x):
    return (z, 1 - y, c, x) if c != x else (z, y, c, x)


def to_z_near(z, y, c, x):
    return (z ^ 1, y, c, x)


def to_z_far(z, y, c, x):
    return (z ^ 2, y, c, x)


def pick(array, index, axis):
    return lax.dynamic_index_in_dim(array, index, axis=axis, keepdims=False)


def gather_kernel(own_ref, out_ref, local_sem, send_sem, recv_sem):
    dp = lax.axis_index("dp")
    x = lax.axis_index("tensor")
    core = dp % 2
    other = dp + 1 - 2 * core
    barrier = pltpu.get_barrier_semaphore()
    pl.semaphore_signal(barrier, inc=1, device_id=(other, x), device_id_type=MESH)
    pl.semaphore_wait(barrier, 1)
    away = pltpu.make_async_remote_copy(
        src_ref=own_ref,
        dst_ref=out_ref.at[core],
        send_sem=send_sem,
        recv_sem=recv_sem,
        device_id=(other, x),
        device_id_type=MESH,
    )
    away.start()
    here = pltpu.make_async_copy(own_ref, out_ref.at[core], local_sem)
    here.start()
    here.wait()
    away.wait()


def gather_cores(own):
    rows, width = own.shape
    return pl.pallas_call(
        gather_kernel,
        out_shape=jax.ShapeDtypeStruct((2, rows, width), own.dtype),
        in_specs=[pl.BlockSpec(memory_space=pltpu.VMEM)],
        out_specs=pl.BlockSpec(memory_space=pl.ANY),
        scratch_shapes=[pltpu.SemaphoreType.DMA] * 3,
        compiler_params=pltpu.CompilerParams(collective_id=0, has_side_effects=True, vmem_limit_bytes=16 << 20),
        cost_estimate=pl.CostEstimate(flops=0, bytes_accessed=12000000, transcendentals=0),
        name="gather_cores",
    )(own).reshape(2 * rows, width)


def split_heads(flat_ref, heads_ref, parts, heads):
    heads_ref[...] = jnp.zeros_like(heads_ref)
    for part in range(parts):
        for head in range(heads):
            begin = (part * heads + head) * HEAD_DIM
            heads_ref[part * heads + head, :, 0:HEAD_DIM] = flat_ref[:, begin : begin + HEAD_DIM]


def join_heads(heads_ref, flat_ref, count):
    rows, columns = flat_ref.shape
    for block in range(rows // LANES):
        span = slice(block * LANES, (block + 1) * LANES)
        pieces = [heads_ref[head, span, 0:HEAD_DIM] for head in range(count)]
        if columns > count * HEAD_DIM:
            pieces.append(jnp.zeros((LANES, columns - count * HEAD_DIM), flat_ref.dtype))
        flat_ref[span, :] = jnp.concatenate(pieces, axis=1)


def per_image(count, run):
    @pl.when(count == 1)
    def _():
        run(SHORT)

    @pl.when(count != 1)
    def _():
        run(4 * SHORT)


def attend_kernel(heads, together, factor, starts, counts, qkv_ref, o_ref, log_ref, part_ref, o_heads):
    split_heads(qkv_ref, part_ref, 3, heads)
    unit_count = o_ref.shape[0] // SHORT

    def some_heads(step, carry):
        def unit(index, carry):
            rows = pl.ds(pl.multiple_of(index * SHORT, SHORT), SHORT)

            def run(length):
                cols = pl.ds(pl.multiple_of(starts[index] * SHORT, SHORT), length)
                for ahead in range(together):
                    head = step * together + ahead
                    scores = dot_nt(part_ref[heads + head, cols, :], part_ref[head, rows, :])
                    top = jnp.max(scores, axis=0, keepdims=True)
                    exponent = jnp.exp2((scores - top) * factor)
                    total = jnp.sum(exponent, axis=0, keepdims=True)
                    summed = dot_tn(part_ref[2 * heads + head, cols, :], exponent.astype(bf16))
                    o_heads[head, rows, :] = (summed * (1.0 / total)).T.astype(bf16)
                    log_ref[head * unit_count + index] = top * factor + jnp.log2(total)

            per_image(counts[index], run)
            return carry

        return lax.fori_loop(0, unit_count, unit, carry)

    lax.fori_loop(0, heads // together, some_heads, 0)
    join_heads(o_heads, o_ref, heads)


def whole_spec(space=pltpu.VMEM):
    return pl.BlockSpec(memory_space=space)


def attend(starts, counts, qkv, heads, out_cols):
    rows = qkv.shape[0]
    factor = HEAD_DIM ** (-0.5) * LOG2_E
    return pl.pallas_call(
        functools.partial(attend_kernel, heads, 4, factor),
        out_shape=(
            jax.ShapeDtypeStruct((rows, out_cols), bf16),
            jax.ShapeDtypeStruct((heads * (rows // SHORT), 1, SHORT), f32),
        ),
        in_specs=[whole_spec(pltpu.SMEM), whole_spec(pltpu.SMEM), whole_spec()],
        out_specs=(whole_spec(), whole_spec()),
        scratch_shapes=[
            pltpu.VMEM((3 * heads, rows, LANES), bf16),
            pltpu.VMEM((heads, rows, LANES), bf16),
        ],
        compiler_params=pltpu.CompilerParams(vmem_limit_bytes=40 << 20),
        cost_estimate=pl.CostEstimate(flops=20 * 10**9, bytes_accessed=13 * 10**6, transcendentals=10**7),
        name="attend",
    )(starts, counts, qkv)


def attend_back_kernel(
    heads,
    together,
    factor,
    starts,
    counts,
    qkv_ref,
    log_ref,
    grad_ref,
    out_ref,
    bias_ref,
    part_ref,
    grad_heads,
    key_acc,
    value_acc,
    sums,
):
    split_heads(qkv_ref, part_ref, 3, heads)
    split_heads(grad_ref, grad_heads, 1, heads)
    unit_count = out_ref.shape[0] // SHORT

    def some_heads(step, carry):
        key_acc[...] = jnp.zeros_like(key_acc)
        value_acc[...] = jnp.zeros_like(value_acc)
        for ahead in range(together):
            sums[step * together + ahead] = jnp.zeros((8, LANES), f32)

        def unit(index, carry):
            rows = pl.ds(pl.multiple_of(index * SHORT, SHORT), SHORT)

            def run(length):
                cols = pl.ds(pl.multiple_of(starts[index] * SHORT, SHORT), length)
                for ahead in range(together):
                    head = step * together + ahead
                    queries = part_ref[head, rows, :]
                    grads = grad_heads[head, rows, :]
                    keys = part_ref[heads + head, cols, :]
                    scores = dot_nt(keys, queries)
                    soft = jnp.exp2(scores * (factor * LOG2_E) - log_ref[head * unit_count + index])
                    grad_soft = dot_nt(part_ref[2 * heads + head, cols, :], grads)
                    product = soft * grad_soft
                    inner = jnp.sum(product, axis=0, keepdims=True)
                    grad_scores = (product - soft * inner).astype(bf16)
                    value_acc[ahead, cols, :] += jnp.dot(soft.astype(bf16), grads, preferred_element_type=f32)
                    key_acc[ahead, cols, :] += jnp.dot(grad_scores, queries, preferred_element_type=f32)
                    grad_query = dot_tn(keys, grad_scores).T * factor
                    sums[head, 0:1, :] += jnp.sum(grad_query, axis=0, keepdims=True)
                    part_ref[head, rows, :] = grad_query.astype(bf16)

            per_image(counts[index], run)
            return carry

        lax.fori_loop(0, unit_count, unit, 0)
        for ahead in range(together):
            head = step * together + ahead
            sums[head, 1:2, :] = jnp.sum(value_acc[ahead], axis=0, keepdims=True)
            part_ref[heads + head] = (key_acc[ahead] * factor).astype(bf16)
            part_ref[2 * heads + head] = value_acc[ahead].astype(bf16)
        return carry

    lax.fori_loop(0, heads // together, some_heads, 0)
    join_heads(part_ref, out_ref, 3 * heads)
    bias_ref[...] = jnp.concatenate([sums[head, :, 0:HEAD_DIM] for head in range(heads)], axis=1)


def attend_back(starts, counts, qkv, log_sums, grad_heads, heads):
    rows, columns = qkv.shape
    factor = HEAD_DIM ** (-0.5)
    together = 4
    return pl.pallas_call(
        functools.partial(attend_back_kernel, heads, together, factor),
        out_shape=(
            jax.ShapeDtypeStruct((rows, columns), bf16),
            jax.ShapeDtypeStruct((8, heads * HEAD_DIM), f32),
        ),
        in_specs=[whole_spec(pltpu.SMEM), whole_spec(pltpu.SMEM)] + [whole_spec()] * 3,
        out_specs=(whole_spec(), whole_spec()),
        scratch_shapes=[
            pltpu.VMEM((3 * heads, rows, LANES), bf16),
            pltpu.VMEM((heads, rows, LANES), bf16),
            pltpu.VMEM((together, rows, LANES), f32),
            pltpu.VMEM((together, rows, LANES), f32),
            pltpu.VMEM((heads, 8, LANES), f32),
        ],
        compiler_params=pltpu.CompilerParams(vmem_limit_bytes=48 << 20),
        cost_estimate=pl.CostEstimate(flops=40 * 10**9, bytes_accessed=25 * 10**6, transcendentals=10**7),
        name="attend_back",
    )(starts, counts, qkv, log_sums, grad_heads)


def reduce_kernel(
    grid_rows,
    first_jobs,
    second_jobs,
    one_left,
    one_right,
    two_left,
    two_right,
    three_left,
    three_right,
    four_left,
    four_right,
    bias_ref,
    slot_ref,
    silu_ref,
    slot_low_ref,
    ada_ref,
    first_out,
    second_out,
    bias_out,
    slot_out,
    silu_out,
    cond_out,
    stage,
    first_left,
    second_left,
    first_right,
    second_right,
    f0,
    f0_turn,
    f0_swap,
    f1,
    f1_got,
    f2,
    f2_got,
    f3,
    f3_got,
    s0,
    s0_got,
    s1,
    s1_got,
    far,
    far_got,
    s2,
    s2_turn,
    s2_swap,
    bias_got,
    slot_x,
    slot_y,
    slot_y_got,
    slot_z,
    slot_z_got,
    silu_x,
    silu_y,
    silu_y_got,
    silu_z,
    silu_z_got,
    ada_tile,
    cond_acc,
    load_sem,
    first_load,
    second_load,
    f0_sems,
    f1_sems,
    f2_sems,
    f3_sems,
    s0_sems,
    s1_sems,
    far_sems,
    s2_sems,
    bias_sems,
    slot_sems,
    slot_z_sems,
    silu_sems,
    silu_z_sems,
    ada_sems,
    cond_sems,
    first_free,
    second_free,
):
    dp = lax.axis_index("dp")
    x = lax.axis_index("tensor")
    core = dp % 2
    y = (dp // 2) % 2
    z = dp // 4
    home = core == x
    away = core != x

    def device(z_at, y_at, core_at, x_at):
        return ((z_at * 2 + y_at) * 2 + core_at, x_at)

    turn_to = device(z, y, core + (1 - 2 * core) * (1 - jnp.abs(core - x)), x + (core - x))
    turn_from = device(z, y, x + 0 * core, x + (1 - 2 * x) * (1 - jnp.abs(core - x)))
    swap_peer = device(z, y, x, core)
    y_peer = device(z, 1 - y, core, x)

    def z_peer(ahead):
        return device(lax.rem(z + ahead, 4), y, core, x)

    barrier = pltpu.get_barrier_semaphore()
    near = [device(z, y, 1 - core, x), device(z, y, core, 1 - x), device(z, y, 1 - core, 1 - x), y_peer]
    for peer in near + [z_peer(1), z_peer(2), z_peer(3)]:
        pl.semaphore_signal(barrier, inc=1, device_id=peer, device_id_type=MESH)
    pl.semaphore_wait(barrier, 7)

    def remote(source, target, sems, index, peer):
        return pltpu.make_async_remote_copy(
            src_ref=source,
            dst_ref=target,
            send_sem=sems.at[(0,) + index],
            recv_sem=sems.at[(1,) + index],
            device_id=peer,
            device_id_type=MESH,
        )

    def added(*terms):
        total = terms[0].astype(f32)
        for term in terms[1:]:
            total = total + term.astype(f32)
        return total

    def load_left(source, through, target):
        height = source.shape[1]
        through = through if height == through.shape[1] else through.at[:, 0:height]
        copy = pltpu.make_async_copy(source, through, load_sem)
        copy.start()
        copy.wait()

        def block(index, carry):
            rows = pl.ds(pl.multiple_of(index * LANES, LANES), LANES)
            target[0:height, rows] = through[rows, :].T
            return carry

        lax.fori_loop(0, source.shape[0] // LANES, block, 0)

    def right_copy(source, tile, target, sems, slot):
        columns = pl.ds(pl.multiple_of(tile * TILE, TILE), TILE)
        return pltpu.make_async_copy(source.at[:, columns], target.at[slot], sems.at[slot])

    first_split = one_right.shape[1] // TILE
    second_split = three_right.shape[1] // TILE

    def first_right_do(job, slot, action):
        @pl.when(job < first_split)
        def _():
            action(right_copy(one_right, job, first_right, first_load, slot))

        @pl.when(job >= first_split)
        def _():
            action(right_copy(two_right, job - first_split, first_right, first_load, slot))

    def second_right_do(job, slot, action):
        @pl.when(job < second_split)
        def _():
            action(right_copy(three_right, job, second_right, second_load, slot))

        @pl.when(job >= second_split)
        def _():
            action(right_copy(four_right, job - second_split, second_right, second_load, slot))

    def begin(copy):
        copy.start()

    def finish(copy):
        copy.wait()

    def multiply(left, right, slot, keep):
        def block(at_z, carry):
            height = 4 * grid_rows
            span = pl.ds(pl.multiple_of(at_z * height, 32), height)
            product = jnp.dot(left[span, :], right[slot], preferred_element_type=f32)
            for at_y in range(2):
                for at_core in range(2):
                    low = (at_y * 2 + at_core) * grid_rows
                    part = product[low : low + grid_rows, :]
                    stacked = jnp.concatenate([part[:, :LANES], part[:, LANES:]], axis=0)
                    keep(at_z, at_y, at_core, stacked.astype(bf16))
            return carry

        lax.fori_loop(0, 4, block, 0)

    def f0_copies(slot):
        turn = remote(f0.at[slot, 1 - x], f0_turn.at[slot], f0_sems, (0, slot), turn_to)
        swap = remote(f0.at[slot, x], f0_swap.at[slot], f0_sems, (1, slot), swap_peer)
        return turn, swap

    def f1_copy(slot):
        return remote(f1.at[slot, 1 - y], f1_got.at[slot], f1_sems, (slot,), y_peer)

    z_low = lax.rem(z, 2)
    z_high = z // 2
    near_peer = device(z + 1 - 2 * z_low, y, core, x)
    far_peer = device(lax.rem(z + 2, 4), y, core, x)

    def f2_copy(slot):
        return remote(f2.at[slot, 1 - z_low], f2_got.at[slot], f2_sems, (slot,), near_peer)

    def f3_copy(slot):
        return remote(f3.at[slot, 1 - z_high], f3_got.at[slot], f3_sems, (slot,), far_peer)

    def s0_copy(slot):
        return remote(s0.at[slot, 1 - y], s0_got.at[slot], s0_sems, (slot,), y_peer)

    def s1_copy(slot):
        return remote(s1.at[slot, 1 - z_low], s1_got.at[slot], s1_sems, (slot,), near_peer)

    def far_copy(slot):
        return remote(far.at[slot, 1 - z_high], far_got.at[slot], far_sems, (slot,), far_peer)

    def s2_copies(slot):
        turn = remote(s2.at[slot, 1 - x], s2_turn.at[slot], s2_sems, (0, slot), turn_to)
        swap = remote(s2.at[slot, x], s2_swap.at[slot], s2_sems, (1, slot), swap_peer)
        return turn, swap

    def inside(job, count):
        return jnp.logical_and(job >= 0, job < count)

    first_right_do(0, 0, begin)
    second_right_do(0, 0, begin)

    def first_tick(tick):
        @pl.when(tick < first_jobs)
        def _():
            slot = lax.rem(tick, 2)
            first_right_do(tick, slot, finish)

            @pl.when(tick + 1 < first_jobs)
            def _():
                first_right_do(tick + 1, 1 - slot, begin)

            @pl.when(tick == 0)
            def _():
                load_left(one_left, stage, first_left)

            @pl.when(tick == first_split)
            def _():
                load_left(two_left, stage, first_left)

            def keep(at_z, at_y, at_core, value):
                f0[lax.rem(tick, SLOTS), at_core, at_y, at_z] = value

            multiply(first_left, first_right, slot, keep)

        last = tick - 4 * GAP

        @pl.when(inside(last, first_jobs))
        def _():
            slot = lax.rem(last, SLOTS)
            f3_copy(slot).wait()
            first_out[last] = added(f3[slot, z_high], f3_got[slot])

        fourth = tick - 3 * GAP

        @pl.when(inside(fourth, first_jobs))
        def _():
            slot = lax.rem(fourth, SLOTS)
            f2_copy(slot).wait()
            f3[slot] = added(f2[slot, z_low], f2_got[slot]).astype(bf16)
            f3_copy(slot).start()

        third = tick - 2 * GAP

        @pl.when(inside(third, first_jobs))
        def _():
            slot = lax.rem(third, SLOTS)
            f1_copy(slot).wait()
            for low in range(2):
                for high in range(2):
                    at = high * 2 + low
                    f2[slot, low, high] = added(f1[slot, y, at], f1_got[slot, at]).astype(bf16)
            f2_copy(slot).start()

        second = tick - GAP

        @pl.when(inside(second, first_jobs))
        def _():
            slot = lax.rem(second, SLOTS)
            turn, swap = f0_copies(slot)
            turn.wait()

            @pl.when(home)
            def _():
                f1[slot] = added(f0_turn[slot], f0[slot, x]).astype(bf16)

            @pl.when(away)
            def _():
                swap.wait()
                f1[slot] = added(f0_turn[slot], f0_swap[slot]).astype(bf16)

            @pl.when(second + SLOTS < first_jobs)
            def _():
                pl.semaphore_signal(first_free, inc=1, device_id=turn_from, device_id_type=MESH)

            f1_copy(slot).start()

        @pl.when(tick < first_jobs)
        def _():
            slot = lax.rem(tick, SLOTS)
            turn, swap = f0_copies(slot)

            @pl.when(tick >= SLOTS)
            def _():
                pl.semaphore_wait(first_free, 1)

            turn.start()

            @pl.when(away)
            def _():
                swap.start()

    def second_tick(tick):
        @pl.when(tick < second_jobs)
        def _():
            slot = lax.rem(tick, 2)
            second_right_do(tick, slot, finish)

            @pl.when(tick + 1 < second_jobs)
            def _():
                second_right_do(tick + 1, 1 - slot, begin)

            @pl.when(tick == 0)
            def _():
                load_left(three_left, stage, second_left)

            @pl.when(tick == second_split)
            def _():
                load_left(four_left, stage, second_left)

            def keep(at_z, at_y, at_core, value):
                s0[lax.rem(tick, SLOTS), at_y, at_z, at_core] = value

            multiply(second_left, second_right, slot, keep)

        last = tick - 4 * GAP

        @pl.when(inside(last, second_jobs))
        def _():
            slot = lax.rem(last, SLOTS)
            turn, swap = s2_copies(slot)
            turn.wait()

            @pl.when(home)
            def _():
                second_out[last] = added(s2_turn[slot], s2[slot, x])

            @pl.when(away)
            def _():
                swap.wait()
                second_out[last] = added(s2_turn[slot], s2_swap[slot])

            @pl.when(last + SLOTS < second_jobs)
            def _():
                pl.semaphore_signal(second_free, inc=1, device_id=turn_from, device_id_type=MESH)

        fourth = tick - 3 * GAP

        @pl.when(inside(fourth, second_jobs))
        def _():
            slot = lax.rem(fourth, SLOTS)
            far_copy(slot).wait()
            s2[slot] = added(far[slot, z_high], far_got[slot]).astype(bf16)
            turn, swap = s2_copies(slot)

            @pl.when(fourth >= SLOTS)
            def _():
                pl.semaphore_wait(second_free, 1)

            turn.start()

            @pl.when(away)
            def _():
                swap.start()

        third = tick - 2 * GAP

        @pl.when(inside(third, second_jobs))
        def _():
            slot = lax.rem(third, SLOTS)
            s1_copy(slot).wait()
            far[slot] = added(s1[slot, z_low], s1_got[slot]).astype(bf16)
            far_copy(slot).start()

        second = tick - GAP

        @pl.when(inside(second, second_jobs))
        def _():
            slot = lax.rem(second, SLOTS)
            s0_copy(slot).wait()
            for low in range(2):
                for high in range(2):
                    at = high * 2 + low
                    s1[slot, low, high] = added(s0[slot, y, at], s0_got[slot, at]).astype(bf16)
            s1_copy(slot).start()

        @pl.when(tick < second_jobs)
        def _():
            s0_copy(lax.rem(tick, SLOTS)).start()

    bias_peers = [
        device(z, y, 1 - core, x),
        device(z, y, core, 1 - x),
        y_peer,
        device(z + 1 - 2 * lax.rem(z, 2), y, core, x),
        device(lax.rem(z + 2, 4), y, core, x),
    ]

    def bias_copy(step):
        return remote(bias_out, bias_got.at[step], bias_sems, (step,), bias_peers[step])

    def slot_x_copy():
        return remote(slot_ref.at[1 - x], slot_x, slot_sems, (0,), device(z, y, core, 1 - x))

    def slot_y_copy():
        return remote(slot_y.at[1 - y], slot_y_got, slot_sems, (1,), y_peer)

    def slot_z_copy(ahead):
        return remote(
            slot_z.at[lax.rem(z + ahead, 4)], slot_z_got.at[ahead - 1], slot_z_sems, (ahead - 1,), z_peer(ahead)
        )

    def silu_x_copy():
        return remote(silu_ref, silu_x, silu_sems, (0,), device(z, y, core, 1 - x))

    def silu_y_copy():
        return remote(silu_y, silu_y_got, silu_sems, (1,), y_peer)

    def silu_z_copy(ahead):
        return remote(silu_z, silu_z_got.at[ahead - 1], silu_z_sems, (ahead - 1,), z_peer(ahead))

    def small_tick(tick):
        @pl.when(tick == 0)
        def _():
            bias_out[...] = bias_ref[...]
            slot_x_copy().start()
            silu_x_copy().start()

        for step in range(5):

            @pl.when(tick == step + 1)
            def _(step=step):
                bias_copy(step).wait()
                bias_out[...] = bias_out[...] + bias_got[step]

        for step in range(5):

            @pl.when(tick == step)
            def _(step=step):
                bias_copy(step).start()

        @pl.when(tick == 1)
        def _():
            slot_x_copy().wait()
            for at_y in range(2):
                slot_y[at_y, x] = slot_ref[x, at_y]
                slot_y[at_y, 1 - x] = slot_x[at_y]
            slot_y_copy().start()
            silu_x_copy().wait()
            silu_y[x] = silu_ref[...]
            silu_y[1 - x] = silu_x[...]
            silu_y_copy().start()

        @pl.when(tick == 2)
        def _():
            slot_y_copy().wait()
            for at_z in range(4):
                slot_z[at_z, y] = slot_y[y, :, at_z]
                slot_z[at_z, 1 - y] = slot_y_got[:, at_z]
            silu_y_copy().wait()
            silu_z[y] = silu_y[...]
            silu_z[1 - y] = silu_y_got[...]
            for ahead in (1, 2, 3):
                slot_z_copy(ahead).start()
                silu_z_copy(ahead).start()

        @pl.when(tick == 3)
        def _():
            slot_out[z] = slot_z[z]
            silu_out[z] = silu_z[...]
            for ahead in (1, 2, 3):
                slot_z_copy(ahead).wait()
                slot_out[lax.rem(z + 4 - ahead, 4)] = slot_z_got[ahead - 1]
                silu_z_copy(ahead).wait()
                silu_out[lax.rem(z + 4 - ahead, 4)] = silu_z_got[ahead - 1]

    ada_cols = ada_tile.shape[2]
    ada_tiles = ada_ref.shape[1] // ada_cols
    cond_copy = remote(cond_acc, cond_out, cond_sems, (), swap_peer)

    def ada_copy(tile, slot):
        columns = pl.ds(pl.multiple_of(tile * ada_cols, LANES), ada_cols)
        return pltpu.make_async_copy(ada_ref.at[:, columns], ada_tile.at[slot], ada_sems.at[slot])

    def cond_tick(tick):
        tile = tick - 4

        @pl.when(tile == -1)
        def _():
            cond_acc[...] = jnp.zeros_like(cond_acc)

        @pl.when(inside(tile + 1, ada_tiles))
        def _():
            ada_copy(tile + 1, lax.rem(tile + 1, 2)).start()

        @pl.when(inside(tile, ada_tiles))
        def _():
            slot = lax.rem(tile, 2)
            ada_copy(tile, slot).wait()
            columns = pl.ds(pl.multiple_of(tile * ada_cols, LANES), ada_cols)
            cond_acc[...] += dot_nt(slot_low_ref[:, columns], ada_tile[slot])

        @pl.when(tile == ada_tiles)
        def _():
            @pl.when(home)
            def _():
                cond_out[...] = cond_acc[...]

            @pl.when(away)
            def _():
                cond_copy.start()

        @pl.when(jnp.logical_and(tile == ada_tiles + 1, away))
        def _():
            cond_copy.wait()

    def tick_body(tick, carry):
        small_tick(tick)
        cond_tick(tick)
        first_tick(tick)

        @pl.when(lax.rem(tick, 3) != 2)
        def _():
            second_tick(tick // 3 * 2 + lax.rem(tick, 3))

        return carry

    ticks = max(first_jobs + 4 * GAP, ada_tiles + 6, -(-3 * (second_jobs + 4 * GAP) // 2))
    lax.fori_loop(0, ticks, tick_body, 0)


def reduce_grads(one, two, three, four, bias, slots, silu, slot_low, ada_weight):
    tokens, width = one[0].shape
    grid_rows = width // 16
    first_jobs = (one[1].shape[1] + two[1].shape[1]) // TILE
    second_jobs = (three[1].shape[1] + four[1].shape[1]) // TILE
    tile = (grid_rows * TILE // LANES, LANES)
    dma = pltpu.SemaphoreType.DMA
    slot_tail = slots.shape[-2:]

    def low(*lead):
        return pltpu.VMEM(lead + tile, bf16)

    scratch = [
        pltpu.VMEM((tokens, width), bf16),
        pltpu.VMEM((width, tokens), bf16),
        pltpu.VMEM((width, tokens), bf16),
        pltpu.VMEM((2, tokens, TILE), bf16),
        pltpu.VMEM((2, tokens, TILE), bf16),
        low(SLOTS, 2, 2, 4),
        low(SLOTS, 2, 4),
        low(SLOTS, 2, 4),
        low(SLOTS, 2, 4),
        low(SLOTS, 4),
        low(SLOTS, 2, 2),
        low(SLOTS, 2),
        low(SLOTS, 2),
        low(SLOTS),
        low(SLOTS, 2, 4, 2),
        low(SLOTS, 4, 2),
        low(SLOTS, 2, 2, 2),
        low(SLOTS, 2, 2),
        low(SLOTS, 2, 2),
        low(SLOTS, 2),
        low(SLOTS, 2),
        low(SLOTS),
        low(SLOTS),
        pltpu.VMEM((5,) + bias.shape, f32),
        pltpu.VMEM((2, 4) + slot_tail, f32),
        pltpu.VMEM((2, 2, 4) + slot_tail, f32),
        pltpu.VMEM((2, 4) + slot_tail, f32),
        pltpu.VMEM((4, 2, 2) + slot_tail, f32),
        pltpu.VMEM((3, 2, 2) + slot_tail, f32),
        pltpu.VMEM(silu.shape, bf16),
        pltpu.VMEM((2,) + silu.shape, bf16),
        pltpu.VMEM((2,) + silu.shape, bf16),
        pltpu.VMEM((2, 2) + silu.shape, bf16),
        pltpu.VMEM((3, 2, 2) + silu.shape, bf16),
        pltpu.VMEM((2, ada_weight.shape[0], ada_weight.shape[1] // 9), bf16),
        pltpu.VMEM((8, ada_weight.shape[0]), f32),
        dma,
        dma((2,)),
        dma((2,)),
        dma((2, 2, SLOTS)),
        dma((2, SLOTS)),
        dma((2, SLOTS)),
        dma((2, SLOTS)),
        dma((2, SLOTS)),
        dma((2, SLOTS)),
        dma((2, SLOTS)),
        dma((2, 2, SLOTS)),
        dma((2, 5)),
        dma((2, 2)),
        dma((2, 3)),
        dma((2, 2)),
        dma((2, 3)),
        dma((2,)),
        dma((2,)),
        pltpu.SemaphoreType.REGULAR,
        pltpu.SemaphoreType.REGULAR,
    ]
    return pl.pallas_call(
        functools.partial(reduce_kernel, grid_rows, first_jobs, second_jobs),
        out_shape=(
            jax.ShapeDtypeStruct((first_jobs,) + tile, f32),
            jax.ShapeDtypeStruct((second_jobs,) + tile, f32),
            jax.ShapeDtypeStruct(bias.shape, f32),
            jax.ShapeDtypeStruct((4, 2, 2) + slot_tail, f32),
            jax.ShapeDtypeStruct((4, 2, 2) + silu.shape, bf16),
            jax.ShapeDtypeStruct((8, ada_weight.shape[0]), f32),
        ),
        in_specs=[whole_spec(pl.ANY)] * 8 + [whole_spec()] * 4 + [whole_spec(pl.ANY)],
        out_specs=(whole_spec(),) * 6,
        scratch_shapes=scratch,
        compiler_params=pltpu.CompilerParams(
            collective_id=1, has_side_effects=True, vmem_limit_bytes=52 << 20
        ),
        cost_estimate=pl.CostEstimate(flops=10**11, bytes_accessed=10**8, transcendentals=0),
        name="reduce_grads",
    )(*one, *two, *three, *four, bias, slots, silu, slot_low, ada_weight)


def mlp_back_kernel(
    proj_jobs,
    own_ref,
    pre_ref,
    down_ref,
    up_ref,
    mid_left,
    mid_right,
    in_left,
    in_right,
    last_left,
    last_right,
    all_out,
    low_out,
    in_out,
    bias_out,
    proj_out,
    pre_tile,
    low_tile,
    part_send,
    part_got,
    proj_stage,
    proj_left,
    proj_right,
    p0,
    p0_got,
    p1,
    p1_got,
    p2,
    p2_got,
    p3,
    p3_got,
    pre_sems,
    low_sems,
    own_sems,
    part_sems,
    load_sem,
    proj_load,
    p0_sems,
    p1_sems,
    p2_sems,
    p3_sems,
):
    dp = lax.axis_index("dp")
    x = lax.axis_index("tensor")
    core = dp % 2
    y = (dp // 2) % 2
    z = dp // 4

    def device(z_at, y_at, core_at, x_at):
        return ((z_at * 2 + y_at) * 2 + core_at, x_at)

    y_peer = device(z, 1 - y, core, x)

    def z_peer(ahead):
        return device(lax.rem(z + ahead, 4), y, core, x)

    barrier = pltpu.get_barrier_semaphore()
    near = [device(z, y, 1 - core, x), device(z, y, core, 1 - x), device(z, y, 1 - core, 1 - x), y_peer]
    for peer in near + [z_peer(1), z_peer(2), z_peer(3)]:
        pl.semaphore_signal(barrier, inc=1, device_id=peer, device_id_type=MESH)
    pl.semaphore_wait(barrier, 7)

    def remote(source, target, sems, index, peer):
        return pltpu.make_async_remote_copy(
            src_ref=source,
            dst_ref=target,
            send_sem=sems.at[(0,) + index],
            recv_sem=sems.at[(1,) + index],
            device_id=peer,
            device_id_type=MESH,
        )

    def added(*terms):
        total = terms[0].astype(f32)
        for term in terms[1:]:
            total = total + term.astype(f32)
        return total

    def load_left(source, through, target):
        height = source.shape[1]
        through = through if height == through.shape[1] else through.at[:, 0:height]
        copy = pltpu.make_async_copy(source, through, load_sem)
        copy.start()
        copy.wait()

        def block(index, carry):
            rows = pl.ds(pl.multiple_of(index * LANES, LANES), LANES)
            target[0:height, rows] = through[rows, :].T
            return carry

        lax.fori_loop(0, source.shape[0] // LANES, block, 0)

    def begin(copy):
        copy.start()

    def finish(copy):
        copy.wait()

    def inside(job, count):
        return jnp.logical_and(job >= 0, job < count)

    core_peer = device(z, y, 1 - core, x)
    own_rows = own_ref.shape[0]
    tile_rows = pre_tile.shape[1]
    hidden = pre_ref.shape[1]
    half_tiles = own_rows // tile_rows

    def own_span(side):
        return pl.ds(pl.multiple_of(side * own_rows, 256), own_rows)

    own_copy = remote(own_ref, all_out.at[own_span(core), :], own_sems, (), core_peer)
    own_copy.start()
    all_out[own_span(core), :] = own_ref[...]
    bias_out[...] = jnp.zeros_like(bias_out)

    def tile_span(tile):
        side = jnp.where(tile < half_tiles, 1 - core, core)
        begin_row = side * own_rows + lax.rem(tile, half_tiles) * tile_rows
        return pl.ds(pl.multiple_of(begin_row, 256), tile_rows)

    def part_span(tile):
        return pl.ds(pl.multiple_of(lax.rem(tile, half_tiles) * tile_rows, 256), tile_rows)

    def pre_copy(tile, slot):
        return pltpu.make_async_copy(pre_ref.at[tile_span(tile), :], pre_tile.at[slot], pre_sems.at[slot])

    def low_copy(tile, slot):
        return pltpu.make_async_copy(low_tile.at[slot], low_out.at[tile_span(tile), :], low_sems.at[slot])

    def part_copy(tile):
        rows = part_span(tile)
        return remote(part_send.at[rows, :], part_got.at[rows, :], part_sems, (tile,), core_peer)

    pre_copy(0, 0).start()
    chunk = 768

    def mlp_tile(tile):
        slot = lax.rem(tile, 2)
        pre_copy(tile, slot).wait()

        @pl.when(tile + 1 < 2 * half_tiles)
        def _():
            pre_copy(tile + 1, 1 - slot).start()

        @pl.when(tile == 0)
        def _():
            own_copy.wait()

        @pl.when(tile >= 2)
        def _():
            low_copy(tile - 2, slot).wait()

        grads = all_out[tile_span(tile), :]
        for at in range(0, hidden, chunk):
            span = slice(at, at + chunk)
            value = pre_tile[slot, :, span]
            square = value * value
            curve = jnp.tanh(GELU_SCALE * (value + GELU_CUBE * (square * value)))
            slope = 0.5 * (1.0 + curve) + (0.5 * GELU_SCALE) * value * (1.0 - curve * curve) * (
                1.0 + (3.0 * GELU_CUBE) * square
            )
            grad = slope * dot_nt(grads, down_ref[span, :])
            bias_out[0:1, span] += jnp.sum(grad, axis=0, keepdims=True)
            low_tile[slot, :, span] = grad.astype(bf16)
        low_copy(tile, slot).start()
        part = dot_nt(low_tile[slot], up_ref[...])

        @pl.when(tile < half_tiles)
        def _():
            part_send[part_span(tile), :] = part.astype(bf16)
            part_copy(tile).start()

        @pl.when(tile >= half_tiles)
        def _():
            in_out[part_span(tile), :] = part

    mid_jobs = mid_right.shape[1] // TILE
    in_jobs = -(-in_right.shape[1] // TILE)
    in_left_over = in_right.shape[1] % TILE
    proj_rows = mid_left.shape[1] // 32
    last_rows = last_left.shape[1] // 32

    def proj_right_do(job, slot, action):
        def copy(source, tile, columns):
            start = pl.multiple_of(tile * columns, LANES)
            return pltpu.make_async_copy(
                source.at[:, pl.ds(start, columns)], proj_right.at[slot, :, pl.ds(0, columns)], proj_load.at[slot]
            )

        @pl.when(job < mid_jobs)
        def _():
            action(copy(mid_right, job, TILE))

        full = in_jobs - (1 if in_left_over else 0)

        @pl.when(inside(job - mid_jobs, full))
        def _():
            action(copy(in_right, job - mid_jobs, TILE))

        if in_left_over:

            @pl.when(job == mid_jobs + full)
            def _():
                rest = pltpu.make_async_copy(
                    in_right.at[:, pl.ds(full * TILE, in_left_over)],
                    proj_right.at[slot, :, pl.ds(0, in_left_over)],
                    proj_load.at[slot],
                )
                action(rest)

        @pl.when(job >= mid_jobs + in_jobs)
        def _():
            action(copy(last_right, job - mid_jobs - in_jobs, 2 * TILE))

    def p0_copy(slot):
        return remote(p0.at[slot, 1 - core], p0_got.at[slot], p0_sems, (slot,), device(z, y, 1 - core, x))

    def route(job):
        odd = lax.rem(job, 2)
        first = x + odd * (y - x)
        second = y + odd * (x - y)
        over_x = device(z, y, core, 1 - x)
        over_y = device(z, 1 - y, core, x)
        toward = tuple(a + odd * (b - a) for a, b in zip(over_x, over_y))
        onward = tuple(b + odd * (a - b) for a, b in zip(over_x, over_y))
        return odd, first, second, toward, onward

    def p1_copy(job):
        odd, first, second, toward, onward = route(job)
        slot = lax.rem(job, SLOTS)
        return remote(p1.at[slot, 1 - first], p1_got.at[slot], p1_sems, (slot,), toward)

    def p2_copy(job):
        odd, first, second, toward, onward = route(job)
        slot = lax.rem(job, SLOTS)
        return remote(p2.at[slot, 1 - second], p2_got.at[slot], p2_sems, (slot,), onward)

    def p3_copy(slot, ahead):
        return remote(
            p3.at[slot, lax.rem(z + ahead, 4)], p3_got.at[slot, ahead - 1], p3_sems, (slot, ahead - 1), z_peer(ahead)
        )

    pltpu.make_async_copy(mid_right.at[:, pl.ds(0, TILE)], proj_right.at[0, :, pl.ds(0, TILE)], proj_load.at[0]).start()

    def proj_tick(tick):
        @pl.when(tick < proj_jobs)
        def _():
            slot = lax.rem(tick, 2)
            odd = slot
            proj_right_do(tick, slot, finish)

            @pl.when(tick + 1 < proj_jobs)
            def _():
                proj_right_do(tick + 1, 1 - slot, begin)

            for at, source in ((0, mid_left), (mid_jobs, in_left), (mid_jobs + in_jobs, last_left)):

                @pl.when(tick == at)
                def _(source=source):
                    load_left(source, proj_stage, proj_left)

            shares = [(at_y, at_core, at_x) for at_y in range(2) for at_core in range(2) for at_x in range(2)]

            @pl.when(tick < mid_jobs + in_jobs)
            def _():
                def block(at_z, carry):
                    span = pl.ds(pl.multiple_of(at_z * 8 * proj_rows, 32), 8 * proj_rows)
                    right = proj_right[slot, :, 0:TILE]
                    product = jnp.dot(proj_left[span, :], right, preferred_element_type=f32).astype(bf16)
                    for low, (at_y, at_core, at_x) in enumerate(shares):
                        p0[lax.rem(tick, SLOTS), at_core, at_x + odd * (at_y - at_x), at_y + odd * (at_x - at_y), at_z] = product[low * proj_rows : (low + 1) * proj_rows, :]
                    return carry

                lax.fori_loop(0, 4, block, 0)

            @pl.when(tick >= mid_jobs + in_jobs)
            def _():
                def block(at_z, carry):
                    span = pl.ds(pl.multiple_of(at_z * 8 * last_rows, 32), 8 * last_rows)
                    for half in range(2):
                        right = proj_right[slot, :, half * TILE : (half + 1) * TILE]
                        product = jnp.dot(proj_left[span, :], right, preferred_element_type=f32)
                        begin_row = half * proj_rows // 2
                        for low, (at_y, at_core, at_x) in enumerate(shares):
                            p0[lax.rem(tick, SLOTS), at_core, at_x + odd * (at_y - at_x), at_y + odd * (at_x - at_y), at_z, begin_row : begin_row + last_rows, :] = product[
                                low * last_rows : (low + 1) * last_rows, :
                            ].astype(bf16)
                    return carry

                lax.fori_loop(0, 4, block, 0)

        fifth = tick - 4 * GAP

        @pl.when(inside(fifth, proj_jobs))
        def _():
            slot = lax.rem(fifth, SLOTS)
            for ahead in (1, 2, 3):
                p3_copy(slot, ahead).wait()
            proj_out[fifth] = added(p3[slot, z], p3_got[slot, 0], p3_got[slot, 1], p3_got[slot, 2])

        fourth = tick - 3 * GAP

        @pl.when(inside(fourth, proj_jobs))
        def _():
            slot = lax.rem(fourth, SLOTS)
            odd, first, second, toward, onward = route(fourth)
            p2_copy(fourth).wait()
            p3[slot] = added(p2[slot, second], p2_got[slot]).astype(bf16)
            for ahead in (1, 2, 3):
                p3_copy(slot, ahead).start()

        third = tick - 2 * GAP

        @pl.when(inside(third, proj_jobs))
        def _():
            slot = lax.rem(third, SLOTS)
            odd, first, second, toward, onward = route(third)
            p1_copy(third).wait()
            p2[slot] = added(p1[slot, first], p1_got[slot]).astype(bf16)
            p2_copy(third).start()

        second_job = tick - GAP

        @pl.when(inside(second_job, proj_jobs))
        def _():
            slot = lax.rem(second_job, SLOTS)
            p0_copy(slot).wait()
            p1[slot] = added(p0[slot, core], p0_got[slot]).astype(bf16)
            p1_copy(second_job).start()

        @pl.when(tick < proj_jobs)
        def _():
            p0_copy(lax.rem(tick, SLOTS)).start()

    def tick_body(tick, carry):
        proj_tick(tick)

        @pl.when(jnp.logical_and(lax.rem(tick, 4) == 3, tick // 4 < 2 * half_tiles))
        def _():
            mlp_tile(tick // 4)

        return carry

    lax.fori_loop(0, max(proj_jobs + 4 * GAP, 8 * half_tiles), tick_body, 0)
    for tile in range(2 * half_tiles - 2, 2 * half_tiles):
        low_copy(tile, tile % 2).wait()
    for tile in range(half_tiles):
        part_copy(tile).wait()
    in_out[...] = in_out[...] + part_got[...].astype(f32)


def mlp_back(own, pre_act, down_weight, up_weight, mid, first, last):
    rows, width = own.shape
    hidden = pre_act.shape[1]
    proj_jobs = mid[1].shape[1] // TILE + -(-first[1].shape[1] // TILE) + last[1].shape[1] // (2 * TILE)
    proj_tokens, proj_hidden = mid[0].shape
    tile = (proj_hidden // 32, TILE)
    dma = pltpu.SemaphoreType.DMA

    def low(*lead):
        return pltpu.VMEM(lead + tile, bf16)

    return pl.pallas_call(
        functools.partial(mlp_back_kernel, proj_jobs),
        out_shape=(
            jax.ShapeDtypeStruct((2 * rows, width), bf16),
            jax.ShapeDtypeStruct((2 * rows, hidden), bf16),
            jax.ShapeDtypeStruct((rows, width), f32),
            jax.ShapeDtypeStruct((8, hidden), f32),
            jax.ShapeDtypeStruct((proj_jobs,) + tile, f32),
        ),
        in_specs=[whole_spec(), whole_spec(pl.ANY), whole_spec(), whole_spec()] + [whole_spec(pl.ANY)] * 6,
        out_specs=(whole_spec(), whole_spec(pl.ANY), whole_spec(), whole_spec(), whole_spec()),
        scratch_shapes=[
            pltpu.VMEM((2, SHORT, hidden), f32),
            pltpu.VMEM((2, SHORT, hidden), bf16),
            pltpu.VMEM((rows, width), bf16),
            pltpu.VMEM((rows, width), bf16),
            pltpu.VMEM((proj_tokens, proj_hidden), bf16),
            pltpu.VMEM((proj_hidden, proj_tokens), bf16),
            pltpu.VMEM((2, proj_tokens, 2 * TILE), bf16),
            low(SLOTS, 2, 2, 2, 4),
            low(SLOTS, 2, 2, 4),
            low(SLOTS, 2, 2, 4),
            low(SLOTS, 2, 4),
            low(SLOTS, 2, 4),
            low(SLOTS, 4),
            low(SLOTS, 4),
            low(SLOTS, 3),
            dma((2,)),
            dma((2,)),
            dma((2,)),
            dma((2, rows // SHORT)),
            dma,
            dma((2,)),
            dma((2, SLOTS)),
            dma((2, SLOTS)),
            dma((2, SLOTS)),
            dma((2, SLOTS, 3)),
        ],
        compiler_params=pltpu.CompilerParams(
            collective_id=3, has_side_effects=True, vmem_limit_bytes=58 << 20
        ),
        cost_estimate=pl.CostEstimate(flops=3 * 10**10, bytes_accessed=5 * 10**7, transcendentals=0),
        name="mlp_back",
    )(own, pre_act, down_weight, up_weight, *mid, *first, *last)


def fetch_kernel(
    tokens_ref,
    qkv_ref,
    out_ref,
    cond_ref,
    bias_ref,
    ids_ref,
    ada_ref,
    ada_bias_ref,
    up_ref,
    down_ref,
    tokens_out,
    qkv_out,
    out_out,
    cond_out,
    bias_out,
    ids_out,
    mod_out,
    up_out,
    down_out,
    ada_tile,
    token_hold,
    qkv_hold,
    out_hold,
    up_hold,
    down_hold,
    token_sems,
    cond_sems,
    x_sems,
    y_sems,
    z_sems,
    local_sems,
    ada_sems,
):
    dp = lax.axis_index("dp")
    x = lax.axis_index("tensor")
    core = dp % 2
    y = (dp // 2) % 2
    z = dp // 4
    z_near = lax.rem(z, 2)
    home = core == x
    away = core != x
    pieces = x_sems.shape[1]
    quarter = qkv_ref.shape[0] // 4
    height = quarter // (pieces - 1)
    out_quarter = out_ref.shape[0] // 4

    def device(z_at, y_at, core_at, x_at):
        return ((z_at * 2 + y_at) * 2 + core_at, x_at)

    core_peer = device(z, y, 1 - core, x)
    swap_peer = device(z, y, x, core)
    y_peer = device(z, 1 - y, core, x)
    z_peer = device(z + 1 - 2 * z_near, y, core, x)
    barrier = pltpu.get_barrier_semaphore()
    peers = [core_peer, device(z, y, core, 1 - x), device(z, y, 1 - core, 1 - x), y_peer, z_peer]
    for peer in peers:
        pl.semaphore_signal(barrier, inc=1, device_id=peer, device_id_type=MESH)
    pl.semaphore_wait(barrier, len(peers))

    def remote(source, target, sems, index, peer):
        return pltpu.make_async_remote_copy(
            src_ref=source,
            dst_ref=target,
            send_sem=sems.at[(0,) + index],
            recv_sem=sems.at[(1,) + index],
            device_id=peer,
            device_id_type=MESH,
        )

    def part(whole, other, y_at, piece):
        at = y_at * 2 + z_near
        if piece == pieces - 1:
            return other.at[pl.ds(pl.multiple_of(at * out_quarter, 16), out_quarter), :]
        return whole.at[pl.ds(pl.multiple_of(at * quarter + piece * height, 32), height), :]

    def x_copy(piece):
        source = part(qkv_ref, out_ref, y, piece)
        return remote(source, part(qkv_out, out_out, y, piece), x_sems, (piece,), swap_peer)

    def y_copy(piece):
        here = part(qkv_out, out_out, y, piece)
        return remote(here, here, y_sems, (piece,), y_peer)

    def z_copy(piece, other):
        here = part(qkv_out, out_out, 1 - y if other else y, piece)
        return remote(here, here, z_sems, (int(other), piece), z_peer)

    token_copy = remote(tokens_ref, tokens_out, token_sems, (), swap_peer)
    cond_copy = remote(cond_ref, cond_out, cond_sems, (0,), core_peer)
    ids_copy = remote(ids_ref, ids_out, cond_sems, (1,), core_peer)
    bias_copy = remote(bias_ref, bias_out, cond_sems, (2,), swap_peer)
    local_in = [
        pltpu.make_async_copy(tokens_ref, token_hold, local_sems.at[0]),
        pltpu.make_async_copy(qkv_ref, qkv_hold, local_sems.at[1]),
        pltpu.make_async_copy(out_ref, out_hold, local_sems.at[2]),
    ]
    local_out = [
        pltpu.make_async_copy(token_hold, tokens_out, local_sems.at[3]),
        pltpu.make_async_copy(qkv_hold, qkv_out, local_sems.at[4]),
        pltpu.make_async_copy(out_hold, out_out, local_sems.at[5]),
    ]

    halves_in, halves_out = [], []
    for at, (source, hold, target) in enumerate(((up_ref, up_hold, up_out), (down_ref, down_hold, down_out))):
        rows = pl.ds(pl.multiple_of(y * hold.shape[0], 64), hold.shape[0])
        halves_in.append(pltpu.make_async_copy(source.at[rows, :], hold, local_sems.at[6 + at]))
        halves_out.append(pltpu.make_async_copy(hold, target, local_sems.at[8 + at]))

    @pl.when(away)
    def _():
        for piece in range(pieces):
            x_copy(piece).start()
        bias_copy.start()

    for copy in halves_in:
        copy.start()

    @pl.when(home)
    def _():
        cond_copy.start()
        ids_copy.start()
        for copy in local_in:
            copy.start()
        cond_out[...] = cond_ref[...]
        ids_out[...] = ids_ref[...]
        bias_out[...] = bias_ref[...]

    tile_cols = ada_tile.shape[2]
    tiles = ada_ref.shape[1] // tile_cols

    def ada_copy(tile, slot):
        columns = pl.ds(tile * tile_cols, tile_cols)
        return pltpu.make_async_copy(ada_ref.at[:, columns], ada_tile.at[slot], ada_sems.at[slot])

    ada_copy(0, 0).start()

    @pl.when(away)
    def _():
        cond_copy.wait_recv()

    cond = cond_out[...].astype(f32)
    low = (cond / (1.0 + jnp.exp(-cond))).astype(bf16)

    def modulate(tile):
        slot = tile % 2
        ada_copy(tile, slot).wait()

        if tile + 1 < tiles:
            ada_copy(tile + 1, 1 - slot).start()

        columns = slice(tile * tile_cols, (tile + 1) * tile_cols)
        product = jnp.dot(low, ada_tile[slot], preferred_element_type=f32)
        mod_out[:, columns] = product + ada_bias_ref[:, columns].astype(f32)

    for tile in range(tiles):
        modulate(tile)
        if tile % 2 == 1 and tile // 2 < pieces:

            @pl.when(away)
            def _(piece=tile // 2):
                x_copy(piece).wait_recv()
                y_copy(piece).start()
                z_copy(piece, False).start()
                if piece == 0:
                    token_copy.start()

    for copy, onward in zip(halves_in, halves_out):
        copy.wait()
        onward.start()

    @pl.when(away)
    def _():
        for piece in range(pieces):
            y_copy(piece).wait_recv()
            z_copy(piece, True).start()
        token_copy.wait()
        ids_copy.wait_recv()
        bias_copy.wait()
        for piece in range(pieces):
            x_copy(piece).wait_send()
            y_copy(piece).wait_send()
            z_copy(piece, False).wait()
            z_copy(piece, True).wait()

    @pl.when(home)
    def _():
        cond_copy.wait_send()
        ids_copy.wait_send()
        for copy, onward in zip(local_in, local_out):
            copy.wait()
            onward.start()
        for copy in local_out:
            copy.wait()

    for copy in halves_out:
        copy.wait()


def fetch(tokens, qkv, out, condition, bias, ids, ada_weight, ada_bias, up, down):
    pieces = 4
    dma = pltpu.SemaphoreType.DMA
    return pl.pallas_call(
        fetch_kernel,
        out_shape=(
            jax.ShapeDtypeStruct(tokens.shape, bf16),
            jax.ShapeDtypeStruct(qkv.shape, bf16),
            jax.ShapeDtypeStruct(out.shape, bf16),
            jax.ShapeDtypeStruct(condition.shape, bf16),
            jax.ShapeDtypeStruct(bias.shape, bf16),
            jax.ShapeDtypeStruct(ids.shape, jnp.int32),
            jax.ShapeDtypeStruct((condition.shape[0], ada_weight.shape[1]), f32),
            jax.ShapeDtypeStruct((up.shape[0] // 2, up.shape[1]), bf16),
            jax.ShapeDtypeStruct((down.shape[0] // 2, down.shape[1]), bf16),
        ),
        in_specs=[whole_spec(pl.ANY)] * 3 + [whole_spec()] * 3 + [whole_spec(pl.ANY), whole_spec()] + [whole_spec(pl.ANY)] * 2,
        out_specs=(whole_spec(pl.ANY),) * 3 + (whole_spec(),) * 4 + (whole_spec(pl.ANY),) * 2,
        scratch_shapes=[
            pltpu.VMEM((2, ada_weight.shape[0], ada_weight.shape[1] // 9), bf16),
            pltpu.VMEM(tokens.shape, bf16),
            pltpu.VMEM(qkv.shape, bf16),
            pltpu.VMEM(out.shape, bf16),
            pltpu.VMEM((up.shape[0] // 2, up.shape[1]), bf16),
            pltpu.VMEM((down.shape[0] // 2, down.shape[1]), bf16),
            dma((2,)),
            dma((2, 3)),
            dma((2, pieces)),
            dma((2, pieces)),
            dma((2, 2, pieces)),
            dma((10,)),
            dma((2,)),
        ],
        compiler_params=pltpu.CompilerParams(
            collective_id=2, has_side_effects=True, vmem_limit_bytes=56 << 20
        ),
        cost_estimate=pl.CostEstimate(flops=10**10, bytes_accessed=3 * 10**7, transcendentals=0),
        name="fetch",
    )(tokens, qkv, out, condition, bias, ids, ada_weight, ada_bias.reshape(1, -1), up, down)


def after(value, earlier):
    return lax.optimization_barrier((value, earlier))[0]


def paired_shards(
    tokens_in,
    condition,
    ada_weight,
    ada_bias,
    qkv_weight,
    qv_bias,
    out_weight,
    out_bias,
    up_weight,
    up_bias,
    down_weight,
    down_bias,
    proj_in,
    proj_in_bias,
    proj_mid,
    proj_mid_bias,
    proj_last,
    proj_last_bias,
    enc_features,
    image_ids,
    target_rows,
    out_grad,
):
    dp = lax.axis_index("dp")
    x = lax.axis_index("tensor")
    core = dp % 2
    y = (dp // 2) % 2
    z = dp // 4
    z_near = z % 2
    z_far = z // 2
    place = dp * 2 + x
    home = core == x
    group = (dp // 2) * 2 + x
    local_rows, width = tokens_in.shape
    shard_rows = image_ids.shape[0]
    slots = condition.shape[0]
    units = local_rows // SHORT
    local_cols = qkv_weight.shape[2]
    local_hidden = up_weight.shape[1]
    heads = local_cols // HEAD_DIM
    qkv_cols = -(-3 * local_cols // TILE) * TILE
    out_cols = -(-local_cols // TILE) * TILE

    def swap(value):
        return jnp.where(home, value, send(value, to_diag))

    bias_pack = jnp.concatenate([qv_bias.reshape(-1), up_bias]).reshape(-1, LANES)
    tokens, qkv_half, out_half, cond_low, bias_half, ids, modulation, up_own, down_own = fetch(
        tokens_in,
        qkv_weight.reshape(width, 3 * local_cols),
        out_weight,
        condition,
        bias_pack,
        image_ids.reshape(-1, LANES),
        ada_weight,
        ada_bias,
        up_weight,
        down_weight,
    )
    bias_half = bias_half.reshape(-1).astype(f32)
    unit_ids = ids[:: SHORT // LANES, 0]

    def over_x(own, earlier):
        return send(after(own, earlier), to_diag)

    def over_y(weight, first):
        second = send(first, to_swapped_y)
        first, second, whole = lax.optimization_barrier((first, second, weight))
        halves = whole.reshape((2,) + first.shape)
        mine = jnp.arange(2).reshape(2, 1, 1) == y
        return jnp.where(home, halves, jnp.where(mine, first[None], second[None])).reshape(weight.shape)

    up_first = over_x(up_own, tokens)
    features = jnp.where(home, enc_features, send(enc_features, to_core))
    qv_half = bias_half[: 2 * local_cols].reshape(2, local_cols)
    up_bias_half = bias_half[2 * local_cols :]

    same = unit_ids[:, None] == unit_ids[None, :]
    starts = jnp.argmax(same, axis=1).astype(jnp.int32)
    counts = jnp.sum(same.astype(jnp.int32), axis=1).astype(jnp.int32)
    my_units = lax.dynamic_slice_in_dim(unit_ids, core * units, units)
    one_hot = (my_units[:, None] == jnp.arange(slots, dtype=jnp.int32)[None, :]).astype(f32)

    silu_low = jax.nn.silu(cond_low.astype(f32)).astype(bf16)
    per_unit = jnp.dot(one_hot, modulation, precision=highest, preferred_element_type=f32)
    shift_one, scale_one, gate_one, shift_two, scale_two, gate_two = [
        piece[:, None, :] for piece in jnp.split(per_unit, 6, axis=1)
    ]

    def by_unit(array):
        return array.reshape(units, SHORT, -1)

    def flat(array):
        return array.reshape(local_rows, -1)

    def reduce_cores(left, matrix, product):
        mine = lax.dynamic_slice_in_dim(left, core * local_rows, local_rows)
        theirs = lax.dynamic_slice_in_dim(left, (1 - core) * local_rows, local_rows)
        got = send(product(theirs, matrix).astype(bf16), to_core)
        return product(mine, matrix).astype(bf16).astype(f32) + got.astype(f32)

    def dot_nn(left, right):
        return jnp.dot(left, right, preferred_element_type=f32)

    resid = by_unit(tokens.astype(f32))
    normed_one, inv_one = layer_norm(resid)
    attn_in = flat((normed_one * (1.0 + scale_one) + shift_one).astype(bf16))
    attn_all = gather_cores(attn_in)

    qkv_pad = jnp.pad(qkv_half, ((0, 0), (0, qkv_cols - 3 * local_cols)))
    out_pad = jnp.pad(out_half, ((0, out_cols - local_cols), (0, 0)))
    qkv_bias = jnp.concatenate(
        [qv_half[0], jnp.zeros_like(qv_half[0]), qv_half[1], jnp.zeros((qkv_cols - 3 * local_cols,), f32)]
    )
    qkv = (dot_nn(attn_all, qkv_pad) + qkv_bias).astype(bf16)
    qkv, up_first = lax.optimization_barrier((qkv, up_first))
    up_half = over_y(up_weight, up_first)
    down_first = over_x(down_own, up_first)
    attended, log_sums = attend(starts, counts, qkv, heads, out_cols)
    attended, down_first = lax.optimization_barrier((attended, down_first))
    down_half = over_y(down_weight, down_first)
    rows_low = swap(after(target_rows, down_first))
    grad_out = swap(after(out_grad, down_first))
    attn_branch = by_unit(reduce_cores(attended, out_pad, dot_nn) + out_bias.astype(f32))
    mid = resid + gate_one * attn_branch

    normed_two, inv_two = layer_norm(mid)
    mlp_in = flat((normed_two * (1.0 + scale_two) + shift_two).astype(bf16))
    mlp_all = gather_cores(mlp_in)
    pre_act = dot_nn(mlp_all, up_half) + up_bias_half
    hidden = gelu_tanh(pre_act).astype(bf16)
    mlp_branch = by_unit(reduce_cores(hidden, down_half, dot_nn) + down_bias.astype(f32))
    block_value = mid + gate_two * mlp_branch
    block_low = flat(block_value.astype(bf16))

    first_pre = dot_nn(block_low, proj_in) + proj_in_bias.astype(f32)
    first_value, first_back = jax.vjp(jax.nn.silu, first_pre)
    first_low = first_value.astype(bf16)
    second_pre = dot_nn(first_low, proj_mid) + proj_mid_bias.astype(f32)
    second_value, second_back = jax.vjp(jax.nn.silu, second_pre)
    second_low = second_value.astype(bf16)
    projected = dot_nn(second_low, proj_last) + proj_last_bias.astype(f32)
    chosen = (rows_low - group * shard_rows)[:, None] == jnp.arange(shard_rows, dtype=jnp.int32)[None, :]
    target_vals = dot_nn(chosen.astype(bf16), features)
    loss_back = jax.vjp(lambda predicted: align_loss(predicted, target_vals), projected)[1]
    grad_projected = loss_back(jnp.ones((), f32))[0]
    grad_last_low = grad_projected.astype(bf16)
    grad_second = second_back(dot_nt(grad_last_low, proj_last))[0]
    grad_second_low = grad_second.astype(bf16)
    grad_first = first_back(dot_nt(grad_second_low, proj_mid))[0]
    grad_first_low = grad_first.astype(bf16)
    grad_block = by_unit(grad_out.astype(f32) + dot_nt(grad_first_low, proj_in))

    grad_mlp_branch = gate_two * grad_block
    grad_mlp_all, grad_pre_low, grad_mlp_in, up_bias_sums, proj_sum = mlp_back(
        flat(grad_mlp_branch.astype(bf16)),
        pre_act,
        down_half,
        up_half,
        (grad_second_low, first_low),
        (grad_first_low, block_low),
        (grad_last_low, second_low),
    )
    grad_mlp_in = by_unit(grad_mlp_in)
    grad_mid = grad_block + norm_back(normed_two, inv_two, grad_mlp_in * (1.0 + scale_two))

    grad_attn_branch = gate_one * grad_mid
    grad_attn_all = gather_cores(flat(grad_attn_branch.astype(bf16)))
    grad_heads = dot_nt(grad_attn_all, out_pad).astype(bf16)
    grad_qkv, qkv_bias_sums = attend_back(starts, counts, qkv, log_sums, grad_heads, heads)
    grad_attn_in = by_unit(reduce_cores(grad_qkv, qkv_pad, dot_nt))
    grad_tokens = grad_mid + norm_back(normed_one, inv_one, grad_attn_in * (1.0 + scale_one))

    def unit_sum(array):
        return jnp.sum(array, axis=1)

    mod_units = jnp.concatenate(
        [
            unit_sum(grad_attn_in),
            unit_sum(grad_attn_in * normed_one),
            unit_sum(attn_branch * grad_mid),
            unit_sum(grad_mlp_in),
            unit_sum(grad_mlp_in * normed_two),
            unit_sum(mlp_branch * grad_block),
        ],
        axis=1,
    )
    slot_part = dot_tn(one_hot, mod_units, precision=highest)
    slot_grad = slot_part + send(slot_part, to_core)
    slot_low = slot_grad.astype(bf16)
    mod_cols = slot_low.shape[1] // 32
    slot_cols = pick(slot_grad.reshape(slots, 4, 2, 2, 2, mod_cols), core, 3).transpose(3, 2, 1, 0, 4)
    slot_cols = jnp.pad(slot_cols, ((0, 0),) * 3 + ((0, 8 - slots), (0, -mod_cols % LANES)))

    qv_sums = qkv_bias_sums[:2]
    qv_full = lax.dynamic_update_slice_in_dim(jnp.zeros((2, width), f32), qv_sums, core * local_cols, axis=1)
    up_full = lax.dynamic_update_slice_in_dim(
        jnp.zeros((2 * local_hidden,), f32), up_bias_sums[0], core * local_hidden, axis=0
    )
    pieces = [
        qv_full.reshape(-1),
        up_full,
        jnp.sum(flat(grad_attn_branch), axis=0),
        jnp.sum(flat(grad_mlp_branch), axis=0),
        jnp.sum(grad_first, axis=0),
        jnp.sum(grad_second, axis=0),
        jnp.sum(grad_projected, axis=0),
    ]
    packed = jnp.concatenate(pieces)
    packed = jnp.pad(packed, (0, -packed.shape[0] % (8 * LANES))).reshape(-1, LANES)
    first_sum, second_sum, sums, slot_sum, silu_sum, cond_sum = reduce_grads(
        (grad_mlp_all, hidden),
        (mlp_all, grad_pre_low),
        (attn_all, grad_qkv),
        (grad_attn_all, attended),
        packed,
        slot_cols,
        jnp.pad(silu_low, ((0, 8 - slots), (0, 0))),
        jnp.pad(slot_low, ((0, 8 - slots), (0, 0))),
        ada_weight,
    )
    grad_condition = jax.vjp(jax.nn.silu, condition.astype(f32))[1](cond_sum[:slots])[0]
    sums = sums.reshape(-1)
    slot_mine = slot_sum.reshape(16, 8, -1)[:, :slots, :mod_cols].astype(bf16).reshape(16 * slots, mod_cols)
    grad_ada = dot_tn(silu_sum.reshape(16, 8, width)[:, :slots].reshape(16 * slots, width), slot_mine)
    ada_bias_grad = jnp.sum(slot_mine.astype(f32), axis=0)
    row_count = width // 16

    def columns(tiles):
        return tiles.reshape(-1, row_count, LANES).transpose(1, 0, 2).reshape(row_count, -1)

    def rows(tiles, height):
        return tiles.reshape(-1, height, tiles.shape[-1]).transpose(0, 2, 1).reshape(-1, height)

    down_tiles = local_hidden // TILE
    sum_down = rows(first_sum[:down_tiles], row_count)
    sum_up = columns(first_sum[down_tiles:])
    qkv_tiles = qkv_cols // TILE
    sum_qkv = columns(second_sum[:qkv_tiles])[:, : 3 * local_cols].reshape(row_count, 3, local_cols)
    sum_out = rows(second_sum[qkv_tiles:], row_count)[:local_cols]
    mid_tiles = proj_mid.shape[0] // TILE
    in_tiles = -(-width // TILE)
    sum_mid = rows(proj_sum[:mid_tiles], proj_sum.shape[1])
    sum_in = rows(proj_sum[mid_tiles : mid_tiles + in_tiles], proj_sum.shape[1])[:width]
    last_share = proj_last.shape[1] // 32
    last_tiles = proj_sum[mid_tiles + in_tiles :]
    last_tiles = last_tiles.reshape(last_tiles.shape[0] * 2, -1, TILE)[:, :last_share]
    sum_last = rows(last_tiles, last_share)
    found = []
    offset = 0
    for piece in pieces:
        found.append(sums[offset : offset + piece.shape[0]])
        offset += piece.shape[0]
    qv_grad = lax.dynamic_slice_in_dim(found[0].reshape(2, width), x * local_cols, local_cols, axis=1)
    up_bias_grad = lax.dynamic_slice_in_dim(found[1], x * local_hidden, local_hidden, axis=0)

    block_out = swap(block_low)
    tokens_out = swap(flat(grad_tokens).astype(bf16))
    return (
        block_out,
        tokens_out.astype(f32),
        grad_condition,
        grad_ada,
        ada_bias_grad,
        sum_qkv,
        qv_grad,
        sum_out,
        found[2],
        sum_up,
        up_bias_grad,
        sum_down,
        found[3],
        sum_in,
        found[4],
        sum_mid,
        found[5],
        sum_last,
        found[6],
    )


def solution(mesh):
    in_specs = (
        P(("dp", "tensor"), None),
        P("dp", None),
        P(),
        P(),
        P(None, None, "tensor"),
        P(None, "tensor"),
        P("tensor", None),
        P(),
        P(None, "tensor"),
        P("tensor"),
        P("tensor", None),
        P(),
        P(),
        P(),
        P(),
        P(),
        P(),
        P(),
        P("dp", None),
        P("dp"),
        P(("dp", "tensor")),
        P(("dp", "tensor"), None),
    )
    out_specs = (
        P(("dp", "tensor"), None),
        P(("dp", "tensor"), None),
        P("dp", None),
        P(None, ("dp", "tensor")),
        P(("dp", "tensor")),
        P("dp", None, "tensor"),
        P(None, "tensor"),
        P("tensor", "dp"),
        P(),
        P("dp", "tensor"),
        P("tensor"),
        P("tensor", "dp"),
        P(),
        P(None, ("dp", "tensor")),
        P(),
        P(None, ("dp", "tensor")),
        P(),
        P(None, ("dp", "tensor")),
        P(),
    )
    paired = mesh.shape["tensor"] == 2 and mesh.shape["dp"] == 16
    body = paired_shards if paired else shards
    return jax.shard_map(body, mesh=mesh, in_specs=in_specs, out_specs=out_specs, check_vma=False)
```

```python
import functools

import jax
import jax.numpy as jnp
from jax import lax
from jax.experimental import pallas as pl
from jax.experimental.pallas import tpu as pltpu
from jax.sharding import PartitionSpec as P

HEAD_DIM = 72
SHORT = 256


highest = lax.Precision.HIGHEST
eps_norm = 1e-06
repa_weight = 1000.0
neg_fill = -1e30


def dot_nt(left_arg, right_arg):
    return lax.dot_general(
        left_arg, right_arg, (((1,), (1,)), ((), ())), preferred_element_type=jnp.float32
    )


def dot_tn(left_arg, right_arg, precision=None):
    return lax.dot_general(
        left_arg,
        right_arg,
        (((0,), (0,)), ((), ())),
        precision=precision,
        preferred_element_type=jnp.float32,
    )


def layer_norm(values):
    center = values - jnp.mean(values, axis=-1, keepdims=True)
    inv_std = lax.rsqrt(jnp.mean(center * center, axis=-1, keepdims=True) + eps_norm)
    return (center * inv_std, inv_std)


def norm_back(normed, inv_std, grad_normed):
    return inv_std * (
        grad_normed
        - jnp.mean(grad_normed, axis=-1, keepdims=True)
        - normed * jnp.mean(grad_normed * normed, axis=-1, keepdims=True)
    )


def gelu_tanh(values):
    return jax.nn.gelu(values, approximate=True)


def align_loss(projected, target_vals):
    inner = jnp.sum(projected * target_vals, axis=1)
    norm_pred = lax.rsqrt(jnp.sum(projected * projected, axis=1) + eps_norm)
    norm_target = lax.rsqrt(jnp.sum(target_vals * target_vals, axis=1) + eps_norm)
    return -repa_weight * jnp.sum(inner * norm_pred * norm_target)


def block_rows(total_rows, unit_rows):
    count = total_rows // unit_rows
    best = 1
    for parts in range(1, count + 1):
        if count % parts == 0 and parts * unit_rows <= 1024:
            best = parts
    return best * unit_rows


def block_scores(queries, key_rows, image_ids, row_start, starts, block_len, score_scale):
    query_blk = queries[row_start : row_start + block_len]
    row_ids = image_ids[row_start : row_start + block_len]
    pieces = []
    for col_start in starts:

        def compute_block(col_start=col_start):
            products = (
                jnp.einsum(
                    "qhd,khd->hqk",
                    query_blk,
                    key_rows[col_start : col_start + block_len],
                    preferred_element_type=jnp.float32,
                )
                * score_scale
            )
            same_image = row_ids[:, None] == image_ids[col_start : col_start + block_len][None, :]
            return jnp.where(same_image[None], products, neg_fill)

        pieces.append(compute_block())
    return jnp.concatenate(pieces, axis=2)


def attention_forward(queries, key_rows, values, image_ids, block_len, score_scale):
    starts = list(range(0, queries.shape[0], block_len))
    outputs = []
    log_sums = []
    for row_start in starts:
        scores = block_scores(
            queries, key_rows, image_ids, row_start, starts, block_len, score_scale
        )
        row_max = jnp.max(scores, axis=2, keepdims=True)
        exponent = jnp.exp(scores - row_max)
        row_total = jnp.sum(exponent, axis=2, keepdims=True)
        prob_low = (exponent / row_total).astype(jnp.bfloat16)
        log_sums.append(row_max + jnp.log(row_total))
        summed = jnp.zeros((block_len, queries.shape[1], queries.shape[2]), jnp.float32)
        for position, col_start in enumerate(starts):

            def weigh_block(position=position, col_start=col_start, prob_low=prob_low):
                return jnp.einsum(
                    "hqk,khd->qhd",
                    prob_low[:, :, position * block_len : (position + 1) * block_len],
                    values[col_start : col_start + block_len],
                    preferred_element_type=jnp.float32,
                )

            summed = summed + weigh_block()
        outputs.append(summed.astype(jnp.bfloat16))
    return (jnp.concatenate(outputs, axis=0), jnp.concatenate(log_sums, axis=1))


def attention_backward(
    queries, key_rows, values, image_ids, log_sums, grad_heads, block_len, score_scale
):
    starts = list(range(0, queries.shape[0], block_len))
    grad_keys = jnp.zeros(key_rows.shape, jnp.float32)
    grad_values = jnp.zeros(values.shape, jnp.float32)
    grad_query_list = []
    for row_start in starts:
        query_blk = queries[row_start : row_start + block_len]
        grad_blk = grad_heads[row_start : row_start + block_len]
        scores = block_scores(
            queries, key_rows, image_ids, row_start, starts, block_len, score_scale
        )
        soft = jnp.exp(scores - log_sums[:, row_start : row_start + block_len])
        grad_pieces = []
        for col_start in starts:

            def pull_block(col_start=col_start):
                return jnp.einsum(
                    "qhd,khd->hqk",
                    grad_blk,
                    values[col_start : col_start + block_len],
                    preferred_element_type=jnp.float32,
                )

            grad_pieces.append(pull_block())
        grad_soft = jnp.concatenate(grad_pieces, axis=2)
        inner = jnp.sum(soft * grad_soft, axis=2, keepdims=True)
        grad_scores = (soft * (grad_soft - inner)).astype(jnp.bfloat16)
        soft_low = soft.astype(jnp.bfloat16)
        grad_query = jnp.zeros(query_blk.shape, jnp.float32)
        for position, col_start in enumerate(starts):

            def both_grads(position=position, col_start=col_start):
                piece = grad_scores[:, :, position * block_len : (position + 1) * block_len]
                soft_piece = soft_low[:, :, position * block_len : (position + 1) * block_len]
                return (
                    jnp.einsum(
                        "hqk,khd->qhd",
                        piece,
                        key_rows[col_start : col_start + block_len],
                        preferred_element_type=jnp.float32,
                    ),
                    jnp.einsum(
                        "hqk,qhd->khd", piece, query_blk, preferred_element_type=jnp.float32
                    ),
                    jnp.einsum(
                        "hqk,qhd->khd", soft_piece, grad_blk, preferred_element_type=jnp.float32
                    ),
                )

            part_query, part_key, part_value = both_grads()
            grad_query = grad_query + part_query
            grad_keys = grad_keys.at[col_start : col_start + block_len].add(part_key)
            grad_values = grad_values.at[col_start : col_start + block_len].add(part_value)
        grad_query_list.append(grad_query * score_scale)
    return (jnp.concatenate(grad_query_list, axis=0), grad_keys * score_scale, grad_values)


def column_set(matrix, data_count, tensor_count, tensor_rank):
    shaped = matrix.reshape(matrix.shape[0], data_count, tensor_count, -1)
    return lax.dynamic_index_in_dim(shaped, tensor_rank, axis=2, keepdims=False).reshape(
        matrix.shape[0], -1
    )


def shards(
    tokens_in,
    condition,
    ada_weight,
    ada_bias,
    qkv_weight,
    qv_bias,
    out_weight,
    out_bias,
    up_weight,
    up_bias,
    down_weight,
    down_bias,
    proj_in,
    proj_in_bias,
    proj_mid,
    proj_mid_bias,
    proj_last,
    proj_last_bias,
    enc_features,
    image_ids,
    target_rows,
    out_grad,
):
    tensor_count = lax.axis_size("tensor")
    data_count = lax.axis_size("dp")
    tensor_rank = lax.axis_index("tensor")
    data_rank = lax.axis_index("dp")
    local_rows, model_width = tokens_in.shape
    shard_rows = image_ids.shape[0]
    slot_count = condition.shape[0]
    local_cols = qkv_weight.shape[2]
    local_hidden = up_weight.shape[1]
    head_count = local_cols // HEAD_DIM
    score_scale = HEAD_DIM ** (-0.5)
    block_len = block_rows(shard_rows, SHORT)
    my_ids = lax.dynamic_slice_in_dim(image_ids, tensor_rank * local_rows, local_rows)
    one_hot = (my_ids[:, None] == jnp.arange(slot_count, dtype=jnp.int32)[None, :]).astype(
        jnp.float32
    )
    cond_float = condition.astype(jnp.float32)
    silu_cond, silu_back = jax.vjp(jax.nn.silu, cond_float)
    silu_low = silu_cond.astype(jnp.bfloat16)
    modulation = jnp.dot(
        silu_low, ada_weight, preferred_element_type=jnp.float32
    ) + ada_bias.astype(jnp.float32)
    per_token = jnp.dot(one_hot, modulation, precision=highest, preferred_element_type=jnp.float32)
    shift_one, scale_one, gate_one, shift_two, scale_two, gate_two = jnp.split(per_token, 6, axis=1)
    resid = tokens_in.astype(jnp.float32)
    normed_one, inv_one = layer_norm(resid)
    attn_in = (normed_one * (1.0 + scale_one) + shift_one).astype(jnp.bfloat16)
    attn_all = lax.all_gather(attn_in, "tensor", axis=0, tiled=True)
    qkv_flat_weight = qkv_weight.reshape(model_width, 3 * local_cols)
    qkv_flat = jnp.dot(attn_all, qkv_flat_weight, preferred_element_type=jnp.float32)
    bias_float = qv_bias.astype(jnp.float32)
    queries = (
        (qkv_flat[:, :local_cols] + bias_float[0])
        .astype(jnp.bfloat16)
        .reshape(shard_rows, head_count, HEAD_DIM)
    )
    key_rows = (
        qkv_flat[:, local_cols : 2 * local_cols]
        .astype(jnp.bfloat16)
        .reshape(shard_rows, head_count, HEAD_DIM)
    )
    values = (
        (qkv_flat[:, 2 * local_cols :] + bias_float[1])
        .astype(jnp.bfloat16)
        .reshape(shard_rows, head_count, HEAD_DIM)
    )
    attended, log_sums = attention_forward(
        queries, key_rows, values, image_ids, block_len, score_scale
    )
    attended = attended.reshape(shard_rows, local_cols)
    attn_branch = lax.psum_scatter(
        jnp.dot(attended, out_weight, preferred_element_type=jnp.float32).astype(jnp.bfloat16),
        "tensor",
        scatter_dimension=0,
        tiled=True,
    ).astype(jnp.float32) + out_bias.astype(jnp.float32)
    mid = resid + gate_one * attn_branch
    normed_two, inv_two = layer_norm(mid)
    mlp_in = (normed_two * (1.0 + scale_two) + shift_two).astype(jnp.bfloat16)
    mlp_all = lax.all_gather(mlp_in, "tensor", axis=0, tiled=True)
    pre_act = jnp.dot(mlp_all, up_weight, preferred_element_type=jnp.float32) + up_bias.astype(
        jnp.float32
    )
    act_value, act_back = jax.vjp(gelu_tanh, pre_act)
    hidden = act_value.astype(jnp.bfloat16)
    mlp_branch = lax.psum_scatter(
        jnp.dot(hidden, down_weight, preferred_element_type=jnp.float32).astype(jnp.bfloat16),
        "tensor",
        scatter_dimension=0,
        tiled=True,
    ).astype(jnp.float32) + down_bias.astype(jnp.float32)
    block_value = mid + gate_two * mlp_branch
    block_low = block_value.astype(jnp.bfloat16)
    first_pre = jnp.dot(
        block_low, proj_in, preferred_element_type=jnp.float32
    ) + proj_in_bias.astype(jnp.float32)
    first_value, first_back = jax.vjp(jax.nn.silu, first_pre)
    first_low = first_value.astype(jnp.bfloat16)
    second_pre = jnp.dot(
        first_low, proj_mid, preferred_element_type=jnp.float32
    ) + proj_mid_bias.astype(jnp.float32)
    second_value, second_back = jax.vjp(jax.nn.silu, second_pre)
    second_low = second_value.astype(jnp.bfloat16)
    projected = jnp.dot(
        second_low, proj_last, preferred_element_type=jnp.float32
    ) + proj_last_bias.astype(jnp.float32)
    target_vals = jnp.take(enc_features, target_rows - data_rank * shard_rows, axis=0).astype(
        jnp.float32
    )
    loss_value, loss_back = jax.vjp(lambda predicted: align_loss(predicted, target_vals), projected)
    grad_projected = loss_back(jnp.ones((), jnp.float32))[0]
    grad_last_low = grad_projected.astype(jnp.bfloat16)
    grad_second = second_back(dot_nt(grad_last_low, proj_last))[0]
    grad_second_low = grad_second.astype(jnp.bfloat16)
    grad_first = first_back(dot_nt(grad_second_low, proj_mid))[0]
    grad_first_low = grad_first.astype(jnp.bfloat16)
    grad_block = out_grad.astype(jnp.float32) + dot_nt(grad_first_low, proj_in)
    gate_two_grad = mlp_branch * grad_block
    grad_mlp_branch = gate_two * grad_block
    grad_mlp_all = lax.all_gather(
        grad_mlp_branch.astype(jnp.bfloat16), "tensor", axis=0, tiled=True
    )
    grad_down_local = dot_tn(hidden, grad_mlp_all)
    grad_pre = act_back(dot_nt(grad_mlp_all, down_weight))[0]
    grad_pre_low = grad_pre.astype(jnp.bfloat16)
    grad_up_local = dot_tn(mlp_all, grad_pre_low)
    up_bias_local = jnp.sum(grad_pre, axis=0)
    grad_mlp_in = lax.psum_scatter(
        dot_nt(grad_pre_low, up_weight).astype(jnp.bfloat16),
        "tensor",
        scatter_dimension=0,
        tiled=True,
    ).astype(jnp.float32)
    scale_two_grad = grad_mlp_in * normed_two
    grad_mid = grad_block + norm_back(normed_two, inv_two, grad_mlp_in * (1.0 + scale_two))
    gate_one_grad = attn_branch * grad_mid
    grad_attn_branch = gate_one * grad_mid
    grad_attn_all = lax.all_gather(
        grad_attn_branch.astype(jnp.bfloat16), "tensor", axis=0, tiled=True
    )
    grad_out_local = dot_tn(attended, grad_attn_all)
    grad_heads = (
        dot_nt(grad_attn_all, out_weight)
        .astype(jnp.bfloat16)
        .reshape(shard_rows, head_count, HEAD_DIM)
    )
    grad_queries, grad_keys, grad_values = attention_backward(
        queries, key_rows, values, image_ids, log_sums, grad_heads, block_len, score_scale
    )
    grad_queries = grad_queries.reshape(shard_rows, local_cols)
    grad_keys = grad_keys.reshape(shard_rows, local_cols)
    grad_values = grad_values.reshape(shard_rows, local_cols)
    qv_local = jnp.stack([jnp.sum(grad_queries, axis=0), jnp.sum(grad_values, axis=0)])
    grad_qkv_low = jnp.concatenate([grad_queries, grad_keys, grad_values], axis=1).astype(
        jnp.bfloat16
    )
    grad_qkv_local = dot_tn(attn_all, grad_qkv_low).reshape(model_width, 3, local_cols)
    grad_attn_in = lax.psum_scatter(
        dot_nt(grad_qkv_low, qkv_flat_weight).astype(jnp.bfloat16),
        "tensor",
        scatter_dimension=0,
        tiled=True,
    ).astype(jnp.float32)
    scale_one_grad = grad_attn_in * normed_one
    grad_tokens = grad_mid + norm_back(normed_one, inv_one, grad_attn_in * (1.0 + scale_one))
    token_mod_grad = jnp.concatenate(
        [grad_attn_in, scale_one_grad, gate_one_grad, grad_mlp_in, scale_two_grad, gate_two_grad],
        axis=1,
    )
    slot_grad_part = dot_tn(one_hot, token_mod_grad, precision=highest)
    slot_grad = lax.psum(slot_grad_part.astype(jnp.bfloat16), "tensor").astype(jnp.float32)
    slot_low = slot_grad.astype(jnp.bfloat16)
    grad_condition = silu_back(dot_nt(slot_low, ada_weight))[0]
    ada_cols = dot_tn(silu_low, column_set(slot_low, data_count, tensor_count, tensor_rank))
    ada_bias_cols = jnp.sum(
        column_set(slot_grad, data_count, tensor_count, tensor_rank), axis=0, keepdims=True
    )
    block_grads = (
        lax.psum_scatter(
            grad_qkv_local.astype(jnp.bfloat16), "dp", scatter_dimension=0, tiled=True
        ).astype(jnp.float32),
        lax.psum_scatter(
            grad_out_local.astype(jnp.bfloat16), "dp", scatter_dimension=1, tiled=True
        ).astype(jnp.float32),
        lax.psum_scatter(
            grad_up_local.astype(jnp.bfloat16), "dp", scatter_dimension=0, tiled=True
        ).astype(jnp.float32),
        lax.psum_scatter(
            grad_down_local.astype(jnp.bfloat16), "dp", scatter_dimension=1, tiled=True
        ).astype(jnp.float32),
        lax.psum_scatter(
            ada_cols.astype(jnp.bfloat16), "dp", scatter_dimension=1, tiled=True
        ).astype(jnp.float32),
        lax.psum_scatter(
            ada_bias_cols.astype(jnp.bfloat16), "dp", scatter_dimension=1, tiled=True
        ).astype(jnp.float32),
    )
    qv_full = lax.dynamic_update_slice_in_dim(
        jnp.zeros((2, model_width), jnp.float32), qv_local, tensor_rank * local_cols, axis=1
    )
    up_full = lax.dynamic_update_slice_in_dim(
        jnp.zeros((local_hidden * tensor_count,), jnp.float32),
        up_bias_local,
        tensor_rank * local_hidden,
        axis=0,
    )
    bias_sums = lax.psum(
        (
            qv_full,
            up_full,
            jnp.sum(grad_attn_branch, axis=0),
            jnp.sum(grad_mlp_branch, axis=0),
            jnp.sum(grad_first, axis=0),
            jnp.sum(grad_second, axis=0),
            jnp.sum(grad_projected, axis=0),
        ),
        ("dp", "tensor"),
    )
    qv_grad = lax.dynamic_slice_in_dim(bias_sums[0], tensor_rank * local_cols, local_cols, axis=1)
    up_bias_grad = lax.dynamic_slice_in_dim(
        bias_sums[1], tensor_rank * local_hidden, local_hidden, axis=0
    )
    proj_grads = (
        lax.psum_scatter(
            dot_tn(block_low, grad_first_low), ("dp", "tensor"), scatter_dimension=1, tiled=True
        ),
        lax.psum_scatter(
            dot_tn(first_low, grad_second_low), ("dp", "tensor"), scatter_dimension=1, tiled=True
        ),
        lax.psum_scatter(
            dot_tn(second_low, grad_last_low), ("dp", "tensor"), scatter_dimension=1, tiled=True
        ),
    )
    return (
        block_low,
        grad_tokens,
        grad_condition,
        block_grads[4],
        block_grads[5].reshape(-1),
        block_grads[0],
        qv_grad,
        block_grads[1],
        bias_sums[2],
        block_grads[2],
        up_bias_grad,
        block_grads[3],
        bias_sums[3],
        proj_grads[0],
        bias_sums[4],
        proj_grads[1],
        bias_sums[5],
        proj_grads[2],
        bias_sums[6],
    )


LANES = 128
MESH = pl.DeviceIdType.MESH
TILE = 256
GAP = 2
SLOTS = 2 * GAP
LOG2_E = 1.4426950408889634
GELU_SCALE = 0.7978845608028654
GELU_CUBE = 0.044715
bf16 = jnp.bfloat16
f32 = jnp.float32


def pairs_of(move):
    found = []
    for index in range(32):
        x, core, y, z = index % 2, (index // 2) % 2, (index // 4) % 2, index // 8
        z2, y2, c2, x2 = move(z, y, core, x)
        if (z2, y2, c2, x2) != (z, y, core, x):
            found.append((index, ((z2 * 2 + y2) * 2 + c2) * 2 + x2))
    return found


def send(value, move):
    return lax.ppermute(value, ("dp", "tensor"), pairs_of(move))


def to_diag(z, y, c, x):
    return (z, y, x, c)


def to_cycle(z, y, c, x):
    return (z, y, c, c) if c != x else (z, y, 1 - c, x)


def to_core(z, y, c, x):
    return (z, y, 1 - c, x)


def to_x(z, y, c, x):
    return (z, y, c, 1 - x)


def to_y(z, y, c, x):
    return (z, 1 - y, c, x)


def to_swapped_y(z, y, c, x):
    return (z, 1 - y, c, x) if c != x else (z, y, c, x)


def to_z_near(z, y, c, x):
    return (z ^ 1, y, c, x)


def to_z_far(z, y, c, x):
    return (z ^ 2, y, c, x)


def pick(array, index, axis):
    return lax.dynamic_index_in_dim(array, index, axis=axis, keepdims=False)


def gather_kernel(own_ref, out_ref, local_sem, send_sem, recv_sem):
    dp = lax.axis_index("dp")
    x = lax.axis_index("tensor")
    core = dp % 2
    other = dp + 1 - 2 * core
    barrier = pltpu.get_barrier_semaphore()
    pl.semaphore_signal(barrier, inc=1, device_id=(other, x), device_id_type=MESH)
    pl.semaphore_wait(barrier, 1)
    away = pltpu.make_async_remote_copy(
        src_ref=own_ref,
        dst_ref=out_ref.at[core],
        send_sem=send_sem,
        recv_sem=recv_sem,
        device_id=(other, x),
        device_id_type=MESH,
    )
    away.start()
    here = pltpu.make_async_copy(own_ref, out_ref.at[core], local_sem)
    here.start()
    here.wait()
    away.wait()


def gather_cores(own):
    rows, width = own.shape
    return pl.pallas_call(
        gather_kernel,
        out_shape=jax.ShapeDtypeStruct((2, rows, width), own.dtype),
        in_specs=[pl.BlockSpec(memory_space=pltpu.VMEM)],
        out_specs=pl.BlockSpec(memory_space=pl.ANY),
        scratch_shapes=[pltpu.SemaphoreType.DMA] * 3,
        compiler_params=pltpu.CompilerParams(collective_id=0, has_side_effects=True, vmem_limit_bytes=16 << 20),
        cost_estimate=pl.CostEstimate(flops=0, bytes_accessed=12000000, transcendentals=0),
        name="gather_cores",
    )(own).reshape(2 * rows, width)


def split_heads(flat_ref, heads_ref, parts, heads):
    heads_ref[...] = jnp.zeros_like(heads_ref)
    for part in range(parts):
        for head in range(heads):
            begin = (part * heads + head) * HEAD_DIM
            heads_ref[part * heads + head, :, 0:HEAD_DIM] = flat_ref[:, begin : begin + HEAD_DIM]


def join_heads(heads_ref, flat_ref, count):
    rows, columns = flat_ref.shape
    for block in range(rows // LANES):
        span = slice(block * LANES, (block + 1) * LANES)
        pieces = [heads_ref[head, span, 0:HEAD_DIM] for head in range(count)]
        if columns > count * HEAD_DIM:
            pieces.append(jnp.zeros((LANES, columns - count * HEAD_DIM), flat_ref.dtype))
        flat_ref[span, :] = jnp.concatenate(pieces, axis=1)


def per_image(count, run):
    @pl.when(count == 1)
    def _():
        run(SHORT)

    @pl.when(count != 1)
    def _():
        run(4 * SHORT)


def attend_kernel(heads, together, factor, starts, counts, qkv_ref, o_ref, log_ref, part_ref, o_heads):
    split_heads(qkv_ref, part_ref, 3, heads)
    unit_count = o_ref.shape[0] // SHORT

    def some_heads(step, carry):
        def unit(index, carry):
            rows = pl.ds(pl.multiple_of(index * SHORT, SHORT), SHORT)

            def run(length):
                cols = pl.ds(pl.multiple_of(starts[index] * SHORT, SHORT), length)
                for ahead in range(together):
                    head = step * together + ahead
                    scores = dot_nt(part_ref[heads + head, cols, :], part_ref[head, rows, :])
                    top = jnp.max(scores, axis=0, keepdims=True)
                    exponent = jnp.exp2((scores - top) * factor)
                    total = jnp.sum(exponent, axis=0, keepdims=True)
                    summed = dot_tn(part_ref[2 * heads + head, cols, :], exponent.astype(bf16))
                    o_heads[head, rows, :] = (summed * (1.0 / total)).T.astype(bf16)
                    log_ref[head * unit_count + index] = top * factor + jnp.log2(total)

            per_image(counts[index], run)
            return carry

        return lax.fori_loop(0, unit_count, unit, carry)

    lax.fori_loop(0, heads // together, some_heads, 0)
    join_heads(o_heads, o_ref, heads)


def whole_spec(space=pltpu.VMEM):
    return pl.BlockSpec(memory_space=space)


def attend(starts, counts, qkv, heads, out_cols):
    rows = qkv.shape[0]
    factor = HEAD_DIM ** (-0.5) * LOG2_E
    return pl.pallas_call(
        functools.partial(attend_kernel, heads, 4, factor),
        out_shape=(
            jax.ShapeDtypeStruct((rows, out_cols), bf16),
            jax.ShapeDtypeStruct((heads * (rows // SHORT), 1, SHORT), f32),
        ),
        in_specs=[whole_spec(pltpu.SMEM), whole_spec(pltpu.SMEM), whole_spec()],
        out_specs=(whole_spec(), whole_spec()),
        scratch_shapes=[
            pltpu.VMEM((3 * heads, rows, LANES), bf16),
            pltpu.VMEM((heads, rows, LANES), bf16),
        ],
        compiler_params=pltpu.CompilerParams(vmem_limit_bytes=40 << 20),
        cost_estimate=pl.CostEstimate(flops=20 * 10**9, bytes_accessed=13 * 10**6, transcendentals=10**7),
        name="attend",
    )(starts, counts, qkv)


def attend_back_kernel(
    heads,
    together,
    factor,
    starts,
    counts,
    qkv_ref,
    log_ref,
    grad_ref,
    out_ref,
    bias_ref,
    part_ref,
    grad_heads,
    key_acc,
    value_acc,
    sums,
):
    split_heads(qkv_ref, part_ref, 3, heads)
    split_heads(grad_ref, grad_heads, 1, heads)
    unit_count = out_ref.shape[0] // SHORT

    def some_heads(step, carry):
        key_acc[...] = jnp.zeros_like(key_acc)
        value_acc[...] = jnp.zeros_like(value_acc)
        for ahead in range(together):
            sums[step * together + ahead] = jnp.zeros((8, LANES), f32)

        def unit(index, carry):
            rows = pl.ds(pl.multiple_of(index * SHORT, SHORT), SHORT)

            def run(length):
                cols = pl.ds(pl.multiple_of(starts[index] * SHORT, SHORT), length)
                for ahead in range(together):
                    head = step * together + ahead
                    queries = part_ref[head, rows, :]
                    grads = grad_heads[head, rows, :]
                    keys = part_ref[heads + head, cols, :]
                    scores = dot_nt(keys, queries)
                    soft = jnp.exp2(scores * (factor * LOG2_E) - log_ref[head * unit_count + index])
                    grad_soft = dot_nt(part_ref[2 * heads + head, cols, :], grads)
                    product = soft * grad_soft
                    inner = jnp.sum(product, axis=0, keepdims=True)
                    grad_scores = (product - soft * inner).astype(bf16)
                    value_acc[ahead, cols, :] += jnp.dot(soft.astype(bf16), grads, preferred_element_type=f32)
                    key_acc[ahead, cols, :] += jnp.dot(grad_scores, queries, preferred_element_type=f32)
                    grad_query = dot_tn(keys, grad_scores).T * factor
                    sums[head, 0:1, :] += jnp.sum(grad_query, axis=0, keepdims=True)
                    part_ref[head, rows, :] = grad_query.astype(bf16)

            per_image(counts[index], run)
            return carry

        lax.fori_loop(0, unit_count, unit, 0)
        for ahead in range(together):
            head = step * together + ahead
            sums[head, 1:2, :] = jnp.sum(value_acc[ahead], axis=0, keepdims=True)
            part_ref[heads + head] = (key_acc[ahead] * factor).astype(bf16)
            part_ref[2 * heads + head] = value_acc[ahead].astype(bf16)
        return carry

    lax.fori_loop(0, heads // together, some_heads, 0)
    join_heads(part_ref, out_ref, 3 * heads)
    bias_ref[...] = jnp.concatenate([sums[head, :, 0:HEAD_DIM] for head in range(heads)], axis=1)


def attend_back(starts, counts, qkv, log_sums, grad_heads, heads):
    rows, columns = qkv.shape
    factor = HEAD_DIM ** (-0.5)
    together = 4
    return pl.pallas_call(
        functools.partial(attend_back_kernel, heads, together, factor),
        out_shape=(
            jax.ShapeDtypeStruct((rows, columns), bf16),
            jax.ShapeDtypeStruct((8, heads * HEAD_DIM), f32),
        ),
        in_specs=[whole_spec(pltpu.SMEM), whole_spec(pltpu.SMEM)] + [whole_spec()] * 3,
        out_specs=(whole_spec(), whole_spec()),
        scratch_shapes=[
            pltpu.VMEM((3 * heads, rows, LANES), bf16),
            pltpu.VMEM((heads, rows, LANES), bf16),
            pltpu.VMEM((together, rows, LANES), f32),
            pltpu.VMEM((together, rows, LANES), f32),
            pltpu.VMEM((heads, 8, LANES), f32),
        ],
        compiler_params=pltpu.CompilerParams(vmem_limit_bytes=48 << 20),
        cost_estimate=pl.CostEstimate(flops=40 * 10**9, bytes_accessed=25 * 10**6, transcendentals=10**7),
        name="attend_back",
    )(starts, counts, qkv, log_sums, grad_heads)


def reduce_kernel(
    grid_rows,
    first_jobs,
    second_jobs,
    one_left,
    one_right,
    two_left,
    two_right,
    three_left,
    three_right,
    four_left,
    four_right,
    bias_ref,
    slot_ref,
    silu_ref,
    slot_low_ref,
    ada_ref,
    first_out,
    second_out,
    bias_out,
    slot_out,
    silu_out,
    cond_out,
    stage,
    first_left,
    second_left,
    first_right,
    second_right,
    f0,
    f0_turn,
    f0_swap,
    f1,
    f1_got,
    f2,
    f2_got,
    f3,
    f3_got,
    s0,
    s0_got,
    s1,
    s1_got,
    far,
    far_got,
    s2,
    s2_turn,
    s2_swap,
    bias_got,
    slot_x,
    slot_y,
    slot_y_got,
    slot_z,
    slot_z_got,
    silu_x,
    silu_y,
    silu_y_got,
    silu_z,
    silu_z_got,
    ada_tile,
    cond_acc,
    load_sem,
    first_load,
    second_load,
    f0_sems,
    f1_sems,
    f2_sems,
    f3_sems,
    s0_sems,
    s1_sems,
    far_sems,
    s2_sems,
    bias_sems,
    slot_sems,
    slot_z_sems,
    silu_sems,
    silu_z_sems,
    ada_sems,
    cond_sems,
    first_free,
    second_free,
):
    dp = lax.axis_index("dp")
    x = lax.axis_index("tensor")
    core = dp % 2
    y = (dp // 2) % 2
    z = dp // 4
    home = core == x
    away = core != x

    def device(z_at, y_at, core_at, x_at):
        return ((z_at * 2 + y_at) * 2 + core_at, x_at)

    turn_to = device(z, y, core + (1 - 2 * core) * (1 - jnp.abs(core - x)), x + (core - x))
    turn_from = device(z, y, x + 0 * core, x + (1 - 2 * x) * (1 - jnp.abs(core - x)))
    swap_peer = device(z, y, x, core)
    y_peer = device(z, 1 - y, core, x)

    def z_peer(ahead):
        return device(lax.rem(z + ahead, 4), y, core, x)

    barrier = pltpu.get_barrier_semaphore()
    near = [device(z, y, 1 - core, x), device(z, y, core, 1 - x), device(z, y, 1 - core, 1 - x), y_peer]
    for peer in near + [z_peer(1), z_peer(2), z_peer(3)]:
        pl.semaphore_signal(barrier, inc=1, device_id=peer, device_id_type=MESH)
    pl.semaphore_wait(barrier, 7)

    def remote(source, target, sems, index, peer):
        return pltpu.make_async_remote_copy(
            src_ref=source,
            dst_ref=target,
            send_sem=sems.at[(0,) + index],
            recv_sem=sems.at[(1,) + index],
            device_id=peer,
            device_id_type=MESH,
        )

    def added(*terms):
        total = terms[0].astype(f32)
        for term in terms[1:]:
            total = total + term.astype(f32)
        return total

    def load_left(source, through, target):
        height = source.shape[1]
        through = through if height == through.shape[1] else through.at[:, 0:height]
        copy = pltpu.make_async_copy(source, through, load_sem)
        copy.start()
        copy.wait()

        def block(index, carry):
            rows = pl.ds(pl.multiple_of(index * LANES, LANES), LANES)
            target[0:height, rows] = through[rows, :].T
            return carry

        lax.fori_loop(0, source.shape[0] // LANES, block, 0)

    def right_copy(source, tile, target, sems, slot):
        columns = pl.ds(pl.multiple_of(tile * TILE, TILE), TILE)
        return pltpu.make_async_copy(source.at[:, columns], target.at[slot], sems.at[slot])

    first_split = one_right.shape[1] // TILE
    second_split = three_right.shape[1] // TILE

    def first_right_do(job, slot, action):
        @pl.when(job < first_split)
        def _():
            action(right_copy(one_right, job, first_right, first_load, slot))

        @pl.when(job >= first_split)
        def _():
            action(right_copy(two_right, job - first_split, first_right, first_load, slot))

    def second_right_do(job, slot, action):
        @pl.when(job < second_split)
        def _():
            action(right_copy(three_right, job, second_right, second_load, slot))

        @pl.when(job >= second_split)
        def _():
            action(right_copy(four_right, job - second_split, second_right, second_load, slot))

    def begin(copy):
        copy.start()

    def finish(copy):
        copy.wait()

    def multiply(left, right, slot, keep):
        def block(at_z, carry):
            height = 4 * grid_rows
            span = pl.ds(pl.multiple_of(at_z * height, 32), height)
            product = jnp.dot(left[span, :], right[slot], preferred_element_type=f32)
            for at_y in range(2):
                for at_core in range(2):
                    low = (at_y * 2 + at_core) * grid_rows
                    part = product[low : low + grid_rows, :]
                    stacked = jnp.concatenate([part[:, :LANES], part[:, LANES:]], axis=0)
                    keep(at_z, at_y, at_core, stacked.astype(bf16))
            return carry

        lax.fori_loop(0, 4, block, 0)

    def f0_copies(slot):
        turn = remote(f0.at[slot, 1 - x], f0_turn.at[slot], f0_sems, (0, slot), turn_to)
        swap = remote(f0.at[slot, x], f0_swap.at[slot], f0_sems, (1, slot), swap_peer)
        return turn, swap

    def f1_copy(slot):
        return remote(f1.at[slot, 1 - y], f1_got.at[slot], f1_sems, (slot,), y_peer)

    z_low = lax.rem(z, 2)
    z_high = z // 2
    near_peer = device(z + 1 - 2 * z_low, y, core, x)
    far_peer = device(lax.rem(z + 2, 4), y, core, x)

    def f2_copy(slot):
        return remote(f2.at[slot, 1 - z_low], f2_got.at[slot], f2_sems, (slot,), near_peer)

    def f3_copy(slot):
        return remote(f3.at[slot, 1 - z_high], f3_got.at[slot], f3_sems, (slot,), far_peer)

    def s0_copy(slot):
        return remote(s0.at[slot, 1 - y], s0_got.at[slot], s0_sems, (slot,), y_peer)

    def s1_copy(slot):
        return remote(s1.at[slot, 1 - z_low], s1_got.at[slot], s1_sems, (slot,), near_peer)

    def far_copy(slot):
        return remote(far.at[slot, 1 - z_high], far_got.at[slot], far_sems, (slot,), far_peer)

    def s2_copies(slot):
        turn = remote(s2.at[slot, 1 - x], s2_turn.at[slot], s2_sems, (0, slot), turn_to)
        swap = remote(s2.at[slot, x], s2_swap.at[slot], s2_sems, (1, slot), swap_peer)
        return turn, swap

    def inside(job, count):
        return jnp.logical_and(job >= 0, job < count)

    first_right_do(0, 0, begin)
    second_right_do(0, 0, begin)

    def first_tick(tick):
        @pl.when(tick < first_jobs)
        def _():
            slot = lax.rem(tick, 2)
            first_right_do(tick, slot, finish)

            @pl.when(tick + 1 < first_jobs)
            def _():
                first_right_do(tick + 1, 1 - slot, begin)

            @pl.when(tick == 0)
            def _():
                load_left(one_left, stage, first_left)

            @pl.when(tick == first_split)
            def _():
                load_left(two_left, stage, first_left)

            def keep(at_z, at_y, at_core, value):
                f0[lax.rem(tick, SLOTS), at_core, at_y, at_z] = value

            multiply(first_left, first_right, slot, keep)

        last = tick - 4 * GAP

        @pl.when(inside(last, first_jobs))
        def _():
            slot = lax.rem(last, SLOTS)
            f3_copy(slot).wait()
            first_out[last] = added(f3[slot, z_high], f3_got[slot])

        fourth = tick - 3 * GAP

        @pl.when(inside(fourth, first_jobs))
        def _():
            slot = lax.rem(fourth, SLOTS)
            f2_copy(slot).wait()
            f3[slot] = added(f2[slot, z_low], f2_got[slot]).astype(bf16)
            f3_copy(slot).start()

        third = tick - 2 * GAP

        @pl.when(inside(third, first_jobs))
        def _():
            slot = lax.rem(third, SLOTS)
            f1_copy(slot).wait()
            for low in range(2):
                for high in range(2):
                    at = high * 2 + low
                    f2[slot, low, high] = added(f1[slot, y, at], f1_got[slot, at]).astype(bf16)
            f2_copy(slot).start()

        second = tick - GAP

        @pl.when(inside(second, first_jobs))
        def _():
            slot = lax.rem(second, SLOTS)
            turn, swap = f0_copies(slot)
            turn.wait()

            @pl.when(home)
            def _():
                f1[slot] = added(f0_turn[slot], f0[slot, x]).astype(bf16)

            @pl.when(away)
            def _():
                swap.wait()
                f1[slot] = added(f0_turn[slot], f0_swap[slot]).astype(bf16)

            @pl.when(second + SLOTS < first_jobs)
            def _():
                pl.semaphore_signal(first_free, inc=1, device_id=turn_from, device_id_type=MESH)

            f1_copy(slot).start()

        @pl.when(tick < first_jobs)
        def _():
            slot = lax.rem(tick, SLOTS)
            turn, swap = f0_copies(slot)

            @pl.when(tick >= SLOTS)
            def _():
                pl.semaphore_wait(first_free, 1)

            turn.start()

            @pl.when(away)
            def _():
                swap.start()

    def second_tick(tick):
        @pl.when(tick < second_jobs)
        def _():
            slot = lax.rem(tick, 2)
            second_right_do(tick, slot, finish)

            @pl.when(tick + 1 < second_jobs)
            def _():
                second_right_do(tick + 1, 1 - slot, begin)

            @pl.when(tick == 0)
            def _():
                load_left(three_left, stage, second_left)

            @pl.when(tick == second_split)
            def _():
                load_left(four_left, stage, second_left)

            def keep(at_z, at_y, at_core, value):
                s0[lax.rem(tick, SLOTS), at_y, at_z, at_core] = value

            multiply(second_left, second_right, slot, keep)

        last = tick - 4 * GAP

        @pl.when(inside(last, second_jobs))
        def _():
            slot = lax.rem(last, SLOTS)
            turn, swap = s2_copies(slot)
            turn.wait()

            @pl.when(home)
            def _():
                second_out[last] = added(s2_turn[slot], s2[slot, x])

            @pl.when(away)
            def _():
                swap.wait()
                second_out[last] = added(s2_turn[slot], s2_swap[slot])

            @pl.when(last + SLOTS < second_jobs)
            def _():
                pl.semaphore_signal(second_free, inc=1, device_id=turn_from, device_id_type=MESH)

        fourth = tick - 3 * GAP

        @pl.when(inside(fourth, second_jobs))
        def _():
            slot = lax.rem(fourth, SLOTS)
            far_copy(slot).wait()
            s2[slot] = added(far[slot, z_high], far_got[slot]).astype(bf16)
            turn, swap = s2_copies(slot)

            @pl.when(fourth >= SLOTS)
            def _():
                pl.semaphore_wait(second_free, 1)

            turn.start()

            @pl.when(away)
            def _():
                swap.start()

        third = tick - 2 * GAP

        @pl.when(inside(third, second_jobs))
        def _():
            slot = lax.rem(third, SLOTS)
            s1_copy(slot).wait()
            far[slot] = added(s1[slot, z_low], s1_got[slot]).astype(bf16)
            far_copy(slot).start()

        second = tick - GAP

        @pl.when(inside(second, second_jobs))
        def _():
            slot = lax.rem(second, SLOTS)
            s0_copy(slot).wait()
            for low in range(2):
                for high in range(2):
                    at = high * 2 + low
                    s1[slot, low, high] = added(s0[slot, y, at], s0_got[slot, at]).astype(bf16)
            s1_copy(slot).start()

        @pl.when(tick < second_jobs)
        def _():
            s0_copy(lax.rem(tick, SLOTS)).start()

    bias_peers = [
        device(z, y, 1 - core, x),
        device(z, y, core, 1 - x),
        y_peer,
        device(z + 1 - 2 * lax.rem(z, 2), y, core, x),
        device(lax.rem(z + 2, 4), y, core, x),
    ]

    def bias_copy(step):
        return remote(bias_out, bias_got.at[step], bias_sems, (step,), bias_peers[step])

    def slot_x_copy():
        return remote(slot_ref.at[1 - x], slot_x, slot_sems, (0,), device(z, y, core, 1 - x))

    def slot_y_copy():
        return remote(slot_y.at[1 - y], slot_y_got, slot_sems, (1,), y_peer)

    def slot_z_copy(ahead):
        return remote(
            slot_z.at[lax.rem(z + ahead, 4)], slot_z_got.at[ahead - 1], slot_z_sems, (ahead - 1,), z_peer(ahead)
        )

    def silu_x_copy():
        return remote(silu_ref, silu_x, silu_sems, (0,), device(z, y, core, 1 - x))

    def silu_y_copy():
        return remote(silu_y, silu_y_got, silu_sems, (1,), y_peer)

    def silu_z_copy(ahead):
        return remote(silu_z, silu_z_got.at[ahead - 1], silu_z_sems, (ahead - 1,), z_peer(ahead))

    def small_tick(tick):
        @pl.when(tick == 0)
        def _():
            bias_out[...] = bias_ref[...]
            slot_x_copy().start()
            silu_x_copy().start()

        for step in range(5):

            @pl.when(tick == step + 1)
            def _(step=step):
                bias_copy(step).wait()
                bias_out[...] = bias_out[...] + bias_got[step]

        for step in range(5):

            @pl.when(tick == step)
            def _(step=step):
                bias_copy(step).start()

        @pl.when(tick == 1)
        def _():
            slot_x_copy().wait()
            for at_y in range(2):
                slot_y[at_y, x] = slot_ref[x, at_y]
                slot_y[at_y, 1 - x] = slot_x[at_y]
            slot_y_copy().start()
            silu_x_copy().wait()
            silu_y[x] = silu_ref[...]
            silu_y[1 - x] = silu_x[...]
            silu_y_copy().start()

        @pl.when(tick == 2)
        def _():
            slot_y_copy().wait()
            for at_z in range(4):
                slot_z[at_z, y] = slot_y[y, :, at_z]
                slot_z[at_z, 1 - y] = slot_y_got[:, at_z]
            silu_y_copy().wait()
            silu_z[y] = silu_y[...]
            silu_z[1 - y] = silu_y_got[...]
            for ahead in (1, 2, 3):
                slot_z_copy(ahead).start()
                silu_z_copy(ahead).start()

        @pl.when(tick == 3)
        def _():
            slot_out[z] = slot_z[z]
            silu_out[z] = silu_z[...]
            for ahead in (1, 2, 3):
                slot_z_copy(ahead).wait()
                slot_out[lax.rem(z + 4 - ahead, 4)] = slot_z_got[ahead - 1]
                silu_z_copy(ahead).wait()
                silu_out[lax.rem(z + 4 - ahead, 4)] = silu_z_got[ahead - 1]

    ada_cols = ada_tile.shape[2]
    ada_tiles = ada_ref.shape[1] // ada_cols
    cond_copy = remote(cond_acc, cond_out, cond_sems, (), swap_peer)

    def ada_copy(tile, slot):
        columns = pl.ds(pl.multiple_of(tile * ada_cols, LANES), ada_cols)
        return pltpu.make_async_copy(ada_ref.at[:, columns], ada_tile.at[slot], ada_sems.at[slot])

    def cond_tick(tick):
        tile = tick - 4

        @pl.when(tile == -1)
        def _():
            cond_acc[...] = jnp.zeros_like(cond_acc)

        @pl.when(inside(tile + 1, ada_tiles))
        def _():
            ada_copy(tile + 1, lax.rem(tile + 1, 2)).start()

        @pl.when(inside(tile, ada_tiles))
        def _():
            slot = lax.rem(tile, 2)
            ada_copy(tile, slot).wait()
            columns = pl.ds(pl.multiple_of(tile * ada_cols, LANES), ada_cols)
            cond_acc[...] += dot_nt(slot_low_ref[:, columns], ada_tile[slot])

        @pl.when(tile == ada_tiles)
        def _():
            @pl.when(home)
            def _():
                cond_out[...] = cond_acc[...]

            @pl.when(away)
            def _():
                cond_copy.start()

        @pl.when(jnp.logical_and(tile == ada_tiles + 1, away))
        def _():
            cond_copy.wait()

    def tick_body(tick, carry):
        small_tick(tick)
        cond_tick(tick)
        first_tick(tick)

        @pl.when(lax.rem(tick, 3) != 2)
        def _():
            second_tick(tick // 3 * 2 + lax.rem(tick, 3))

        return carry

    ticks = max(first_jobs + 4 * GAP, ada_tiles + 6, -(-3 * (second_jobs + 4 * GAP) // 2))
    lax.fori_loop(0, ticks, tick_body, 0)


def reduce_grads(one, two, three, four, bias, slots, silu, slot_low, ada_weight):
    tokens, width = one[0].shape
    grid_rows = width // 16
    first_jobs = (one[1].shape[1] + two[1].shape[1]) // TILE
    second_jobs = (three[1].shape[1] + four[1].shape[1]) // TILE
    tile = (grid_rows * TILE // LANES, LANES)
    dma = pltpu.SemaphoreType.DMA
    slot_tail = slots.shape[-2:]

    def low(*lead):
        return pltpu.VMEM(lead + tile, bf16)

    scratch = [
        pltpu.VMEM((tokens, width), bf16),
        pltpu.VMEM((width, tokens), bf16),
        pltpu.VMEM((width, tokens), bf16),
        pltpu.VMEM((2, tokens, TILE), bf16),
        pltpu.VMEM((2, tokens, TILE), bf16),
        low(SLOTS, 2, 2, 4),
        low(SLOTS, 2, 4),
        low(SLOTS, 2, 4),
        low(SLOTS, 2, 4),
        low(SLOTS, 4),
        low(SLOTS, 2, 2),
        low(SLOTS, 2),
        low(SLOTS, 2),
        low(SLOTS),
        low(SLOTS, 2, 4, 2),
        low(SLOTS, 4, 2),
        low(SLOTS, 2, 2, 2),
        low(SLOTS, 2, 2),
        low(SLOTS, 2, 2),
        low(SLOTS, 2),
        low(SLOTS, 2),
        low(SLOTS),
        low(SLOTS),
        pltpu.VMEM((5,) + bias.shape, f32),
        pltpu.VMEM((2, 4) + slot_tail, f32),
        pltpu.VMEM((2, 2, 4) + slot_tail, f32),
        pltpu.VMEM((2, 4) + slot_tail, f32),
        pltpu.VMEM((4, 2, 2) + slot_tail, f32),
        pltpu.VMEM((3, 2, 2) + slot_tail, f32),
        pltpu.VMEM(silu.shape, bf16),
        pltpu.VMEM((2,) + silu.shape, bf16),
        pltpu.VMEM((2,) + silu.shape, bf16),
        pltpu.VMEM((2, 2) + silu.shape, bf16),
        pltpu.VMEM((3, 2, 2) + silu.shape, bf16),
        pltpu.VMEM((2, ada_weight.shape[0], ada_weight.shape[1] // 9), bf16),
        pltpu.VMEM((8, ada_weight.shape[0]), f32),
        dma,
        dma((2,)),
        dma((2,)),
        dma((2, 2, SLOTS)),
        dma((2, SLOTS)),
        dma((2, SLOTS)),
        dma((2, SLOTS)),
        dma((2, SLOTS)),
        dma((2, SLOTS)),
        dma((2, SLOTS)),
        dma((2, 2, SLOTS)),
        dma((2, 5)),
        dma((2, 2)),
        dma((2, 3)),
        dma((2, 2)),
        dma((2, 3)),
        dma((2,)),
        dma((2,)),
        pltpu.SemaphoreType.REGULAR,
        pltpu.SemaphoreType.REGULAR,
    ]
    return pl.pallas_call(
        functools.partial(reduce_kernel, grid_rows, first_jobs, second_jobs),
        out_shape=(
            jax.ShapeDtypeStruct((first_jobs,) + tile, f32),
            jax.ShapeDtypeStruct((second_jobs,) + tile, f32),
            jax.ShapeDtypeStruct(bias.shape, f32),
            jax.ShapeDtypeStruct((4, 2, 2) + slot_tail, f32),
            jax.ShapeDtypeStruct((4, 2, 2) + silu.shape, bf16),
            jax.ShapeDtypeStruct((8, ada_weight.shape[0]), f32),
        ),
        in_specs=[whole_spec(pl.ANY)] * 8 + [whole_spec()] * 4 + [whole_spec(pl.ANY)],
        out_specs=(whole_spec(),) * 6,
        scratch_shapes=scratch,
        compiler_params=pltpu.CompilerParams(
            collective_id=1, has_side_effects=True, vmem_limit_bytes=52 << 20
        ),
        cost_estimate=pl.CostEstimate(flops=10**11, bytes_accessed=10**8, transcendentals=0),
        name="reduce_grads",
    )(*one, *two, *three, *four, bias, slots, silu, slot_low, ada_weight)


def mlp_back_kernel(
    proj_jobs,
    own_ref,
    pre_ref,
    down_ref,
    up_ref,
    mid_left,
    mid_right,
    in_left,
    in_right,
    last_left,
    last_right,
    all_out,
    low_out,
    in_out,
    bias_out,
    proj_out,
    pre_tile,
    low_tile,
    part_send,
    part_got,
    proj_stage,
    proj_left,
    proj_right,
    p0,
    p0_got,
    p1,
    p1_got,
    p2,
    p2_got,
    p3,
    p3_got,
    pre_sems,
    low_sems,
    own_sems,
    part_sems,
    load_sem,
    proj_load,
    p0_sems,
    p1_sems,
    p2_sems,
    p3_sems,
):
    dp = lax.axis_index("dp")
    x = lax.axis_index("tensor")
    core = dp % 2
    y = (dp // 2) % 2
    z = dp // 4

    def device(z_at, y_at, core_at, x_at):
        return ((z_at * 2 + y_at) * 2 + core_at, x_at)

    y_peer = device(z, 1 - y, core, x)

    def z_peer(ahead):
        return device(lax.rem(z + ahead, 4), y, core, x)

    barrier = pltpu.get_barrier_semaphore()
    near = [device(z, y, 1 - core, x), device(z, y, core, 1 - x), device(z, y, 1 - core, 1 - x), y_peer]
    for peer in near + [z_peer(1), z_peer(2), z_peer(3)]:
        pl.semaphore_signal(barrier, inc=1, device_id=peer, device_id_type=MESH)
    pl.semaphore_wait(barrier, 7)

    def remote(source, target, sems, index, peer):
        return pltpu.make_async_remote_copy(
            src_ref=source,
            dst_ref=target,
            send_sem=sems.at[(0,) + index],
            recv_sem=sems.at[(1,) + index],
            device_id=peer,
            device_id_type=MESH,
        )

    def added(*terms):
        total = terms[0].astype(f32)
        for term in terms[1:]:
            total = total + term.astype(f32)
        return total

    def load_left(source, through, target):
        height = source.shape[1]
        through = through if height == through.shape[1] else through.at[:, 0:height]
        copy = pltpu.make_async_copy(source, through, load_sem)
        copy.start()
        copy.wait()

        def block(index, carry):
            rows = pl.ds(pl.multiple_of(index * LANES, LANES), LANES)
            target[0:height, rows] = through[rows, :].T
            return carry

        lax.fori_loop(0, source.shape[0] // LANES, block, 0)

    def begin(copy):
        copy.start()

    def finish(copy):
        copy.wait()

    def inside(job, count):
        return jnp.logical_and(job >= 0, job < count)

    core_peer = device(z, y, 1 - core, x)
    own_rows = own_ref.shape[0]
    tile_rows = pre_tile.shape[1]
    hidden = pre_ref.shape[1]
    half_tiles = own_rows // tile_rows

    def own_span(side):
        return pl.ds(pl.multiple_of(side * own_rows, 256), own_rows)

    own_copy = remote(own_ref, all_out.at[own_span(core), :], own_sems, (), core_peer)
    own_copy.start()
    all_out[own_span(core), :] = own_ref[...]
    bias_out[...] = jnp.zeros_like(bias_out)

    def tile_span(tile):
        side = jnp.where(tile < half_tiles, 1 - core, core)
        begin_row = side * own_rows + lax.rem(tile, half_tiles) * tile_rows
        return pl.ds(pl.multiple_of(begin_row, 256), tile_rows)

    def part_span(tile):
        return pl.ds(pl.multiple_of(lax.rem(tile, half_tiles) * tile_rows, 256), tile_rows)

    def pre_copy(tile, slot):
        return pltpu.make_async_copy(pre_ref.at[tile_span(tile), :], pre_tile.at[slot], pre_sems.at[slot])

    def low_copy(tile, slot):
        return pltpu.make_async_copy(low_tile.at[slot], low_out.at[tile_span(tile), :], low_sems.at[slot])

    def part_copy(tile):
        rows = part_span(tile)
        return remote(part_send.at[rows, :], part_got.at[rows, :], part_sems, (tile,), core_peer)

    pre_copy(0, 0).start()
    chunk = 768

    def mlp_tile(tile):
        slot = lax.rem(tile, 2)
        pre_copy(tile, slot).wait()

        @pl.when(tile + 1 < 2 * half_tiles)
        def _():
            pre_copy(tile + 1, 1 - slot).start()

        @pl.when(tile == 0)
        def _():
            own_copy.wait()

        @pl.when(tile >= 2)
        def _():
            low_copy(tile - 2, slot).wait()

        grads = all_out[tile_span(tile), :]
        for at in range(0, hidden, chunk):
            span = slice(at, at + chunk)
            value = pre_tile[slot, :, span]
            square = value * value
            curve = jnp.tanh(GELU_SCALE * (value + GELU_CUBE * (square * value)))
            slope = 0.5 * (1.0 + curve) + (0.5 * GELU_SCALE) * value * (1.0 - curve * curve) * (
                1.0 + (3.0 * GELU_CUBE) * square
            )
            grad = slope * dot_nt(grads, down_ref[span, :])
            bias_out[0:1, span] += jnp.sum(grad, axis=0, keepdims=True)
            low_tile[slot, :, span] = grad.astype(bf16)
        low_copy(tile, slot).start()
        part = dot_nt(low_tile[slot], up_ref[...])

        @pl.when(tile < half_tiles)
        def _():
            part_send[part_span(tile), :] = part.astype(bf16)
            part_copy(tile).start()

        @pl.when(tile >= half_tiles)
        def _():
            in_out[part_span(tile), :] = part

    mid_jobs = mid_right.shape[1] // TILE
    in_jobs = -(-in_right.shape[1] // TILE)
    in_left_over = in_right.shape[1] % TILE
    proj_rows = mid_left.shape[1] // 32
    last_rows = last_left.shape[1] // 32

    def proj_right_do(job, slot, action):
        def copy(source, tile, columns):
            start = pl.multiple_of(tile * columns, LANES)
            return pltpu.make_async_copy(
                source.at[:, pl.ds(start, columns)], proj_right.at[slot, :, pl.ds(0, columns)], proj_load.at[slot]
            )

        @pl.when(job < mid_jobs)
        def _():
            action(copy(mid_right, job, TILE))

        full = in_jobs - (1 if in_left_over else 0)

        @pl.when(inside(job - mid_jobs, full))
        def _():
            action(copy(in_right, job - mid_jobs, TILE))

        if in_left_over:

            @pl.when(job == mid_jobs + full)
            def _():
                rest = pltpu.make_async_copy(
                    in_right.at[:, pl.ds(full * TILE, in_left_over)],
                    proj_right.at[slot, :, pl.ds(0, in_left_over)],
                    proj_load.at[slot],
                )
                action(rest)

        @pl.when(job >= mid_jobs + in_jobs)
        def _():
            action(copy(last_right, job - mid_jobs - in_jobs, 2 * TILE))

    def p0_copy(slot):
        return remote(p0.at[slot, 1 - core], p0_got.at[slot], p0_sems, (slot,), device(z, y, 1 - core, x))

    def route(job):
        odd = lax.rem(job, 2)
        first = x + odd * (y - x)
        second = y + odd * (x - y)
        over_x = device(z, y, core, 1 - x)
        over_y = device(z, 1 - y, core, x)
        toward = tuple(a + odd * (b - a) for a, b in zip(over_x, over_y))
        onward = tuple(b + odd * (a - b) for a, b in zip(over_x, over_y))
        return odd, first, second, toward, onward

    def p1_copy(job):
        odd, first, second, toward, onward = route(job)
        slot = lax.rem(job, SLOTS)
        return remote(p1.at[slot, 1 - first], p1_got.at[slot], p1_sems, (slot,), toward)

    def p2_copy(job):
        odd, first, second, toward, onward = route(job)
        slot = lax.rem(job, SLOTS)
        return remote(p2.at[slot, 1 - second], p2_got.at[slot], p2_sems, (slot,), onward)

    def p3_copy(slot, ahead):
        return remote(
            p3.at[slot, lax.rem(z + ahead, 4)], p3_got.at[slot, ahead - 1], p3_sems, (slot, ahead - 1), z_peer(ahead)
        )

    pltpu.make_async_copy(mid_right.at[:, pl.ds(0, TILE)], proj_right.at[0, :, pl.ds(0, TILE)], proj_load.at[0]).start()

    def proj_tick(tick):
        @pl.when(tick < proj_jobs)
        def _():
            slot = lax.rem(tick, 2)
            odd = slot
            proj_right_do(tick, slot, finish)

            @pl.when(tick + 1 < proj_jobs)
            def _():
                proj_right_do(tick + 1, 1 - slot, begin)

            for at, source in ((0, mid_left), (mid_jobs, in_left), (mid_jobs + in_jobs, last_left)):

                @pl.when(tick == at)
                def _(source=source):
                    load_left(source, proj_stage, proj_left)

            shares = [(at_y, at_core, at_x) for at_y in range(2) for at_core in range(2) for at_x in range(2)]

            @pl.when(tick < mid_jobs + in_jobs)
            def _():
                def block(at_z, carry):
                    span = pl.ds(pl.multiple_of(at_z * 8 * proj_rows, 32), 8 * proj_rows)
                    right = proj_right[slot, :, 0:TILE]
                    product = jnp.dot(proj_left[span, :], right, preferred_element_type=f32).astype(bf16)
                    for low, (at_y, at_core, at_x) in enumerate(shares):
                        p0[lax.rem(tick, SLOTS), at_core, at_x + odd * (at_y - at_x), at_y + odd * (at_x - at_y), at_z] = product[low * proj_rows : (low + 1) * proj_rows, :]
                    return carry

                lax.fori_loop(0, 4, block, 0)

            @pl.when(tick >= mid_jobs + in_jobs)
            def _():
                def block(at_z, carry):
                    span = pl.ds(pl.multiple_of(at_z * 8 * last_rows, 32), 8 * last_rows)
                    for half in range(2):
                        right = proj_right[slot, :, half * TILE : (half + 1) * TILE]
                        product = jnp.dot(proj_left[span, :], right, preferred_element_type=f32)
                        begin_row = half * proj_rows // 2
                        for low, (at_y, at_core, at_x) in enumerate(shares):
                            p0[lax.rem(tick, SLOTS), at_core, at_x + odd * (at_y - at_x), at_y + odd * (at_x - at_y), at_z, begin_row : begin_row + last_rows, :] = product[
                                low * last_rows : (low + 1) * last_rows, :
                            ].astype(bf16)
                    return carry

                lax.fori_loop(0, 4, block, 0)

        fifth = tick - 4 * GAP

        @pl.when(inside(fifth, proj_jobs))
        def _():
            slot = lax.rem(fifth, SLOTS)
            for ahead in (1, 2, 3):
                p3_copy(slot, ahead).wait()
            proj_out[fifth] = added(p3[slot, z], p3_got[slot, 0], p3_got[slot, 1], p3_got[slot, 2])

        fourth = tick - 3 * GAP

        @pl.when(inside(fourth, proj_jobs))
        def _():
            slot = lax.rem(fourth, SLOTS)
            odd, first, second, toward, onward = route(fourth)
            p2_copy(fourth).wait()
            p3[slot] = added(p2[slot, second], p2_got[slot]).astype(bf16)
            for ahead in (1, 2, 3):
                p3_copy(slot, ahead).start()

        third = tick - 2 * GAP

        @pl.when(inside(third, proj_jobs))
        def _():
            slot = lax.rem(third, SLOTS)
            odd, first, second, toward, onward = route(third)
            p1_copy(third).wait()
            p2[slot] = added(p1[slot, first], p1_got[slot]).astype(bf16)
            p2_copy(third).start()

        second_job = tick - GAP

        @pl.when(inside(second_job, proj_jobs))
        def _():
            slot = lax.rem(second_job, SLOTS)
            p0_copy(slot).wait()
            p1[slot] = added(p0[slot, core], p0_got[slot]).astype(bf16)
            p1_copy(second_job).start()

        @pl.when(tick < proj_jobs)
        def _():
            p0_copy(lax.rem(tick, SLOTS)).start()

    def tick_body(tick, carry):
        proj_tick(tick)

        @pl.when(jnp.logical_and(lax.rem(tick, 4) == 3, tick // 4 < 2 * half_tiles))
        def _():
            mlp_tile(tick // 4)

        return carry

    lax.fori_loop(0, max(proj_jobs + 4 * GAP, 8 * half_tiles), tick_body, 0)
    for tile in range(2 * half_tiles - 2, 2 * half_tiles):
        low_copy(tile, tile % 2).wait()
    for tile in range(half_tiles):
        part_copy(tile).wait()
    in_out[...] = in_out[...] + part_got[...].astype(f32)


def mlp_back(own, pre_act, down_weight, up_weight, mid, first, last):
    rows, width = own.shape
    hidden = pre_act.shape[1]
    proj_jobs = mid[1].shape[1] // TILE + -(-first[1].shape[1] // TILE) + last[1].shape[1] // (2 * TILE)
    proj_tokens, proj_hidden = mid[0].shape
    tile = (proj_hidden // 32, TILE)
    dma = pltpu.SemaphoreType.DMA

    def low(*lead):
        return pltpu.VMEM(lead + tile, bf16)

    return pl.pallas_call(
        functools.partial(mlp_back_kernel, proj_jobs),
        out_shape=(
            jax.ShapeDtypeStruct((2 * rows, width), bf16),
            jax.ShapeDtypeStruct((2 * rows, hidden), bf16),
            jax.ShapeDtypeStruct((rows, width), f32),
            jax.ShapeDtypeStruct((8, hidden), f32),
            jax.ShapeDtypeStruct((proj_jobs,) + tile, f32),
        ),
        in_specs=[whole_spec(), whole_spec(pl.ANY), whole_spec(), whole_spec()] + [whole_spec(pl.ANY)] * 6,
        out_specs=(whole_spec(), whole_spec(pl.ANY), whole_spec(), whole_spec(), whole_spec()),
        scratch_shapes=[
            pltpu.VMEM((2, SHORT, hidden), f32),
            pltpu.VMEM((2, SHORT, hidden), bf16),
            pltpu.VMEM((rows, width), bf16),
            pltpu.VMEM((rows, width), bf16),
            pltpu.VMEM((proj_tokens, proj_hidden), bf16),
            pltpu.VMEM((proj_hidden, proj_tokens), bf16),
            pltpu.VMEM((2, proj_tokens, 2 * TILE), bf16),
            low(SLOTS, 2, 2, 2, 4),
            low(SLOTS, 2, 2, 4),
            low(SLOTS, 2, 2, 4),
            low(SLOTS, 2, 4),
            low(SLOTS, 2, 4),
            low(SLOTS, 4),
            low(SLOTS, 4),
            low(SLOTS, 3),
            dma((2,)),
            dma((2,)),
            dma((2,)),
            dma((2, rows // SHORT)),
            dma,
            dma((2,)),
            dma((2, SLOTS)),
            dma((2, SLOTS)),
            dma((2, SLOTS)),
            dma((2, SLOTS, 3)),
        ],
        compiler_params=pltpu.CompilerParams(
            collective_id=3, has_side_effects=True, vmem_limit_bytes=58 << 20
        ),
        cost_estimate=pl.CostEstimate(flops=3 * 10**10, bytes_accessed=5 * 10**7, transcendentals=0),
        name="mlp_back",
    )(own, pre_act, down_weight, up_weight, *mid, *first, *last)


def fetch_kernel(
    tokens_ref,
    qkv_ref,
    out_ref,
    cond_ref,
    bias_ref,
    ids_ref,
    ada_ref,
    ada_bias_ref,
    up_ref,
    down_ref,
    tokens_out,
    qkv_out,
    out_out,
    cond_out,
    bias_out,
    ids_out,
    mod_out,
    up_out,
    down_out,
    ada_tile,
    token_hold,
    qkv_hold,
    out_hold,
    up_hold,
    down_hold,
    token_sems,
    cond_sems,
    x_sems,
    y_sems,
    z_sems,
    local_sems,
    ada_sems,
):
    dp = lax.axis_index("dp")
    x = lax.axis_index("tensor")
    core = dp % 2
    y = (dp // 2) % 2
    z = dp // 4
    z_near = lax.rem(z, 2)
    home = core == x
    away = core != x
    pieces = x_sems.shape[1]
    quarter = qkv_ref.shape[0] // 4
    height = quarter // (pieces - 1)
    out_quarter = out_ref.shape[0] // 4

    def device(z_at, y_at, core_at, x_at):
        return ((z_at * 2 + y_at) * 2 + core_at, x_at)

    core_peer = device(z, y, 1 - core, x)
    swap_peer = device(z, y, x, core)
    y_peer = device(z, 1 - y, core, x)
    z_peer = device(z + 1 - 2 * z_near, y, core, x)
    barrier = pltpu.get_barrier_semaphore()
    peers = [core_peer, device(z, y, core, 1 - x), device(z, y, 1 - core, 1 - x), y_peer, z_peer]
    for peer in peers:
        pl.semaphore_signal(barrier, inc=1, device_id=peer, device_id_type=MESH)
    pl.semaphore_wait(barrier, len(peers))

    def remote(source, target, sems, index, peer):
        return pltpu.make_async_remote_copy(
            src_ref=source,
            dst_ref=target,
            send_sem=sems.at[(0,) + index],
            recv_sem=sems.at[(1,) + index],
            device_id=peer,
            device_id_type=MESH,
        )

    def part(whole, other, y_at, piece):
        at = y_at * 2 + z_near
        if piece == pieces - 1:
            return other.at[pl.ds(pl.multiple_of(at * out_quarter, 16), out_quarter), :]
        return whole.at[pl.ds(pl.multiple_of(at * quarter + piece * height, 32), height), :]

    def x_copy(piece):
        source = part(qkv_ref, out_ref, y, piece)
        return remote(source, part(qkv_out, out_out, y, piece), x_sems, (piece,), swap_peer)

    def y_copy(piece):
        here = part(qkv_out, out_out, y, piece)
        return remote(here, here, y_sems, (piece,), y_peer)

    def z_copy(piece, other):
        here = part(qkv_out, out_out, 1 - y if other else y, piece)
        return remote(here, here, z_sems, (int(other), piece), z_peer)

    token_copy = remote(tokens_ref, tokens_out, token_sems, (), swap_peer)
    cond_copy = remote(cond_ref, cond_out, cond_sems, (0,), core_peer)
    ids_copy = remote(ids_ref, ids_out, cond_sems, (1,), core_peer)
    bias_copy = remote(bias_ref, bias_out, cond_sems, (2,), swap_peer)
    local_in = [
        pltpu.make_async_copy(tokens_ref, token_hold, local_sems.at[0]),
        pltpu.make_async_copy(qkv_ref, qkv_hold, local_sems.at[1]),
        pltpu.make_async_copy(out_ref, out_hold, local_sems.at[2]),
    ]
    local_out = [
        pltpu.make_async_copy(token_hold, tokens_out, local_sems.at[3]),
        pltpu.make_async_copy(qkv_hold, qkv_out, local_sems.at[4]),
        pltpu.make_async_copy(out_hold, out_out, local_sems.at[5]),
    ]

    halves_in, halves_out = [], []
    for at, (source, hold, target) in enumerate(((up_ref, up_hold, up_out), (down_ref, down_hold, down_out))):
        rows = pl.ds(pl.multiple_of(y * hold.shape[0], 64), hold.shape[0])
        halves_in.append(pltpu.make_async_copy(source.at[rows, :], hold, local_sems.at[6 + at]))
        halves_out.append(pltpu.make_async_copy(hold, target, local_sems.at[8 + at]))

    @pl.when(away)
    def _():
        for piece in range(pieces):
            x_copy(piece).start()
        bias_copy.start()

    for copy in halves_in:
        copy.start()

    @pl.when(home)
    def _():
        cond_copy.start()
        ids_copy.start()
        for copy in local_in:
            copy.start()
        cond_out[...] = cond_ref[...]
        ids_out[...] = ids_ref[...]
        bias_out[...] = bias_ref[...]

    tile_cols = ada_tile.shape[2]
    tiles = ada_ref.shape[1] // tile_cols

    def ada_copy(tile, slot):
        columns = pl.ds(tile * tile_cols, tile_cols)
        return pltpu.make_async_copy(ada_ref.at[:, columns], ada_tile.at[slot], ada_sems.at[slot])

    ada_copy(0, 0).start()

    @pl.when(away)
    def _():
        cond_copy.wait_recv()

    cond = cond_out[...].astype(f32)
    low = (cond / (1.0 + jnp.exp(-cond))).astype(bf16)

    def modulate(tile):
        slot = tile % 2
        ada_copy(tile, slot).wait()

        if tile + 1 < tiles:
            ada_copy(tile + 1, 1 - slot).start()

        columns = slice(tile * tile_cols, (tile + 1) * tile_cols)
        product = jnp.dot(low, ada_tile[slot], preferred_element_type=f32)
        mod_out[:, columns] = product + ada_bias_ref[:, columns].astype(f32)

    for tile in range(tiles):
        modulate(tile)
        if tile % 2 == 1 and tile // 2 < pieces:

            @pl.when(away)
            def _(piece=tile // 2):
                x_copy(piece).wait_recv()
                y_copy(piece).start()
                z_copy(piece, False).start()
                if piece == 0:
                    token_copy.start()

    for copy, onward in zip(halves_in, halves_out):
        copy.wait()
        onward.start()

    @pl.when(away)
    def _():
        for piece in range(pieces):
            y_copy(piece).wait_recv()
            z_copy(piece, True).start()
        token_copy.wait()
        ids_copy.wait_recv()
        bias_copy.wait()
        for piece in range(pieces):
            x_copy(piece).wait_send()
            y_copy(piece).wait_send()
            z_copy(piece, False).wait()
            z_copy(piece, True).wait()

    @pl.when(home)
    def _():
        cond_copy.wait_send()
        ids_copy.wait_send()
        for copy, onward in zip(local_in, local_out):
            copy.wait()
            onward.start()
        for copy in local_out:
            copy.wait()

    for copy in halves_out:
        copy.wait()


def fetch(tokens, qkv, out, condition, bias, ids, ada_weight, ada_bias, up, down):
    pieces = 4
    dma = pltpu.SemaphoreType.DMA
    return pl.pallas_call(
        fetch_kernel,
        out_shape=(
            jax.ShapeDtypeStruct(tokens.shape, bf16),
            jax.ShapeDtypeStruct(qkv.shape, bf16),
            jax.ShapeDtypeStruct(out.shape, bf16),
            jax.ShapeDtypeStruct(condition.shape, bf16),
            jax.ShapeDtypeStruct(bias.shape, bf16),
            jax.ShapeDtypeStruct(ids.shape, jnp.int32),
            jax.ShapeDtypeStruct((condition.shape[0], ada_weight.shape[1]), f32),
            jax.ShapeDtypeStruct((up.shape[0] // 2, up.shape[1]), bf16),
            jax.ShapeDtypeStruct((down.shape[0] // 2, down.shape[1]), bf16),
        ),
        in_specs=[whole_spec(pl.ANY)] * 3 + [whole_spec()] * 3 + [whole_spec(pl.ANY), whole_spec()] + [whole_spec(pl.ANY)] * 2,
        out_specs=(whole_spec(pl.ANY),) * 3 + (whole_spec(),) * 4 + (whole_spec(pl.ANY),) * 2,
        scratch_shapes=[
            pltpu.VMEM((2, ada_weight.shape[0], ada_weight.shape[1] // 9), bf16),
            pltpu.VMEM(tokens.shape, bf16),
            pltpu.VMEM(qkv.shape, bf16),
            pltpu.VMEM(out.shape, bf16),
            pltpu.VMEM((up.shape[0] // 2, up.shape[1]), bf16),
            pltpu.VMEM((down.shape[0] // 2, down.shape[1]), bf16),
            dma((2,)),
            dma((2, 3)),
            dma((2, pieces)),
            dma((2, pieces)),
            dma((2, 2, pieces)),
            dma((10,)),
            dma((2,)),
        ],
        compiler_params=pltpu.CompilerParams(
            collective_id=2, has_side_effects=True, vmem_limit_bytes=56 << 20
        ),
        cost_estimate=pl.CostEstimate(flops=10**10, bytes_accessed=3 * 10**7, transcendentals=0),
        name="fetch",
    )(tokens, qkv, out, condition, bias, ids, ada_weight, ada_bias.reshape(1, -1), up, down)


def after(value, earlier):
    return lax.optimization_barrier((value, earlier))[0]


def paired_shards(
    tokens_in,
    condition,
    ada_weight,
    ada_bias,
    qkv_weight,
    qv_bias,
    out_weight,
    out_bias,
    up_weight,
    up_bias,
    down_weight,
    down_bias,
    proj_in,
    proj_in_bias,
    proj_mid,
    proj_mid_bias,
    proj_last,
    proj_last_bias,
    enc_features,
    image_ids,
    target_rows,
    out_grad,
):
    dp = lax.axis_index("dp")
    x = lax.axis_index("tensor")
    core = dp % 2
    y = (dp // 2) % 2
    z = dp // 4
    z_near = z % 2
    z_far = z // 2
    place = dp * 2 + x
    home = core == x
    local_rows, width = tokens_in.shape
    shard_rows = image_ids.shape[0]
    slots = condition.shape[0]
    units = local_rows // SHORT
    local_cols = qkv_weight.shape[2]
    local_hidden = up_weight.shape[1]
    heads = local_cols // HEAD_DIM
    qkv_cols = -(-3 * local_cols // TILE) * TILE
    out_cols = -(-local_cols // TILE) * TILE

    def swap(value):
        return jnp.where(home, value, send(value, to_diag))

    bias_pack = jnp.concatenate([qv_bias.reshape(-1), up_bias]).reshape(-1, LANES)
    tokens, qkv_half, out_half, cond_low, bias_half, ids, modulation, up_own, down_own = fetch(
        tokens_in,
        qkv_weight.reshape(width, 3 * local_cols),
        out_weight,
        condition,
        bias_pack,
        image_ids.reshape(-1, LANES),
        ada_weight,
        ada_bias,
        up_weight,
        down_weight,
    )
    bias_half = bias_half.reshape(-1).astype(f32)
    unit_ids = ids[:: SHORT // LANES, 0]

    def over_x(own, earlier):
        return send(after(own, earlier), to_diag)

    def over_y(weight, first):
        second = send(first, to_swapped_y)
        first, second, whole = lax.optimization_barrier((first, second, weight))
        halves = whole.reshape((2,) + first.shape)
        mine = jnp.arange(2).reshape(2, 1, 1) == y
        return jnp.where(home, halves, jnp.where(mine, first[None], second[None])).reshape(weight.shape)

    up_first = over_x(up_own, tokens)
    chosen = (target_rows - dp * shard_rows)[:, None] == jnp.arange(shard_rows, dtype=jnp.int32)[None, :]
    target_low = jnp.dot(chosen.astype(bf16), enc_features, preferred_element_type=f32).astype(bf16)
    qv_half = bias_half[: 2 * local_cols].reshape(2, local_cols)
    up_bias_half = bias_half[2 * local_cols :]

    same = unit_ids[:, None] == unit_ids[None, :]
    starts = jnp.argmax(same, axis=1).astype(jnp.int32)
    counts = jnp.sum(same.astype(jnp.int32), axis=1).astype(jnp.int32)
    my_units = lax.dynamic_slice_in_dim(unit_ids, core * units, units)
    one_hot = (my_units[:, None] == jnp.arange(slots, dtype=jnp.int32)[None, :]).astype(f32)

    silu_low = jax.nn.silu(cond_low.astype(f32)).astype(bf16)
    per_unit = jnp.dot(one_hot, modulation, precision=highest, preferred_element_type=f32)
    shift_one, scale_one, gate_one, shift_two, scale_two, gate_two = [
        piece[:, None, :] for piece in jnp.split(per_unit, 6, axis=1)
    ]

    def by_unit(array):
        return array.reshape(units, SHORT, -1)

    def flat(array):
        return array.reshape(local_rows, -1)

    def reduce_cores(left, matrix, product):
        mine = lax.dynamic_slice_in_dim(left, core * local_rows, local_rows)
        theirs = lax.dynamic_slice_in_dim(left, (1 - core) * local_rows, local_rows)
        got = send(product(theirs, matrix).astype(bf16), to_core)
        return product(mine, matrix).astype(bf16).astype(f32) + got.astype(f32)

    def dot_nn(left, right):
        return jnp.dot(left, right, preferred_element_type=f32)

    resid = by_unit(tokens.astype(f32))
    normed_one, inv_one = layer_norm(resid)
    attn_in = flat((normed_one * (1.0 + scale_one) + shift_one).astype(bf16))
    attn_all = gather_cores(attn_in)

    qkv_pad = jnp.pad(qkv_half, ((0, 0), (0, qkv_cols - 3 * local_cols)))
    out_pad = jnp.pad(out_half, ((0, out_cols - local_cols), (0, 0)))
    qkv_bias = jnp.concatenate(
        [qv_half[0], jnp.zeros_like(qv_half[0]), qv_half[1], jnp.zeros((qkv_cols - 3 * local_cols,), f32)]
    )
    qkv = (dot_nn(attn_all, qkv_pad) + qkv_bias).astype(bf16)
    qkv, up_first = lax.optimization_barrier((qkv, up_first))
    up_half = over_y(up_weight, up_first)
    down_first = over_x(down_own, up_first)
    attended, log_sums = attend(starts, counts, qkv, heads, out_cols)
    attended, down_first = lax.optimization_barrier((attended, down_first))
    down_half = over_y(down_weight, down_first)
    target_vals = swap(after(target_low, down_first)).astype(f32)
    grad_out = swap(after(out_grad, down_first))
    attn_branch = by_unit(reduce_cores(attended, out_pad, dot_nn) + out_bias.astype(f32))
    mid = resid + gate_one * attn_branch

    normed_two, inv_two = layer_norm(mid)
    mlp_in = flat((normed_two * (1.0 + scale_two) + shift_two).astype(bf16))
    mlp_all = gather_cores(mlp_in)
    pre_act = dot_nn(mlp_all, up_half) + up_bias_half
    hidden = gelu_tanh(pre_act).astype(bf16)
    mlp_branch = by_unit(reduce_cores(hidden, down_half, dot_nn) + down_bias.astype(f32))
    block_value = mid + gate_two * mlp_branch
    block_low = flat(block_value.astype(bf16))

    first_pre = dot_nn(block_low, proj_in) + proj_in_bias.astype(f32)
    first_value, first_back = jax.vjp(jax.nn.silu, first_pre)
    first_low = first_value.astype(bf16)
    second_pre = dot_nn(first_low, proj_mid) + proj_mid_bias.astype(f32)
    second_value, second_back = jax.vjp(jax.nn.silu, second_pre)
    second_low = second_value.astype(bf16)
    projected = dot_nn(second_low, proj_last) + proj_last_bias.astype(f32)
    loss_back = jax.vjp(lambda predicted: align_loss(predicted, target_vals), projected)[1]
    grad_projected = loss_back(jnp.ones((), f32))[0]
    grad_last_low = grad_projected.astype(bf16)
    grad_second = second_back(dot_nt(grad_last_low, proj_last))[0]
    grad_second_low = grad_second.astype(bf16)
    grad_first = first_back(dot_nt(grad_second_low, proj_mid))[0]
    grad_first_low = grad_first.astype(bf16)
    grad_block = by_unit(grad_out.astype(f32) + dot_nt(grad_first_low, proj_in))

    grad_mlp_branch = gate_two * grad_block
    grad_mlp_all, grad_pre_low, grad_mlp_in, up_bias_sums, proj_sum = mlp_back(
        flat(grad_mlp_branch.astype(bf16)),
        pre_act,
        down_half,
        up_half,
        (grad_second_low, first_low),
        (grad_first_low, block_low),
        (grad_last_low, second_low),
    )
    grad_mlp_in = by_unit(grad_mlp_in)
    grad_mid = grad_block + norm_back(normed_two, inv_two, grad_mlp_in * (1.0 + scale_two))

    grad_attn_branch = gate_one * grad_mid
    grad_attn_all = gather_cores(flat(grad_attn_branch.astype(bf16)))
    grad_heads = dot_nt(grad_attn_all, out_pad).astype(bf16)
    grad_qkv, qkv_bias_sums = attend_back(starts, counts, qkv, log_sums, grad_heads, heads)
    grad_attn_in = by_unit(reduce_cores(grad_qkv, qkv_pad, dot_nt))
    grad_tokens = grad_mid + norm_back(normed_one, inv_one, grad_attn_in * (1.0 + scale_one))

    def unit_sum(array):
        return jnp.sum(array, axis=1)

    mod_units = jnp.concatenate(
        [
            unit_sum(grad_attn_in),
            unit_sum(grad_attn_in * normed_one),
            unit_sum(attn_branch * grad_mid),
            unit_sum(grad_mlp_in),
            unit_sum(grad_mlp_in * normed_two),
            unit_sum(mlp_branch * grad_block),
        ],
        axis=1,
    )
    slot_part = dot_tn(one_hot, mod_units, precision=highest)
    slot_grad = slot_part + send(slot_part, to_core)
    slot_low = slot_grad.astype(bf16)
    mod_cols = slot_low.shape[1] // 32
    slot_cols = pick(slot_grad.reshape(slots, 4, 2, 2, 2, mod_cols), core, 3).transpose(3, 2, 1, 0, 4)
    slot_cols = jnp.pad(slot_cols, ((0, 0),) * 3 + ((0, 8 - slots), (0, -mod_cols % LANES)))

    qv_sums = qkv_bias_sums[:2]
    qv_full = lax.dynamic_update_slice_in_dim(jnp.zeros((2, width), f32), qv_sums, core * local_cols, axis=1)
    up_full = lax.dynamic_update_slice_in_dim(
        jnp.zeros((2 * local_hidden,), f32), up_bias_sums[0], core * local_hidden, axis=0
    )
    pieces = [
        qv_full.reshape(-1),
        up_full,
        jnp.sum(flat(grad_attn_branch), axis=0),
        jnp.sum(flat(grad_mlp_branch), axis=0),
        jnp.sum(grad_first, axis=0),
        jnp.sum(grad_second, axis=0),
        jnp.sum(grad_projected, axis=0),
    ]
    packed = jnp.concatenate(pieces)
    packed = jnp.pad(packed, (0, -packed.shape[0] % (8 * LANES))).reshape(-1, LANES)
    first_sum, second_sum, sums, slot_sum, silu_sum, cond_sum = reduce_grads(
        (grad_mlp_all, hidden),
        (mlp_all, grad_pre_low),
        (attn_all, grad_qkv),
        (grad_attn_all, attended),
        packed,
        slot_cols,
        jnp.pad(silu_low, ((0, 8 - slots), (0, 0))),
        jnp.pad(slot_low, ((0, 8 - slots), (0, 0))),
        ada_weight,
    )
    grad_condition = jax.vjp(jax.nn.silu, condition.astype(f32))[1](cond_sum[:slots])[0]
    sums = sums.reshape(-1)
    slot_mine = slot_sum.reshape(16, 8, -1)[:, :slots, :mod_cols].astype(bf16).reshape(16 * slots, mod_cols)
    grad_ada = dot_tn(silu_sum.reshape(16, 8, width)[:, :slots].reshape(16 * slots, width), slot_mine)
    ada_bias_grad = jnp.sum(slot_mine.astype(f32), axis=0)
    row_count = width // 16

    def columns(tiles):
        return tiles.reshape(-1, row_count, LANES).transpose(1, 0, 2).reshape(row_count, -1)

    def rows(tiles, height):
        return tiles.reshape(-1, height, tiles.shape[-1]).transpose(0, 2, 1).reshape(-1, height)

    down_tiles = local_hidden // TILE
    sum_down = rows(first_sum[:down_tiles], row_count)
    sum_up = columns(first_sum[down_tiles:])
    qkv_tiles = qkv_cols // TILE
    sum_qkv = columns(second_sum[:qkv_tiles])[:, : 3 * local_cols].reshape(row_count, 3, local_cols)
    sum_out = rows(second_sum[qkv_tiles:], row_count)[:local_cols]
    mid_tiles = proj_mid.shape[0] // TILE
    in_tiles = -(-width // TILE)
    sum_mid = rows(proj_sum[:mid_tiles], proj_sum.shape[1])
    sum_in = rows(proj_sum[mid_tiles : mid_tiles + in_tiles], proj_sum.shape[1])[:width]
    last_share = proj_last.shape[1] // 32
    last_tiles = proj_sum[mid_tiles + in_tiles :]
    last_tiles = last_tiles.reshape(last_tiles.shape[0] * 2, -1, TILE)[:, :last_share]
    sum_last = rows(last_tiles, last_share)
    found = []
    offset = 0
    for piece in pieces:
        found.append(sums[offset : offset + piece.shape[0]])
        offset += piece.shape[0]
    qv_grad = lax.dynamic_slice_in_dim(found[0].reshape(2, width), x * local_cols, local_cols, axis=1)
    up_bias_grad = lax.dynamic_slice_in_dim(found[1], x * local_hidden, local_hidden, axis=0)

    block_out = swap(block_low)
    tokens_out = swap(flat(grad_tokens).astype(bf16))
    return (
        block_out,
        tokens_out.astype(f32),
        grad_condition,
        grad_ada,
        ada_bias_grad,
        sum_qkv,
        qv_grad,
        sum_out,
        found[2],
        sum_up,
        up_bias_grad,
        sum_down,
        found[3],
        sum_in,
        found[4],
        sum_mid,
        found[5],
        sum_last,
        found[6],
    )


def solution(mesh):
    in_specs = (
        P(("dp", "tensor"), None),
        P("dp", None),
        P(),
        P(),
        P(None, None, "tensor"),
        P(None, "tensor"),
        P("tensor", None),
        P(),
        P(None, "tensor"),
        P("tensor"),
        P("tensor", None),
        P(),
        P(),
        P(),
        P(),
        P(),
        P(),
        P(),
        P("dp", None),
        P("dp"),
        P(("dp", "tensor")),
        P(("dp", "tensor"), None),
    )
    out_specs = (
        P(("dp", "tensor"), None),
        P(("dp", "tensor"), None),
        P("dp", None),
        P(None, ("dp", "tensor")),
        P(("dp", "tensor")),
        P("dp", None, "tensor"),
        P(None, "tensor"),
        P("tensor", "dp"),
        P(),
        P("dp", "tensor"),
        P("tensor"),
        P("tensor", "dp"),
        P(),
        P(None, ("dp", "tensor")),
        P(),
        P(None, ("dp", "tensor")),
        P(),
        P(None, ("dp", "tensor")),
        P(),
    )
    paired = mesh.shape["tensor"] == 2 and mesh.shape["dp"] == 16
    body = paired_shards if paired else shards
    return jax.shard_map(body, mesh=mesh, in_specs=in_specs, out_specs=out_specs, check_vma=False)
```
